512 devices in a mesh: tok: 32 (over z, core), feat: 16 (over y, x).
Axes of the slice: x: 4, y: 4, z: 16, core: 2. Of those that a mesh axis runs over, the one named last changes fastest.
Arguments:
- tokens: bfloat16 [12288, 1408], P(('tok', 'feat')), may hold values from -24 to 24
- segment_ids: int32 [12288], P('tok'), may hold values from 0 to 1023, as said below
- owners: int32 [1024], P('tok'), may hold values from 0 to 31, as said below
- project_in: bfloat16 [1408, 3, 1408], P(None, None, 'feat'), may hold values from -2 to 2
- project_out: bfloat16 [1408, 1408], P('feat'), may hold values from -0.15625 to 0.15625
- weight_up: bfloat16 [1408, 6144], P('tok', 'feat'), may hold values from -0.15625 to 0.15625
- weight_down: bfloat16 [6144, 1408], P('feat', 'tok'), may hold values from -0.078125 to 0.078125
- weight_merge: bfloat16 [5632, 4096], P(None, 'feat'), may hold values from -0.078125 to 0.078125
- gain_attend: bfloat16 [1408], replicated, may hold values from 0.25 to 1.75
- gain_hidden: bfloat16 [1408], replicated, may hold values from 0.25 to 1.75
- gain_final: bfloat16 [1408], replicated, may hold values from 0.25 to 1.75
Outputs:
- routed: bfloat16 [16384, 4096], P('tok', 'feat')
The draws below stay inside these ranges and needn't reach their ends.
Inputs may be any that keep to these rules, and one draw needn't show every extreme that they name: `segment_ids`: patches 384 * s to 384 * s + 383 form shard s; their ids never fall, run without gaps and lie in 32 * s to 32 * s + 31; in every shard but the last they start at 32 * s, in the last they end at 1023. Every segment has 16 to 64 patches, a multiple of 4, and every shard holds one of 64 patches. Each 2x2 window of an image is four consecutive patches. owners[g] is the tok index that owns segment g; the 32 entries from 32 * s to 32 * s + 31 are distinct.
All inputs are finite; a program needn't handle non-finite values.
Results may differ from the reference program's by a relative error of at most 0.025.
Values may be sent and summed in bfloat16 or wider, within the bound.
A program may use at most 64 MiB of HBM per device.

```python
import jax
import jax.numpy as jnp
from jax import lax

D = 1408
HEADS = 16
FF = 6144
OUT = 4096
TOK_DEV = 384
TOKENS = 12288
UNITS = 96
HEAD_DIM = 88
SEG_LEAST = 4
SEG_MOST = 16
SEGS = 1024
N_TOK = 32
N_FEAT = 16


def draw_tokens(key, part):
    base_key = jax.random.fold_in(key, 101)
    key_cols, key_rows, key_vals = jax.random.split(base_key, 3)
    column_scale = 10.0 ** jax.random.uniform(key_cols, (1, D), jnp.float32, -0.5, 0.5)
    row_scale = 10.0 ** jax.random.uniform(key_rows, (TOKENS, 1), jnp.float32, -0.5, 0.5)
    values = jax.random.truncated_normal(key_vals, -4.0, 4.0, (TOKENS, D), jnp.float32)
    return (0.5 * values * row_scale * column_scale).astype(jnp.bfloat16)


def draw_project_in(key, part):
    base_key = jax.random.fold_in(key, 202)
    key_shared = jax.random.fold_in(base_key, 0)
    fan_scale = D ** (-0.5)
    stacked = jax.random.truncated_normal(key_shared, -5.0, 5.0, (D, 3, D), jnp.float32) * fan_scale
    return jnp.clip(stacked, -2.0, 2.0).astype(jnp.bfloat16)


def segment_plan(key):
    base_key = jax.random.fold_in(key, 811)
    merged_units = TOK_DEV // 4
    least_units = SEG_LEAST
    most_units = SEG_MOST
    forced_cap = max(0, (merged_units - least_units) // most_units - 1)
    star_owner = jax.random.randint(jax.random.fold_in(base_key, 1), (), 0, N_TOK, dtype=jnp.int32)

    def one_shard(shard_index):
        shard_key = jax.random.fold_in(base_key, shard_index + 7)
        length_key, place_key, owner_key = jax.random.split(shard_key, 3)
        wanted = jax.random.randint(length_key, (N_TOK,), least_units, most_units + 1, dtype=jnp.int32)
        forced = jax.random.randint(place_key, (), 0, forced_cap + 1, dtype=jnp.int32)
        step_index = jnp.arange(N_TOK, dtype=jnp.int32)
        wanted = jnp.where(step_index == forced, most_units, wanted)

        def take_step(left_over, wanted_len):
            taken_len = jnp.where(left_over == 0, 0, jnp.where(left_over <= most_units, left_over, jnp.minimum(wanted_len, left_over - least_units)))
            return (left_over - taken_len, taken_len)
        remaining, lengths = lax.scan(take_step, jnp.int32(merged_units), wanted)
        segment_count = jnp.sum((lengths > 0).astype(jnp.int32))
        id_shift = jnp.where(shard_index == N_TOK - 1, N_TOK - segment_count, 0).astype(jnp.int32)
        segment_ends = jnp.cumsum(lengths).astype(jnp.int32)
        unit_index = jnp.arange(merged_units, dtype=jnp.int32)
        local_ids = jnp.sum((segment_ends[None, :] <= unit_index[:, None]).astype(jnp.int32), axis=1)
        shuffled = jax.random.permutation(owner_key, N_TOK).astype(jnp.int32)
        rotated = shuffled[(step_index - id_shift - forced) % N_TOK]
        owner_list = (star_owner + rotated - shuffled[0]) % N_TOK
        patch_ids = jnp.repeat(shard_index * N_TOK + id_shift + local_ids, 4)
        return (patch_ids.astype(jnp.int32), owner_list.astype(jnp.int32))
    patch_ids, owner_list = jax.vmap(one_shard)(jnp.arange(N_TOK, dtype=jnp.int32))
    return (patch_ids.reshape(TOKENS), owner_list.reshape(SEGS))


def draw_segment_ids(key, part):
    return segment_plan(key)[0]


def draw_owners(key, part):
    return segment_plan(key)[1]


def shard_levels(stream_key, extent, shards, low, largest):
    def one(dim, shards_of):
        draws = jax.random.uniform(jax.random.fold_in(jax.random.fold_in(stream_key, 6), dim), (shards_of,), jnp.float32, low / len(shards), largest / len(shards))
        return jnp.repeat(jnp.exp(draws), extent[dim] // shards_of).reshape((-1,) + (1,) * (len(extent) - dim - 1))

    gain = one(*shards[0])
    for cut in shards[1:]:
        gain = gain * one(*cut)
    return gain


def normal_values(rng, shape, scale, limit, shards=(), held_as=jnp.bfloat16):
    level = shard_levels(rng, shape, shards, -0.22, 0.18) if shards else 1.0
    values = jax.random.normal(rng, shape, jnp.float32) * scale * level
    return jnp.minimum(jnp.maximum(values, -limit), limit).astype(held_as)


def setup_inputs(seed: int = 0) -> dict:
    arg_keys = jax.random.split(jax.random.key(seed), 12)
    return {
        "tokens": draw_tokens(jax.random.fold_in(arg_keys[11], 71), 0),
        "segment_ids": draw_segment_ids(jax.random.fold_in(arg_keys[11], 71), 0),
        "owners": draw_owners(jax.random.fold_in(arg_keys[11], 71), 0),
        "project_in": draw_project_in(jax.random.fold_in(arg_keys[11], 71), 0),
        "project_out": normal_values(arg_keys[4], (D, D), D ** -0.5, 0.15625, ((0, 16),)),
        "weight_up": normal_values(arg_keys[5], (D, FF), D ** -0.5, 0.15625, ((0, 32), (1, 16))),
        "weight_down": normal_values(arg_keys[6], (FF, D), FF ** -0.5, 0.078125, ((0, 16), (1, 32))),
        "weight_merge": normal_values(arg_keys[7], (4 * D, OUT), (4 * D) ** -0.5, 0.078125, ((1, 16),)),
        "gain_attend": jnp.clip(1.0 + 0.15 * jax.random.normal(arg_keys[8], (D,), jnp.float32), 0.25, 1.75).astype(jnp.bfloat16),
        "gain_hidden": jnp.clip(1.0 + 0.15 * jax.random.normal(arg_keys[9], (D,), jnp.float32), 0.25, 1.75).astype(jnp.bfloat16),
        "gain_final": jnp.clip(1.0 + 0.15 * jax.random.normal(arg_keys[10], (D,), jnp.float32), 0.25, 1.75).astype(jnp.bfloat16),
    }


epsilon = 1e-06

def layer_norm(row_block, gain_row):
    as_float = row_block.astype(jnp.float32)
    center = lax.optimization_barrier(jnp.mean(as_float, axis=-1, keepdims=True))
    spread = lax.optimization_barrier(jnp.mean(jnp.square(as_float - center), axis=-1, keepdims=True))
    scaled = (as_float - center) * lax.rsqrt(spread + epsilon) * gain_row.astype(jnp.float32)
    return scaled.astype(jnp.bfloat16)

def grouped_sum(left_rows, right_rows, groups):
    row_count = left_rows.shape[0]
    group_width = left_rows.shape[1] // groups
    left_blocks = left_rows.reshape(row_count, groups, group_width).astype(jnp.float32)
    right_blocks = right_rows.reshape(groups, group_width, right_rows.shape[1]).astype(jnp.float32)
    partial_terms = jnp.einsum('rgk,gkd->grd', left_blocks, right_blocks).astype(jnp.bfloat16)
    partial_terms = lax.optimization_barrier(partial_terms)
    return lax.optimization_barrier(jnp.sum(partial_terms.astype(jnp.float32), axis=0))

def encode_shard(row_block, shard_ids, project_in, project_out, weight_up, weight_down, weight_merge, gain_attend, gain_hidden, gain_final):
    token_count = row_block.shape[0]
    normed = layer_norm(row_block, gain_attend)
    projected = jnp.dot(normed, project_in.reshape(D, 3 * D), preferred_element_type=jnp.float32)
    projected = projected.reshape(token_count, 3, HEADS, HEAD_DIM)
    queries = (projected[:, 0] * HEAD_DIM ** (-0.5)).astype(jnp.bfloat16)
    keys_all = projected[:, 1].astype(jnp.bfloat16)
    values_all = projected[:, 2].astype(jnp.bfloat16)
    scores = jnp.einsum('qhd,khd->hqk', queries.astype(jnp.float32), keys_all.astype(jnp.float32))
    same_segment = shard_ids[:, None] == shard_ids[None, :]
    scores = jnp.where(same_segment[None, :, :], scores, -1e+30)
    highest = lax.optimization_barrier(jnp.max(scores, axis=-1, keepdims=True))
    raised = jnp.exp(scores - highest)
    weights_soft = (raised / lax.optimization_barrier(jnp.sum(raised, axis=-1, keepdims=True))).astype(jnp.bfloat16)
    attended = jnp.einsum('hqk,khd->qhd', weights_soft.astype(jnp.float32), values_all.astype(jnp.float32)).astype(jnp.bfloat16)
    attention_sum = grouped_sum(attended.reshape(token_count, D), project_out, N_FEAT)
    second = (row_block.astype(jnp.float32) + attention_sum).astype(jnp.bfloat16)
    normed_hidden = layer_norm(second, gain_hidden)
    hidden = jax.nn.gelu(jnp.dot(normed_hidden, weight_up, preferred_element_type=jnp.float32), approximate=False).astype(jnp.bfloat16)
    residual_out = (second.astype(jnp.float32) + grouped_sum(hidden, weight_down, N_FEAT)).astype(jnp.bfloat16)
    normed_final = layer_norm(residual_out, gain_final)
    merged = normed_final.reshape(token_count // 4, 4 * D)
    return jnp.dot(merged, weight_merge, preferred_element_type=jnp.float32).astype(jnp.bfloat16)

def reference(tokens, segment_ids, owners, project_in, project_out, weight_up, weight_down, weight_merge, gain_attend, gain_hidden, gain_final):
    shard_rows = tokens.reshape(N_TOK, TOK_DEV, D)
    shard_ids = segment_ids.reshape(N_TOK, TOK_DEV)

    def encode_pair(pair_in):
        return encode_shard(pair_in[0], pair_in[1], project_in, project_out, weight_up, weight_down, weight_merge, gain_attend, gain_hidden, gain_final)
    embedded = lax.map(encode_pair, (shard_rows, shard_ids)).reshape(N_TOK * UNITS, OUT)
    first_ids = segment_ids.reshape(N_TOK * UNITS, 4)[:, 0]
    owner_of = owners[first_ids]
    positions = jnp.arange(N_TOK * UNITS, dtype=jnp.int32)
    is_start = jnp.concatenate([jnp.ones((1,), dtype=jnp.bool_), first_ids[1:] != first_ids[:-1]])
    starts = lax.cummax(jnp.where(is_start, positions, 0), axis=0)
    target = (owner_of * N_TOK + positions // UNITS) * SEG_MOST + (positions - starts)
    routed = jnp.zeros((N_TOK * N_TOK * SEG_MOST, OUT), jnp.bfloat16)
    return routed.at[target].set(embedded)
```

```python
import functools
import jax
import jax.numpy as jnp
from jax import lax
from jax.experimental import pallas as pl
from jax.experimental.pallas import tpu as pltpu
from jax.sharding import PartitionSpec as P


def _greet(peers, tok_index):
    barrier = pltpu.get_barrier_semaphore()
    for peer in peers:
        pl.semaphore_signal(barrier, inc=1, device_id=(tok_index, peer), device_id_type=MESH)
    pl.semaphore_wait(barrier, len(peers))


def _gather_kernel(n, row_ref, out_ref, send_sem, recv_sem):
    me = lax.axis_index("feat")
    tok_index = lax.axis_index("tok")
    peers = [lax.rem(me + d, n) for d in range(1, n)]
    _greet(peers, tok_index)
    for peer in peers:
        pltpu.make_async_remote_copy(
            src_ref=row_ref, dst_ref=out_ref.at[me], send_sem=send_sem.at[peer],
            recv_sem=recv_sem.at[me], device_id=(tok_index, peer), device_id_type=MESH,
        ).start()
    out_ref[me] = row_ref[...]
    for peer in peers:
        pltpu.make_async_remote_copy(
            src_ref=row_ref, dst_ref=out_ref.at[peer], send_sem=send_sem.at[peer],
            recv_sem=recv_sem.at[peer], device_id=(tok_index, peer), device_id_type=MESH,
        ).wait_recv()
    for peer in peers:
        pltpu.make_async_remote_copy(
            src_ref=row_ref, dst_ref=out_ref.at[me], send_sem=send_sem.at[peer],
            recv_sem=recv_sem.at[me], device_id=(tok_index, peer), device_id_type=MESH,
        ).wait_send()


def gather_feat(row_block, n, collective_id):
    rows, width = row_block.shape
    return pl.pallas_call(
        functools.partial(_gather_kernel, n),
        out_shape=jax.ShapeDtypeStruct((n, rows, width), row_block.dtype),
        in_specs=[pl.BlockSpec(memory_space=pltpu.VMEM)],
        out_specs=pl.BlockSpec(memory_space=pltpu.VMEM),
        scratch_shapes=[pltpu.SemaphoreType.DMA((n,)), pltpu.SemaphoreType.DMA((n,))],
        compiler_params=pltpu.CompilerParams(collective_id=collective_id, has_side_effects=True),
    )(row_block).reshape(n * rows, width)


def _scatter_kernel(n, part_ref, out_ref, held, send_sem, recv_sem):
    me = lax.axis_index("feat")
    tok_index = lax.axis_index("tok")
    peers = [lax.rem(me + d, n) for d in range(1, n)]
    _greet(peers, tok_index)
    for peer in peers:
        pltpu.make_async_remote_copy(
            src_ref=part_ref.at[peer], dst_ref=held.at[me], send_sem=send_sem.at[peer],
            recv_sem=recv_sem.at[me], device_id=(tok_index, peer), device_id_type=MESH,
        ).start()
    total = part_ref[me].astype(jnp.float32)
    for peer in peers:
        pltpu.make_async_remote_copy(
            src_ref=part_ref.at[peer], dst_ref=held.at[peer], send_sem=send_sem.at[peer],
            recv_sem=recv_sem.at[peer], device_id=(tok_index, peer), device_id_type=MESH,
        ).wait_recv()
        total = total + held[peer].astype(jnp.float32)
    out_ref[...] = total
    for peer in peers:
        pltpu.make_async_remote_copy(
            src_ref=part_ref.at[peer], dst_ref=held.at[me], send_sem=send_sem.at[peer],
            recv_sem=recv_sem.at[me], device_id=(tok_index, peer), device_id_type=MESH,
        ).wait_send()


def scatter_feat(parts, n, collective_id):
    _, rows, width = parts.shape
    return pl.pallas_call(
        functools.partial(_scatter_kernel, n),
        out_shape=jax.ShapeDtypeStruct((rows, width), jnp.float32),
        in_specs=[pl.BlockSpec(memory_space=pltpu.VMEM)],
        out_specs=pl.BlockSpec(memory_space=pltpu.VMEM),
        scratch_shapes=[
            pltpu.VMEM((n, rows, width), parts.dtype),
            pltpu.SemaphoreType.DMA((n,)),
            pltpu.SemaphoreType.DMA((n,)),
        ],
        compiler_params=pltpu.CompilerParams(collective_id=collective_id, has_side_effects=True),
    )(parts)

MESH = pl.DeviceIdType.MESH
LEAST_UNITS = 4
MOST_UNITS = 16
HEAD_DIM = 88


epsilon = 1e-06


def layer_norm(row_block, gain_row):
    as_float = row_block.astype(jnp.float32)
    center = jnp.mean(as_float, axis=-1, keepdims=True)
    spread = jnp.mean(jnp.square(as_float - center), axis=-1, keepdims=True)
    scaled = (as_float - center) * lax.rsqrt(spread + epsilon) * gain_row.astype(jnp.float32)
    return scaled.astype(jnp.bfloat16)


def project_rows(row_block, weight_block, collective_id):
    n = lax.axis_size("feat")
    return jnp.dot(
        gather_feat(row_block, n, collective_id),
        weight_block,
        preferred_element_type=jnp.float32,
    )


def scatter_rows(left_rows, right_rows, collective_id):
    n = lax.axis_size("feat")
    parts = jnp.dot(left_rows, right_rows, preferred_element_type=jnp.float32).astype(jnp.bfloat16)
    return scatter_feat(parts.reshape(n, parts.shape[0] // n, parts.shape[1]), n, collective_id)


def early_weights(weight_up, weight_down):
    return (weight_up, weight_down)


def upper_weight(fetched):
    return lax.all_gather(fetched[0], "tok", axis=0, tiled=True)


def lower_weight(fetched):
    return lax.all_gather(fetched[1], "tok", axis=1, tiled=True)


def attend(projected, segment_ids, head_count):
    token_count = projected.shape[0]
    parts_all = projected.reshape(token_count, 3, head_count, HEAD_DIM)
    queries = (parts_all[:, 0] * HEAD_DIM ** (-0.5)).astype(jnp.bfloat16)
    keys_here = parts_all[:, 1].astype(jnp.bfloat16)
    values_here = parts_all[:, 2].astype(jnp.bfloat16)
    scores = jnp.einsum("qhd,khd->hqk", queries, keys_here, preferred_element_type=jnp.float32)
    same_segment = segment_ids[:, None] == segment_ids[None, :]
    scores = jnp.where(same_segment[None, :, :], scores, -1e30)
    highest = jnp.max(scores, axis=-1, keepdims=True)
    raised = jnp.exp(scores - highest)
    weights_soft = (raised / jnp.sum(raised, axis=-1, keepdims=True)).astype(jnp.bfloat16)
    attended = jnp.einsum(
        "hqk,khd->qhd", weights_soft, values_here, preferred_element_type=jnp.float32
    )
    return attended.astype(jnp.bfloat16).reshape(token_count, head_count * HEAD_DIM)


def route_rows(embedded, segment_ids, owners):
    merged_count = embedded.shape[0]
    peer_count = owners.shape[0]
    least_units = max(LEAST_UNITS, (merged_count + peer_count - 1) // peer_count)
    slot_count = max(MOST_UNITS, 2 * least_units)
    first_ids = segment_ids.reshape(merged_count, 4)[:, 0]
    id_base = lax.axis_index("tok") * peer_count
    local_index = first_ids - id_base
    owner_pick = local_index[:, None] == jnp.arange(peer_count, dtype=jnp.int32)[None, :]
    owner_of = jnp.sum(jnp.where(owner_pick, owners[None, :], 0), axis=1)
    row_index = jnp.arange(merged_count, dtype=jnp.int32)
    earlier = (row_index[None, :] < row_index[:, None]) & (first_ids[None, :] == first_ids[:, None])
    within = jnp.sum(earlier.astype(jnp.int32), axis=1)
    target = owner_of * slot_count + within
    select = (
        jnp.arange(peer_count * slot_count, dtype=jnp.int32)[:, None] == target[None, :]
    ).astype(jnp.bfloat16)
    packed = jnp.dot(select, embedded, preferred_element_type=jnp.float32).astype(jnp.bfloat16)
    packed = packed.reshape(peer_count, slot_count, embedded.shape[1])
    received = lax.all_to_all(packed, "tok", split_axis=0, concat_axis=0, tiled=True)
    return received.reshape(peer_count * slot_count, embedded.shape[1])


def body(
    tokens,
    segment_ids,
    owners,
    project_in,
    project_out,
    weight_up,
    weight_down,
    weight_merge,
    gain_attend,
    gain_hidden,
    gain_final,
):
    model_width = tokens.shape[1]
    head_count = project_in.shape[2] // HEAD_DIM
    fetched = early_weights(weight_up, weight_down)
    flat_in = project_in.reshape(model_width, 3 * project_in.shape[2])
    local_count = tokens.shape[0]
    normed = layer_norm(tokens, gain_attend)
    projected = project_rows(normed, flat_in, 0)
    attended = attend(projected, segment_ids, head_count)
    second = (tokens.astype(jnp.float32) + scatter_rows(attended, project_out, 1)).astype(jnp.bfloat16)
    normed_hidden = layer_norm(second, gain_hidden)
    hidden = jax.nn.gelu(
        project_rows(normed_hidden, upper_weight(fetched), 2), approximate=False
    ).astype(jnp.bfloat16)
    residual_out = (
        second.astype(jnp.float32) + scatter_rows(hidden, lower_weight(fetched), 3)
    ).astype(jnp.bfloat16)
    normed_final = layer_norm(residual_out, gain_final)
    merged = normed_final.reshape(local_count // 4, 4 * model_width)
    embedded = project_rows(merged, weight_merge, 4).astype(jnp.bfloat16)
    return route_rows(embedded, segment_ids, owners)


def solution(mesh):
    return jax.shard_map(
        body,
        mesh=mesh,
        in_specs=(
            P(("tok", "feat"), None),
            P("tok"),
            P("tok"),
            P(None, None, "feat"),
            P("feat", None),
            P("tok", "feat"),
            P("feat", "tok"),
            P(None, "feat"),
            P(),
            P(),
            P(),
        ),
        out_specs=P("tok", "feat"),
        check_vma=False,
    )
```

```python
import functools
import jax
import jax.numpy as jnp
from jax import lax
from jax.experimental import pallas as pl
from jax.experimental.pallas import tpu as pltpu
from jax.sharding import PartitionSpec as P


def _greet(peers, tok_index):
    barrier = pltpu.get_barrier_semaphore()
    for peer in peers:
        pl.semaphore_signal(barrier, inc=1, device_id=(tok_index, peer), device_id_type=MESH)
    pl.semaphore_wait(barrier, len(peers))


def _gather_kernel(n, row_ref, out_ref, send_sem, recv_sem):
    me = lax.axis_index("feat")
    tok_index = lax.axis_index("tok")
    peers = [lax.rem(me + d, n) for d in range(1, n)]
    _greet(peers, tok_index)
    for peer in peers:
        pltpu.make_async_remote_copy(
            src_ref=row_ref, dst_ref=out_ref.at[me], send_sem=send_sem.at[peer],
            recv_sem=recv_sem.at[me], device_id=(tok_index, peer), device_id_type=MESH,
        ).start()
    out_ref[me] = row_ref[...]
    for peer in peers:
        pltpu.make_async_remote_copy(
            src_ref=row_ref, dst_ref=out_ref.at[peer], send_sem=send_sem.at[peer],
            recv_sem=recv_sem.at[peer], device_id=(tok_index, peer), device_id_type=MESH,
        ).wait_recv()
    for peer in peers:
        pltpu.make_async_remote_copy(
            src_ref=row_ref, dst_ref=out_ref.at[me], send_sem=send_sem.at[peer],
            recv_sem=recv_sem.at[me], device_id=(tok_index, peer), device_id_type=MESH,
        ).wait_send()


def gather_feat(row_block, n, collective_id):
    rows, width = row_block.shape
    return pl.pallas_call(
        functools.partial(_gather_kernel, n),
        out_shape=jax.ShapeDtypeStruct((n, rows, width), row_block.dtype),
        in_specs=[pl.BlockSpec(memory_space=pltpu.VMEM)],
        out_specs=pl.BlockSpec(memory_space=pltpu.VMEM),
        scratch_shapes=[pltpu.SemaphoreType.DMA((n,)), pltpu.SemaphoreType.DMA((n,))],
        compiler_params=pltpu.CompilerParams(collective_id=collective_id, has_side_effects=True),
    )(row_block).reshape(n * rows, width)


def _ring_gather(x_ref, out_ref, send_right, send_left, send_partner, recv_sem, feat_index):
    tok_count = out_ref.shape[0]
    chips = tok_count // 2
    right_steps = chips // 2
    left_steps = chips - 1 - right_steps
    me = lax.axis_index("tok")
    chip = me // 2
    core = me % 2
    right = lax.rem(chip + 1, chips) * 2 + core
    left = lax.rem(chip + chips - 1, chips) * 2 + core
    partner = chip * 2 + (1 - core)

    def slot_of(offset):
        return lax.rem(chip + offset + 2 * chips, chips) * 2 + core

    def remote(src, slot, sem, target):
        return pltpu.make_async_remote_copy(
            src_ref=src, dst_ref=out_ref.at[slot], send_sem=sem, recv_sem=recv_sem.at[slot],
            device_id=(target, feat_index), device_id_type=MESH,
        )

    sends = []

    def forward_partner(src, slot):
        copy = remote(src, slot, send_partner.at[len(sends_partner)], partner)
        copy.start()
        sends_partner.append(copy)

    sends_partner = []
    out_ref[me] = x_ref[...]
    forward_partner(x_ref, me)
    for step in range(1, right_steps + 1):
        if step == 1:
            src_right = x_ref
            src_left = x_ref
        else:
            from_left = slot_of(-(step - 1))
            remote(x_ref, from_left, send_right.at[0], right).wait_recv()
            forward_partner(out_ref.at[from_left], from_left)
            src_right = out_ref.at[from_left]
            if step - 1 <= left_steps:
                from_right = slot_of(step - 1)
                remote(x_ref, from_right, send_left.at[0], left).wait_recv()
                forward_partner(out_ref.at[from_right], from_right)
                src_left = out_ref.at[from_right]
        copy = remote(src_right, slot_of(-(step - 1)), send_right.at[step - 1], right)
        copy.start()
        sends.append(copy)
        if step <= left_steps:
            copy = remote(src_left, slot_of(step - 1), send_left.at[step - 1], left)
            copy.start()
            sends.append(copy)
    last_left = slot_of(-right_steps)
    remote(x_ref, last_left, send_right.at[0], right).wait_recv()
    forward_partner(out_ref.at[last_left], last_left)
    if left_steps >= 1 and left_steps + 1 > right_steps:
        last_right = slot_of(left_steps)
        remote(x_ref, last_right, send_left.at[0], left).wait_recv()
        forward_partner(out_ref.at[last_right], last_right)
    for other_chip in range(chips):
        remote(x_ref, other_chip * 2 + (1 - core), send_partner.at[0], partner).wait_recv()
    for copy in sends + sends_partner:
        copy.wait_send()


def _first_kernel(n, row_ref, weight_ref, out_ref, weight_out, send_sem, recv_sem,
                  send_right, send_left, send_partner, weight_recv):
    me = lax.axis_index("feat")
    tok_index = lax.axis_index("tok")
    chips = weight_out.shape[0] // 2
    chip = tok_index // 2
    core = tok_index % 2
    peers = [lax.rem(me + d, n) for d in range(1, n)]
    barrier = pltpu.get_barrier_semaphore()
    for peer in peers:
        pl.semaphore_signal(barrier, inc=1, device_id=(tok_index, peer), device_id_type=MESH)
    ring_peers = [
        lax.rem(chip + 1, chips) * 2 + core,
        lax.rem(chip + chips - 1, chips) * 2 + core,
        chip * 2 + (1 - core),
    ]
    for peer in ring_peers:
        pl.semaphore_signal(barrier, inc=1, device_id=(peer, me), device_id_type=MESH)
    pl.semaphore_wait(barrier, len(peers) + len(ring_peers))
    for peer in peers:
        pltpu.make_async_remote_copy(
            src_ref=row_ref, dst_ref=out_ref.at[me], send_sem=send_sem.at[peer],
            recv_sem=recv_sem.at[me], device_id=(tok_index, peer), device_id_type=MESH,
        ).start()
    out_ref[me] = row_ref[...]
    _ring_gather(weight_ref, weight_out, send_right, send_left, send_partner, weight_recv, me)
    for peer in peers:
        pltpu.make_async_remote_copy(
            src_ref=row_ref, dst_ref=out_ref.at[peer], send_sem=send_sem.at[peer],
            recv_sem=recv_sem.at[peer], device_id=(tok_index, peer), device_id_type=MESH,
        ).wait_recv()
    for peer in peers:
        pltpu.make_async_remote_copy(
            src_ref=row_ref, dst_ref=out_ref.at[me], send_sem=send_sem.at[peer],
            recv_sem=recv_sem.at[me], device_id=(tok_index, peer), device_id_type=MESH,
        ).wait_send()


def first_exchange(row_block, weight_block, n, tok_count, collective_id):
    rows, width = row_block.shape
    weight_rows, weight_width = weight_block.shape
    chips = tok_count // 2
    gathered, weights = pl.pallas_call(
        functools.partial(_first_kernel, n),
        out_shape=(
            jax.ShapeDtypeStruct((n, rows, width), row_block.dtype),
            jax.ShapeDtypeStruct((tok_count, weight_rows, weight_width), weight_block.dtype),
        ),
        in_specs=[pl.BlockSpec(memory_space=pltpu.VMEM)] * 2,
        out_specs=(pl.BlockSpec(memory_space=pltpu.VMEM),) * 2,
        scratch_shapes=[
            pltpu.SemaphoreType.DMA((n,)),
            pltpu.SemaphoreType.DMA((n,)),
            pltpu.SemaphoreType.DMA((chips,)),
            pltpu.SemaphoreType.DMA((chips,)),
            pltpu.SemaphoreType.DMA((chips,)),
            pltpu.SemaphoreType.DMA((tok_count,)),
        ],
        compiler_params=pltpu.CompilerParams(collective_id=collective_id, has_side_effects=True),
    )(row_block, weight_block)
    return gathered.reshape(n * rows, width), weights


def _scatter_kernel(n, part_ref, out_ref, held, send_sem, recv_sem):
    me = lax.axis_index("feat")
    tok_index = lax.axis_index("tok")
    peers = [lax.rem(me + d, n) for d in range(1, n)]
    _greet(peers, tok_index)
    for peer in peers:
        pltpu.make_async_remote_copy(
            src_ref=part_ref.at[peer], dst_ref=held.at[me], send_sem=send_sem.at[peer],
            recv_sem=recv_sem.at[me], device_id=(tok_index, peer), device_id_type=MESH,
        ).start()
    total = part_ref[me].astype(jnp.float32)
    for peer in peers:
        pltpu.make_async_remote_copy(
            src_ref=part_ref.at[peer], dst_ref=held.at[peer], send_sem=send_sem.at[peer],
            recv_sem=recv_sem.at[peer], device_id=(tok_index, peer), device_id_type=MESH,
        ).wait_recv()
        total = total + held[peer].astype(jnp.float32)
    out_ref[...] = total
    for peer in peers:
        pltpu.make_async_remote_copy(
            src_ref=part_ref.at[peer], dst_ref=held.at[me], send_sem=send_sem.at[peer],
            recv_sem=recv_sem.at[me], device_id=(tok_index, peer), device_id_type=MESH,
        ).wait_send()


def scatter_feat(parts, n, collective_id):
    _, rows, width = parts.shape
    return pl.pallas_call(
        functools.partial(_scatter_kernel, n),
        out_shape=jax.ShapeDtypeStruct((rows, width), jnp.float32),
        in_specs=[pl.BlockSpec(memory_space=pltpu.VMEM)],
        out_specs=pl.BlockSpec(memory_space=pltpu.VMEM),
        scratch_shapes=[
            pltpu.VMEM((n, rows, width), parts.dtype),
            pltpu.SemaphoreType.DMA((n,)),
            pltpu.SemaphoreType.DMA((n,)),
        ],
        compiler_params=pltpu.CompilerParams(collective_id=collective_id, has_side_effects=True),
    )(parts)

MESH = pl.DeviceIdType.MESH
LEAST_UNITS = 4
MOST_UNITS = 16
HEAD_DIM = 88


epsilon = 1e-06


def layer_norm(row_block, gain_row):
    as_float = row_block.astype(jnp.float32)
    center = jnp.mean(as_float, axis=-1, keepdims=True)
    spread = jnp.mean(jnp.square(as_float - center), axis=-1, keepdims=True)
    scaled = (as_float - center) * lax.rsqrt(spread + epsilon) * gain_row.astype(jnp.float32)
    return scaled.astype(jnp.bfloat16)


def project_rows(row_block, weight_block, collective_id):
    n = lax.axis_size("feat")
    return jnp.dot(
        gather_feat(row_block, n, collective_id),
        weight_block,
        preferred_element_type=jnp.float32,
    )


def scatter_rows(left_rows, right_rows, collective_id):
    n = lax.axis_size("feat")
    parts = jnp.dot(left_rows, right_rows, preferred_element_type=jnp.float32).astype(jnp.bfloat16)
    return scatter_feat(parts.reshape(n, parts.shape[0] // n, parts.shape[1]), n, collective_id)


def early_weights(weight_up, weight_down):
    return (weight_up, weight_down)


def upper_weight(fetched):
    return lax.all_gather(fetched[0], "tok", axis=0, tiled=True)


def lower_weight(fetched):
    return lax.all_gather(fetched[1], "tok", axis=1, tiled=True)


def attend(projected, segment_ids, head_count):
    token_count = projected.shape[0]
    parts_all = projected.reshape(token_count, 3, head_count, HEAD_DIM)
    queries = (parts_all[:, 0] * HEAD_DIM ** (-0.5)).astype(jnp.bfloat16)
    keys_here = parts_all[:, 1].astype(jnp.bfloat16)
    values_here = parts_all[:, 2].astype(jnp.bfloat16)
    scores = jnp.einsum("qhd,khd->hqk", queries, keys_here, preferred_element_type=jnp.float32)
    same_segment = segment_ids[:, None] == segment_ids[None, :]
    scores = jnp.where(same_segment[None, :, :], scores, -1e30)
    highest = jnp.max(scores, axis=-1, keepdims=True)
    raised = jnp.exp(scores - highest)
    weights_soft = (raised / jnp.sum(raised, axis=-1, keepdims=True)).astype(jnp.bfloat16)
    attended = jnp.einsum(
        "hqk,khd->qhd", weights_soft, values_here, preferred_element_type=jnp.float32
    )
    return attended.astype(jnp.bfloat16).reshape(token_count, head_count * HEAD_DIM)


def route_rows(embedded, segment_ids, owners):
    merged_count = embedded.shape[0]
    peer_count = owners.shape[0]
    least_units = max(LEAST_UNITS, (merged_count + peer_count - 1) // peer_count)
    slot_count = max(MOST_UNITS, 2 * least_units)
    first_ids = segment_ids.reshape(merged_count, 4)[:, 0]
    id_base = lax.axis_index("tok") * peer_count
    local_index = first_ids - id_base
    owner_pick = local_index[:, None] == jnp.arange(peer_count, dtype=jnp.int32)[None, :]
    owner_of = jnp.sum(jnp.where(owner_pick, owners[None, :], 0), axis=1)
    row_index = jnp.arange(merged_count, dtype=jnp.int32)
    earlier = (row_index[None, :] < row_index[:, None]) & (first_ids[None, :] == first_ids[:, None])
    within = jnp.sum(earlier.astype(jnp.int32), axis=1)
    target = owner_of * slot_count + within
    select = (
        jnp.arange(peer_count * slot_count, dtype=jnp.int32)[:, None] == target[None, :]
    ).astype(jnp.bfloat16)
    packed = jnp.dot(select, embedded, preferred_element_type=jnp.float32).astype(jnp.bfloat16)
    packed = packed.reshape(peer_count, slot_count, embedded.shape[1])
    received = lax.all_to_all(packed, "tok", split_axis=0, concat_axis=0, tiled=True)
    return received.reshape(peer_count * slot_count, embedded.shape[1])


def body(
    tokens,
    segment_ids,
    owners,
    project_in,
    project_out,
    weight_up,
    weight_down,
    weight_merge,
    gain_attend,
    gain_hidden,
    gain_final,
):
    model_width = tokens.shape[1]
    head_count = project_in.shape[2] // HEAD_DIM
    units = weight_up.shape[1]
    feat_count = lax.axis_size("feat")
    tok_count = lax.axis_size("tok")
    flat_in = project_in.reshape(model_width, 3 * project_in.shape[2])
    local_count = tokens.shape[0]
    normed = layer_norm(tokens, gain_attend)
    stacked = jnp.concatenate([weight_up, weight_down.T], axis=1)
    gathered, weights = first_exchange(normed, stacked, feat_count, tok_count, 0)
    upper = weights[:, :, :units].reshape(tok_count * weight_up.shape[0], units)
    lower_t = weights[:, :, units:].reshape(tok_count * weight_up.shape[0], units)
    projected = jnp.dot(gathered, flat_in, preferred_element_type=jnp.float32)
    attended = attend(projected, segment_ids, head_count)
    second = (tokens.astype(jnp.float32) + scatter_rows(attended, project_out, 1)).astype(jnp.bfloat16)
    normed_hidden = layer_norm(second, gain_hidden)
    hidden = jax.nn.gelu(
        project_rows(normed_hidden, upper, 2), approximate=False
    ).astype(jnp.bfloat16)
    down_parts = lax.dot_general(
        hidden, lower_t, (((1,), (1,)), ((), ())), preferred_element_type=jnp.float32
    ).astype(jnp.bfloat16)
    mlp_sum = scatter_feat(
        down_parts.reshape(feat_count, down_parts.shape[0] // feat_count, down_parts.shape[1]),
        feat_count,
        3,
    )
    residual_out = (second.astype(jnp.float32) + mlp_sum).astype(jnp.bfloat16)
    normed_final = layer_norm(residual_out, gain_final)
    merged = normed_final.reshape(local_count // 4, 4 * model_width)
    embedded = project_rows(merged, weight_merge, 4).astype(jnp.bfloat16)
    return route_rows(embedded, segment_ids, owners)


def solution(mesh):
    return jax.shard_map(
        body,
        mesh=mesh,
        in_specs=(
            P(("tok", "feat"), None),
            P("tok"),
            P("tok"),
            P(None, None, "feat"),
            P("feat", None),
            P("tok", "feat"),
            P("feat", "tok"),
            P(None, "feat"),
            P(),
            P(),
            P(),
        ),
        out_specs=P("tok", "feat"),
        check_vma=False,
    )
```

```python
import functools
import jax
import jax.numpy as jnp
from jax import lax
from jax.experimental import pallas as pl
from jax.experimental.pallas import tpu as pltpu
from jax.sharding import PartitionSpec as P


def _greet(peers, tok_index):
    barrier = pltpu.get_barrier_semaphore()
    for peer in peers:
        pl.semaphore_signal(barrier, inc=1, device_id=(tok_index, peer), device_id_type=MESH)
    pl.semaphore_wait(barrier, len(peers))


def _gather_kernel(n, row_ref, out_ref, send_sem, recv_sem):
    me = lax.axis_index("feat")
    tok_index = lax.axis_index("tok")
    peers = [lax.rem(me + d, n) for d in range(1, n)]
    _greet(peers, tok_index)
    for peer in peers:
        pltpu.make_async_remote_copy(
            src_ref=row_ref, dst_ref=out_ref.at[me], send_sem=send_sem.at[peer],
            recv_sem=recv_sem.at[me], device_id=(tok_index, peer), device_id_type=MESH,
        ).start()
    out_ref[me] = row_ref[...]
    for peer in peers:
        pltpu.make_async_remote_copy(
            src_ref=row_ref, dst_ref=out_ref.at[peer], send_sem=send_sem.at[peer],
            recv_sem=recv_sem.at[peer], device_id=(tok_index, peer), device_id_type=MESH,
        ).wait_recv()
    for peer in peers:
        pltpu.make_async_remote_copy(
            src_ref=row_ref, dst_ref=out_ref.at[me], send_sem=send_sem.at[peer],
            recv_sem=recv_sem.at[me], device_id=(tok_index, peer), device_id_type=MESH,
        ).wait_send()


def gather_feat(row_block, n, collective_id):
    rows, width = row_block.shape
    return pl.pallas_call(
        functools.partial(_gather_kernel, n),
        out_shape=jax.ShapeDtypeStruct((n, rows, width), row_block.dtype),
        in_specs=[pl.BlockSpec(memory_space=pltpu.VMEM)],
        out_specs=pl.BlockSpec(memory_space=pltpu.VMEM),
        scratch_shapes=[pltpu.SemaphoreType.DMA((n,)), pltpu.SemaphoreType.DMA((n,))],
        compiler_params=pltpu.CompilerParams(collective_id=collective_id, has_side_effects=True),
    )(row_block).reshape(n * rows, width)


def _ring_gather(x_ref, out_ref, send_right, send_left, send_partner, recv_sem, feat_index):
    tok_count = out_ref.shape[0]
    chips = tok_count // 2
    right_steps = chips // 2
    left_steps = chips - 1 - right_steps
    me = lax.axis_index("tok")
    chip = me // 2
    core = me % 2
    right = lax.rem(chip + 1, chips) * 2 + core
    left = lax.rem(chip + chips - 1, chips) * 2 + core
    partner = chip * 2 + (1 - core)

    def slot_of(offset):
        return lax.rem(chip + offset + 2 * chips, chips) * 2 + core

    def remote(src, slot, sem, target):
        return pltpu.make_async_remote_copy(
            src_ref=src, dst_ref=out_ref.at[slot], send_sem=sem, recv_sem=recv_sem.at[slot],
            device_id=(target, feat_index), device_id_type=MESH,
        )

    sends = []

    def forward_partner(src, slot):
        copy = remote(src, slot, send_partner.at[len(sends_partner)], partner)
        copy.start()
        sends_partner.append(copy)

    sends_partner = []
    out_ref[me] = x_ref[...]
    forward_partner(x_ref, me)
    for step in range(1, right_steps + 1):
        if step == 1:
            src_right = x_ref
            src_left = x_ref
        else:
            from_left = slot_of(-(step - 1))
            remote(x_ref, from_left, send_right.at[0], right).wait_recv()
            forward_partner(out_ref.at[from_left], from_left)
            src_right = out_ref.at[from_left]
            if step - 1 <= left_steps:
                from_right = slot_of(step - 1)
                remote(x_ref, from_right, send_left.at[0], left).wait_recv()
                forward_partner(out_ref.at[from_right], from_right)
                src_left = out_ref.at[from_right]
        copy = remote(src_right, slot_of(-(step - 1)), send_right.at[step - 1], right)
        copy.start()
        sends.append(copy)
        if step <= left_steps:
            copy = remote(src_left, slot_of(step - 1), send_left.at[step - 1], left)
            copy.start()
            sends.append(copy)
    last_left = slot_of(-right_steps)
    remote(x_ref, last_left, send_right.at[0], right).wait_recv()
    forward_partner(out_ref.at[last_left], last_left)
    if left_steps >= 1 and left_steps + 1 > right_steps:
        last_right = slot_of(left_steps)
        remote(x_ref, last_right, send_left.at[0], left).wait_recv()
        forward_partner(out_ref.at[last_right], last_right)
    for other_chip in range(chips):
        remote(x_ref, other_chip * 2 + (1 - core), send_partner.at[0], partner).wait_recv()
    for copy in sends + sends_partner:
        copy.wait_send()


def _first_kernel(n, row_ref, weight_ref, out_ref, weight_out, send_sem, recv_sem,
                  send_right, send_left, send_partner, weight_recv):
    me = lax.axis_index("feat")
    tok_index = lax.axis_index("tok")
    chips = weight_out.shape[0] // 2
    chip = tok_index // 2
    core = tok_index % 2
    peers = [lax.rem(me + d, n) for d in range(1, n)]
    barrier = pltpu.get_barrier_semaphore()
    for peer in peers:
        pl.semaphore_signal(barrier, inc=1, device_id=(tok_index, peer), device_id_type=MESH)
    ring_peers = [
        lax.rem(chip + 1, chips) * 2 + core,
        lax.rem(chip + chips - 1, chips) * 2 + core,
        chip * 2 + (1 - core),
    ]
    for peer in ring_peers:
        pl.semaphore_signal(barrier, inc=1, device_id=(peer, me), device_id_type=MESH)
    pl.semaphore_wait(barrier, len(peers) + len(ring_peers))
    for peer in peers:
        pltpu.make_async_remote_copy(
            src_ref=row_ref, dst_ref=out_ref.at[me], send_sem=send_sem.at[peer],
            recv_sem=recv_sem.at[me], device_id=(tok_index, peer), device_id_type=MESH,
        ).start()
    out_ref[me] = row_ref[...]
    _ring_gather(weight_ref, weight_out, send_right, send_left, send_partner, weight_recv, me)
    for peer in peers:
        pltpu.make_async_remote_copy(
            src_ref=row_ref, dst_ref=out_ref.at[peer], send_sem=send_sem.at[peer],
            recv_sem=recv_sem.at[peer], device_id=(tok_index, peer), device_id_type=MESH,
        ).wait_recv()
    for peer in peers:
        pltpu.make_async_remote_copy(
            src_ref=row_ref, dst_ref=out_ref.at[me], send_sem=send_sem.at[peer],
            recv_sem=recv_sem.at[me], device_id=(tok_index, peer), device_id_type=MESH,
        ).wait_send()


def first_exchange(row_block, weight_block, n, tok_count, collective_id):
    rows, width = row_block.shape
    weight_rows, weight_width = weight_block.shape
    chips = tok_count // 2
    gathered, weights = pl.pallas_call(
        functools.partial(_first_kernel, n),
        out_shape=(
            jax.ShapeDtypeStruct((n, rows, width), row_block.dtype),
            jax.ShapeDtypeStruct((tok_count, weight_rows, weight_width), weight_block.dtype),
        ),
        in_specs=[pl.BlockSpec(memory_space=pltpu.VMEM)] * 2,
        out_specs=(pl.BlockSpec(memory_space=pltpu.VMEM),) * 2,
        scratch_shapes=[
            pltpu.SemaphoreType.DMA((n,)),
            pltpu.SemaphoreType.DMA((n,)),
            pltpu.SemaphoreType.DMA((chips,)),
            pltpu.SemaphoreType.DMA((chips,)),
            pltpu.SemaphoreType.DMA((chips,)),
            pltpu.SemaphoreType.DMA((tok_count,)),
        ],
        compiler_params=pltpu.CompilerParams(collective_id=collective_id, has_side_effects=True),
    )(row_block, weight_block)
    return gathered.reshape(n * rows, width), weights


def _scatter_kernel(n, part_ref, out_ref, held, send_sem, recv_sem):
    me = lax.axis_index("feat")
    tok_index = lax.axis_index("tok")
    peers = [lax.rem(me + d, n) for d in range(1, n)]
    _greet(peers, tok_index)
    for peer in peers:
        pltpu.make_async_remote_copy(
            src_ref=part_ref.at[peer], dst_ref=held.at[me], send_sem=send_sem.at[peer],
            recv_sem=recv_sem.at[me], device_id=(tok_index, peer), device_id_type=MESH,
        ).start()
    total = part_ref[me].astype(jnp.float32)
    for peer in peers:
        pltpu.make_async_remote_copy(
            src_ref=part_ref.at[peer], dst_ref=held.at[peer], send_sem=send_sem.at[peer],
            recv_sem=recv_sem.at[peer], device_id=(tok_index, peer), device_id_type=MESH,
        ).wait_recv()
        total = total + held[peer].astype(jnp.float32)
    out_ref[...] = total
    for peer in peers:
        pltpu.make_async_remote_copy(
            src_ref=part_ref.at[peer], dst_ref=held.at[me], send_sem=send_sem.at[peer],
            recv_sem=recv_sem.at[me], device_id=(tok_index, peer), device_id_type=MESH,
        ).wait_send()


def scatter_feat(parts, n, collective_id):
    _, rows, width = parts.shape
    return pl.pallas_call(
        functools.partial(_scatter_kernel, n),
        out_shape=jax.ShapeDtypeStruct((rows, width), jnp.float32),
        in_specs=[pl.BlockSpec(memory_space=pltpu.VMEM)],
        out_specs=pl.BlockSpec(memory_space=pltpu.VMEM),
        scratch_shapes=[
            pltpu.VMEM((n, rows, width), parts.dtype),
            pltpu.SemaphoreType.DMA((n,)),
            pltpu.SemaphoreType.DMA((n,)),
        ],
        compiler_params=pltpu.CompilerParams(collective_id=collective_id, has_side_effects=True),
    )(parts)

MESH = pl.DeviceIdType.MESH
LEAST_UNITS = 4
MOST_UNITS = 16
HEAD_DIM = 88


epsilon = 1e-06


def layer_norm(row_block, gain_row):
    as_float = row_block.astype(jnp.float32)
    center = jnp.mean(as_float, axis=-1, keepdims=True)
    spread = jnp.mean(jnp.square(as_float - center), axis=-1, keepdims=True)
    scaled = (as_float - center) * lax.rsqrt(spread + epsilon) * gain_row.astype(jnp.float32)
    return scaled.astype(jnp.bfloat16)


def project_rows(row_block, weight_block, collective_id):
    n = lax.axis_size("feat")
    return jnp.dot(
        gather_feat(row_block, n, collective_id),
        weight_block,
        preferred_element_type=jnp.float32,
    )


def scatter_rows(left_rows, right_rows, collective_id):
    n = lax.axis_size("feat")
    parts = jnp.dot(left_rows, right_rows, preferred_element_type=jnp.float32).astype(jnp.bfloat16)
    return scatter_feat(parts.reshape(n, parts.shape[0] // n, parts.shape[1]), n, collective_id)


def early_weights(weight_up, weight_down):
    return (weight_up, weight_down)


def upper_weight(fetched):
    return lax.all_gather(fetched[0], "tok", axis=0, tiled=True)


def lower_weight(fetched):
    return lax.all_gather(fetched[1], "tok", axis=1, tiled=True)


def attend(projected, segment_ids, head_count):
    token_count = projected.shape[0]
    parts_all = projected.reshape(token_count, 3, head_count, HEAD_DIM)
    queries = (parts_all[:, 0] * HEAD_DIM ** (-0.5)).astype(jnp.bfloat16)
    keys_here = parts_all[:, 1].astype(jnp.bfloat16)
    values_here = parts_all[:, 2].astype(jnp.bfloat16)
    scores = jnp.einsum("qhd,khd->hqk", queries, keys_here, preferred_element_type=jnp.float32)
    same_segment = segment_ids[:, None] == segment_ids[None, :]
    scores = jnp.where(same_segment[None, :, :], scores, -1e30)
    highest = jnp.max(scores, axis=-1, keepdims=True)
    raised = jnp.exp(scores - highest)
    weights_soft = (raised / jnp.sum(raised, axis=-1, keepdims=True)).astype(jnp.bfloat16)
    attended = jnp.einsum(
        "hqk,khd->qhd", weights_soft, values_here, preferred_element_type=jnp.float32
    )
    return attended.astype(jnp.bfloat16).reshape(token_count, head_count * HEAD_DIM)


def route_rows(embedded, segment_ids, owners):
    merged_count = embedded.shape[0]
    peer_count = owners.shape[0]
    least_units = max(LEAST_UNITS, (merged_count + peer_count - 1) // peer_count)
    slot_count = max(MOST_UNITS, 2 * least_units)
    first_ids = segment_ids.reshape(merged_count, 4)[:, 0]
    id_base = lax.axis_index("tok") * peer_count
    local_index = first_ids - id_base
    owner_pick = local_index[:, None] == jnp.arange(peer_count, dtype=jnp.int32)[None, :]
    owner_of = jnp.sum(jnp.where(owner_pick, owners[None, :], 0), axis=1)
    row_index = jnp.arange(merged_count, dtype=jnp.int32)
    earlier = (row_index[None, :] < row_index[:, None]) & (first_ids[None, :] == first_ids[:, None])
    within = jnp.sum(earlier.astype(jnp.int32), axis=1)
    target = owner_of * slot_count + within
    select = (
        jnp.arange(peer_count * slot_count, dtype=jnp.int32)[:, None] == target[None, :]
    ).astype(jnp.bfloat16)
    packed = jnp.dot(select, embedded, preferred_element_type=jnp.float32).astype(jnp.bfloat16)
    packed = packed.reshape(peer_count, slot_count, embedded.shape[1])
    received = lax.all_to_all(packed, "tok", split_axis=0, concat_axis=0, tiled=True)
    return received.reshape(peer_count * slot_count, embedded.shape[1])


def body(
    tokens,
    segment_ids,
    owners,
    project_in,
    project_out,
    weight_up,
    weight_down,
    weight_merge,
    gain_attend,
    gain_hidden,
    gain_final,
):
    model_width = tokens.shape[1]
    head_count = project_in.shape[2] // HEAD_DIM
    units = weight_up.shape[1]
    feat_count = lax.axis_size("feat")
    tok_count = lax.axis_size("tok")
    flat_in = project_in.reshape(model_width, 3 * project_in.shape[2])
    local_count = tokens.shape[0]
    normed = layer_norm(tokens, gain_attend)
    lower = lax.all_gather(weight_down, "tok", axis=1, tiled=True)
    gathered, weights = first_exchange(normed, weight_up, feat_count, tok_count, 0)
    upper = weights.reshape(tok_count * weight_up.shape[0], units)
    projected = jnp.dot(gathered, flat_in, preferred_element_type=jnp.float32)
    attended = attend(projected, segment_ids, head_count)
    second = (tokens.astype(jnp.float32) + scatter_rows(attended, project_out, 1)).astype(jnp.bfloat16)
    normed_hidden = layer_norm(second, gain_hidden)
    hidden = jax.nn.gelu(
        project_rows(normed_hidden, upper, 2), approximate=False
    ).astype(jnp.bfloat16)
    down_parts = jnp.dot(hidden, lower, preferred_element_type=jnp.float32).astype(jnp.bfloat16)
    mlp_sum = scatter_feat(
        down_parts.reshape(feat_count, down_parts.shape[0] // feat_count, down_parts.shape[1]),
        feat_count,
        3,
    )
    residual_out = (second.astype(jnp.float32) + mlp_sum).astype(jnp.bfloat16)
    normed_final = layer_norm(residual_out, gain_final)
    merged = normed_final.reshape(local_count // 4, 4 * model_width)
    embedded = project_rows(merged, weight_merge, 4).astype(jnp.bfloat16)
    return route_rows(embedded, segment_ids, owners)


def solution(mesh):
    return jax.shard_map(
        body,
        mesh=mesh,
        in_specs=(
            P(("tok", "feat"), None),
            P("tok"),
            P("tok"),
            P(None, None, "feat"),
            P("feat", None),
            P("tok", "feat"),
            P("feat", "tok"),
            P(None, "feat"),
            P(),
            P(),
            P(),
        ),
        out_specs=P("tok", "feat"),
        check_vma=False,
    )
```

```python
import functools
import jax
import jax.numpy as jnp
from jax import lax
from jax.experimental import pallas as pl
from jax.experimental.pallas import tpu as pltpu
from jax.sharding import PartitionSpec as P


def _greet(peers, tok_index):
    barrier = pltpu.get_barrier_semaphore()
    for peer in peers:
        pl.semaphore_signal(barrier, inc=1, device_id=(tok_index, peer), device_id_type=MESH)
    pl.semaphore_wait(barrier, len(peers))


def _gather_kernel(n, row_ref, out_ref, send_sem, recv_sem):
    me = lax.axis_index("feat")
    tok_index = lax.axis_index("tok")
    peers = [lax.rem(me + d, n) for d in range(1, n)]
    _greet(peers, tok_index)
    for peer in peers:
        pltpu.make_async_remote_copy(
            src_ref=row_ref, dst_ref=out_ref.at[me], send_sem=send_sem.at[peer],
            recv_sem=recv_sem.at[me], device_id=(tok_index, peer), device_id_type=MESH,
        ).start()
    out_ref[me] = row_ref[...]
    for peer in peers:
        pltpu.make_async_remote_copy(
            src_ref=row_ref, dst_ref=out_ref.at[peer], send_sem=send_sem.at[peer],
            recv_sem=recv_sem.at[peer], device_id=(tok_index, peer), device_id_type=MESH,
        ).wait_recv()
    for peer in peers:
        pltpu.make_async_remote_copy(
            src_ref=row_ref, dst_ref=out_ref.at[me], send_sem=send_sem.at[peer],
            recv_sem=recv_sem.at[me], device_id=(tok_index, peer), device_id_type=MESH,
        ).wait_send()


def gather_feat(row_block, n, collective_id):
    rows, width = row_block.shape
    return pl.pallas_call(
        functools.partial(_gather_kernel, n),
        out_shape=jax.ShapeDtypeStruct((n, rows, width), row_block.dtype),
        in_specs=[pl.BlockSpec(memory_space=pltpu.VMEM)],
        out_specs=pl.BlockSpec(memory_space=pltpu.VMEM),
        scratch_shapes=[pltpu.SemaphoreType.DMA((n,)), pltpu.SemaphoreType.DMA((n,))],
        compiler_params=pltpu.CompilerParams(collective_id=collective_id, has_side_effects=True),
    )(row_block).reshape(n * rows, width)


def _ring_gather(x_ref, out_ref, send_right, send_left, send_partner, recv_sem, feat_index, after_first=None):
    tok_count = out_ref.shape[0]
    chips = tok_count // 2
    right_steps = chips // 2
    left_steps = chips - 1 - right_steps
    me = lax.axis_index("tok")
    chip = me // 2
    core = me % 2
    right = lax.rem(chip + 1, chips) * 2 + core
    left = lax.rem(chip + chips - 1, chips) * 2 + core
    partner = chip * 2 + (1 - core)

    def slot_of(offset):
        return lax.rem(chip + offset + 2 * chips, chips) * 2 + core

    def remote(src, slot, sem, target):
        return pltpu.make_async_remote_copy(
            src_ref=src, dst_ref=out_ref.at[slot], send_sem=sem, recv_sem=recv_sem.at[slot],
            device_id=(target, feat_index), device_id_type=MESH,
        )

    sends = []

    def forward_partner(src, slot):
        copy = remote(src, slot, send_partner.at[len(sends_partner)], partner)
        copy.start()
        sends_partner.append(copy)

    sends_partner = []
    out_ref[me] = x_ref[...]
    arrived = []
    for step in range(1, right_steps + 1):
        if step == 1:
            src_right = x_ref
            src_left = x_ref
        else:
            from_left = slot_of(-(step - 1))
            remote(x_ref, from_left, send_right.at[0], right).wait_recv()
            src_right = out_ref.at[from_left]
            arrived.append(from_left)
        copy = remote(src_right, slot_of(-(step - 1)), send_right.at[step - 1], right)
        copy.start()
        sends.append(copy)
        if step > 1 and step - 1 <= left_steps:
            from_right = slot_of(step - 1)
            remote(x_ref, from_right, send_left.at[0], left).wait_recv()
            src_left = out_ref.at[from_right]
            arrived.append(from_right)
        if step <= left_steps:
            copy = remote(src_left, slot_of(step - 1), send_left.at[step - 1], left)
            copy.start()
            sends.append(copy)
        if step == 1:
            if after_first is not None:
                after_first()
            forward_partner(x_ref, me)
        for slot in arrived:
            forward_partner(out_ref.at[slot], slot)
        arrived = []
    last_left = slot_of(-right_steps)
    remote(x_ref, last_left, send_right.at[0], right).wait_recv()
    forward_partner(out_ref.at[last_left], last_left)
    if left_steps >= 1 and left_steps + 1 > right_steps:
        last_right = slot_of(left_steps)
        remote(x_ref, last_right, send_left.at[0], left).wait_recv()
        forward_partner(out_ref.at[last_right], last_right)
    for other_chip in range(chips):
        remote(x_ref, other_chip * 2 + (1 - core), send_partner.at[0], partner).wait_recv()
    for copy in sends + sends_partner:
        copy.wait_send()


def _first_kernel(n, row_ref, weight_ref, out_ref, weight_out, send_sem, recv_sem,
                  send_right, send_left, send_partner, weight_recv):
    me = lax.axis_index("feat")
    tok_index = lax.axis_index("tok")
    chips = weight_out.shape[0] // 2
    chip = tok_index // 2
    core = tok_index % 2
    peers = [lax.rem(me + d, n) for d in range(1, n)]
    barrier = pltpu.get_barrier_semaphore()
    for peer in peers:
        pl.semaphore_signal(barrier, inc=1, device_id=(tok_index, peer), device_id_type=MESH)
    ring_peers = [
        lax.rem(chip + 1, chips) * 2 + core,
        lax.rem(chip + chips - 1, chips) * 2 + core,
        chip * 2 + (1 - core),
    ]
    for peer in ring_peers:
        pl.semaphore_signal(barrier, inc=1, device_id=(peer, me), device_id_type=MESH)
    pl.semaphore_wait(barrier, len(peers) + len(ring_peers))

    def start_rows():
        for peer in peers:
            pltpu.make_async_remote_copy(
                src_ref=row_ref, dst_ref=out_ref.at[me], send_sem=send_sem.at[peer],
                recv_sem=recv_sem.at[me], device_id=(tok_index, peer), device_id_type=MESH,
            ).start()

    _ring_gather(weight_ref, weight_out, send_right, send_left, send_partner, weight_recv, me, start_rows)
    out_ref[me] = row_ref[...]
    for peer in peers:
        pltpu.make_async_remote_copy(
            src_ref=row_ref, dst_ref=out_ref.at[peer], send_sem=send_sem.at[peer],
            recv_sem=recv_sem.at[peer], device_id=(tok_index, peer), device_id_type=MESH,
        ).wait_recv()
    for peer in peers:
        pltpu.make_async_remote_copy(
            src_ref=row_ref, dst_ref=out_ref.at[me], send_sem=send_sem.at[peer],
            recv_sem=recv_sem.at[me], device_id=(tok_index, peer), device_id_type=MESH,
        ).wait_send()


def first_exchange(row_block, weight_block, n, tok_count, collective_id):
    rows, width = row_block.shape
    weight_rows, weight_width = weight_block.shape
    chips = tok_count // 2
    gathered, weights = pl.pallas_call(
        functools.partial(_first_kernel, n),
        out_shape=(
            jax.ShapeDtypeStruct((n, rows, width), row_block.dtype),
            jax.ShapeDtypeStruct((tok_count, weight_rows, weight_width), weight_block.dtype),
        ),
        in_specs=[pl.BlockSpec(memory_space=pltpu.VMEM)] * 2,
        out_specs=(pl.BlockSpec(memory_space=pltpu.VMEM),) * 2,
        scratch_shapes=[
            pltpu.SemaphoreType.DMA((n,)),
            pltpu.SemaphoreType.DMA((n,)),
            pltpu.SemaphoreType.DMA((chips,)),
            pltpu.SemaphoreType.DMA((chips,)),
            pltpu.SemaphoreType.DMA((chips,)),
            pltpu.SemaphoreType.DMA((tok_count,)),
        ],
        compiler_params=pltpu.CompilerParams(collective_id=collective_id, has_side_effects=True),
    )(row_block, weight_block)
    return gathered.reshape(n * rows, width), weights


def _route_kernel(n, packed_ref, out_ref, send_sem, recv_sem):
    me = lax.axis_index("tok")
    feat_index = lax.axis_index("feat")
    peers = [lax.rem(me + d, n) for d in range(1, n)]
    barrier = pltpu.get_barrier_semaphore()
    for peer in peers:
        pl.semaphore_signal(barrier, inc=1, device_id=(peer, feat_index), device_id_type=MESH)
    pl.semaphore_wait(barrier, len(peers))
    for peer in peers:
        pltpu.make_async_remote_copy(
            src_ref=packed_ref.at[peer], dst_ref=out_ref.at[me], send_sem=send_sem.at[peer],
            recv_sem=recv_sem.at[me], device_id=(peer, feat_index), device_id_type=MESH,
        ).start()
    out_ref[me] = packed_ref[me]
    for peer in peers:
        pltpu.make_async_remote_copy(
            src_ref=packed_ref.at[peer], dst_ref=out_ref.at[peer], send_sem=send_sem.at[peer],
            recv_sem=recv_sem.at[peer], device_id=(peer, feat_index), device_id_type=MESH,
        ).wait_recv()
    for peer in peers:
        pltpu.make_async_remote_copy(
            src_ref=packed_ref.at[peer], dst_ref=out_ref.at[me], send_sem=send_sem.at[peer],
            recv_sem=recv_sem.at[me], device_id=(peer, feat_index), device_id_type=MESH,
        ).wait_send()


def route_exchange(packed, collective_id):
    n = packed.shape[0]
    return pl.pallas_call(
        functools.partial(_route_kernel, n),
        out_shape=jax.ShapeDtypeStruct(packed.shape, packed.dtype),
        in_specs=[pl.BlockSpec(memory_space=pltpu.VMEM)],
        out_specs=pl.BlockSpec(memory_space=pltpu.VMEM),
        scratch_shapes=[pltpu.SemaphoreType.DMA((n,)), pltpu.SemaphoreType.DMA((n,))],
        compiler_params=pltpu.CompilerParams(collective_id=collective_id, has_side_effects=True),
    )(packed)


def _scatter_kernel(n, part_ref, out_ref, held, send_sem, recv_sem):
    me = lax.axis_index("feat")
    tok_index = lax.axis_index("tok")
    peers = [lax.rem(me + d, n) for d in range(1, n)]
    _greet(peers, tok_index)
    for peer in peers:
        pltpu.make_async_remote_copy(
            src_ref=part_ref.at[peer], dst_ref=held.at[me], send_sem=send_sem.at[peer],
            recv_sem=recv_sem.at[me], device_id=(tok_index, peer), device_id_type=MESH,
        ).start()
    total = part_ref[me].astype(jnp.float32)
    for peer in peers:
        pltpu.make_async_remote_copy(
            src_ref=part_ref.at[peer], dst_ref=held.at[peer], send_sem=send_sem.at[peer],
            recv_sem=recv_sem.at[peer], device_id=(tok_index, peer), device_id_type=MESH,
        ).wait_recv()
        total = total + held[peer].astype(jnp.float32)
    out_ref[...] = total
    for peer in peers:
        pltpu.make_async_remote_copy(
            src_ref=part_ref.at[peer], dst_ref=held.at[me], send_sem=send_sem.at[peer],
            recv_sem=recv_sem.at[me], device_id=(tok_index, peer), device_id_type=MESH,
        ).wait_send()


def scatter_feat(parts, n, collective_id):
    _, rows, width = parts.shape
    return pl.pallas_call(
        functools.partial(_scatter_kernel, n),
        out_shape=jax.ShapeDtypeStruct((rows, width), jnp.float32),
        in_specs=[pl.BlockSpec(memory_space=pltpu.VMEM)],
        out_specs=pl.BlockSpec(memory_space=pltpu.VMEM),
        scratch_shapes=[
            pltpu.VMEM((n, rows, width), parts.dtype),
            pltpu.SemaphoreType.DMA((n,)),
            pltpu.SemaphoreType.DMA((n,)),
        ],
        compiler_params=pltpu.CompilerParams(collective_id=collective_id, has_side_effects=True),
    )(parts)

MESH = pl.DeviceIdType.MESH
LEAST_UNITS = 4
MOST_UNITS = 16
HEAD_DIM = 88


epsilon = 1e-06


def layer_norm(row_block, gain_row):
    as_float = row_block.astype(jnp.float32)
    center = jnp.mean(as_float, axis=-1, keepdims=True)
    spread = jnp.mean(jnp.square(as_float - center), axis=-1, keepdims=True)
    scaled = (as_float - center) * lax.rsqrt(spread + epsilon) * gain_row.astype(jnp.float32)
    return scaled.astype(jnp.bfloat16)


def project_rows(row_block, weight_block, collective_id):
    n = lax.axis_size("feat")
    return jnp.dot(
        gather_feat(row_block, n, collective_id),
        weight_block,
        preferred_element_type=jnp.float32,
    )


def scatter_rows(left_rows, right_rows, collective_id):
    n = lax.axis_size("feat")
    parts = jnp.dot(left_rows, right_rows, preferred_element_type=jnp.float32).astype(jnp.bfloat16)
    return scatter_feat(parts.reshape(n, parts.shape[0] // n, parts.shape[1]), n, collective_id)


def early_weights(weight_up, weight_down):
    return (weight_up, weight_down)


def upper_weight(fetched):
    return lax.all_gather(fetched[0], "tok", axis=0, tiled=True)


def lower_weight(fetched):
    return lax.all_gather(fetched[1], "tok", axis=1, tiled=True)


def attend(projected, segment_ids, head_count):
    token_count = projected.shape[0]
    parts_all = projected.reshape(token_count, 3, head_count, HEAD_DIM)
    queries = (parts_all[:, 0] * HEAD_DIM ** (-0.5)).astype(jnp.bfloat16)
    keys_here = parts_all[:, 1].astype(jnp.bfloat16)
    values_here = parts_all[:, 2].astype(jnp.bfloat16)
    scores = jnp.einsum("qhd,khd->hqk", queries, keys_here, preferred_element_type=jnp.float32)
    same_segment = segment_ids[:, None] == segment_ids[None, :]
    scores = jnp.where(same_segment[None, :, :], scores, -1e30)
    highest = jnp.max(scores, axis=-1, keepdims=True)
    raised = jnp.exp(scores - highest)
    weights_soft = (raised / jnp.sum(raised, axis=-1, keepdims=True)).astype(jnp.bfloat16)
    attended = jnp.einsum(
        "hqk,khd->qhd", weights_soft, values_here, preferred_element_type=jnp.float32
    )
    return attended.astype(jnp.bfloat16).reshape(token_count, head_count * HEAD_DIM)


def route_rows(embedded, segment_ids, owners):
    merged_count = embedded.shape[0]
    peer_count = owners.shape[0]
    least_units = max(LEAST_UNITS, (merged_count + peer_count - 1) // peer_count)
    slot_count = max(MOST_UNITS, 2 * least_units)
    first_ids = segment_ids.reshape(merged_count, 4)[:, 0]
    id_base = lax.axis_index("tok") * peer_count
    local_index = first_ids - id_base
    owner_pick = local_index[:, None] == jnp.arange(peer_count, dtype=jnp.int32)[None, :]
    owner_of = jnp.sum(jnp.where(owner_pick, owners[None, :], 0), axis=1)
    row_index = jnp.arange(merged_count, dtype=jnp.int32)
    earlier = (row_index[None, :] < row_index[:, None]) & (first_ids[None, :] == first_ids[:, None])
    within = jnp.sum(earlier.astype(jnp.int32), axis=1)
    target = owner_of * slot_count + within
    select = (
        jnp.arange(peer_count * slot_count, dtype=jnp.int32)[:, None] == target[None, :]
    ).astype(jnp.bfloat16)
    packed = jnp.dot(select, embedded, preferred_element_type=jnp.float32).astype(jnp.bfloat16)
    packed = packed.reshape(peer_count, slot_count, embedded.shape[1])
    received = route_exchange(packed, 5)
    return received.reshape(peer_count * slot_count, embedded.shape[1])


def body(
    tokens,
    segment_ids,
    owners,
    project_in,
    project_out,
    weight_up,
    weight_down,
    weight_merge,
    gain_attend,
    gain_hidden,
    gain_final,
):
    model_width = tokens.shape[1]
    head_count = project_in.shape[2] // HEAD_DIM
    units = weight_up.shape[1]
    feat_count = lax.axis_size("feat")
    tok_count = lax.axis_size("tok")
    flat_in = project_in.reshape(model_width, 3 * project_in.shape[2])
    local_count = tokens.shape[0]
    normed = layer_norm(tokens, gain_attend)
    lower = lax.all_gather(weight_down, "tok", axis=1, tiled=True)
    gathered, weights = first_exchange(normed, weight_up, feat_count, tok_count, 0)
    upper = weights.reshape(tok_count * weight_up.shape[0], units)
    projected = jnp.dot(gathered, flat_in, preferred_element_type=jnp.float32)
    attended = attend(projected, segment_ids, head_count)
    second = (tokens.astype(jnp.float32) + scatter_rows(attended, project_out, 1)).astype(jnp.bfloat16)
    normed_hidden = layer_norm(second, gain_hidden)
    hidden = jax.nn.gelu(
        project_rows(normed_hidden, upper, 2), approximate=False
    ).astype(jnp.bfloat16)
    down_parts = jnp.dot(hidden, lower, preferred_element_type=jnp.float32).astype(jnp.bfloat16)
    mlp_sum = scatter_feat(
        down_parts.reshape(feat_count, down_parts.shape[0] // feat_count, down_parts.shape[1]),
        feat_count,
        3,
    )
    residual_out = (second.astype(jnp.float32) + mlp_sum).astype(jnp.bfloat16)
    normed_final = layer_norm(residual_out, gain_final)
    merged = normed_final.reshape(local_count // 4, 4 * model_width)
    embedded = project_rows(merged, weight_merge, 4).astype(jnp.bfloat16)
    return route_rows(embedded, segment_ids, owners)


def solution(mesh):
    return jax.shard_map(
        body,
        mesh=mesh,
        in_specs=(
            P(("tok", "feat"), None),
            P("tok"),
            P("tok"),
            P(None, None, "feat"),
            P("feat", None),
            P("tok", "feat"),
            P("feat", "tok"),
            P(None, "feat"),
            P(),
            P(),
            P(),
        ),
        out_specs=P("tok", "feat"),
        check_vma=False,
    )
```

```python
import functools
import jax
import jax.numpy as jnp
from jax import lax
from jax.experimental import pallas as pl
from jax.experimental.pallas import tpu as pltpu
from jax.sharding import PartitionSpec as P


def _greet(peers, tok_index):
    barrier = pltpu.get_barrier_semaphore()
    for peer in peers:
        pl.semaphore_signal(barrier, inc=1, device_id=(tok_index, peer), device_id_type=MESH)
    pl.semaphore_wait(barrier, len(peers))


def _gather_kernel(n, row_ref, out_ref, send_sem, recv_sem):
    me = lax.axis_index("feat")
    tok_index = lax.axis_index("tok")
    peers = [lax.rem(me + d, n) for d in range(1, n)]
    _greet(peers, tok_index)
    for peer in peers:
        pltpu.make_async_remote_copy(
            src_ref=row_ref, dst_ref=out_ref.at[me], send_sem=send_sem.at[peer],
            recv_sem=recv_sem.at[me], device_id=(tok_index, peer), device_id_type=MESH,
        ).start()
    out_ref[me] = row_ref[...]
    for peer in peers:
        pltpu.make_async_remote_copy(
            src_ref=row_ref, dst_ref=out_ref.at[peer], send_sem=send_sem.at[peer],
            recv_sem=recv_sem.at[peer], device_id=(tok_index, peer), device_id_type=MESH,
        ).wait_recv()
    for peer in peers:
        pltpu.make_async_remote_copy(
            src_ref=row_ref, dst_ref=out_ref.at[me], send_sem=send_sem.at[peer],
            recv_sem=recv_sem.at[me], device_id=(tok_index, peer), device_id_type=MESH,
        ).wait_send()


def gather_feat(row_block, n, collective_id):
    rows, width = row_block.shape
    return pl.pallas_call(
        functools.partial(_gather_kernel, n),
        out_shape=jax.ShapeDtypeStruct((n, rows, width), row_block.dtype),
        in_specs=[pl.BlockSpec(memory_space=pltpu.VMEM)],
        out_specs=pl.BlockSpec(memory_space=pltpu.VMEM),
        scratch_shapes=[pltpu.SemaphoreType.DMA((n,)), pltpu.SemaphoreType.DMA((n,))],
        compiler_params=pltpu.CompilerParams(collective_id=collective_id, has_side_effects=True),
    )(row_block).reshape(n * rows, width)


def _ring_gather(x_ref, out_ref, send_right, send_left, send_partner, recv_sem, feat_index, after_first=None):
    tok_count = out_ref.shape[0]
    chips = tok_count // 2
    right_steps = chips // 2
    left_steps = chips - 1 - right_steps
    me = lax.axis_index("tok")
    chip = me // 2
    core = me % 2
    right = lax.rem(chip + 1, chips) * 2 + core
    left = lax.rem(chip + chips - 1, chips) * 2 + core
    partner = chip * 2 + (1 - core)

    def slot_of(offset):
        return lax.rem(chip + offset + 2 * chips, chips) * 2 + core

    def remote(src, slot, sem, target):
        return pltpu.make_async_remote_copy(
            src_ref=src, dst_ref=out_ref.at[slot], send_sem=sem, recv_sem=recv_sem.at[slot],
            device_id=(target, feat_index), device_id_type=MESH,
        )

    sends = []

    def forward_partner(src, slot):
        copy = remote(src, slot, send_partner.at[len(sends_partner)], partner)
        copy.start()
        sends_partner.append(copy)

    sends_partner = []
    out_ref[me] = x_ref[...]
    arrived = []
    for step in range(1, right_steps + 1):
        if step == 1:
            src_right = x_ref
            src_left = x_ref
        else:
            from_left = slot_of(-(step - 1))
            remote(x_ref, from_left, send_right.at[0], right).wait_recv()
            src_right = out_ref.at[from_left]
            arrived.append(from_left)
        copy = remote(src_right, slot_of(-(step - 1)), send_right.at[step - 1], right)
        copy.start()
        sends.append(copy)
        if step > 1 and step - 1 <= left_steps:
            from_right = slot_of(step - 1)
            remote(x_ref, from_right, send_left.at[0], left).wait_recv()
            src_left = out_ref.at[from_right]
            arrived.append(from_right)
        if step <= left_steps:
            copy = remote(src_left, slot_of(step - 1), send_left.at[step - 1], left)
            copy.start()
            sends.append(copy)
        if step == 1:
            if after_first is not None:
                after_first()
            forward_partner(x_ref, me)
        for slot in arrived:
            forward_partner(out_ref.at[slot], slot)
        arrived = []
    last_left = slot_of(-right_steps)
    remote(x_ref, last_left, send_right.at[0], right).wait_recv()
    forward_partner(out_ref.at[last_left], last_left)
    if left_steps >= 1 and left_steps + 1 > right_steps:
        last_right = slot_of(left_steps)
        remote(x_ref, last_right, send_left.at[0], left).wait_recv()
        forward_partner(out_ref.at[last_right], last_right)
    for other_chip in range(chips):
        remote(x_ref, other_chip * 2 + (1 - core), send_partner.at[0], partner).wait_recv()
    for copy in sends + sends_partner:
        copy.wait_send()


def _first_kernel(n, row_ref, weight_ref, out_ref, weight_out, send_sem, recv_sem,
                  send_right, send_left, send_partner, weight_recv):
    me = lax.axis_index("feat")
    tok_index = lax.axis_index("tok")
    chips = weight_out.shape[0] // 2
    chip = tok_index // 2
    core = tok_index % 2
    peers = [lax.rem(me + d, n) for d in range(1, n)]
    barrier = pltpu.get_barrier_semaphore()
    for peer in peers:
        pl.semaphore_signal(barrier, inc=1, device_id=(tok_index, peer), device_id_type=MESH)
    ring_peers = [
        lax.rem(chip + 1, chips) * 2 + core,
        lax.rem(chip + chips - 1, chips) * 2 + core,
        chip * 2 + (1 - core),
    ]
    for peer in ring_peers:
        pl.semaphore_signal(barrier, inc=1, device_id=(peer, me), device_id_type=MESH)
    pl.semaphore_wait(barrier, len(peers) + len(ring_peers))

    def start_rows():
        for peer in peers:
            pltpu.make_async_remote_copy(
                src_ref=row_ref, dst_ref=out_ref.at[me], send_sem=send_sem.at[peer],
                recv_sem=recv_sem.at[me], device_id=(tok_index, peer), device_id_type=MESH,
            ).start()

    _ring_gather(weight_ref, weight_out, send_right, send_left, send_partner, weight_recv, me, start_rows)
    out_ref[me] = row_ref[...]
    for peer in peers:
        pltpu.make_async_remote_copy(
            src_ref=row_ref, dst_ref=out_ref.at[peer], send_sem=send_sem.at[peer],
            recv_sem=recv_sem.at[peer], device_id=(tok_index, peer), device_id_type=MESH,
        ).wait_recv()
    for peer in peers:
        pltpu.make_async_remote_copy(
            src_ref=row_ref, dst_ref=out_ref.at[me], send_sem=send_sem.at[peer],
            recv_sem=recv_sem.at[me], device_id=(tok_index, peer), device_id_type=MESH,
        ).wait_send()


def first_exchange(row_block, weight_block, n, tok_count, collective_id):
    rows, width = row_block.shape
    weight_rows, weight_width = weight_block.shape
    chips = tok_count // 2
    gathered, weights = pl.pallas_call(
        functools.partial(_first_kernel, n),
        out_shape=(
            jax.ShapeDtypeStruct((n, rows, width), row_block.dtype),
            jax.ShapeDtypeStruct((tok_count, weight_rows, weight_width), weight_block.dtype),
        ),
        in_specs=[pl.BlockSpec(memory_space=pltpu.VMEM)] * 2,
        out_specs=(pl.BlockSpec(memory_space=pltpu.VMEM),) * 2,
        scratch_shapes=[
            pltpu.SemaphoreType.DMA((n,)),
            pltpu.SemaphoreType.DMA((n,)),
            pltpu.SemaphoreType.DMA((chips,)),
            pltpu.SemaphoreType.DMA((chips,)),
            pltpu.SemaphoreType.DMA((chips,)),
            pltpu.SemaphoreType.DMA((tok_count,)),
        ],
        compiler_params=pltpu.CompilerParams(collective_id=collective_id, has_side_effects=True),
    )(row_block, weight_block)
    return gathered.reshape(n * rows, width), weights


def _route_kernel(n, packed_ref, out_ref, send_sem, recv_sem):
    me = lax.axis_index("tok")
    feat_index = lax.axis_index("feat")
    peers = [lax.rem(me + d, n) for d in range(1, n)]
    barrier = pltpu.get_barrier_semaphore()
    for peer in peers:
        pl.semaphore_signal(barrier, inc=1, device_id=(peer, feat_index), device_id_type=MESH)
    pl.semaphore_wait(barrier, len(peers))
    for peer in peers:
        pltpu.make_async_remote_copy(
            src_ref=packed_ref.at[peer], dst_ref=out_ref.at[me], send_sem=send_sem.at[peer],
            recv_sem=recv_sem.at[me], device_id=(peer, feat_index), device_id_type=MESH,
        ).start()
    out_ref[me] = packed_ref[me]
    for peer in peers:
        pltpu.make_async_remote_copy(
            src_ref=packed_ref.at[peer], dst_ref=out_ref.at[peer], send_sem=send_sem.at[peer],
            recv_sem=recv_sem.at[peer], device_id=(peer, feat_index), device_id_type=MESH,
        ).wait_recv()
    for peer in peers:
        pltpu.make_async_remote_copy(
            src_ref=packed_ref.at[peer], dst_ref=out_ref.at[me], send_sem=send_sem.at[peer],
            recv_sem=recv_sem.at[me], device_id=(peer, feat_index), device_id_type=MESH,
        ).wait_send()


def route_exchange(packed, collective_id):
    n = packed.shape[0]
    return pl.pallas_call(
        functools.partial(_route_kernel, n),
        out_shape=jax.ShapeDtypeStruct(packed.shape, packed.dtype),
        in_specs=[pl.BlockSpec(memory_space=pltpu.VMEM)],
        out_specs=pl.BlockSpec(memory_space=pltpu.VMEM),
        scratch_shapes=[pltpu.SemaphoreType.DMA((n,)), pltpu.SemaphoreType.DMA((n,))],
        compiler_params=pltpu.CompilerParams(collective_id=collective_id, has_side_effects=True),
    )(packed)


def _mix_kernel(n, part_ref, resid_ref, gain_ref, resid_out, out_ref, held, mine,
                scatter_send, scatter_recv, gather_send, gather_recv):
    me = lax.axis_index("feat")
    tok_index = lax.axis_index("tok")
    peers = [lax.rem(me + d, n) for d in range(1, n)]
    _greet(peers, tok_index)

    def scatter_copy(peer, slot):
        return pltpu.make_async_remote_copy(
            src_ref=part_ref.at[peer], dst_ref=held.at[slot], send_sem=scatter_send.at[peer],
            recv_sem=scatter_recv.at[slot], device_id=(tok_index, peer), device_id_type=MESH,
        )

    def gather_copy(peer, slot):
        return pltpu.make_async_remote_copy(
            src_ref=mine, dst_ref=out_ref.at[slot], send_sem=gather_send.at[peer],
            recv_sem=gather_recv.at[slot], device_id=(tok_index, peer), device_id_type=MESH,
        )

    for peer in peers:
        scatter_copy(peer, me).start()
    total = part_ref[me].astype(jnp.float32)
    for peer in peers:
        scatter_copy(peer, peer).wait_recv()
        total = total + held[peer].astype(jnp.float32)
    summed = (resid_ref[...].astype(jnp.float32) + total).astype(jnp.bfloat16)
    resid_out[...] = summed
    as_float = summed.astype(jnp.float32)
    center = jnp.mean(as_float, axis=-1, keepdims=True)
    spread = jnp.mean(jnp.square(as_float - center), axis=-1, keepdims=True)
    normed = ((as_float - center) * lax.rsqrt(spread + epsilon) * gain_ref[...]).astype(jnp.bfloat16)
    mine[...] = normed
    out_ref[me] = normed
    for peer in peers:
        gather_copy(peer, me).start()
    for peer in peers:
        gather_copy(peer, peer).wait_recv()
    for peer in peers:
        scatter_copy(peer, me).wait_send()
        gather_copy(peer, me).wait_send()


def mix_feat(parts, resid, gain, n, collective_id):
    _, rows, width = parts.shape
    new_resid, gathered = pl.pallas_call(
        functools.partial(_mix_kernel, n),
        out_shape=(
            jax.ShapeDtypeStruct((rows, width), jnp.bfloat16),
            jax.ShapeDtypeStruct((n, rows, width), jnp.bfloat16),
        ),
        in_specs=[pl.BlockSpec(memory_space=pltpu.VMEM)] * 3,
        out_specs=(pl.BlockSpec(memory_space=pltpu.VMEM),) * 2,
        scratch_shapes=[
            pltpu.VMEM((n, rows, width), parts.dtype),
            pltpu.VMEM((rows, width), jnp.bfloat16),
            pltpu.SemaphoreType.DMA((n,)),
            pltpu.SemaphoreType.DMA((n,)),
            pltpu.SemaphoreType.DMA((n,)),
            pltpu.SemaphoreType.DMA((n,)),
        ],
        compiler_params=pltpu.CompilerParams(collective_id=collective_id, has_side_effects=True),
    )(parts, resid, gain.astype(jnp.float32).reshape(1, width))
    return new_resid, gathered.reshape(n * rows, width)


def _scatter_kernel(n, part_ref, out_ref, held, send_sem, recv_sem):
    me = lax.axis_index("feat")
    tok_index = lax.axis_index("tok")
    peers = [lax.rem(me + d, n) for d in range(1, n)]
    _greet(peers, tok_index)
    for peer in peers:
        pltpu.make_async_remote_copy(
            src_ref=part_ref.at[peer], dst_ref=held.at[me], send_sem=send_sem.at[peer],
            recv_sem=recv_sem.at[me], device_id=(tok_index, peer), device_id_type=MESH,
        ).start()
    total = part_ref[me].astype(jnp.float32)
    for peer in peers:
        pltpu.make_async_remote_copy(
            src_ref=part_ref.at[peer], dst_ref=held.at[peer], send_sem=send_sem.at[peer],
            recv_sem=recv_sem.at[peer], device_id=(tok_index, peer), device_id_type=MESH,
        ).wait_recv()
        total = total + held[peer].astype(jnp.float32)
    out_ref[...] = total
    for peer in peers:
        pltpu.make_async_remote_copy(
            src_ref=part_ref.at[peer], dst_ref=held.at[me], send_sem=send_sem.at[peer],
            recv_sem=recv_sem.at[me], device_id=(tok_index, peer), device_id_type=MESH,
        ).wait_send()


def scatter_feat(parts, n, collective_id):
    _, rows, width = parts.shape
    return pl.pallas_call(
        functools.partial(_scatter_kernel, n),
        out_shape=jax.ShapeDtypeStruct((rows, width), jnp.float32),
        in_specs=[pl.BlockSpec(memory_space=pltpu.VMEM)],
        out_specs=pl.BlockSpec(memory_space=pltpu.VMEM),
        scratch_shapes=[
            pltpu.VMEM((n, rows, width), parts.dtype),
            pltpu.SemaphoreType.DMA((n,)),
            pltpu.SemaphoreType.DMA((n,)),
        ],
        compiler_params=pltpu.CompilerParams(collective_id=collective_id, has_side_effects=True),
    )(parts)

MESH = pl.DeviceIdType.MESH
LEAST_UNITS = 4
MOST_UNITS = 16
HEAD_DIM = 88


epsilon = 1e-06


def layer_norm(row_block, gain_row):
    as_float = row_block.astype(jnp.float32)
    center = jnp.mean(as_float, axis=-1, keepdims=True)
    spread = jnp.mean(jnp.square(as_float - center), axis=-1, keepdims=True)
    scaled = (as_float - center) * lax.rsqrt(spread + epsilon) * gain_row.astype(jnp.float32)
    return scaled.astype(jnp.bfloat16)


def project_rows(row_block, weight_block, collective_id):
    n = lax.axis_size("feat")
    return jnp.dot(
        gather_feat(row_block, n, collective_id),
        weight_block,
        preferred_element_type=jnp.float32,
    )


def scatter_rows(left_rows, right_rows, collective_id):
    n = lax.axis_size("feat")
    parts = jnp.dot(left_rows, right_rows, preferred_element_type=jnp.float32).astype(jnp.bfloat16)
    return scatter_feat(parts.reshape(n, parts.shape[0] // n, parts.shape[1]), n, collective_id)


def early_weights(weight_up, weight_down):
    return (weight_up, weight_down)


def upper_weight(fetched):
    return lax.all_gather(fetched[0], "tok", axis=0, tiled=True)


def lower_weight(fetched):
    return lax.all_gather(fetched[1], "tok", axis=1, tiled=True)


def attend(projected, segment_ids, head_count):
    token_count = projected.shape[0]
    parts_all = projected.reshape(token_count, 3, head_count, HEAD_DIM)
    queries = (parts_all[:, 0] * HEAD_DIM ** (-0.5)).astype(jnp.bfloat16)
    keys_here = parts_all[:, 1].astype(jnp.bfloat16)
    values_here = parts_all[:, 2].astype(jnp.bfloat16)
    scores = jnp.einsum("qhd,khd->hqk", queries, keys_here, preferred_element_type=jnp.float32)
    same_segment = segment_ids[:, None] == segment_ids[None, :]
    scores = jnp.where(same_segment[None, :, :], scores, -1e30)
    highest = jnp.max(scores, axis=-1, keepdims=True)
    raised = jnp.exp(scores - highest)
    weights_soft = (raised / jnp.sum(raised, axis=-1, keepdims=True)).astype(jnp.bfloat16)
    attended = jnp.einsum(
        "hqk,khd->qhd", weights_soft, values_here, preferred_element_type=jnp.float32
    )
    return attended.astype(jnp.bfloat16).reshape(token_count, head_count * HEAD_DIM)


def route_rows(embedded, segment_ids, owners):
    merged_count = embedded.shape[0]
    peer_count = owners.shape[0]
    least_units = max(LEAST_UNITS, (merged_count + peer_count - 1) // peer_count)
    slot_count = max(MOST_UNITS, 2 * least_units)
    first_ids = segment_ids.reshape(merged_count, 4)[:, 0]
    id_base = lax.axis_index("tok") * peer_count
    local_index = first_ids - id_base
    owner_pick = local_index[:, None] == jnp.arange(peer_count, dtype=jnp.int32)[None, :]
    owner_of = jnp.sum(jnp.where(owner_pick, owners[None, :], 0), axis=1)
    row_index = jnp.arange(merged_count, dtype=jnp.int32)
    earlier = (row_index[None, :] < row_index[:, None]) & (first_ids[None, :] == first_ids[:, None])
    within = jnp.sum(earlier.astype(jnp.int32), axis=1)
    target = owner_of * slot_count + within
    select = (
        jnp.arange(peer_count * slot_count, dtype=jnp.int32)[:, None] == target[None, :]
    ).astype(jnp.bfloat16)
    packed = jnp.dot(select, embedded, preferred_element_type=jnp.float32).astype(jnp.bfloat16)
    packed = packed.reshape(peer_count, slot_count, embedded.shape[1])
    received = route_exchange(packed, 5)
    return received.reshape(peer_count * slot_count, embedded.shape[1])


def body(
    tokens,
    segment_ids,
    owners,
    project_in,
    project_out,
    weight_up,
    weight_down,
    weight_merge,
    gain_attend,
    gain_hidden,
    gain_final,
):
    model_width = tokens.shape[1]
    head_count = project_in.shape[2] // HEAD_DIM
    units = weight_up.shape[1]
    feat_count = lax.axis_size("feat")
    tok_count = lax.axis_size("tok")
    flat_in = project_in.reshape(model_width, 3 * project_in.shape[2])
    local_count = tokens.shape[0]
    normed = layer_norm(tokens, gain_attend)
    lower = lax.all_gather(weight_down, "tok", axis=1, tiled=True)
    gathered, weights = first_exchange(normed, weight_up, feat_count, tok_count, 0)
    upper = weights.reshape(tok_count * weight_up.shape[0], units)
    projected = jnp.dot(gathered, flat_in, preferred_element_type=jnp.float32)
    attended = attend(projected, segment_ids, head_count)
    attn_parts = jnp.dot(attended, project_out, preferred_element_type=jnp.float32).astype(jnp.bfloat16)
    second, hidden_rows = mix_feat(
        attn_parts.reshape(feat_count, local_count, model_width), tokens, gain_hidden, feat_count, 1
    )
    hidden = jax.nn.gelu(
        jnp.dot(hidden_rows, upper, preferred_element_type=jnp.float32), approximate=False
    ).astype(jnp.bfloat16)
    down_parts = jnp.dot(hidden, lower, preferred_element_type=jnp.float32).astype(jnp.bfloat16)
    _, final_rows = mix_feat(
        down_parts.reshape(feat_count, local_count, model_width), second, gain_final, feat_count, 3
    )
    merged = final_rows.reshape(final_rows.shape[0] // 4, 4 * model_width)
    embedded = jnp.dot(merged, weight_merge, preferred_element_type=jnp.float32).astype(jnp.bfloat16)
    return route_rows(embedded, segment_ids, owners)


def solution(mesh):
    return jax.shard_map(
        body,
        mesh=mesh,
        in_specs=(
            P(("tok", "feat"), None),
            P("tok"),
            P("tok"),
            P(None, None, "feat"),
            P("feat", None),
            P("tok", "feat"),
            P("feat", "tok"),
            P(None, "feat"),
            P(),
            P(),
            P(),
        ),
        out_specs=P("tok", "feat"),
        check_vma=False,
    )
```

```python
import functools
import jax
import jax.numpy as jnp
from jax import lax
from jax.experimental import pallas as pl
from jax.experimental.pallas import tpu as pltpu
from jax.sharding import PartitionSpec as P


def _greet(peers, tok_index):
    barrier = pltpu.get_barrier_semaphore()
    for peer in peers:
        pl.semaphore_signal(barrier, inc=1, device_id=(tok_index, peer), device_id_type=MESH)
    pl.semaphore_wait(barrier, len(peers))


def _gather_kernel(n, row_ref, out_ref, send_sem, recv_sem):
    me = lax.axis_index("feat")
    tok_index = lax.axis_index("tok")
    peers = [lax.rem(me + d, n) for d in range(1, n)]
    _greet(peers, tok_index)
    for peer in peers:
        pltpu.make_async_remote_copy(
            src_ref=row_ref, dst_ref=out_ref.at[me], send_sem=send_sem.at[peer],
            recv_sem=recv_sem.at[me], device_id=(tok_index, peer), device_id_type=MESH,
        ).start()
    out_ref[me] = row_ref[...]
    for peer in peers:
        pltpu.make_async_remote_copy(
            src_ref=row_ref, dst_ref=out_ref.at[peer], send_sem=send_sem.at[peer],
            recv_sem=recv_sem.at[peer], device_id=(tok_index, peer), device_id_type=MESH,
        ).wait_recv()
    for peer in peers:
        pltpu.make_async_remote_copy(
            src_ref=row_ref, dst_ref=out_ref.at[me], send_sem=send_sem.at[peer],
            recv_sem=recv_sem.at[me], device_id=(tok_index, peer), device_id_type=MESH,
        ).wait_send()


def gather_feat(row_block, n, collective_id):
    rows, width = row_block.shape
    return pl.pallas_call(
        functools.partial(_gather_kernel, n),
        out_shape=jax.ShapeDtypeStruct((n, rows, width), row_block.dtype),
        in_specs=[pl.BlockSpec(memory_space=pltpu.VMEM)],
        out_specs=pl.BlockSpec(memory_space=pltpu.VMEM),
        scratch_shapes=[pltpu.SemaphoreType.DMA((n,)), pltpu.SemaphoreType.DMA((n,))],
        compiler_params=pltpu.CompilerParams(collective_id=collective_id, has_side_effects=True),
    )(row_block).reshape(n * rows, width)


def _ring_gather(x_ref, out_ref, send_right, send_left, send_partner, recv_sem, feat_index, after_first=None):
    tok_count = out_ref.shape[0]
    chips = tok_count // 2
    right_steps = chips // 2
    left_steps = chips - 1 - right_steps
    me = lax.axis_index("tok")
    chip = me // 2
    core = me % 2
    right = lax.rem(chip + 1, chips) * 2 + core
    left = lax.rem(chip + chips - 1, chips) * 2 + core
    partner = chip * 2 + (1 - core)

    def slot_of(offset):
        return lax.rem(chip + offset + 2 * chips, chips) * 2 + core

    def remote(src, slot, sem, target):
        return pltpu.make_async_remote_copy(
            src_ref=src, dst_ref=out_ref.at[slot], send_sem=sem, recv_sem=recv_sem.at[slot],
            device_id=(target, feat_index), device_id_type=MESH,
        )

    sends = []

    def forward_partner(src, slot):
        copy = remote(src, slot, send_partner.at[len(sends_partner)], partner)
        copy.start()
        sends_partner.append(copy)

    sends_partner = []
    out_ref[me] = x_ref[...]
    arrived = []
    for step in range(1, right_steps + 1):
        if step == 1:
            src_right = x_ref
            src_left = x_ref
        else:
            from_left = slot_of(-(step - 1))
            remote(x_ref, from_left, send_right.at[0], right).wait_recv()
            src_right = out_ref.at[from_left]
            arrived.append(from_left)
        copy = remote(src_right, slot_of(-(step - 1)), send_right.at[step - 1], right)
        copy.start()
        sends.append(copy)
        if step > 1 and step - 1 <= left_steps:
            from_right = slot_of(step - 1)
            remote(x_ref, from_right, send_left.at[0], left).wait_recv()
            src_left = out_ref.at[from_right]
            arrived.append(from_right)
        if step <= left_steps:
            copy = remote(src_left, slot_of(step - 1), send_left.at[step - 1], left)
            copy.start()
            sends.append(copy)
        if step == 1:
            if after_first is not None:
                after_first()
            forward_partner(x_ref, me)
        for slot in arrived:
            forward_partner(out_ref.at[slot], slot)
        arrived = []
    last_left = slot_of(-right_steps)
    remote(x_ref, last_left, send_right.at[0], right).wait_recv()
    forward_partner(out_ref.at[last_left], last_left)
    if left_steps >= 1 and left_steps + 1 > right_steps:
        last_right = slot_of(left_steps)
        remote(x_ref, last_right, send_left.at[0], left).wait_recv()
        forward_partner(out_ref.at[last_right], last_right)
    for other_chip in range(chips):
        remote(x_ref, other_chip * 2 + (1 - core), send_partner.at[0], partner).wait_recv()
    for copy in sends + sends_partner:
        copy.wait_send()


def _first_kernel(n, row_ref, weight_ref, out_ref, weight_out, send_sem, recv_sem,
                  send_right, send_left, send_partner, weight_recv):
    me = lax.axis_index("feat")
    tok_index = lax.axis_index("tok")
    chips = weight_out.shape[0] // 2
    chip = tok_index // 2
    core = tok_index % 2
    peers = [lax.rem(me + d, n) for d in range(1, n)]
    barrier = pltpu.get_barrier_semaphore()
    for peer in peers:
        pl.semaphore_signal(barrier, inc=1, device_id=(tok_index, peer), device_id_type=MESH)
    ring_peers = [
        lax.rem(chip + 1, chips) * 2 + core,
        lax.rem(chip + chips - 1, chips) * 2 + core,
        chip * 2 + (1 - core),
    ]
    for peer in ring_peers:
        pl.semaphore_signal(barrier, inc=1, device_id=(peer, me), device_id_type=MESH)
    pl.semaphore_wait(barrier, len(peers) + len(ring_peers))

    def start_rows():
        for peer in peers:
            pltpu.make_async_remote_copy(
                src_ref=row_ref, dst_ref=out_ref.at[me], send_sem=send_sem.at[peer],
                recv_sem=recv_sem.at[me], device_id=(tok_index, peer), device_id_type=MESH,
            ).start()

    _ring_gather(weight_ref, weight_out, send_right, send_left, send_partner, weight_recv, me, start_rows)
    out_ref[me] = row_ref[...]
    for peer in peers:
        pltpu.make_async_remote_copy(
            src_ref=row_ref, dst_ref=out_ref.at[peer], send_sem=send_sem.at[peer],
            recv_sem=recv_sem.at[peer], device_id=(tok_index, peer), device_id_type=MESH,
        ).wait_recv()
    for peer in peers:
        pltpu.make_async_remote_copy(
            src_ref=row_ref, dst_ref=out_ref.at[me], send_sem=send_sem.at[peer],
            recv_sem=recv_sem.at[me], device_id=(tok_index, peer), device_id_type=MESH,
        ).wait_send()


def first_exchange(row_block, weight_block, n, tok_count, collective_id):
    rows, width = row_block.shape
    weight_rows, weight_width = weight_block.shape
    chips = tok_count // 2
    gathered, weights = pl.pallas_call(
        functools.partial(_first_kernel, n),
        out_shape=(
            jax.ShapeDtypeStruct((n, rows, width), row_block.dtype),
            jax.ShapeDtypeStruct((tok_count, weight_rows, weight_width), weight_block.dtype),
        ),
        in_specs=[pl.BlockSpec(memory_space=pltpu.VMEM)] * 2,
        out_specs=(pl.BlockSpec(memory_space=pltpu.VMEM),) * 2,
        scratch_shapes=[
            pltpu.SemaphoreType.DMA((n,)),
            pltpu.SemaphoreType.DMA((n,)),
            pltpu.SemaphoreType.DMA((chips,)),
            pltpu.SemaphoreType.DMA((chips,)),
            pltpu.SemaphoreType.DMA((chips,)),
            pltpu.SemaphoreType.DMA((tok_count,)),
        ],
        compiler_params=pltpu.CompilerParams(collective_id=collective_id, has_side_effects=True),
    )(row_block, weight_block)
    return gathered.reshape(n * rows, width), weights


def _route_kernel(n, packed_ref, out_ref, send_sem, recv_sem):
    me = lax.axis_index("tok")
    feat_index = lax.axis_index("feat")
    peers = [lax.rem(me + d, n) for d in range(1, n)]
    barrier = pltpu.get_barrier_semaphore()
    for peer in peers:
        pl.semaphore_signal(barrier, inc=1, device_id=(peer, feat_index), device_id_type=MESH)
    pl.semaphore_wait(barrier, len(peers))
    for peer in peers:
        pltpu.make_async_remote_copy(
            src_ref=packed_ref.at[peer], dst_ref=out_ref.at[me], send_sem=send_sem.at[peer],
            recv_sem=recv_sem.at[me], device_id=(peer, feat_index), device_id_type=MESH,
        ).start()
    out_ref[me] = packed_ref[me]
    for peer in peers:
        pltpu.make_async_remote_copy(
            src_ref=packed_ref.at[peer], dst_ref=out_ref.at[peer], send_sem=send_sem.at[peer],
            recv_sem=recv_sem.at[peer], device_id=(peer, feat_index), device_id_type=MESH,
        ).wait_recv()
    for peer in peers:
        pltpu.make_async_remote_copy(
            src_ref=packed_ref.at[peer], dst_ref=out_ref.at[me], send_sem=send_sem.at[peer],
            recv_sem=recv_sem.at[me], device_id=(peer, feat_index), device_id_type=MESH,
        ).wait_send()


def route_exchange(packed, collective_id):
    n = packed.shape[0]
    return pl.pallas_call(
        functools.partial(_route_kernel, n),
        out_shape=jax.ShapeDtypeStruct(packed.shape, packed.dtype),
        in_specs=[pl.BlockSpec(memory_space=pltpu.VMEM)],
        out_specs=pl.BlockSpec(memory_space=pltpu.VMEM),
        scratch_shapes=[pltpu.SemaphoreType.DMA((n,)), pltpu.SemaphoreType.DMA((n,))],
        compiler_params=pltpu.CompilerParams(collective_id=collective_id, has_side_effects=True),
    )(packed)


def _mix_kernel(n, part_ref, resid_ref, gain_ref, resid_out, out_ref, held, mine,
                scatter_send, scatter_recv, gather_send, gather_recv):
    me = lax.axis_index("feat")
    tok_index = lax.axis_index("tok")
    peers = [lax.rem(me + d, n) for d in range(1, n)]
    _greet(peers, tok_index)

    def scatter_copy(peer, slot):
        return pltpu.make_async_remote_copy(
            src_ref=part_ref.at[peer], dst_ref=held.at[slot], send_sem=scatter_send.at[peer],
            recv_sem=scatter_recv.at[slot], device_id=(tok_index, peer), device_id_type=MESH,
        )

    def gather_copy(peer, slot):
        return pltpu.make_async_remote_copy(
            src_ref=mine, dst_ref=out_ref.at[slot], send_sem=gather_send.at[peer],
            recv_sem=gather_recv.at[slot], device_id=(tok_index, peer), device_id_type=MESH,
        )

    for peer in peers:
        scatter_copy(peer, me).start()
    total = part_ref[me].astype(jnp.float32)
    for peer in peers:
        scatter_copy(peer, peer).wait_recv()
        total = total + held[peer].astype(jnp.float32)
    summed = (resid_ref[...].astype(jnp.float32) + total).astype(jnp.bfloat16)
    resid_out[...] = summed
    as_float = summed.astype(jnp.float32)
    center = jnp.mean(as_float, axis=-1, keepdims=True)
    spread = jnp.mean(jnp.square(as_float - center), axis=-1, keepdims=True)
    normed = ((as_float - center) * lax.rsqrt(spread + epsilon) * gain_ref[...]).astype(jnp.bfloat16)
    mine[...] = normed
    out_ref[me] = normed
    for peer in peers:
        gather_copy(peer, me).start()
    for peer in peers:
        gather_copy(peer, peer).wait_recv()
    for peer in peers:
        scatter_copy(peer, me).wait_send()
        gather_copy(peer, me).wait_send()


def mix_feat(parts, resid, gain, n, collective_id):
    _, rows, width = parts.shape
    new_resid, gathered = pl.pallas_call(
        functools.partial(_mix_kernel, n),
        out_shape=(
            jax.ShapeDtypeStruct((rows, width), jnp.bfloat16),
            jax.ShapeDtypeStruct((n, rows, width), jnp.bfloat16),
        ),
        in_specs=[pl.BlockSpec(memory_space=pltpu.VMEM)] * 3,
        out_specs=(pl.BlockSpec(memory_space=pltpu.VMEM),) * 2,
        scratch_shapes=[
            pltpu.VMEM((n, rows, width), parts.dtype),
            pltpu.VMEM((rows, width), jnp.bfloat16),
            pltpu.SemaphoreType.DMA((n,)),
            pltpu.SemaphoreType.DMA((n,)),
            pltpu.SemaphoreType.DMA((n,)),
            pltpu.SemaphoreType.DMA((n,)),
        ],
        compiler_params=pltpu.CompilerParams(collective_id=collective_id, has_side_effects=True),
    )(parts, resid, gain.astype(jnp.float32).reshape(1, width))
    return new_resid, gathered.reshape(n * rows, width)


def _scatter_kernel(n, part_ref, out_ref, held, send_sem, recv_sem):
    me = lax.axis_index("feat")
    tok_index = lax.axis_index("tok")
    peers = [lax.rem(me + d, n) for d in range(1, n)]
    _greet(peers, tok_index)
    for peer in peers:
        pltpu.make_async_remote_copy(
            src_ref=part_ref.at[peer], dst_ref=held.at[me], send_sem=send_sem.at[peer],
            recv_sem=recv_sem.at[me], device_id=(tok_index, peer), device_id_type=MESH,
        ).start()
    total = part_ref[me].astype(jnp.float32)
    for peer in peers:
        pltpu.make_async_remote_copy(
            src_ref=part_ref.at[peer], dst_ref=held.at[peer], send_sem=send_sem.at[peer],
            recv_sem=recv_sem.at[peer], device_id=(tok_index, peer), device_id_type=MESH,
        ).wait_recv()
        total = total + held[peer].astype(jnp.float32)
    out_ref[...] = total
    for peer in peers:
        pltpu.make_async_remote_copy(
            src_ref=part_ref.at[peer], dst_ref=held.at[me], send_sem=send_sem.at[peer],
            recv_sem=recv_sem.at[me], device_id=(tok_index, peer), device_id_type=MESH,
        ).wait_send()


def scatter_feat(parts, n, collective_id):
    _, rows, width = parts.shape
    return pl.pallas_call(
        functools.partial(_scatter_kernel, n),
        out_shape=jax.ShapeDtypeStruct((rows, width), jnp.float32),
        in_specs=[pl.BlockSpec(memory_space=pltpu.VMEM)],
        out_specs=pl.BlockSpec(memory_space=pltpu.VMEM),
        scratch_shapes=[
            pltpu.VMEM((n, rows, width), parts.dtype),
            pltpu.SemaphoreType.DMA((n,)),
            pltpu.SemaphoreType.DMA((n,)),
        ],
        compiler_params=pltpu.CompilerParams(collective_id=collective_id, has_side_effects=True),
    )(parts)

MESH = pl.DeviceIdType.MESH
LEAST_UNITS = 4
MOST_UNITS = 16
HEAD_DIM = 88


epsilon = 1e-06


def layer_norm(row_block, gain_row):
    as_float = row_block.astype(jnp.float32)
    center = jnp.mean(as_float, axis=-1, keepdims=True)
    spread = jnp.mean(jnp.square(as_float - center), axis=-1, keepdims=True)
    scaled = (as_float - center) * lax.rsqrt(spread + epsilon) * gain_row.astype(jnp.float32)
    return scaled.astype(jnp.bfloat16)


def project_rows(row_block, weight_block, collective_id):
    n = lax.axis_size("feat")
    return jnp.dot(
        gather_feat(row_block, n, collective_id),
        weight_block,
        preferred_element_type=jnp.float32,
    )


def scatter_rows(left_rows, right_rows, collective_id):
    n = lax.axis_size("feat")
    parts = jnp.dot(left_rows, right_rows, preferred_element_type=jnp.float32).astype(jnp.bfloat16)
    return scatter_feat(parts.reshape(n, parts.shape[0] // n, parts.shape[1]), n, collective_id)


def early_weights(weight_up, weight_down):
    return (weight_up, weight_down)


def upper_weight(fetched):
    return lax.all_gather(fetched[0], "tok", axis=0, tiled=True)


def lower_weight(fetched):
    return lax.all_gather(fetched[1], "tok", axis=1, tiled=True)


def attend(projected, segment_ids, head_count):
    token_count = projected.shape[0]
    parts_all = projected.reshape(token_count, 3, head_count, HEAD_DIM)
    queries = (parts_all[:, 0] * HEAD_DIM ** (-0.5)).astype(jnp.bfloat16)
    keys_here = parts_all[:, 1].astype(jnp.bfloat16)
    values_here = parts_all[:, 2].astype(jnp.bfloat16)
    scores = jnp.einsum("qhd,khd->hqk", queries, keys_here, preferred_element_type=jnp.float32)
    same_segment = segment_ids[:, None] == segment_ids[None, :]
    scores = jnp.where(same_segment[None, :, :], scores, -1e30)
    highest = jnp.max(scores, axis=-1, keepdims=True)
    raised = jnp.exp(scores - highest)
    weights_soft = (raised / jnp.sum(raised, axis=-1, keepdims=True)).astype(jnp.bfloat16)
    attended = jnp.einsum(
        "hqk,khd->qhd", weights_soft, values_here, preferred_element_type=jnp.float32
    )
    return attended.astype(jnp.bfloat16).reshape(token_count, head_count * HEAD_DIM)


def route_rows(embedded, segment_ids, owners):
    merged_count = embedded.shape[0]
    peer_count = owners.shape[0]
    least_units = max(LEAST_UNITS, (merged_count + peer_count - 1) // peer_count)
    slot_count = max(MOST_UNITS, 2 * least_units)
    first_ids = segment_ids.reshape(merged_count, 4)[:, 0]
    id_base = lax.axis_index("tok") * peer_count
    local_index = first_ids - id_base
    owner_pick = local_index[:, None] == jnp.arange(peer_count, dtype=jnp.int32)[None, :]
    owner_of = jnp.sum(jnp.where(owner_pick, owners[None, :], 0), axis=1)
    row_index = jnp.arange(merged_count, dtype=jnp.int32)
    earlier = (row_index[None, :] < row_index[:, None]) & (first_ids[None, :] == first_ids[:, None])
    within = jnp.sum(earlier.astype(jnp.int32), axis=1)
    target = owner_of * slot_count + within
    select = (
        jnp.arange(peer_count * slot_count, dtype=jnp.int32)[:, None] == target[None, :]
    ).astype(jnp.bfloat16)
    packed = jnp.dot(select, embedded, preferred_element_type=jnp.float32).astype(jnp.bfloat16)
    packed = packed.reshape(peer_count, slot_count, embedded.shape[1])
    received = route_exchange(packed, 5)
    return received.reshape(peer_count * slot_count, embedded.shape[1])


def body(
    tokens,
    segment_ids,
    owners,
    project_in,
    project_out,
    weight_up,
    weight_down,
    weight_merge,
    gain_attend,
    gain_hidden,
    gain_final,
):
    model_width = tokens.shape[1]
    head_count = project_in.shape[2] // HEAD_DIM
    units = weight_up.shape[1]
    feat_count = lax.axis_size("feat")
    tok_count = lax.axis_size("tok")
    flat_in = project_in.reshape(model_width, 3 * project_in.shape[2])
    local_count = tokens.shape[0]
    normed = layer_norm(tokens, gain_attend)
    stacked = jnp.concatenate([weight_up, weight_down.T], axis=1)
    gathered, weights = first_exchange(normed, stacked, feat_count, tok_count, 0)
    upper = weights[:, :, :units].reshape(tok_count * weight_up.shape[0], units)
    lower_t = weights[:, :, units:].reshape(tok_count * weight_up.shape[0], units)
    projected = jnp.dot(gathered, flat_in, preferred_element_type=jnp.float32)
    attended = attend(projected, segment_ids, head_count)
    attn_parts = jnp.dot(attended, project_out, preferred_element_type=jnp.float32).astype(jnp.bfloat16)
    second, hidden_rows = mix_feat(
        attn_parts.reshape(feat_count, local_count, model_width), tokens, gain_hidden, feat_count, 1
    )
    hidden = jax.nn.gelu(
        jnp.dot(hidden_rows, upper, preferred_element_type=jnp.float32), approximate=False
    ).astype(jnp.bfloat16)
    down_parts = lax.dot_general(
        hidden, lower_t, (((1,), (1,)), ((), ())), preferred_element_type=jnp.float32
    ).astype(jnp.bfloat16)
    _, final_rows = mix_feat(
        down_parts.reshape(feat_count, local_count, model_width), second, gain_final, feat_count, 3
    )
    merged = final_rows.reshape(final_rows.shape[0] // 4, 4 * model_width)
    embedded = jnp.dot(merged, weight_merge, preferred_element_type=jnp.float32).astype(jnp.bfloat16)
    return route_rows(embedded, segment_ids, owners)


def solution(mesh):
    return jax.shard_map(
        body,
        mesh=mesh,
        in_specs=(
            P(("tok", "feat"), None),
            P("tok"),
            P("tok"),
            P(None, None, "feat"),
            P("feat", None),
            P("tok", "feat"),
            P("feat", "tok"),
            P(None, "feat"),
            P(),
            P(),
            P(),
        ),
        out_specs=P("tok", "feat"),
        check_vma=False,
    )
```

```python
import functools
import jax
import jax.numpy as jnp
from jax import lax
from jax.experimental import pallas as pl
from jax.experimental.pallas import tpu as pltpu
from jax.sharding import PartitionSpec as P


def _greet(peers, tok_index):
    barrier = pltpu.get_barrier_semaphore()
    for peer in peers:
        pl.semaphore_signal(barrier, inc=1, device_id=(tok_index, peer), device_id_type=MESH)
    pl.semaphore_wait(barrier, len(peers))


def _gather_kernel(n, row_ref, out_ref, send_sem, recv_sem):
    me = lax.axis_index("feat")
    tok_index = lax.axis_index("tok")
    peers = [lax.rem(me + d, n) for d in range(1, n)]
    _greet(peers, tok_index)
    for peer in peers:
        pltpu.make_async_remote_copy(
            src_ref=row_ref, dst_ref=out_ref.at[me], send_sem=send_sem.at[peer],
            recv_sem=recv_sem.at[me], device_id=(tok_index, peer), device_id_type=MESH,
        ).start()
    out_ref[me] = row_ref[...]
    for peer in peers:
        pltpu.make_async_remote_copy(
            src_ref=row_ref, dst_ref=out_ref.at[peer], send_sem=send_sem.at[peer],
            recv_sem=recv_sem.at[peer], device_id=(tok_index, peer), device_id_type=MESH,
        ).wait_recv()
    for peer in peers:
        pltpu.make_async_remote_copy(
            src_ref=row_ref, dst_ref=out_ref.at[me], send_sem=send_sem.at[peer],
            recv_sem=recv_sem.at[me], device_id=(tok_index, peer), device_id_type=MESH,
        ).wait_send()


def gather_feat(row_block, n, collective_id):
    rows, width = row_block.shape
    return pl.pallas_call(
        functools.partial(_gather_kernel, n),
        out_shape=jax.ShapeDtypeStruct((n, rows, width), row_block.dtype),
        in_specs=[pl.BlockSpec(memory_space=pltpu.VMEM)],
        out_specs=pl.BlockSpec(memory_space=pltpu.VMEM),
        scratch_shapes=[pltpu.SemaphoreType.DMA((n,)), pltpu.SemaphoreType.DMA((n,))],
        compiler_params=pltpu.CompilerParams(collective_id=collective_id, has_side_effects=True),
    )(row_block).reshape(n * rows, width)


def _ring_gather(x_ref, out_ref, send_right, send_left, send_partner, recv_sem, feat_index, after_first=None):
    tok_count = out_ref.shape[0]
    chips = tok_count // 2
    right_steps = chips // 2
    left_steps = chips - 1 - right_steps
    me = lax.axis_index("tok")
    chip = me // 2
    core = me % 2
    right = lax.rem(chip + 1, chips) * 2 + core
    left = lax.rem(chip + chips - 1, chips) * 2 + core
    partner = chip * 2 + (1 - core)

    def slot_of(offset):
        return lax.rem(chip + offset + 2 * chips, chips) * 2 + core

    def remote(src, slot, sem, target):
        return pltpu.make_async_remote_copy(
            src_ref=src, dst_ref=out_ref.at[slot], send_sem=sem, recv_sem=recv_sem.at[slot],
            device_id=(target, feat_index), device_id_type=MESH,
        )

    sends = []

    def forward_partner(src, slot):
        copy = remote(src, slot, send_partner.at[len(sends_partner)], partner)
        copy.start()
        sends_partner.append(copy)

    sends_partner = []
    out_ref[me] = x_ref[...]
    arrived = []
    for step in range(1, right_steps + 1):
        if step == 1:
            src_right = x_ref
            src_left = x_ref
        else:
            from_left = slot_of(-(step - 1))
            remote(x_ref, from_left, send_right.at[0], right).wait_recv()
            src_right = out_ref.at[from_left]
            arrived.append(from_left)
        copy = remote(src_right, slot_of(-(step - 1)), send_right.at[step - 1], right)
        copy.start()
        sends.append(copy)
        if step > 1 and step - 1 <= left_steps:
            from_right = slot_of(step - 1)
            remote(x_ref, from_right, send_left.at[0], left).wait_recv()
            src_left = out_ref.at[from_right]
            arrived.append(from_right)
        if step <= left_steps:
            copy = remote(src_left, slot_of(step - 1), send_left.at[step - 1], left)
            copy.start()
            sends.append(copy)
        if step == 1:
            if after_first is not None:
                after_first()
            forward_partner(x_ref, me)
        for slot in arrived:
            forward_partner(out_ref.at[slot], slot)
        arrived = []
    last_left = slot_of(-right_steps)
    remote(x_ref, last_left, send_right.at[0], right).wait_recv()
    forward_partner(out_ref.at[last_left], last_left)
    if left_steps >= 1 and left_steps + 1 > right_steps:
        last_right = slot_of(left_steps)
        remote(x_ref, last_right, send_left.at[0], left).wait_recv()
        forward_partner(out_ref.at[last_right], last_right)
    for other_chip in range(chips):
        remote(x_ref, other_chip * 2 + (1 - core), send_partner.at[0], partner).wait_recv()
    for copy in sends + sends_partner:
        copy.wait_send()


def _first_kernel(n, row_ref, weight_ref, out_ref, weight_out, send_sem, recv_sem,
                  send_right, send_left, send_partner, weight_recv):
    me = lax.axis_index("feat")
    tok_index = lax.axis_index("tok")
    chips = weight_out.shape[0] // 2
    chip = tok_index // 2
    core = tok_index % 2
    peers = [lax.rem(me + d, n) for d in range(1, n)]
    barrier = pltpu.get_barrier_semaphore()
    for peer in peers:
        pl.semaphore_signal(barrier, inc=1, device_id=(tok_index, peer), device_id_type=MESH)
    ring_peers = [
        lax.rem(chip + 1, chips) * 2 + core,
        lax.rem(chip + chips - 1, chips) * 2 + core,
        chip * 2 + (1 - core),
    ]
    for peer in ring_peers:
        pl.semaphore_signal(barrier, inc=1, device_id=(peer, me), device_id_type=MESH)
    pl.semaphore_wait(barrier, len(peers) + len(ring_peers))

    def start_rows():
        for peer in peers:
            pltpu.make_async_remote_copy(
                src_ref=row_ref, dst_ref=out_ref.at[me], send_sem=send_sem.at[peer],
                recv_sem=recv_sem.at[me], device_id=(tok_index, peer), device_id_type=MESH,
            ).start()

    _ring_gather(weight_ref, weight_out, send_right, send_left, send_partner, weight_recv, me, start_rows)
    out_ref[me] = row_ref[...]
    for peer in peers:
        pltpu.make_async_remote_copy(
            src_ref=row_ref, dst_ref=out_ref.at[peer], send_sem=send_sem.at[peer],
            recv_sem=recv_sem.at[peer], device_id=(tok_index, peer), device_id_type=MESH,
        ).wait_recv()
    for peer in peers:
        pltpu.make_async_remote_copy(
            src_ref=row_ref, dst_ref=out_ref.at[me], send_sem=send_sem.at[peer],
            recv_sem=recv_sem.at[me], device_id=(tok_index, peer), device_id_type=MESH,
        ).wait_send()


def first_exchange(row_block, weight_block, n, tok_count, collective_id):
    rows, width = row_block.shape
    weight_rows, weight_width = weight_block.shape
    chips = tok_count // 2
    gathered, weights = pl.pallas_call(
        functools.partial(_first_kernel, n),
        out_shape=(
            jax.ShapeDtypeStruct((n, rows, width), row_block.dtype),
            jax.ShapeDtypeStruct((tok_count, weight_rows, weight_width), weight_block.dtype),
        ),
        in_specs=[pl.BlockSpec(memory_space=pltpu.VMEM)] * 2,
        out_specs=(pl.BlockSpec(memory_space=pltpu.VMEM),) * 2,
        scratch_shapes=[
            pltpu.SemaphoreType.DMA((n,)),
            pltpu.SemaphoreType.DMA((n,)),
            pltpu.SemaphoreType.DMA((chips,)),
            pltpu.SemaphoreType.DMA((chips,)),
            pltpu.SemaphoreType.DMA((chips,)),
            pltpu.SemaphoreType.DMA((tok_count,)),
        ],
        compiler_params=pltpu.CompilerParams(collective_id=collective_id, has_side_effects=True),
    )(row_block, weight_block)
    return gathered.reshape(n * rows, width), weights


def _route_kernel(n, packed_ref, out_ref, send_sem, recv_sem):
    me = lax.axis_index("tok")
    feat_index = lax.axis_index("feat")
    peers = [lax.rem(me + d, n) for d in range(1, n)]
    barrier = pltpu.get_barrier_semaphore()
    for peer in peers:
        pl.semaphore_signal(barrier, inc=1, device_id=(peer, feat_index), device_id_type=MESH)
    pl.semaphore_wait(barrier, len(peers))
    for peer in peers:
        pltpu.make_async_remote_copy(
            src_ref=packed_ref.at[peer], dst_ref=out_ref.at[me], send_sem=send_sem.at[peer],
            recv_sem=recv_sem.at[me], device_id=(peer, feat_index), device_id_type=MESH,
        ).start()
    out_ref[me] = packed_ref[me]
    for peer in peers:
        pltpu.make_async_remote_copy(
            src_ref=packed_ref.at[peer], dst_ref=out_ref.at[peer], send_sem=send_sem.at[peer],
            recv_sem=recv_sem.at[peer], device_id=(peer, feat_index), device_id_type=MESH,
        ).wait_recv()
    for peer in peers:
        pltpu.make_async_remote_copy(
            src_ref=packed_ref.at[peer], dst_ref=out_ref.at[me], send_sem=send_sem.at[peer],
            recv_sem=recv_sem.at[me], device_id=(peer, feat_index), device_id_type=MESH,
        ).wait_send()


def route_exchange(packed, collective_id):
    n = packed.shape[0]
    return pl.pallas_call(
        functools.partial(_route_kernel, n),
        out_shape=jax.ShapeDtypeStruct(packed.shape, packed.dtype),
        in_specs=[pl.BlockSpec(memory_space=pltpu.VMEM)],
        out_specs=pl.BlockSpec(memory_space=pltpu.VMEM),
        scratch_shapes=[pltpu.SemaphoreType.DMA((n,)), pltpu.SemaphoreType.DMA((n,))],
        compiler_params=pltpu.CompilerParams(collective_id=collective_id, has_side_effects=True),
    )(packed)


def _mix_kernel(n, part_ref, resid_ref, gain_ref, resid_out, out_ref, held, mine,
                scatter_send, scatter_recv, gather_send, gather_recv):
    me = lax.axis_index("feat")
    tok_index = lax.axis_index("tok")
    peers = [lax.rem(me + d, n) for d in range(1, n)]
    _greet(peers, tok_index)

    def scatter_copy(peer, slot):
        return pltpu.make_async_remote_copy(
            src_ref=part_ref.at[peer], dst_ref=held.at[slot], send_sem=scatter_send.at[peer],
            recv_sem=scatter_recv.at[slot], device_id=(tok_index, peer), device_id_type=MESH,
        )

    def gather_copy(peer, slot):
        return pltpu.make_async_remote_copy(
            src_ref=mine, dst_ref=out_ref.at[slot], send_sem=gather_send.at[peer],
            recv_sem=gather_recv.at[slot], device_id=(tok_index, peer), device_id_type=MESH,
        )

    for peer in peers:
        scatter_copy(peer, me).start()
    total = part_ref[me].astype(jnp.float32)
    for peer in peers:
        scatter_copy(peer, peer).wait_recv()
        total = total + held[peer].astype(jnp.float32)
    summed = (resid_ref[...].astype(jnp.float32) + total).astype(jnp.bfloat16)
    resid_out[...] = summed
    as_float = summed.astype(jnp.float32)
    center = jnp.mean(as_float, axis=-1, keepdims=True)
    spread = jnp.mean(jnp.square(as_float - center), axis=-1, keepdims=True)
    normed = ((as_float - center) * lax.rsqrt(spread + epsilon) * gain_ref[...]).astype(jnp.bfloat16)
    mine[...] = normed
    out_ref[me] = normed
    for peer in peers:
        gather_copy(peer, me).start()
    for peer in peers:
        gather_copy(peer, peer).wait_recv()
    for peer in peers:
        scatter_copy(peer, me).wait_send()
        gather_copy(peer, me).wait_send()


def mix_feat(parts, resid, gain, n, collective_id):
    _, rows, width = parts.shape
    new_resid, gathered = pl.pallas_call(
        functools.partial(_mix_kernel, n),
        out_shape=(
            jax.ShapeDtypeStruct((rows, width), jnp.bfloat16),
            jax.ShapeDtypeStruct((n, rows, width), jnp.bfloat16),
        ),
        in_specs=[pl.BlockSpec(memory_space=pltpu.VMEM)] * 3,
        out_specs=(pl.BlockSpec(memory_space=pltpu.VMEM),) * 2,
        scratch_shapes=[
            pltpu.VMEM((n, rows, width), parts.dtype),
            pltpu.VMEM((rows, width), jnp.bfloat16),
            pltpu.SemaphoreType.DMA((n,)),
            pltpu.SemaphoreType.DMA((n,)),
            pltpu.SemaphoreType.DMA((n,)),
            pltpu.SemaphoreType.DMA((n,)),
        ],
        compiler_params=pltpu.CompilerParams(collective_id=collective_id, has_side_effects=True),
    )(parts, resid, gain.astype(jnp.float32).reshape(1, width))
    return new_resid, gathered.reshape(n * rows, width)


def _scatter_kernel(n, part_ref, out_ref, held, send_sem, recv_sem):
    me = lax.axis_index("feat")
    tok_index = lax.axis_index("tok")
    peers = [lax.rem(me + d, n) for d in range(1, n)]
    _greet(peers, tok_index)
    for peer in peers:
        pltpu.make_async_remote_copy(
            src_ref=part_ref.at[peer], dst_ref=held.at[me], send_sem=send_sem.at[peer],
            recv_sem=recv_sem.at[me], device_id=(tok_index, peer), device_id_type=MESH,
        ).start()
    total = part_ref[me].astype(jnp.float32)
    for peer in peers:
        pltpu.make_async_remote_copy(
            src_ref=part_ref.at[peer], dst_ref=held.at[peer], send_sem=send_sem.at[peer],
            recv_sem=recv_sem.at[peer], device_id=(tok_index, peer), device_id_type=MESH,
        ).wait_recv()
        total = total + held[peer].astype(jnp.float32)
    out_ref[...] = total
    for peer in peers:
        pltpu.make_async_remote_copy(
            src_ref=part_ref.at[peer], dst_ref=held.at[me], send_sem=send_sem.at[peer],
            recv_sem=recv_sem.at[me], device_id=(tok_index, peer), device_id_type=MESH,
        ).wait_send()


def scatter_feat(parts, n, collective_id):
    _, rows, width = parts.shape
    return pl.pallas_call(
        functools.partial(_scatter_kernel, n),
        out_shape=jax.ShapeDtypeStruct((rows, width), jnp.float32),
        in_specs=[pl.BlockSpec(memory_space=pltpu.VMEM)],
        out_specs=pl.BlockSpec(memory_space=pltpu.VMEM),
        scratch_shapes=[
            pltpu.VMEM((n, rows, width), parts.dtype),
            pltpu.SemaphoreType.DMA((n,)),
            pltpu.SemaphoreType.DMA((n,)),
        ],
        compiler_params=pltpu.CompilerParams(collective_id=collective_id, has_side_effects=True),
    )(parts)

MESH = pl.DeviceIdType.MESH
LEAST_UNITS = 4
MOST_UNITS = 16
HEAD_DIM = 88


epsilon = 1e-06


def layer_norm(row_block, gain_row):
    as_float = row_block.astype(jnp.float32)
    center = jnp.mean(as_float, axis=-1, keepdims=True)
    spread = jnp.mean(jnp.square(as_float - center), axis=-1, keepdims=True)
    scaled = (as_float - center) * lax.rsqrt(spread + epsilon) * gain_row.astype(jnp.float32)
    return scaled.astype(jnp.bfloat16)


def project_rows(row_block, weight_block, collective_id):
    n = lax.axis_size("feat")
    return jnp.dot(
        gather_feat(row_block, n, collective_id),
        weight_block,
        preferred_element_type=jnp.float32,
    )


def scatter_rows(left_rows, right_rows, collective_id):
    n = lax.axis_size("feat")
    parts = jnp.dot(left_rows, right_rows, preferred_element_type=jnp.float32).astype(jnp.bfloat16)
    return scatter_feat(parts.reshape(n, parts.shape[0] // n, parts.shape[1]), n, collective_id)


def early_weights(weight_up, weight_down):
    return (weight_up, weight_down)


def upper_weight(fetched):
    return lax.all_gather(fetched[0], "tok", axis=0, tiled=True)


def lower_weight(fetched):
    return lax.all_gather(fetched[1], "tok", axis=1, tiled=True)


def attend(projected, segment_ids, head_count):
    token_count = projected.shape[0]
    parts_all = projected.reshape(token_count, 3, head_count, HEAD_DIM)
    queries = (parts_all[:, 0] * HEAD_DIM ** (-0.5)).astype(jnp.bfloat16)
    keys_here = parts_all[:, 1].astype(jnp.bfloat16)
    values_here = parts_all[:, 2].astype(jnp.bfloat16)
    scores = jnp.einsum("qhd,khd->hqk", queries, keys_here, preferred_element_type=jnp.float32)
    same_segment = segment_ids[:, None] == segment_ids[None, :]
    scores = jnp.where(same_segment[None, :, :], scores, -1e30)
    highest = jnp.max(scores, axis=-1, keepdims=True)
    raised = jnp.exp(scores - highest)
    weights_soft = (raised / jnp.sum(raised, axis=-1, keepdims=True)).astype(jnp.bfloat16)
    attended = jnp.einsum(
        "hqk,khd->qhd", weights_soft, values_here, preferred_element_type=jnp.float32
    )
    return attended.astype(jnp.bfloat16).reshape(token_count, head_count * HEAD_DIM)


def route_rows(embedded, segment_ids, owners):
    merged_count = embedded.shape[0]
    peer_count = owners.shape[0]
    least_units = max(LEAST_UNITS, (merged_count + peer_count - 1) // peer_count)
    slot_count = max(MOST_UNITS, 2 * least_units)
    first_ids = segment_ids.reshape(merged_count, 4)[:, 0]
    id_base = lax.axis_index("tok") * peer_count
    local_index = first_ids - id_base
    owner_pick = local_index[:, None] == jnp.arange(peer_count, dtype=jnp.int32)[None, :]
    owner_of = jnp.sum(jnp.where(owner_pick, owners[None, :], 0), axis=1)
    row_index = jnp.arange(merged_count, dtype=jnp.int32)
    earlier = (row_index[None, :] < row_index[:, None]) & (first_ids[None, :] == first_ids[:, None])
    within = jnp.sum(earlier.astype(jnp.int32), axis=1)
    target = owner_of * slot_count + within
    select = (
        jnp.arange(peer_count * slot_count, dtype=jnp.int32)[:, None] == target[None, :]
    ).astype(jnp.bfloat16)
    packed = jnp.dot(select, embedded, preferred_element_type=jnp.float32).astype(jnp.bfloat16)
    packed = packed.reshape(peer_count, slot_count, embedded.shape[1])
    received = route_exchange(packed, 5)
    return received.reshape(peer_count * slot_count, embedded.shape[1])


def body(
    tokens,
    segment_ids,
    owners,
    project_in,
    project_out,
    weight_up,
    weight_down,
    weight_merge,
    gain_attend,
    gain_hidden,
    gain_final,
):
    model_width = tokens.shape[1]
    head_count = project_in.shape[2] // HEAD_DIM
    units = weight_up.shape[1]
    feat_count = lax.axis_size("feat")
    tok_count = lax.axis_size("tok")
    flat_in = project_in.reshape(model_width, 3 * project_in.shape[2])
    local_count = tokens.shape[0]
    normed = layer_norm(tokens, gain_attend)
    stacked = jnp.concatenate([weight_up, weight_down.T], axis=1)
    gathered, weights = first_exchange(normed, stacked, feat_count, tok_count, 0)
    both = weights.reshape(tok_count * weight_up.shape[0], 2 * units)
    upper = both[:, :units]
    lower_t = both[:, units:]
    projected = jnp.dot(gathered, flat_in, preferred_element_type=jnp.float32)
    attended = attend(projected, segment_ids, head_count)
    attn_parts = jnp.dot(attended, project_out, preferred_element_type=jnp.float32).astype(jnp.bfloat16)
    second, hidden_rows = mix_feat(
        attn_parts.reshape(feat_count, local_count, model_width), tokens, gain_hidden, feat_count, 1
    )
    hidden = jax.nn.gelu(
        jnp.dot(hidden_rows, upper, preferred_element_type=jnp.float32), approximate=False
    ).astype(jnp.bfloat16)
    down_parts = lax.dot_general(
        hidden, lower_t, (((1,), (1,)), ((), ())), preferred_element_type=jnp.float32
    ).astype(jnp.bfloat16)
    _, final_rows = mix_feat(
        down_parts.reshape(feat_count, local_count, model_width), second, gain_final, feat_count, 3
    )
    merged = final_rows.reshape(final_rows.shape[0] // 4, 4 * model_width)
    embedded = jnp.dot(merged, weight_merge, preferred_element_type=jnp.float32).astype(jnp.bfloat16)
    return route_rows(embedded, segment_ids, owners)


def solution(mesh):
    return jax.shard_map(
        body,
        mesh=mesh,
        in_specs=(
            P(("tok", "feat"), None),
            P("tok"),
            P("tok"),
            P(None, None, "feat"),
            P("feat", None),
            P("tok", "feat"),
            P("feat", "tok"),
            P(None, "feat"),
            P(),
            P(),
            P(),
        ),
        out_specs=P("tok", "feat"),
        check_vma=False,
    )
```

```python
import functools
import jax
import jax.numpy as jnp
from jax import lax
from jax.experimental import pallas as pl
from jax.experimental.pallas import tpu as pltpu
from jax.sharding import PartitionSpec as P


def _greet(peers, tok_index):
    barrier = pltpu.get_barrier_semaphore()
    for peer in peers:
        pl.semaphore_signal(barrier, inc=1, device_id=(tok_index, peer), device_id_type=MESH)
    pl.semaphore_wait(barrier, len(peers))


def _gather_kernel(n, row_ref, out_ref, send_sem, recv_sem):
    me = lax.axis_index("feat")
    tok_index = lax.axis_index("tok")
    peers = [lax.rem(me + d, n) for d in range(1, n)]
    _greet(peers, tok_index)
    for peer in peers:
        pltpu.make_async_remote_copy(
            src_ref=row_ref, dst_ref=out_ref.at[me], send_sem=send_sem.at[peer],
            recv_sem=recv_sem.at[me], device_id=(tok_index, peer), device_id_type=MESH,
        ).start()
    out_ref[me] = row_ref[...]
    for peer in peers:
        pltpu.make_async_remote_copy(
            src_ref=row_ref, dst_ref=out_ref.at[peer], send_sem=send_sem.at[peer],
            recv_sem=recv_sem.at[peer], device_id=(tok_index, peer), device_id_type=MESH,
        ).wait_recv()
    for peer in peers:
        pltpu.make_async_remote_copy(
            src_ref=row_ref, dst_ref=out_ref.at[me], send_sem=send_sem.at[peer],
            recv_sem=recv_sem.at[me], device_id=(tok_index, peer), device_id_type=MESH,
        ).wait_send()


def gather_feat(row_block, n, collective_id):
    rows, width = row_block.shape
    return pl.pallas_call(
        functools.partial(_gather_kernel, n),
        out_shape=jax.ShapeDtypeStruct((n, rows, width), row_block.dtype),
        in_specs=[pl.BlockSpec(memory_space=pltpu.VMEM)],
        out_specs=pl.BlockSpec(memory_space=pltpu.VMEM),
        scratch_shapes=[pltpu.SemaphoreType.DMA((n,)), pltpu.SemaphoreType.DMA((n,))],
        compiler_params=pltpu.CompilerParams(collective_id=collective_id, has_side_effects=True),
    )(row_block).reshape(n * rows, width)


def _ring_gather(x_ref, out_ref, send_right, send_left, send_partner, recv_sem, feat_index, after_first=None,
                 hook=None, hook_step=1):
    tok_count = out_ref.shape[0]
    chips = tok_count // 2
    right_steps = chips // 2
    left_steps = chips - 1 - right_steps
    me = lax.axis_index("tok")
    chip = me // 2
    core = me % 2
    right = lax.rem(chip + 1, chips) * 2 + core
    left = lax.rem(chip + chips - 1, chips) * 2 + core
    partner = chip * 2 + (1 - core)

    def slot_of(offset):
        return lax.rem(chip + offset + 2 * chips, chips) * 2 + core

    def remote(src, slot, sem, target):
        return pltpu.make_async_remote_copy(
            src_ref=src, dst_ref=out_ref.at[slot], send_sem=sem, recv_sem=recv_sem.at[slot],
            device_id=(target, feat_index), device_id_type=MESH,
        )

    sends = []

    def forward_partner(src, slot):
        copy = remote(src, slot, send_partner.at[len(sends_partner)], partner)
        copy.start()
        sends_partner.append(copy)

    sends_partner = []
    out_ref[me] = x_ref[...]
    arrived = []
    for step in range(1, right_steps + 1):
        if step == 1:
            src_right = x_ref
            src_left = x_ref
        else:
            from_left = slot_of(-(step - 1))
            remote(x_ref, from_left, send_right.at[0], right).wait_recv()
            src_right = out_ref.at[from_left]
            arrived.append(from_left)
        copy = remote(src_right, slot_of(-(step - 1)), send_right.at[step - 1], right)
        copy.start()
        sends.append(copy)
        if step > 1 and step - 1 <= left_steps:
            from_right = slot_of(step - 1)
            remote(x_ref, from_right, send_left.at[0], left).wait_recv()
            src_left = out_ref.at[from_right]
            arrived.append(from_right)
        if step <= left_steps:
            copy = remote(src_left, slot_of(step - 1), send_left.at[step - 1], left)
            copy.start()
            sends.append(copy)
        if step == 1:
            if after_first is not None:
                after_first()
            forward_partner(x_ref, me)
        for slot in arrived:
            forward_partner(out_ref.at[slot], slot)
        arrived = []
        if hook is not None and step == min(hook_step, right_steps):
            hook()
    last_left = slot_of(-right_steps)
    remote(x_ref, last_left, send_right.at[0], right).wait_recv()
    forward_partner(out_ref.at[last_left], last_left)
    if left_steps >= 1 and left_steps + 1 > right_steps:
        last_right = slot_of(left_steps)
        remote(x_ref, last_right, send_left.at[0], left).wait_recv()
        forward_partner(out_ref.at[last_right], last_right)
    for other_chip in range(chips):
        remote(x_ref, other_chip * 2 + (1 - core), send_partner.at[0], partner).wait_recv()
    for copy in sends + sends_partner:
        copy.wait_send()


def _first_kernel(n, row_ref, weight_ref, out_ref, weight_out, send_sem, recv_sem,
                  send_right, send_left, send_partner, weight_recv):
    me = lax.axis_index("feat")
    tok_index = lax.axis_index("tok")
    chips = weight_out.shape[0] // 2
    chip = tok_index // 2
    core = tok_index % 2
    peers = [lax.rem(me + d, n) for d in range(1, n)]
    barrier = pltpu.get_barrier_semaphore()
    for peer in peers:
        pl.semaphore_signal(barrier, inc=1, device_id=(tok_index, peer), device_id_type=MESH)
    ring_peers = [
        lax.rem(chip + 1, chips) * 2 + core,
        lax.rem(chip + chips - 1, chips) * 2 + core,
        chip * 2 + (1 - core),
    ]
    for peer in ring_peers:
        pl.semaphore_signal(barrier, inc=1, device_id=(peer, me), device_id_type=MESH)
    pl.semaphore_wait(barrier, len(peers) + len(ring_peers))

    def start_rows():
        for peer in peers:
            pltpu.make_async_remote_copy(
                src_ref=row_ref, dst_ref=out_ref.at[me], send_sem=send_sem.at[peer],
                recv_sem=recv_sem.at[me], device_id=(tok_index, peer), device_id_type=MESH,
            ).start()

    _ring_gather(weight_ref, weight_out, send_right, send_left, send_partner, weight_recv, me, start_rows)
    out_ref[me] = row_ref[...]
    for peer in peers:
        pltpu.make_async_remote_copy(
            src_ref=row_ref, dst_ref=out_ref.at[peer], send_sem=send_sem.at[peer],
            recv_sem=recv_sem.at[peer], device_id=(tok_index, peer), device_id_type=MESH,
        ).wait_recv()
    for peer in peers:
        pltpu.make_async_remote_copy(
            src_ref=row_ref, dst_ref=out_ref.at[me], send_sem=send_sem.at[peer],
            recv_sem=recv_sem.at[me], device_id=(tok_index, peer), device_id_type=MESH,
        ).wait_send()


def first_exchange(row_block, weight_block, n, tok_count, collective_id):
    rows, width = row_block.shape
    weight_rows, weight_width = weight_block.shape
    chips = tok_count // 2
    gathered, weights = pl.pallas_call(
        functools.partial(_first_kernel, n),
        out_shape=(
            jax.ShapeDtypeStruct((n, rows, width), row_block.dtype),
            jax.ShapeDtypeStruct((tok_count, weight_rows, weight_width), weight_block.dtype),
        ),
        in_specs=[pl.BlockSpec(memory_space=pltpu.VMEM)] * 2,
        out_specs=(pl.BlockSpec(memory_space=pltpu.VMEM),) * 2,
        scratch_shapes=[
            pltpu.SemaphoreType.DMA((n,)),
            pltpu.SemaphoreType.DMA((n,)),
            pltpu.SemaphoreType.DMA((chips,)),
            pltpu.SemaphoreType.DMA((chips,)),
            pltpu.SemaphoreType.DMA((chips,)),
            pltpu.SemaphoreType.DMA((tok_count,)),
        ],
        compiler_params=pltpu.CompilerParams(collective_id=collective_id, has_side_effects=True),
    )(row_block, weight_block)
    return gathered.reshape(n * rows, width), weights


def _route_kernel(n, packed_ref, out_ref, send_sem, recv_sem):
    me = lax.axis_index("tok")
    feat_index = lax.axis_index("feat")
    peers = [lax.rem(me + d, n) for d in range(1, n)]
    barrier = pltpu.get_barrier_semaphore()
    for peer in peers:
        pl.semaphore_signal(barrier, inc=1, device_id=(peer, feat_index), device_id_type=MESH)
    pl.semaphore_wait(barrier, len(peers))
    for peer in peers:
        pltpu.make_async_remote_copy(
            src_ref=packed_ref.at[peer], dst_ref=out_ref.at[me], send_sem=send_sem.at[peer],
            recv_sem=recv_sem.at[me], device_id=(peer, feat_index), device_id_type=MESH,
        ).start()
    out_ref[me] = packed_ref[me]
    for peer in peers:
        pltpu.make_async_remote_copy(
            src_ref=packed_ref.at[peer], dst_ref=out_ref.at[peer], send_sem=send_sem.at[peer],
            recv_sem=recv_sem.at[peer], device_id=(peer, feat_index), device_id_type=MESH,
        ).wait_recv()
    for peer in peers:
        pltpu.make_async_remote_copy(
            src_ref=packed_ref.at[peer], dst_ref=out_ref.at[me], send_sem=send_sem.at[peer],
            recv_sem=recv_sem.at[me], device_id=(peer, feat_index), device_id_type=MESH,
        ).wait_send()


def route_exchange(packed, collective_id):
    n = packed.shape[0]
    return pl.pallas_call(
        functools.partial(_route_kernel, n),
        out_shape=jax.ShapeDtypeStruct(packed.shape, packed.dtype),
        in_specs=[pl.BlockSpec(memory_space=pltpu.VMEM)],
        out_specs=pl.BlockSpec(memory_space=pltpu.VMEM),
        scratch_shapes=[pltpu.SemaphoreType.DMA((n,)), pltpu.SemaphoreType.DMA((n,))],
        compiler_params=pltpu.CompilerParams(collective_id=collective_id, has_side_effects=True),
    )(packed)


def _mix_kernel(n, part_ref, resid_ref, gain_ref, resid_out, out_ref, held, mine,
                scatter_send, scatter_recv, gather_send, gather_recv):
    me = lax.axis_index("feat")
    tok_index = lax.axis_index("tok")
    peers = [lax.rem(me + d, n) for d in range(1, n)]
    _greet(peers, tok_index)

    def scatter_copy(peer, slot):
        return pltpu.make_async_remote_copy(
            src_ref=part_ref.at[peer], dst_ref=held.at[slot], send_sem=scatter_send.at[peer],
            recv_sem=scatter_recv.at[slot], device_id=(tok_index, peer), device_id_type=MESH,
        )

    def gather_copy(peer, slot):
        return pltpu.make_async_remote_copy(
            src_ref=mine, dst_ref=out_ref.at[slot], send_sem=gather_send.at[peer],
            recv_sem=gather_recv.at[slot], device_id=(tok_index, peer), device_id_type=MESH,
        )

    for peer in peers:
        scatter_copy(peer, me).start()
    total = part_ref[me].astype(jnp.float32)
    for peer in peers:
        scatter_copy(peer, peer).wait_recv()
        total = total + held[peer].astype(jnp.float32)
    summed = (resid_ref[...].astype(jnp.float32) + total).astype(jnp.bfloat16)
    resid_out[...] = summed
    as_float = summed.astype(jnp.float32)
    center = jnp.mean(as_float, axis=-1, keepdims=True)
    spread = jnp.mean(jnp.square(as_float - center), axis=-1, keepdims=True)
    normed = ((as_float - center) * lax.rsqrt(spread + epsilon) * gain_ref[...]).astype(jnp.bfloat16)
    mine[...] = normed
    out_ref[me] = normed
    for peer in peers:
        gather_copy(peer, me).start()
    for peer in peers:
        gather_copy(peer, peer).wait_recv()
    for peer in peers:
        scatter_copy(peer, me).wait_send()
        gather_copy(peer, me).wait_send()


def mix_feat(parts, resid, gain, n, collective_id):
    _, rows, width = parts.shape
    new_resid, gathered = pl.pallas_call(
        functools.partial(_mix_kernel, n),
        out_shape=(
            jax.ShapeDtypeStruct((rows, width), jnp.bfloat16),
            jax.ShapeDtypeStruct((n, rows, width), jnp.bfloat16),
        ),
        in_specs=[pl.BlockSpec(memory_space=pltpu.VMEM)] * 3,
        out_specs=(pl.BlockSpec(memory_space=pltpu.VMEM),) * 2,
        scratch_shapes=[
            pltpu.VMEM((n, rows, width), parts.dtype),
            pltpu.VMEM((rows, width), jnp.bfloat16),
            pltpu.SemaphoreType.DMA((n,)),
            pltpu.SemaphoreType.DMA((n,)),
            pltpu.SemaphoreType.DMA((n,)),
            pltpu.SemaphoreType.DMA((n,)),
        ],
        compiler_params=pltpu.CompilerParams(collective_id=collective_id, has_side_effects=True),
    )(parts, resid, gain.astype(jnp.float32).reshape(1, width))
    return new_resid, gathered.reshape(n * rows, width)


def _mix_ring_kernel(n, part_ref, resid_ref, gain_ref, weight_ref, resid_out, out_ref, weight_out,
                     held, mine, scatter_send, scatter_recv, gather_send, gather_recv,
                     send_right, send_left, send_partner, weight_recv):
    me = lax.axis_index("feat")
    tok_index = lax.axis_index("tok")
    chips = weight_out.shape[0] // 2
    chip = tok_index // 2
    core = tok_index % 2
    peers = [lax.rem(me + d, n) for d in range(1, n)]
    barrier = pltpu.get_barrier_semaphore()
    for peer in peers:
        pl.semaphore_signal(barrier, inc=1, device_id=(tok_index, peer), device_id_type=MESH)
    ring_peers = [
        lax.rem(chip + 1, chips) * 2 + core,
        lax.rem(chip + chips - 1, chips) * 2 + core,
        chip * 2 + (1 - core),
    ]
    for peer in ring_peers:
        pl.semaphore_signal(barrier, inc=1, device_id=(peer, me), device_id_type=MESH)
    pl.semaphore_wait(barrier, len(peers) + len(ring_peers))

    def scatter_copy(peer, slot):
        return pltpu.make_async_remote_copy(
            src_ref=part_ref.at[peer], dst_ref=held.at[slot], send_sem=scatter_send.at[peer],
            recv_sem=scatter_recv.at[slot], device_id=(tok_index, peer), device_id_type=MESH,
        )

    def gather_copy(peer, slot):
        return pltpu.make_async_remote_copy(
            src_ref=mine, dst_ref=out_ref.at[slot], send_sem=gather_send.at[peer],
            recv_sem=gather_recv.at[slot], device_id=(tok_index, peer), device_id_type=MESH,
        )

    for peer in peers:
        scatter_copy(peer, me).start()

    def norm_and_send():
        total = part_ref[me].astype(jnp.float32)
        for peer in peers:
            scatter_copy(peer, peer).wait_recv()
            total = total + held[peer].astype(jnp.float32)
        summed = (resid_ref[...].astype(jnp.float32) + total).astype(jnp.bfloat16)
        resid_out[...] = summed
        as_float = summed.astype(jnp.float32)
        center = jnp.mean(as_float, axis=-1, keepdims=True)
        spread = jnp.mean(jnp.square(as_float - center), axis=-1, keepdims=True)
        normed = ((as_float - center) * lax.rsqrt(spread + epsilon) * gain_ref[...]).astype(jnp.bfloat16)
        mine[...] = normed
        out_ref[me] = normed
        for peer in peers:
            gather_copy(peer, me).start()

    _ring_gather(weight_ref, weight_out, send_right, send_left, send_partner, weight_recv, me,
                 hook=norm_and_send, hook_step=3)
    for peer in peers:
        gather_copy(peer, peer).wait_recv()
    for peer in peers:
        scatter_copy(peer, me).wait_send()
        gather_copy(peer, me).wait_send()


def mix_ring_feat(parts, resid, gain, weight_block, n, tok_count, collective_id):
    _, rows, width = parts.shape
    weight_rows, weight_width = weight_block.shape
    chips = tok_count // 2
    new_resid, gathered, weights = pl.pallas_call(
        functools.partial(_mix_ring_kernel, n),
        out_shape=(
            jax.ShapeDtypeStruct((rows, width), jnp.bfloat16),
            jax.ShapeDtypeStruct((n, rows, width), jnp.bfloat16),
            jax.ShapeDtypeStruct((tok_count, weight_rows, weight_width), weight_block.dtype),
        ),
        in_specs=[pl.BlockSpec(memory_space=pltpu.VMEM)] * 4,
        out_specs=(pl.BlockSpec(memory_space=pltpu.VMEM),) * 3,
        scratch_shapes=[
            pltpu.VMEM((n, rows, width), parts.dtype),
            pltpu.VMEM((rows, width), jnp.bfloat16),
            pltpu.SemaphoreType.DMA((n,)),
            pltpu.SemaphoreType.DMA((n,)),
            pltpu.SemaphoreType.DMA((n,)),
            pltpu.SemaphoreType.DMA((n,)),
            pltpu.SemaphoreType.DMA((chips,)),
            pltpu.SemaphoreType.DMA((chips,)),
            pltpu.SemaphoreType.DMA((chips,)),
            pltpu.SemaphoreType.DMA((tok_count,)),
        ],
        compiler_params=pltpu.CompilerParams(collective_id=collective_id, has_side_effects=True),
    )(parts, resid, gain.astype(jnp.float32).reshape(1, width), weight_block)
    return new_resid, gathered.reshape(n * rows, width), weights


def _scatter_kernel(n, part_ref, out_ref, held, send_sem, recv_sem):
    me = lax.axis_index("feat")
    tok_index = lax.axis_index("tok")
    peers = [lax.rem(me + d, n) for d in range(1, n)]
    _greet(peers, tok_index)
    for peer in peers:
        pltpu.make_async_remote_copy(
            src_ref=part_ref.at[peer], dst_ref=held.at[me], send_sem=send_sem.at[peer],
            recv_sem=recv_sem.at[me], device_id=(tok_index, peer), device_id_type=MESH,
        ).start()
    total = part_ref[me].astype(jnp.float32)
    for peer in peers:
        pltpu.make_async_remote_copy(
            src_ref=part_ref.at[peer], dst_ref=held.at[peer], send_sem=send_sem.at[peer],
            recv_sem=recv_sem.at[peer], device_id=(tok_index, peer), device_id_type=MESH,
        ).wait_recv()
        total = total + held[peer].astype(jnp.float32)
    out_ref[...] = total
    for peer in peers:
        pltpu.make_async_remote_copy(
            src_ref=part_ref.at[peer], dst_ref=held.at[me], send_sem=send_sem.at[peer],
            recv_sem=recv_sem.at[me], device_id=(tok_index, peer), device_id_type=MESH,
        ).wait_send()


def scatter_feat(parts, n, collective_id):
    _, rows, width = parts.shape
    return pl.pallas_call(
        functools.partial(_scatter_kernel, n),
        out_shape=jax.ShapeDtypeStruct((rows, width), jnp.float32),
        in_specs=[pl.BlockSpec(memory_space=pltpu.VMEM)],
        out_specs=pl.BlockSpec(memory_space=pltpu.VMEM),
        scratch_shapes=[
            pltpu.VMEM((n, rows, width), parts.dtype),
            pltpu.SemaphoreType.DMA((n,)),
            pltpu.SemaphoreType.DMA((n,)),
        ],
        compiler_params=pltpu.CompilerParams(collective_id=collective_id, has_side_effects=True),
    )(parts)

MESH = pl.DeviceIdType.MESH
LEAST_UNITS = 4
MOST_UNITS = 16
HEAD_DIM = 88


epsilon = 1e-06


def layer_norm(row_block, gain_row):
    as_float = row_block.astype(jnp.float32)
    center = jnp.mean(as_float, axis=-1, keepdims=True)
    spread = jnp.mean(jnp.square(as_float - center), axis=-1, keepdims=True)
    scaled = (as_float - center) * lax.rsqrt(spread + epsilon) * gain_row.astype(jnp.float32)
    return scaled.astype(jnp.bfloat16)


def project_rows(row_block, weight_block, collective_id):
    n = lax.axis_size("feat")
    return jnp.dot(
        gather_feat(row_block, n, collective_id),
        weight_block,
        preferred_element_type=jnp.float32,
    )


def scatter_rows(left_rows, right_rows, collective_id):
    n = lax.axis_size("feat")
    parts = jnp.dot(left_rows, right_rows, preferred_element_type=jnp.float32).astype(jnp.bfloat16)
    return scatter_feat(parts.reshape(n, parts.shape[0] // n, parts.shape[1]), n, collective_id)


def early_weights(weight_up, weight_down):
    return (weight_up, weight_down)


def upper_weight(fetched):
    return lax.all_gather(fetched[0], "tok", axis=0, tiled=True)


def lower_weight(fetched):
    return lax.all_gather(fetched[1], "tok", axis=1, tiled=True)


def attend(projected, segment_ids, head_count):
    token_count = projected.shape[0]
    parts_all = projected.reshape(token_count, 3, head_count, HEAD_DIM)
    queries = (parts_all[:, 0] * HEAD_DIM ** (-0.5)).astype(jnp.bfloat16)
    keys_here = parts_all[:, 1].astype(jnp.bfloat16)
    values_here = parts_all[:, 2].astype(jnp.bfloat16)
    scores = jnp.einsum("qhd,khd->hqk", queries, keys_here, preferred_element_type=jnp.float32)
    same_segment = segment_ids[:, None] == segment_ids[None, :]
    scores = jnp.where(same_segment[None, :, :], scores, -1e30)
    highest = jnp.max(scores, axis=-1, keepdims=True)
    raised = jnp.exp(scores - highest)
    weights_soft = (raised / jnp.sum(raised, axis=-1, keepdims=True)).astype(jnp.bfloat16)
    attended = jnp.einsum(
        "hqk,khd->qhd", weights_soft, values_here, preferred_element_type=jnp.float32
    )
    return attended.astype(jnp.bfloat16).reshape(token_count, head_count * HEAD_DIM)


def route_rows(embedded, segment_ids, owners):
    merged_count = embedded.shape[0]
    peer_count = owners.shape[0]
    least_units = max(LEAST_UNITS, (merged_count + peer_count - 1) // peer_count)
    slot_count = max(MOST_UNITS, 2 * least_units)
    first_ids = segment_ids.reshape(merged_count, 4)[:, 0]
    id_base = lax.axis_index("tok") * peer_count
    local_index = first_ids - id_base
    owner_pick = local_index[:, None] == jnp.arange(peer_count, dtype=jnp.int32)[None, :]
    owner_of = jnp.sum(jnp.where(owner_pick, owners[None, :], 0), axis=1)
    row_index = jnp.arange(merged_count, dtype=jnp.int32)
    earlier = (row_index[None, :] < row_index[:, None]) & (first_ids[None, :] == first_ids[:, None])
    within = jnp.sum(earlier.astype(jnp.int32), axis=1)
    target = owner_of * slot_count + within
    select = (
        jnp.arange(peer_count * slot_count, dtype=jnp.int32)[:, None] == target[None, :]
    ).astype(jnp.bfloat16)
    packed = jnp.dot(select, embedded, preferred_element_type=jnp.float32).astype(jnp.bfloat16)
    packed = packed.reshape(peer_count, slot_count, embedded.shape[1])
    received = route_exchange(packed, 5)
    return received.reshape(peer_count * slot_count, embedded.shape[1])


def body(
    tokens,
    segment_ids,
    owners,
    project_in,
    project_out,
    weight_up,
    weight_down,
    weight_merge,
    gain_attend,
    gain_hidden,
    gain_final,
):
    model_width = tokens.shape[1]
    head_count = project_in.shape[2] // HEAD_DIM
    units = weight_up.shape[1]
    feat_count = lax.axis_size("feat")
    tok_count = lax.axis_size("tok")
    flat_in = project_in.reshape(model_width, 3 * project_in.shape[2])
    local_count = tokens.shape[0]
    normed = layer_norm(tokens, gain_attend)
    stacked = jnp.concatenate([weight_up, weight_down.T], axis=1)
    gathered = gather_feat(normed, feat_count, 0)
    projected = jnp.dot(gathered, flat_in, preferred_element_type=jnp.float32)
    attended = attend(projected, segment_ids, head_count)
    attn_parts = jnp.dot(attended, project_out, preferred_element_type=jnp.float32).astype(jnp.bfloat16)
    second, hidden_rows, weights = mix_ring_feat(
        attn_parts.reshape(feat_count, local_count, model_width), tokens, gain_hidden, stacked,
        feat_count, tok_count, 1,
    )
    both = weights.reshape(tok_count * weight_up.shape[0], 2 * units)
    upper = both[:, :units]
    lower_t = both[:, units:]
    hidden = jax.nn.gelu(
        jnp.dot(hidden_rows, upper, preferred_element_type=jnp.float32), approximate=False
    ).astype(jnp.bfloat16)
    down_parts = lax.dot_general(
        hidden, lower_t, (((1,), (1,)), ((), ())), preferred_element_type=jnp.float32
    ).astype(jnp.bfloat16)
    _, final_rows = mix_feat(
        down_parts.reshape(feat_count, local_count, model_width), second, gain_final, feat_count, 3
    )
    merged = final_rows.reshape(final_rows.shape[0] // 4, 4 * model_width)
    embedded = jnp.dot(merged, weight_merge, preferred_element_type=jnp.float32).astype(jnp.bfloat16)
    return route_rows(embedded, segment_ids, owners)


def solution(mesh):
    return jax.shard_map(
        body,
        mesh=mesh,
        in_specs=(
            P(("tok", "feat"), None),
            P("tok"),
            P("tok"),
            P(None, None, "feat"),
            P("feat", None),
            P("tok", "feat"),
            P("feat", "tok"),
            P(None, "feat"),
            P(),
            P(),
            P(),
        ),
        out_specs=P("tok", "feat"),
        check_vma=False,
    )
```

```python
import functools
import jax
import jax.numpy as jnp
from jax import lax
from jax.experimental import pallas as pl
from jax.experimental.pallas import tpu as pltpu
from jax.sharding import PartitionSpec as P


def _greet(peers, tok_index):
    barrier = pltpu.get_barrier_semaphore()
    for peer in peers:
        pl.semaphore_signal(barrier, inc=1, device_id=(tok_index, peer), device_id_type=MESH)
    pl.semaphore_wait(barrier, len(peers))


def _gather_kernel(n, row_ref, out_ref, send_sem, recv_sem):
    me = lax.axis_index("feat")
    tok_index = lax.axis_index("tok")
    peers = [lax.rem(me + d, n) for d in range(1, n)]
    _greet(peers, tok_index)
    for peer in peers:
        pltpu.make_async_remote_copy(
            src_ref=row_ref, dst_ref=out_ref.at[me], send_sem=send_sem.at[peer],
            recv_sem=recv_sem.at[me], device_id=(tok_index, peer), device_id_type=MESH,
        ).start()
    out_ref[me] = row_ref[...]
    for peer in peers:
        pltpu.make_async_remote_copy(
            src_ref=row_ref, dst_ref=out_ref.at[peer], send_sem=send_sem.at[peer],
            recv_sem=recv_sem.at[peer], device_id=(tok_index, peer), device_id_type=MESH,
        ).wait_recv()
    for peer in peers:
        pltpu.make_async_remote_copy(
            src_ref=row_ref, dst_ref=out_ref.at[me], send_sem=send_sem.at[peer],
            recv_sem=recv_sem.at[me], device_id=(tok_index, peer), device_id_type=MESH,
        ).wait_send()


def gather_feat(row_block, n, collective_id):
    rows, width = row_block.shape
    return pl.pallas_call(
        functools.partial(_gather_kernel, n),
        out_shape=jax.ShapeDtypeStruct((n, rows, width), row_block.dtype),
        in_specs=[pl.BlockSpec(memory_space=pltpu.VMEM)],
        out_specs=pl.BlockSpec(memory_space=pltpu.VMEM),
        scratch_shapes=[pltpu.SemaphoreType.DMA((n,)), pltpu.SemaphoreType.DMA((n,))],
        compiler_params=pltpu.CompilerParams(collective_id=collective_id, has_side_effects=True),
    )(row_block).reshape(n * rows, width)


def _ring_gather(x_ref, out_ref, send_right, send_left, send_partner, recv_sem, feat_index, after_first=None,
                 hook=None, hook_step=1):
    tok_count = out_ref.shape[0]
    chips = tok_count // 2
    right_steps = chips // 2
    left_steps = chips - 1 - right_steps
    me = lax.axis_index("tok")
    chip = me // 2
    core = me % 2
    right = lax.rem(chip + 1, chips) * 2 + core
    left = lax.rem(chip + chips - 1, chips) * 2 + core
    partner = chip * 2 + (1 - core)

    def slot_of(offset):
        return lax.rem(chip + offset + 2 * chips, chips) * 2 + core

    def remote(src, slot, sem, target):
        return pltpu.make_async_remote_copy(
            src_ref=src, dst_ref=out_ref.at[slot], send_sem=sem, recv_sem=recv_sem.at[slot],
            device_id=(target, feat_index), device_id_type=MESH,
        )

    sends = []

    def forward_partner(src, slot):
        copy = remote(src, slot, send_partner.at[len(sends_partner)], partner)
        copy.start()
        sends_partner.append(copy)

    sends_partner = []
    out_ref[me] = x_ref[...]
    arrived = []
    for step in range(1, right_steps + 1):
        if step == 1:
            src_right = x_ref
            src_left = x_ref
        else:
            from_left = slot_of(-(step - 1))
            remote(x_ref, from_left, send_right.at[0], right).wait_recv()
            src_right = out_ref.at[from_left]
            arrived.append(from_left)
        copy = remote(src_right, slot_of(-(step - 1)), send_right.at[step - 1], right)
        copy.start()
        sends.append(copy)
        if step > 1 and step - 1 <= left_steps:
            from_right = slot_of(step - 1)
            remote(x_ref, from_right, send_left.at[0], left).wait_recv()
            src_left = out_ref.at[from_right]
            arrived.append(from_right)
        if step <= left_steps:
            copy = remote(src_left, slot_of(step - 1), send_left.at[step - 1], left)
            copy.start()
            sends.append(copy)
        if step == 1:
            if after_first is not None:
                after_first()
            forward_partner(x_ref, me)
        for slot in arrived:
            forward_partner(out_ref.at[slot], slot)
        arrived = []
        if hook is not None and step == min(hook_step, right_steps):
            hook()
    last_left = slot_of(-right_steps)
    remote(x_ref, last_left, send_right.at[0], right).wait_recv()
    forward_partner(out_ref.at[last_left], last_left)
    if left_steps >= 1 and left_steps + 1 > right_steps:
        last_right = slot_of(left_steps)
        remote(x_ref, last_right, send_left.at[0], left).wait_recv()
        forward_partner(out_ref.at[last_right], last_right)
    for other_chip in range(chips):
        remote(x_ref, other_chip * 2 + (1 - core), send_partner.at[0], partner).wait_recv()
    for copy in sends + sends_partner:
        copy.wait_send()


def _first_kernel(n, row_ref, weight_ref, out_ref, weight_out, send_sem, recv_sem,
                  send_right, send_left, send_partner, weight_recv):
    me = lax.axis_index("feat")
    tok_index = lax.axis_index("tok")
    chips = weight_out.shape[0] // 2
    chip = tok_index // 2
    core = tok_index % 2
    peers = [lax.rem(me + d, n) for d in range(1, n)]
    barrier = pltpu.get_barrier_semaphore()
    for peer in peers:
        pl.semaphore_signal(barrier, inc=1, device_id=(tok_index, peer), device_id_type=MESH)
    ring_peers = [
        lax.rem(chip + 1, chips) * 2 + core,
        lax.rem(chip + chips - 1, chips) * 2 + core,
        chip * 2 + (1 - core),
    ]
    for peer in ring_peers:
        pl.semaphore_signal(barrier, inc=1, device_id=(peer, me), device_id_type=MESH)
    pl.semaphore_wait(barrier, len(peers) + len(ring_peers))

    def start_rows():
        for peer in peers:
            pltpu.make_async_remote_copy(
                src_ref=row_ref, dst_ref=out_ref.at[me], send_sem=send_sem.at[peer],
                recv_sem=recv_sem.at[me], device_id=(tok_index, peer), device_id_type=MESH,
            ).start()

    _ring_gather(weight_ref, weight_out, send_right, send_left, send_partner, weight_recv, me, start_rows)
    out_ref[me] = row_ref[...]
    for peer in peers:
        pltpu.make_async_remote_copy(
            src_ref=row_ref, dst_ref=out_ref.at[peer], send_sem=send_sem.at[peer],
            recv_sem=recv_sem.at[peer], device_id=(tok_index, peer), device_id_type=MESH,
        ).wait_recv()
    for peer in peers:
        pltpu.make_async_remote_copy(
            src_ref=row_ref, dst_ref=out_ref.at[me], send_sem=send_sem.at[peer],
            recv_sem=recv_sem.at[me], device_id=(tok_index, peer), device_id_type=MESH,
        ).wait_send()


def first_exchange(row_block, weight_block, n, tok_count, collective_id):
    rows, width = row_block.shape
    weight_rows, weight_width = weight_block.shape
    chips = tok_count // 2
    gathered, weights = pl.pallas_call(
        functools.partial(_first_kernel, n),
        out_shape=(
            jax.ShapeDtypeStruct((n, rows, width), row_block.dtype),
            jax.ShapeDtypeStruct((tok_count, weight_rows, weight_width), weight_block.dtype),
        ),
        in_specs=[pl.BlockSpec(memory_space=pltpu.VMEM)] * 2,
        out_specs=(pl.BlockSpec(memory_space=pltpu.VMEM),) * 2,
        scratch_shapes=[
            pltpu.SemaphoreType.DMA((n,)),
            pltpu.SemaphoreType.DMA((n,)),
            pltpu.SemaphoreType.DMA((chips,)),
            pltpu.SemaphoreType.DMA((chips,)),
            pltpu.SemaphoreType.DMA((chips,)),
            pltpu.SemaphoreType.DMA((tok_count,)),
        ],
        compiler_params=pltpu.CompilerParams(collective_id=collective_id, has_side_effects=True),
    )(row_block, weight_block)
    return gathered.reshape(n * rows, width), weights


def _route_kernel(n, packed_ref, out_ref, send_sem, recv_sem):
    me = lax.axis_index("tok")
    feat_index = lax.axis_index("feat")
    peers = [lax.rem(me + d, n) for d in range(1, n)]
    barrier = pltpu.get_barrier_semaphore()
    for peer in peers:
        pl.semaphore_signal(barrier, inc=1, device_id=(peer, feat_index), device_id_type=MESH)
    pl.semaphore_wait(barrier, len(peers))
    for peer in peers:
        pltpu.make_async_remote_copy(
            src_ref=packed_ref.at[peer], dst_ref=out_ref.at[me], send_sem=send_sem.at[peer],
            recv_sem=recv_sem.at[me], device_id=(peer, feat_index), device_id_type=MESH,
        ).start()
    out_ref[me] = packed_ref[me]
    for peer in peers:
        pltpu.make_async_remote_copy(
            src_ref=packed_ref.at[peer], dst_ref=out_ref.at[peer], send_sem=send_sem.at[peer],
            recv_sem=recv_sem.at[peer], device_id=(peer, feat_index), device_id_type=MESH,
        ).wait_recv()
    for peer in peers:
        pltpu.make_async_remote_copy(
            src_ref=packed_ref.at[peer], dst_ref=out_ref.at[me], send_sem=send_sem.at[peer],
            recv_sem=recv_sem.at[me], device_id=(peer, feat_index), device_id_type=MESH,
        ).wait_send()


def route_exchange(packed, collective_id):
    n = packed.shape[0]
    return pl.pallas_call(
        functools.partial(_route_kernel, n),
        out_shape=jax.ShapeDtypeStruct(packed.shape, packed.dtype),
        in_specs=[pl.BlockSpec(memory_space=pltpu.VMEM)],
        out_specs=pl.BlockSpec(memory_space=pltpu.VMEM),
        scratch_shapes=[pltpu.SemaphoreType.DMA((n,)), pltpu.SemaphoreType.DMA((n,))],
        compiler_params=pltpu.CompilerParams(collective_id=collective_id, has_side_effects=True),
    )(packed)


def _mix_kernel(n, gain_row, part_ref, resid_ref, gain_ref, resid_out, out_ref, held, mine,
                scatter_send, scatter_recv, gather_send, gather_recv):
    me = lax.axis_index("feat")
    tok_index = lax.axis_index("tok")
    peers = [lax.rem(me + d, n) for d in range(1, n)]
    _greet(peers, tok_index)

    def scatter_copy(peer, slot):
        return pltpu.make_async_remote_copy(
            src_ref=part_ref.at[peer], dst_ref=held.at[slot], send_sem=scatter_send.at[peer],
            recv_sem=scatter_recv.at[slot], device_id=(tok_index, peer), device_id_type=MESH,
        )

    def gather_copy(peer, slot):
        return pltpu.make_async_remote_copy(
            src_ref=mine, dst_ref=out_ref.at[slot], send_sem=gather_send.at[peer],
            recv_sem=gather_recv.at[slot], device_id=(tok_index, peer), device_id_type=MESH,
        )

    for peer in peers:
        scatter_copy(peer, me).start()
    total = part_ref[me].astype(jnp.float32)
    for peer in peers:
        scatter_copy(peer, peer).wait_recv()
        total = total + held[peer].astype(jnp.float32)
    summed = (resid_ref[...].astype(jnp.float32) + total).astype(jnp.bfloat16)
    resid_out[...] = summed
    as_float = summed.astype(jnp.float32)
    center = jnp.mean(as_float, axis=-1, keepdims=True)
    spread = jnp.mean(jnp.square(as_float - center), axis=-1, keepdims=True)
    normed = ((as_float - center) * lax.rsqrt(spread + epsilon) * gain_ref[gain_row:gain_row + 1, :]).astype(jnp.bfloat16)
    mine[...] = normed
    out_ref[me] = normed
    for peer in peers:
        gather_copy(peer, me).start()
    for peer in peers:
        gather_copy(peer, peer).wait_recv()
    for peer in peers:
        scatter_copy(peer, me).wait_send()
        gather_copy(peer, me).wait_send()


def mix_feat(parts, resid, gains, gain_row, n, collective_id):
    _, rows, width = parts.shape
    new_resid, gathered = pl.pallas_call(
        functools.partial(_mix_kernel, n, gain_row),
        out_shape=(
            jax.ShapeDtypeStruct((rows, width), jnp.bfloat16),
            jax.ShapeDtypeStruct((n, rows, width), jnp.bfloat16),
        ),
        in_specs=[pl.BlockSpec(memory_space=pltpu.VMEM)] * 3,
        out_specs=(pl.BlockSpec(memory_space=pltpu.VMEM),) * 2,
        scratch_shapes=[
            pltpu.VMEM((n, rows, width), parts.dtype),
            pltpu.VMEM((rows, width), jnp.bfloat16),
            pltpu.SemaphoreType.DMA((n,)),
            pltpu.SemaphoreType.DMA((n,)),
            pltpu.SemaphoreType.DMA((n,)),
            pltpu.SemaphoreType.DMA((n,)),
        ],
        compiler_params=pltpu.CompilerParams(collective_id=collective_id, has_side_effects=True),
    )(parts, resid, gains)
    return new_resid, gathered.reshape(n * rows, width)


def _mix_ring_kernel(n, gain_row, part_ref, resid_ref, gain_ref, weight_ref, resid_out, out_ref, weight_out,
                     held, mine, scatter_send, scatter_recv, gather_send, gather_recv,
                     send_right, send_left, send_partner, weight_recv):
    me = lax.axis_index("feat")
    tok_index = lax.axis_index("tok")
    chips = weight_out.shape[0] // 2
    chip = tok_index // 2
    core = tok_index % 2
    peers = [lax.rem(me + d, n) for d in range(1, n)]
    barrier = pltpu.get_barrier_semaphore()
    for peer in peers:
        pl.semaphore_signal(barrier, inc=1, device_id=(tok_index, peer), device_id_type=MESH)
    ring_peers = [
        lax.rem(chip + 1, chips) * 2 + core,
        lax.rem(chip + chips - 1, chips) * 2 + core,
        chip * 2 + (1 - core),
    ]
    for peer in ring_peers:
        pl.semaphore_signal(barrier, inc=1, device_id=(peer, me), device_id_type=MESH)
    pl.semaphore_wait(barrier, len(peers) + len(ring_peers))

    def scatter_copy(peer, slot):
        return pltpu.make_async_remote_copy(
            src_ref=part_ref.at[peer], dst_ref=held.at[slot], send_sem=scatter_send.at[peer],
            recv_sem=scatter_recv.at[slot], device_id=(tok_index, peer), device_id_type=MESH,
        )

    def gather_copy(peer, slot):
        return pltpu.make_async_remote_copy(
            src_ref=mine, dst_ref=out_ref.at[slot], send_sem=gather_send.at[peer],
            recv_sem=gather_recv.at[slot], device_id=(tok_index, peer), device_id_type=MESH,
        )

    for peer in peers:
        scatter_copy(peer, me).start()

    def norm_and_send():
        total = part_ref[me].astype(jnp.float32)
        for peer in peers:
            scatter_copy(peer, peer).wait_recv()
            total = total + held[peer].astype(jnp.float32)
        summed = (resid_ref[...].astype(jnp.float32) + total).astype(jnp.bfloat16)
        resid_out[...] = summed
        as_float = summed.astype(jnp.float32)
        center = jnp.mean(as_float, axis=-1, keepdims=True)
        spread = jnp.mean(jnp.square(as_float - center), axis=-1, keepdims=True)
        normed = ((as_float - center) * lax.rsqrt(spread + epsilon) * gain_ref[gain_row:gain_row + 1, :]).astype(jnp.bfloat16)
        mine[...] = normed
        out_ref[me] = normed
        for peer in peers:
            gather_copy(peer, me).start()

    _ring_gather(weight_ref, weight_out, send_right, send_left, send_partner, weight_recv, me,
                 hook=norm_and_send, hook_step=3)
    for peer in peers:
        gather_copy(peer, peer).wait_recv()
    for peer in peers:
        scatter_copy(peer, me).wait_send()
        gather_copy(peer, me).wait_send()


def mix_ring_feat(parts, resid, gains, gain_row, weight_block, n, tok_count, collective_id):
    _, rows, width = parts.shape
    weight_rows, weight_width = weight_block.shape
    chips = tok_count // 2
    new_resid, gathered, weights = pl.pallas_call(
        functools.partial(_mix_ring_kernel, n, gain_row),
        out_shape=(
            jax.ShapeDtypeStruct((rows, width), jnp.bfloat16),
            jax.ShapeDtypeStruct((n, rows, width), jnp.bfloat16),
            jax.ShapeDtypeStruct((tok_count, weight_rows, weight_width), weight_block.dtype),
        ),
        in_specs=[pl.BlockSpec(memory_space=pltpu.VMEM)] * 4,
        out_specs=(pl.BlockSpec(memory_space=pltpu.VMEM),) * 3,
        scratch_shapes=[
            pltpu.VMEM((n, rows, width), parts.dtype),
            pltpu.VMEM((rows, width), jnp.bfloat16),
            pltpu.SemaphoreType.DMA((n,)),
            pltpu.SemaphoreType.DMA((n,)),
            pltpu.SemaphoreType.DMA((n,)),
            pltpu.SemaphoreType.DMA((n,)),
            pltpu.SemaphoreType.DMA((chips,)),
            pltpu.SemaphoreType.DMA((chips,)),
            pltpu.SemaphoreType.DMA((chips,)),
            pltpu.SemaphoreType.DMA((tok_count,)),
        ],
        compiler_params=pltpu.CompilerParams(collective_id=collective_id, has_side_effects=True),
    )(parts, resid, gains, weight_block)
    return new_resid, gathered.reshape(n * rows, width), weights


def _norm_gather_kernel(n, gain_row, tok_ref, gain_ref, out_ref, mine, send_sem, recv_sem):
    me = lax.axis_index("feat")
    tok_index = lax.axis_index("tok")
    peers = [lax.rem(me + d, n) for d in range(1, n)]
    _greet(peers, tok_index)
    as_float = tok_ref[...].astype(jnp.float32)
    center = jnp.mean(as_float, axis=-1, keepdims=True)
    spread = jnp.mean(jnp.square(as_float - center), axis=-1, keepdims=True)
    normed = ((as_float - center) * lax.rsqrt(spread + epsilon) * gain_ref[gain_row:gain_row + 1, :]).astype(jnp.bfloat16)
    mine[...] = normed
    out_ref[me] = normed

    def copy(peer, slot):
        return pltpu.make_async_remote_copy(
            src_ref=mine, dst_ref=out_ref.at[slot], send_sem=send_sem.at[peer],
            recv_sem=recv_sem.at[slot], device_id=(tok_index, peer), device_id_type=MESH,
        )

    for peer in peers:
        copy(peer, me).start()
    for peer in peers:
        copy(peer, peer).wait_recv()
    for peer in peers:
        copy(peer, me).wait_send()


def norm_gather_feat(rows, gains, gain_row, n, collective_id):
    count, width = rows.shape
    return pl.pallas_call(
        functools.partial(_norm_gather_kernel, n, gain_row),
        out_shape=jax.ShapeDtypeStruct((n, count, width), jnp.bfloat16),
        in_specs=[pl.BlockSpec(memory_space=pltpu.VMEM)] * 2,
        out_specs=pl.BlockSpec(memory_space=pltpu.VMEM),
        scratch_shapes=[
            pltpu.VMEM((count, width), jnp.bfloat16),
            pltpu.SemaphoreType.DMA((n,)),
            pltpu.SemaphoreType.DMA((n,)),
        ],
        compiler_params=pltpu.CompilerParams(collective_id=collective_id, has_side_effects=True),
    )(rows, gains).reshape(n * count, width)


def _scatter_kernel(n, part_ref, out_ref, held, send_sem, recv_sem):
    me = lax.axis_index("feat")
    tok_index = lax.axis_index("tok")
    peers = [lax.rem(me + d, n) for d in range(1, n)]
    _greet(peers, tok_index)
    for peer in peers:
        pltpu.make_async_remote_copy(
            src_ref=part_ref.at[peer], dst_ref=held.at[me], send_sem=send_sem.at[peer],
            recv_sem=recv_sem.at[me], device_id=(tok_index, peer), device_id_type=MESH,
        ).start()
    total = part_ref[me].astype(jnp.float32)
    for peer in peers:
        pltpu.make_async_remote_copy(
            src_ref=part_ref.at[peer], dst_ref=held.at[peer], send_sem=send_sem.at[peer],
            recv_sem=recv_sem.at[peer], device_id=(tok_index, peer), device_id_type=MESH,
        ).wait_recv()
        total = total + held[peer].astype(jnp.float32)
    out_ref[...] = total
    for peer in peers:
        pltpu.make_async_remote_copy(
            src_ref=part_ref.at[peer], dst_ref=held.at[me], send_sem=send_sem.at[peer],
            recv_sem=recv_sem.at[me], device_id=(tok_index, peer), device_id_type=MESH,
        ).wait_send()


def scatter_feat(parts, n, collective_id):
    _, rows, width = parts.shape
    return pl.pallas_call(
        functools.partial(_scatter_kernel, n),
        out_shape=jax.ShapeDtypeStruct((rows, width), jnp.float32),
        in_specs=[pl.BlockSpec(memory_space=pltpu.VMEM)],
        out_specs=pl.BlockSpec(memory_space=pltpu.VMEM),
        scratch_shapes=[
            pltpu.VMEM((n, rows, width), parts.dtype),
            pltpu.SemaphoreType.DMA((n,)),
            pltpu.SemaphoreType.DMA((n,)),
        ],
        compiler_params=pltpu.CompilerParams(collective_id=collective_id, has_side_effects=True),
    )(parts)

MESH = pl.DeviceIdType.MESH
LEAST_UNITS = 4
MOST_UNITS = 16
HEAD_DIM = 88


epsilon = 1e-06


def layer_norm(row_block, gain_row):
    as_float = row_block.astype(jnp.float32)
    center = jnp.mean(as_float, axis=-1, keepdims=True)
    spread = jnp.mean(jnp.square(as_float - center), axis=-1, keepdims=True)
    scaled = (as_float - center) * lax.rsqrt(spread + epsilon) * gain_row.astype(jnp.float32)
    return scaled.astype(jnp.bfloat16)


def project_rows(row_block, weight_block, collective_id):
    n = lax.axis_size("feat")
    return jnp.dot(
        gather_feat(row_block, n, collective_id),
        weight_block,
        preferred_element_type=jnp.float32,
    )


def scatter_rows(left_rows, right_rows, collective_id):
    n = lax.axis_size("feat")
    parts = jnp.dot(left_rows, right_rows, preferred_element_type=jnp.float32).astype(jnp.bfloat16)
    return scatter_feat(parts.reshape(n, parts.shape[0] // n, parts.shape[1]), n, collective_id)


def early_weights(weight_up, weight_down):
    return (weight_up, weight_down)


def upper_weight(fetched):
    return lax.all_gather(fetched[0], "tok", axis=0, tiled=True)


def lower_weight(fetched):
    return lax.all_gather(fetched[1], "tok", axis=1, tiled=True)


def attend(projected, segment_ids, head_count):
    token_count = projected.shape[0]
    parts_all = projected.reshape(token_count, 3, head_count, HEAD_DIM)
    queries = (parts_all[:, 0] * HEAD_DIM ** (-0.5)).astype(jnp.bfloat16)
    keys_here = parts_all[:, 1].astype(jnp.bfloat16)
    values_here = parts_all[:, 2].astype(jnp.bfloat16)
    scores = jnp.einsum("qhd,khd->hqk", queries, keys_here, preferred_element_type=jnp.float32)
    same_segment = segment_ids[:, None] == segment_ids[None, :]
    scores = jnp.where(same_segment[None, :, :], scores, -1e30)
    highest = jnp.max(scores, axis=-1, keepdims=True)
    raised = jnp.exp(scores - highest)
    weights_soft = (raised / jnp.sum(raised, axis=-1, keepdims=True)).astype(jnp.bfloat16)
    attended = jnp.einsum(
        "hqk,khd->qhd", weights_soft, values_here, preferred_element_type=jnp.float32
    )
    return attended.astype(jnp.bfloat16).reshape(token_count, head_count * HEAD_DIM)


def route_rows(embedded, segment_ids, owners):
    merged_count = embedded.shape[0]
    peer_count = owners.shape[0]
    least_units = max(LEAST_UNITS, (merged_count + peer_count - 1) // peer_count)
    slot_count = max(MOST_UNITS, 2 * least_units)
    first_ids = segment_ids.reshape(merged_count, 4)[:, 0]
    id_base = lax.axis_index("tok") * peer_count
    local_index = first_ids - id_base
    owner_pick = local_index[:, None] == jnp.arange(peer_count, dtype=jnp.int32)[None, :]
    owner_of = jnp.sum(jnp.where(owner_pick, owners[None, :], 0), axis=1)
    row_index = jnp.arange(merged_count, dtype=jnp.int32)
    earlier = (row_index[None, :] < row_index[:, None]) & (first_ids[None, :] == first_ids[:, None])
    within = jnp.sum(earlier.astype(jnp.int32), axis=1)
    target = owner_of * slot_count + within
    select = (
        jnp.arange(peer_count * slot_count, dtype=jnp.int32)[:, None] == target[None, :]
    ).astype(jnp.bfloat16)
    packed = jnp.dot(select, embedded, preferred_element_type=jnp.float32).astype(jnp.bfloat16)
    packed = packed.reshape(peer_count, slot_count, embedded.shape[1])
    received = route_exchange(packed, 5)
    return received.reshape(peer_count * slot_count, embedded.shape[1])


def body(
    tokens,
    segment_ids,
    owners,
    project_in,
    project_out,
    weight_up,
    weight_down,
    weight_merge,
    gain_attend,
    gain_hidden,
    gain_final,
):
    model_width = tokens.shape[1]
    head_count = project_in.shape[2] // HEAD_DIM
    units = weight_up.shape[1]
    feat_count = lax.axis_size("feat")
    tok_count = lax.axis_size("tok")
    flat_in = project_in.reshape(model_width, 3 * project_in.shape[2])
    local_count = tokens.shape[0]
    gains = jnp.stack([gain_attend, gain_hidden, gain_final]).astype(jnp.float32)
    stacked = jnp.concatenate([weight_up, weight_down.T], axis=1)
    gathered = norm_gather_feat(tokens, gains, 0, feat_count, 0)
    projected = jnp.dot(gathered, flat_in, preferred_element_type=jnp.float32)
    attended = attend(projected, segment_ids, head_count)
    attn_parts = jnp.dot(attended, project_out, preferred_element_type=jnp.float32).astype(jnp.bfloat16)
    second, hidden_rows, weights = mix_ring_feat(
        attn_parts.reshape(feat_count, local_count, model_width), tokens, gains, 1, stacked,
        feat_count, tok_count, 1,
    )
    both = weights.reshape(tok_count * weight_up.shape[0], 2 * units)
    upper = both[:, :units]
    lower_t = both[:, units:]
    hidden = jax.nn.gelu(
        jnp.dot(hidden_rows, upper, preferred_element_type=jnp.float32), approximate=False
    ).astype(jnp.bfloat16)
    down_parts = lax.dot_general(
        hidden, lower_t, (((1,), (1,)), ((), ())), preferred_element_type=jnp.float32
    ).astype(jnp.bfloat16)
    _, final_rows = mix_feat(
        down_parts.reshape(feat_count, local_count, model_width), second, gains, 2, feat_count, 3
    )
    merged = final_rows.reshape(final_rows.shape[0] // 4, 4 * model_width)
    embedded = jnp.dot(merged, weight_merge, preferred_element_type=jnp.float32).astype(jnp.bfloat16)
    return route_rows(embedded, segment_ids, owners)


def solution(mesh):
    return jax.shard_map(
        body,
        mesh=mesh,
        in_specs=(
            P(("tok", "feat"), None),
            P("tok"),
            P("tok"),
            P(None, None, "feat"),
            P("feat", None),
            P("tok", "feat"),
            P("feat", "tok"),
            P(None, "feat"),
            P(),
            P(),
            P(),
        ),
        out_specs=P("tok", "feat"),
        check_vma=False,
    )
```

```python
import functools
import jax
import jax.numpy as jnp
from jax import lax
from jax.experimental import pallas as pl
from jax.experimental.pallas import tpu as pltpu
from jax.sharding import PartitionSpec as P


def _greet(peers, tok_index):
    barrier = pltpu.get_barrier_semaphore()
    for peer in peers:
        pl.semaphore_signal(barrier, inc=1, device_id=(tok_index, peer), device_id_type=MESH)
    pl.semaphore_wait(barrier, len(peers))


def _gather_kernel(n, row_ref, out_ref, send_sem, recv_sem):
    me = lax.axis_index("feat")
    tok_index = lax.axis_index("tok")
    peers = [lax.rem(me + d, n) for d in range(1, n)]
    _greet(peers, tok_index)
    for peer in peers:
        pltpu.make_async_remote_copy(
            src_ref=row_ref, dst_ref=out_ref.at[me], send_sem=send_sem.at[peer],
            recv_sem=recv_sem.at[me], device_id=(tok_index, peer), device_id_type=MESH,
        ).start()
    out_ref[me] = row_ref[...]
    for peer in peers:
        pltpu.make_async_remote_copy(
            src_ref=row_ref, dst_ref=out_ref.at[peer], send_sem=send_sem.at[peer],
            recv_sem=recv_sem.at[peer], device_id=(tok_index, peer), device_id_type=MESH,
        ).wait_recv()
    for peer in peers:
        pltpu.make_async_remote_copy(
            src_ref=row_ref, dst_ref=out_ref.at[me], send_sem=send_sem.at[peer],
            recv_sem=recv_sem.at[me], device_id=(tok_index, peer), device_id_type=MESH,
        ).wait_send()


def gather_feat(row_block, n, collective_id):
    rows, width = row_block.shape
    return pl.pallas_call(
        functools.partial(_gather_kernel, n),
        out_shape=jax.ShapeDtypeStruct((n, rows, width), row_block.dtype),
        in_specs=[pl.BlockSpec(memory_space=pltpu.VMEM)],
        out_specs=pl.BlockSpec(memory_space=pltpu.VMEM),
        scratch_shapes=[pltpu.SemaphoreType.DMA((n,)), pltpu.SemaphoreType.DMA((n,))],
        compiler_params=pltpu.CompilerParams(collective_id=collective_id, has_side_effects=True),
    )(row_block).reshape(n * rows, width)


def _ring_gather(x_ref, out_ref, send_right, send_left, send_partner, recv_sem, feat_index, after_first=None,
                 hook=None, hook_step=1):
    tok_count = out_ref.shape[0]
    chips = tok_count // 2
    right_steps = chips // 2
    left_steps = chips - 1 - right_steps
    me = lax.axis_index("tok")
    chip = me // 2
    core = me % 2
    right = lax.rem(chip + 1, chips) * 2 + core
    left = lax.rem(chip + chips - 1, chips) * 2 + core
    partner = chip * 2 + (1 - core)

    def slot_of(offset):
        return lax.rem(chip + offset + 2 * chips, chips) * 2 + core

    def remote(src, slot, sem, target):
        return pltpu.make_async_remote_copy(
            src_ref=src, dst_ref=out_ref.at[slot], send_sem=sem, recv_sem=recv_sem.at[slot],
            device_id=(target, feat_index), device_id_type=MESH,
        )

    sends = []

    def forward_partner(src, slot):
        copy = remote(src, slot, send_partner.at[len(sends_partner)], partner)
        copy.start()
        sends_partner.append(copy)

    sends_partner = []
    out_ref[me] = x_ref[...]
    arrived = []
    for step in range(1, right_steps + 1):
        if step == 1:
            src_right = x_ref
            src_left = x_ref
        else:
            from_left = slot_of(-(step - 1))
            remote(x_ref, from_left, send_right.at[0], right).wait_recv()
            src_right = out_ref.at[from_left]
            arrived.append(from_left)
        copy = remote(src_right, slot_of(-(step - 1)), send_right.at[step - 1], right)
        copy.start()
        sends.append(copy)
        if step > 1 and step - 1 <= left_steps:
            from_right = slot_of(step - 1)
            remote(x_ref, from_right, send_left.at[0], left).wait_recv()
            src_left = out_ref.at[from_right]
            arrived.append(from_right)
        if step <= left_steps:
            copy = remote(src_left, slot_of(step - 1), send_left.at[step - 1], left)
            copy.start()
            sends.append(copy)
        if step == 1:
            if after_first is not None:
                after_first()
            forward_partner(x_ref, me)
        for slot in arrived:
            forward_partner(out_ref.at[slot], slot)
        arrived = []
        if hook is not None and step == min(hook_step, right_steps):
            hook()
    last_left = slot_of(-right_steps)
    remote(x_ref, last_left, send_right.at[0], right).wait_recv()
    forward_partner(out_ref.at[last_left], last_left)
    if left_steps >= 1 and left_steps + 1 > right_steps:
        last_right = slot_of(left_steps)
        remote(x_ref, last_right, send_left.at[0], left).wait_recv()
        forward_partner(out_ref.at[last_right], last_right)
    for other_chip in range(chips):
        remote(x_ref, other_chip * 2 + (1 - core), send_partner.at[0], partner).wait_recv()
    for copy in sends + sends_partner:
        copy.wait_send()


def _first_kernel(n, row_ref, weight_ref, out_ref, weight_out, send_sem, recv_sem,
                  send_right, send_left, send_partner, weight_recv):
    me = lax.axis_index("feat")
    tok_index = lax.axis_index("tok")
    chips = weight_out.shape[0] // 2
    chip = tok_index // 2
    core = tok_index % 2
    peers = [lax.rem(me + d, n) for d in range(1, n)]
    barrier = pltpu.get_barrier_semaphore()
    for peer in peers:
        pl.semaphore_signal(barrier, inc=1, device_id=(tok_index, peer), device_id_type=MESH)
    ring_peers = [
        lax.rem(chip + 1, chips) * 2 + core,
        lax.rem(chip + chips - 1, chips) * 2 + core,
        chip * 2 + (1 - core),
    ]
    for peer in ring_peers:
        pl.semaphore_signal(barrier, inc=1, device_id=(peer, me), device_id_type=MESH)
    pl.semaphore_wait(barrier, len(peers) + len(ring_peers))

    def start_rows():
        for peer in peers:
            pltpu.make_async_remote_copy(
                src_ref=row_ref, dst_ref=out_ref.at[me], send_sem=send_sem.at[peer],
                recv_sem=recv_sem.at[me], device_id=(tok_index, peer), device_id_type=MESH,
            ).start()

    _ring_gather(weight_ref, weight_out, send_right, send_left, send_partner, weight_recv, me, start_rows)
    out_ref[me] = row_ref[...]
    for peer in peers:
        pltpu.make_async_remote_copy(
            src_ref=row_ref, dst_ref=out_ref.at[peer], send_sem=send_sem.at[peer],
            recv_sem=recv_sem.at[peer], device_id=(tok_index, peer), device_id_type=MESH,
        ).wait_recv()
    for peer in peers:
        pltpu.make_async_remote_copy(
            src_ref=row_ref, dst_ref=out_ref.at[me], send_sem=send_sem.at[peer],
            recv_sem=recv_sem.at[me], device_id=(tok_index, peer), device_id_type=MESH,
        ).wait_send()


def first_exchange(row_block, weight_block, n, tok_count, collective_id):
    rows, width = row_block.shape
    weight_rows, weight_width = weight_block.shape
    chips = tok_count // 2
    gathered, weights = pl.pallas_call(
        functools.partial(_first_kernel, n),
        out_shape=(
            jax.ShapeDtypeStruct((n, rows, width), row_block.dtype),
            jax.ShapeDtypeStruct((tok_count, weight_rows, weight_width), weight_block.dtype),
        ),
        in_specs=[pl.BlockSpec(memory_space=pltpu.VMEM)] * 2,
        out_specs=(pl.BlockSpec(memory_space=pltpu.VMEM),) * 2,
        scratch_shapes=[
            pltpu.SemaphoreType.DMA((n,)),
            pltpu.SemaphoreType.DMA((n,)),
            pltpu.SemaphoreType.DMA((chips,)),
            pltpu.SemaphoreType.DMA((chips,)),
            pltpu.SemaphoreType.DMA((chips,)),
            pltpu.SemaphoreType.DMA((tok_count,)),
        ],
        compiler_params=pltpu.CompilerParams(collective_id=collective_id, has_side_effects=True),
    )(row_block, weight_block)
    return gathered.reshape(n * rows, width), weights


def _route_kernel(n, packed_ref, out_ref, send_sem, recv_sem):
    me = lax.axis_index("tok")
    feat_index = lax.axis_index("feat")
    peers = [lax.rem(me + d, n) for d in range(1, n)]
    barrier = pltpu.get_barrier_semaphore()
    for peer in peers:
        pl.semaphore_signal(barrier, inc=1, device_id=(peer, feat_index), device_id_type=MESH)
    pl.semaphore_wait(barrier, len(peers))
    for peer in peers:
        pltpu.make_async_remote_copy(
            src_ref=packed_ref.at[peer], dst_ref=out_ref.at[me], send_sem=send_sem.at[peer],
            recv_sem=recv_sem.at[me], device_id=(peer, feat_index), device_id_type=MESH,
        ).start()
    out_ref[me] = packed_ref[me]
    for peer in peers:
        pltpu.make_async_remote_copy(
            src_ref=packed_ref.at[peer], dst_ref=out_ref.at[peer], send_sem=send_sem.at[peer],
            recv_sem=recv_sem.at[peer], device_id=(peer, feat_index), device_id_type=MESH,
        ).wait_recv()
    for peer in peers:
        pltpu.make_async_remote_copy(
            src_ref=packed_ref.at[peer], dst_ref=out_ref.at[me], send_sem=send_sem.at[peer],
            recv_sem=recv_sem.at[me], device_id=(peer, feat_index), device_id_type=MESH,
        ).wait_send()


def route_exchange(packed, collective_id):
    n = packed.shape[0]
    return pl.pallas_call(
        functools.partial(_route_kernel, n),
        out_shape=jax.ShapeDtypeStruct(packed.shape, packed.dtype),
        in_specs=[pl.BlockSpec(memory_space=pltpu.VMEM)],
        out_specs=pl.BlockSpec(memory_space=pltpu.VMEM),
        scratch_shapes=[pltpu.SemaphoreType.DMA((n,)), pltpu.SemaphoreType.DMA((n,))],
        compiler_params=pltpu.CompilerParams(collective_id=collective_id, has_side_effects=True),
    )(packed)


def _mix_kernel(n, gain_row, part_ref, resid_ref, gain_ref, resid_out, out_ref, held, mine,
                scatter_send, scatter_recv, gather_send, gather_recv):
    me = lax.axis_index("feat")
    tok_index = lax.axis_index("tok")
    peers = [lax.rem(me + d, n) for d in range(1, n)]
    _greet(peers, tok_index)

    def scatter_copy(peer, slot):
        return pltpu.make_async_remote_copy(
            src_ref=part_ref.at[peer], dst_ref=held.at[slot], send_sem=scatter_send.at[peer],
            recv_sem=scatter_recv.at[slot], device_id=(tok_index, peer), device_id_type=MESH,
        )

    def gather_copy(peer, slot):
        return pltpu.make_async_remote_copy(
            src_ref=mine, dst_ref=out_ref.at[slot], send_sem=gather_send.at[peer],
            recv_sem=gather_recv.at[slot], device_id=(tok_index, peer), device_id_type=MESH,
        )

    for peer in peers:
        scatter_copy(peer, me).start()
    total = part_ref[me].astype(jnp.float32)
    for peer in peers:
        scatter_copy(peer, peer).wait_recv()
        total = total + held[peer].astype(jnp.float32)
    summed = (resid_ref[...].astype(jnp.float32) + total).astype(jnp.bfloat16)
    resid_out[...] = summed
    as_float = summed.astype(jnp.float32)
    center = jnp.mean(as_float, axis=-1, keepdims=True)
    spread = jnp.mean(jnp.square(as_float - center), axis=-1, keepdims=True)
    normed = ((as_float - center) * lax.rsqrt(spread + epsilon) * gain_ref[gain_row:gain_row + 1, :]).astype(jnp.bfloat16)
    mine[...] = normed
    out_ref[me] = normed
    for peer in peers:
        gather_copy(peer, me).start()
    for peer in peers:
        gather_copy(peer, peer).wait_recv()
    for peer in peers:
        scatter_copy(peer, me).wait_send()
        gather_copy(peer, me).wait_send()


def mix_feat(parts, resid, gains, gain_row, n, collective_id):
    _, rows, width = parts.shape
    new_resid, gathered = pl.pallas_call(
        functools.partial(_mix_kernel, n, gain_row),
        out_shape=(
            jax.ShapeDtypeStruct((rows, width), jnp.bfloat16),
            jax.ShapeDtypeStruct((n, rows, width), jnp.bfloat16),
        ),
        in_specs=[pl.BlockSpec(memory_space=pltpu.VMEM)] * 3,
        out_specs=(pl.BlockSpec(memory_space=pltpu.VMEM),) * 2,
        scratch_shapes=[
            pltpu.VMEM((n, rows, width), parts.dtype),
            pltpu.VMEM((rows, width), jnp.bfloat16),
            pltpu.SemaphoreType.DMA((n,)),
            pltpu.SemaphoreType.DMA((n,)),
            pltpu.SemaphoreType.DMA((n,)),
            pltpu.SemaphoreType.DMA((n,)),
        ],
        compiler_params=pltpu.CompilerParams(collective_id=collective_id, has_side_effects=True),
    )(parts, resid, gains)
    return new_resid, gathered.reshape(n * rows, width)


def _mix_ring_kernel(n, gain_row, part_ref, resid_ref, gain_ref, weight_ref, resid_out, out_ref, weight_flat,
                     weight_out, held, mine, scatter_send, scatter_recv, gather_send, gather_recv,
                     send_right, send_left, send_partner, weight_recv):
    me = lax.axis_index("feat")
    tok_index = lax.axis_index("tok")
    chips = weight_out.shape[0] // 2
    chip = tok_index // 2
    core = tok_index % 2
    peers = [lax.rem(me + d, n) for d in range(1, n)]
    barrier = pltpu.get_barrier_semaphore()
    for peer in peers:
        pl.semaphore_signal(barrier, inc=1, device_id=(tok_index, peer), device_id_type=MESH)
    ring_peers = [
        lax.rem(chip + 1, chips) * 2 + core,
        lax.rem(chip + chips - 1, chips) * 2 + core,
        chip * 2 + (1 - core),
    ]
    for peer in ring_peers:
        pl.semaphore_signal(barrier, inc=1, device_id=(peer, me), device_id_type=MESH)
    pl.semaphore_wait(barrier, len(peers) + len(ring_peers))

    def scatter_copy(peer, slot):
        return pltpu.make_async_remote_copy(
            src_ref=part_ref.at[peer], dst_ref=held.at[slot], send_sem=scatter_send.at[peer],
            recv_sem=scatter_recv.at[slot], device_id=(tok_index, peer), device_id_type=MESH,
        )

    def gather_copy(peer, slot):
        return pltpu.make_async_remote_copy(
            src_ref=mine, dst_ref=out_ref.at[slot], send_sem=gather_send.at[peer],
            recv_sem=gather_recv.at[slot], device_id=(tok_index, peer), device_id_type=MESH,
        )

    for peer in peers:
        scatter_copy(peer, me).start()

    def norm_and_send():
        total = part_ref[me].astype(jnp.float32)
        for peer in peers:
            scatter_copy(peer, peer).wait_recv()
            total = total + held[peer].astype(jnp.float32)
        summed = (resid_ref[...].astype(jnp.float32) + total).astype(jnp.bfloat16)
        resid_out[...] = summed
        as_float = summed.astype(jnp.float32)
        center = jnp.mean(as_float, axis=-1, keepdims=True)
        spread = jnp.mean(jnp.square(as_float - center), axis=-1, keepdims=True)
        normed = ((as_float - center) * lax.rsqrt(spread + epsilon) * gain_ref[gain_row:gain_row + 1, :]).astype(jnp.bfloat16)
        mine[...] = normed
        out_ref[me] = normed
        for peer in peers:
            gather_copy(peer, me).start()

    _ring_gather(weight_ref, weight_out, send_right, send_left, send_partner, weight_recv, me,
                 hook=norm_and_send, hook_step=3)
    block_rows = weight_out.shape[1]
    for slot in range(weight_out.shape[0]):
        weight_flat[slot * block_rows:(slot + 1) * block_rows, :] = weight_out[slot]
    for peer in peers:
        gather_copy(peer, peer).wait_recv()
    for peer in peers:
        scatter_copy(peer, me).wait_send()
        gather_copy(peer, me).wait_send()


def mix_ring_feat(parts, resid, gains, gain_row, weight_block, n, tok_count, collective_id):
    _, rows, width = parts.shape
    weight_rows, weight_width = weight_block.shape
    chips = tok_count // 2
    new_resid, gathered, weights = pl.pallas_call(
        functools.partial(_mix_ring_kernel, n, gain_row),
        out_shape=(
            jax.ShapeDtypeStruct((rows, width), jnp.bfloat16),
            jax.ShapeDtypeStruct((n, rows, width), jnp.bfloat16),
            jax.ShapeDtypeStruct((tok_count * weight_rows, weight_width), weight_block.dtype),
        ),
        in_specs=[pl.BlockSpec(memory_space=pltpu.VMEM)] * 4,
        out_specs=(pl.BlockSpec(memory_space=pltpu.VMEM),) * 3,
        scratch_shapes=[
            pltpu.VMEM((tok_count, weight_rows, weight_width), weight_block.dtype),
            pltpu.VMEM((n, rows, width), parts.dtype),
            pltpu.VMEM((rows, width), jnp.bfloat16),
            pltpu.SemaphoreType.DMA((n,)),
            pltpu.SemaphoreType.DMA((n,)),
            pltpu.SemaphoreType.DMA((n,)),
            pltpu.SemaphoreType.DMA((n,)),
            pltpu.SemaphoreType.DMA((chips,)),
            pltpu.SemaphoreType.DMA((chips,)),
            pltpu.SemaphoreType.DMA((chips,)),
            pltpu.SemaphoreType.DMA((tok_count,)),
        ],
        compiler_params=pltpu.CompilerParams(collective_id=collective_id, has_side_effects=True),
    )(parts, resid, gains, weight_block)
    return new_resid, gathered.reshape(n * rows, width), weights


def _norm_gather_kernel(n, gain_row, tok_ref, gain_ref, out_ref, mine, send_sem, recv_sem):
    me = lax.axis_index("feat")
    tok_index = lax.axis_index("tok")
    peers = [lax.rem(me + d, n) for d in range(1, n)]
    _greet(peers, tok_index)
    as_float = tok_ref[...].astype(jnp.float32)
    center = jnp.mean(as_float, axis=-1, keepdims=True)
    spread = jnp.mean(jnp.square(as_float - center), axis=-1, keepdims=True)
    normed = ((as_float - center) * lax.rsqrt(spread + epsilon) * gain_ref[gain_row:gain_row + 1, :]).astype(jnp.bfloat16)
    mine[...] = normed
    out_ref[me] = normed

    def copy(peer, slot):
        return pltpu.make_async_remote_copy(
            src_ref=mine, dst_ref=out_ref.at[slot], send_sem=send_sem.at[peer],
            recv_sem=recv_sem.at[slot], device_id=(tok_index, peer), device_id_type=MESH,
        )

    for peer in peers:
        copy(peer, me).start()
    for peer in peers:
        copy(peer, peer).wait_recv()
    for peer in peers:
        copy(peer, me).wait_send()


def norm_gather_feat(rows, gains, gain_row, n, collective_id):
    count, width = rows.shape
    return pl.pallas_call(
        functools.partial(_norm_gather_kernel, n, gain_row),
        out_shape=jax.ShapeDtypeStruct((n, count, width), jnp.bfloat16),
        in_specs=[pl.BlockSpec(memory_space=pltpu.VMEM)] * 2,
        out_specs=pl.BlockSpec(memory_space=pltpu.VMEM),
        scratch_shapes=[
            pltpu.VMEM((count, width), jnp.bfloat16),
            pltpu.SemaphoreType.DMA((n,)),
            pltpu.SemaphoreType.DMA((n,)),
        ],
        compiler_params=pltpu.CompilerParams(collective_id=collective_id, has_side_effects=True),
    )(rows, gains).reshape(n * count, width)


def _scatter_kernel(n, part_ref, out_ref, held, send_sem, recv_sem):
    me = lax.axis_index("feat")
    tok_index = lax.axis_index("tok")
    peers = [lax.rem(me + d, n) for d in range(1, n)]
    _greet(peers, tok_index)
    for peer in peers:
        pltpu.make_async_remote_copy(
            src_ref=part_ref.at[peer], dst_ref=held.at[me], send_sem=send_sem.at[peer],
            recv_sem=recv_sem.at[me], device_id=(tok_index, peer), device_id_type=MESH,
        ).start()
    total = part_ref[me].astype(jnp.float32)
    for peer in peers:
        pltpu.make_async_remote_copy(
            src_ref=part_ref.at[peer], dst_ref=held.at[peer], send_sem=send_sem.at[peer],
            recv_sem=recv_sem.at[peer], device_id=(tok_index, peer), device_id_type=MESH,
        ).wait_recv()
        total = total + held[peer].astype(jnp.float32)
    out_ref[...] = total
    for peer in peers:
        pltpu.make_async_remote_copy(
            src_ref=part_ref.at[peer], dst_ref=held.at[me], send_sem=send_sem.at[peer],
            recv_sem=recv_sem.at[me], device_id=(tok_index, peer), device_id_type=MESH,
        ).wait_send()


def scatter_feat(parts, n, collective_id):
    _, rows, width = parts.shape
    return pl.pallas_call(
        functools.partial(_scatter_kernel, n),
        out_shape=jax.ShapeDtypeStruct((rows, width), jnp.float32),
        in_specs=[pl.BlockSpec(memory_space=pltpu.VMEM)],
        out_specs=pl.BlockSpec(memory_space=pltpu.VMEM),
        scratch_shapes=[
            pltpu.VMEM((n, rows, width), parts.dtype),
            pltpu.SemaphoreType.DMA((n,)),
            pltpu.SemaphoreType.DMA((n,)),
        ],
        compiler_params=pltpu.CompilerParams(collective_id=collective_id, has_side_effects=True),
    )(parts)

MESH = pl.DeviceIdType.MESH
LEAST_UNITS = 4
MOST_UNITS = 16
HEAD_DIM = 88


epsilon = 1e-06


def layer_norm(row_block, gain_row):
    as_float = row_block.astype(jnp.float32)
    center = jnp.mean(as_float, axis=-1, keepdims=True)
    spread = jnp.mean(jnp.square(as_float - center), axis=-1, keepdims=True)
    scaled = (as_float - center) * lax.rsqrt(spread + epsilon) * gain_row.astype(jnp.float32)
    return scaled.astype(jnp.bfloat16)


def project_rows(row_block, weight_block, collective_id):
    n = lax.axis_size("feat")
    return jnp.dot(
        gather_feat(row_block, n, collective_id),
        weight_block,
        preferred_element_type=jnp.float32,
    )


def scatter_rows(left_rows, right_rows, collective_id):
    n = lax.axis_size("feat")
    parts = jnp.dot(left_rows, right_rows, preferred_element_type=jnp.float32).astype(jnp.bfloat16)
    return scatter_feat(parts.reshape(n, parts.shape[0] // n, parts.shape[1]), n, collective_id)


def early_weights(weight_up, weight_down):
    return (weight_up, weight_down)


def upper_weight(fetched):
    return lax.all_gather(fetched[0], "tok", axis=0, tiled=True)


def lower_weight(fetched):
    return lax.all_gather(fetched[1], "tok", axis=1, tiled=True)


def attend(projected, segment_ids, head_count):
    token_count = projected.shape[0]
    parts_all = projected.reshape(token_count, 3, head_count, HEAD_DIM)
    queries = (parts_all[:, 0] * HEAD_DIM ** (-0.5)).astype(jnp.bfloat16)
    keys_here = parts_all[:, 1].astype(jnp.bfloat16)
    values_here = parts_all[:, 2].astype(jnp.bfloat16)
    scores = jnp.einsum("qhd,khd->hqk", queries, keys_here, preferred_element_type=jnp.float32)
    same_segment = segment_ids[:, None] == segment_ids[None, :]
    scores = jnp.where(same_segment[None, :, :], scores, -1e30)
    highest = jnp.max(scores, axis=-1, keepdims=True)
    raised = jnp.exp(scores - highest)
    weights_soft = (raised / jnp.sum(raised, axis=-1, keepdims=True)).astype(jnp.bfloat16)
    attended = jnp.einsum(
        "hqk,khd->qhd", weights_soft, values_here, preferred_element_type=jnp.float32
    )
    return attended.astype(jnp.bfloat16).reshape(token_count, head_count * HEAD_DIM)


def route_rows(embedded, segment_ids, owners):
    merged_count = embedded.shape[0]
    peer_count = owners.shape[0]
    least_units = max(LEAST_UNITS, (merged_count + peer_count - 1) // peer_count)
    slot_count = max(MOST_UNITS, 2 * least_units)
    first_ids = segment_ids.reshape(merged_count, 4)[:, 0]
    id_base = lax.axis_index("tok") * peer_count
    local_index = first_ids - id_base
    owner_pick = local_index[:, None] == jnp.arange(peer_count, dtype=jnp.int32)[None, :]
    owner_of = jnp.sum(jnp.where(owner_pick, owners[None, :], 0), axis=1)
    row_index = jnp.arange(merged_count, dtype=jnp.int32)
    earlier = (row_index[None, :] < row_index[:, None]) & (first_ids[None, :] == first_ids[:, None])
    within = jnp.sum(earlier.astype(jnp.int32), axis=1)
    target = owner_of * slot_count + within
    select = (
        jnp.arange(peer_count * slot_count, dtype=jnp.int32)[:, None] == target[None, :]
    ).astype(jnp.bfloat16)
    packed = jnp.dot(select, embedded, preferred_element_type=jnp.float32).astype(jnp.bfloat16)
    packed = packed.reshape(peer_count, slot_count, embedded.shape[1])
    received = route_exchange(packed, 5)
    return received.reshape(peer_count * slot_count, embedded.shape[1])


def body(
    tokens,
    segment_ids,
    owners,
    project_in,
    project_out,
    weight_up,
    weight_down,
    weight_merge,
    gain_attend,
    gain_hidden,
    gain_final,
):
    model_width = tokens.shape[1]
    head_count = project_in.shape[2] // HEAD_DIM
    units = weight_up.shape[1]
    feat_count = lax.axis_size("feat")
    tok_count = lax.axis_size("tok")
    flat_in = project_in.reshape(model_width, 3 * project_in.shape[2])
    local_count = tokens.shape[0]
    gains = jnp.stack([gain_attend, gain_hidden, gain_final]).astype(jnp.float32)
    stacked = jnp.concatenate([weight_up, weight_down.T], axis=1)
    gathered = norm_gather_feat(tokens, gains, 0, feat_count, 0)
    projected = jnp.dot(gathered, flat_in, preferred_element_type=jnp.float32)
    attended = attend(projected, segment_ids, head_count)
    attn_parts = jnp.dot(attended, project_out, preferred_element_type=jnp.float32).astype(jnp.bfloat16)
    second, hidden_rows, weights = mix_ring_feat(
        attn_parts.reshape(feat_count, local_count, model_width), tokens, gains, 1, stacked,
        feat_count, tok_count, 1,
    )
    both = weights
    upper = both[:, :units]
    lower_t = both[:, units:]
    hidden = jax.nn.gelu(
        jnp.dot(hidden_rows, upper, preferred_element_type=jnp.float32), approximate=False
    ).astype(jnp.bfloat16)
    down_parts = lax.dot_general(
        hidden, lower_t, (((1,), (1,)), ((), ())), preferred_element_type=jnp.float32
    ).astype(jnp.bfloat16)
    _, final_rows = mix_feat(
        down_parts.reshape(feat_count, local_count, model_width), second, gains, 2, feat_count, 3
    )
    merged = final_rows.reshape(final_rows.shape[0] // 4, 4 * model_width)
    embedded = jnp.dot(merged, weight_merge, preferred_element_type=jnp.float32).astype(jnp.bfloat16)
    return route_rows(embedded, segment_ids, owners)


def solution(mesh):
    return jax.shard_map(
        body,
        mesh=mesh,
        in_specs=(
            P(("tok", "feat"), None),
            P("tok"),
            P("tok"),
            P(None, None, "feat"),
            P("feat", None),
            P("tok", "feat"),
            P("feat", "tok"),
            P(None, "feat"),
            P(),
            P(),
            P(),
        ),
        out_specs=P("tok", "feat"),
        check_vma=False,
    )
```

```python
import functools
import jax
import jax.numpy as jnp
from jax import lax
from jax.experimental import pallas as pl
from jax.experimental.pallas import tpu as pltpu
from jax.sharding import PartitionSpec as P


def _greet(peers, tok_index):
    barrier = pltpu.get_barrier_semaphore()
    for peer in peers:
        pl.semaphore_signal(barrier, inc=1, device_id=(tok_index, peer), device_id_type=MESH)
    pl.semaphore_wait(barrier, len(peers))


def _gather_kernel(n, row_ref, out_ref, send_sem, recv_sem):
    me = lax.axis_index("feat")
    tok_index = lax.axis_index("tok")
    peers = [lax.rem(me + d, n) for d in range(1, n)]
    _greet(peers, tok_index)
    for peer in peers:
        pltpu.make_async_remote_copy(
            src_ref=row_ref, dst_ref=out_ref.at[me], send_sem=send_sem.at[peer],
            recv_sem=recv_sem.at[me], device_id=(tok_index, peer), device_id_type=MESH,
        ).start()
    out_ref[me] = row_ref[...]
    for peer in peers:
        pltpu.make_async_remote_copy(
            src_ref=row_ref, dst_ref=out_ref.at[peer], send_sem=send_sem.at[peer],
            recv_sem=recv_sem.at[peer], device_id=(tok_index, peer), device_id_type=MESH,
        ).wait_recv()
    for peer in peers:
        pltpu.make_async_remote_copy(
            src_ref=row_ref, dst_ref=out_ref.at[me], send_sem=send_sem.at[peer],
            recv_sem=recv_sem.at[me], device_id=(tok_index, peer), device_id_type=MESH,
        ).wait_send()


def gather_feat(row_block, n, collective_id):
    rows, width = row_block.shape
    return pl.pallas_call(
        functools.partial(_gather_kernel, n),
        out_shape=jax.ShapeDtypeStruct((n, rows, width), row_block.dtype),
        in_specs=[pl.BlockSpec(memory_space=pltpu.VMEM)],
        out_specs=pl.BlockSpec(memory_space=pltpu.VMEM),
        scratch_shapes=[pltpu.SemaphoreType.DMA((n,)), pltpu.SemaphoreType.DMA((n,))],
        compiler_params=pltpu.CompilerParams(collective_id=collective_id, has_side_effects=True),
    )(row_block).reshape(n * rows, width)


def _ring_gather(x_ref, out_ref, send_right, send_left, send_partner, recv_sem, feat_index, after_first=None,
                 hook=None, hook_step=1):
    tok_count = out_ref.shape[0]
    chips = tok_count // 2
    right_steps = chips // 2
    left_steps = chips - 1 - right_steps
    me = lax.axis_index("tok")
    chip = me // 2
    core = me % 2
    right = lax.rem(chip + 1, chips) * 2 + core
    left = lax.rem(chip + chips - 1, chips) * 2 + core
    partner = chip * 2 + (1 - core)

    def slot_of(offset):
        return lax.rem(chip + offset + 2 * chips, chips) * 2 + core

    def remote(src, slot, sem, target):
        return pltpu.make_async_remote_copy(
            src_ref=src, dst_ref=out_ref.at[slot], send_sem=sem, recv_sem=recv_sem.at[slot],
            device_id=(target, feat_index), device_id_type=MESH,
        )

    sends = []

    def forward_partner(src, slot):
        copy = remote(src, slot, send_partner.at[len(sends_partner)], partner)
        copy.start()
        sends_partner.append(copy)

    sends_partner = []
    out_ref[me] = x_ref[...]
    arrived = []
    for step in range(1, right_steps + 1):
        if step == 1:
            src_right = x_ref
            src_left = x_ref
        else:
            from_left = slot_of(-(step - 1))
            remote(x_ref, from_left, send_right.at[0], right).wait_recv()
            src_right = out_ref.at[from_left]
            arrived.append(from_left)
        copy = remote(src_right, slot_of(-(step - 1)), send_right.at[step - 1], right)
        copy.start()
        sends.append(copy)
        if step > 1 and step - 1 <= left_steps:
            from_right = slot_of(step - 1)
            remote(x_ref, from_right, send_left.at[0], left).wait_recv()
            src_left = out_ref.at[from_right]
            arrived.append(from_right)
        if step <= left_steps:
            copy = remote(src_left, slot_of(step - 1), send_left.at[step - 1], left)
            copy.start()
            sends.append(copy)
        if step == 1:
            if after_first is not None:
                after_first()
            forward_partner(x_ref, me)
        for slot in arrived:
            forward_partner(out_ref.at[slot], slot)
        arrived = []
        if hook is not None and step == min(hook_step, right_steps):
            hook()
    last_left = slot_of(-right_steps)
    remote(x_ref, last_left, send_right.at[0], right).wait_recv()
    forward_partner(out_ref.at[last_left], last_left)
    if left_steps >= 1 and left_steps + 1 > right_steps:
        last_right = slot_of(left_steps)
        remote(x_ref, last_right, send_left.at[0], left).wait_recv()
        forward_partner(out_ref.at[last_right], last_right)
    for other_chip in range(chips):
        remote(x_ref, other_chip * 2 + (1 - core), send_partner.at[0], partner).wait_recv()
    for copy in sends + sends_partner:
        copy.wait_send()


def _first_kernel(n, row_ref, weight_ref, out_ref, weight_out, send_sem, recv_sem,
                  send_right, send_left, send_partner, weight_recv):
    me = lax.axis_index("feat")
    tok_index = lax.axis_index("tok")
    chips = weight_out.shape[0] // 2
    chip = tok_index // 2
    core = tok_index % 2
    peers = [lax.rem(me + d, n) for d in range(1, n)]
    barrier = pltpu.get_barrier_semaphore()
    for peer in peers:
        pl.semaphore_signal(barrier, inc=1, device_id=(tok_index, peer), device_id_type=MESH)
    ring_peers = [
        lax.rem(chip + 1, chips) * 2 + core,
        lax.rem(chip + chips - 1, chips) * 2 + core,
        chip * 2 + (1 - core),
    ]
    for peer in ring_peers:
        pl.semaphore_signal(barrier, inc=1, device_id=(peer, me), device_id_type=MESH)
    pl.semaphore_wait(barrier, len(peers) + len(ring_peers))

    def start_rows():
        for peer in peers:
            pltpu.make_async_remote_copy(
                src_ref=row_ref, dst_ref=out_ref.at[me], send_sem=send_sem.at[peer],
                recv_sem=recv_sem.at[me], device_id=(tok_index, peer), device_id_type=MESH,
            ).start()

    _ring_gather(weight_ref, weight_out, send_right, send_left, send_partner, weight_recv, me, start_rows)
    out_ref[me] = row_ref[...]
    for peer in peers:
        pltpu.make_async_remote_copy(
            src_ref=row_ref, dst_ref=out_ref.at[peer], send_sem=send_sem.at[peer],
            recv_sem=recv_sem.at[peer], device_id=(tok_index, peer), device_id_type=MESH,
        ).wait_recv()
    for peer in peers:
        pltpu.make_async_remote_copy(
            src_ref=row_ref, dst_ref=out_ref.at[me], send_sem=send_sem.at[peer],
            recv_sem=recv_sem.at[me], device_id=(tok_index, peer), device_id_type=MESH,
        ).wait_send()


def first_exchange(row_block, weight_block, n, tok_count, collective_id):
    rows, width = row_block.shape
    weight_rows, weight_width = weight_block.shape
    chips = tok_count // 2
    gathered, weights = pl.pallas_call(
        functools.partial(_first_kernel, n),
        out_shape=(
            jax.ShapeDtypeStruct((n, rows, width), row_block.dtype),
            jax.ShapeDtypeStruct((tok_count, weight_rows, weight_width), weight_block.dtype),
        ),
        in_specs=[pl.BlockSpec(memory_space=pltpu.VMEM)] * 2,
        out_specs=(pl.BlockSpec(memory_space=pltpu.VMEM),) * 2,
        scratch_shapes=[
            pltpu.SemaphoreType.DMA((n,)),
            pltpu.SemaphoreType.DMA((n,)),
            pltpu.SemaphoreType.DMA((chips,)),
            pltpu.SemaphoreType.DMA((chips,)),
            pltpu.SemaphoreType.DMA((chips,)),
            pltpu.SemaphoreType.DMA((tok_count,)),
        ],
        compiler_params=pltpu.CompilerParams(collective_id=collective_id, has_side_effects=True),
    )(row_block, weight_block)
    return gathered.reshape(n * rows, width), weights


def _route_kernel(n, packed_ref, out_ref, send_sem, recv_sem):
    me = lax.axis_index("tok")
    feat_index = lax.axis_index("feat")
    peers = [lax.rem(me + d, n) for d in range(1, n)]
    barrier = pltpu.get_barrier_semaphore()
    for peer in peers:
        pl.semaphore_signal(barrier, inc=1, device_id=(peer, feat_index), device_id_type=MESH)
    pl.semaphore_wait(barrier, len(peers))
    for peer in peers:
        pltpu.make_async_remote_copy(
            src_ref=packed_ref.at[peer], dst_ref=out_ref.at[me], send_sem=send_sem.at[peer],
            recv_sem=recv_sem.at[me], device_id=(peer, feat_index), device_id_type=MESH,
        ).start()
    out_ref[me] = packed_ref[me]
    for peer in peers:
        pltpu.make_async_remote_copy(
            src_ref=packed_ref.at[peer], dst_ref=out_ref.at[peer], send_sem=send_sem.at[peer],
            recv_sem=recv_sem.at[peer], device_id=(peer, feat_index), device_id_type=MESH,
        ).wait_recv()
    for peer in peers:
        pltpu.make_async_remote_copy(
            src_ref=packed_ref.at[peer], dst_ref=out_ref.at[me], send_sem=send_sem.at[peer],
            recv_sem=recv_sem.at[me], device_id=(peer, feat_index), device_id_type=MESH,
        ).wait_send()


def route_exchange(packed, collective_id):
    n = packed.shape[0]
    return pl.pallas_call(
        functools.partial(_route_kernel, n),
        out_shape=jax.ShapeDtypeStruct(packed.shape, packed.dtype),
        in_specs=[pl.BlockSpec(memory_space=pltpu.VMEM)],
        out_specs=pl.BlockSpec(memory_space=pltpu.VMEM),
        scratch_shapes=[pltpu.SemaphoreType.DMA((n,)), pltpu.SemaphoreType.DMA((n,))],
        compiler_params=pltpu.CompilerParams(collective_id=collective_id, has_side_effects=True),
    )(packed)


def _mix_kernel(n, gain_row, part_ref, resid_ref, gain_ref, resid_out, out_ref, merged_out, held, mine,
                scatter_send, scatter_recv, gather_send, gather_recv):
    me = lax.axis_index("feat")
    tok_index = lax.axis_index("tok")
    peers = [lax.rem(me + d, n) for d in range(1, n)]
    _greet(peers, tok_index)

    def scatter_copy(peer, slot):
        return pltpu.make_async_remote_copy(
            src_ref=part_ref.at[peer], dst_ref=held.at[slot], send_sem=scatter_send.at[peer],
            recv_sem=scatter_recv.at[slot], device_id=(tok_index, peer), device_id_type=MESH,
        )

    def gather_copy(peer, slot):
        return pltpu.make_async_remote_copy(
            src_ref=mine, dst_ref=out_ref.at[slot], send_sem=gather_send.at[peer],
            recv_sem=gather_recv.at[slot], device_id=(tok_index, peer), device_id_type=MESH,
        )

    for peer in peers:
        scatter_copy(peer, me).start()
    total = part_ref[me].astype(jnp.float32)
    for peer in peers:
        scatter_copy(peer, peer).wait_recv()
        total = total + held[peer].astype(jnp.float32)
    summed = (resid_ref[...].astype(jnp.float32) + total).astype(jnp.bfloat16)
    resid_out[...] = summed
    as_float = summed.astype(jnp.float32)
    center = jnp.mean(as_float, axis=-1, keepdims=True)
    spread = jnp.mean(jnp.square(as_float - center), axis=-1, keepdims=True)
    normed = ((as_float - center) * lax.rsqrt(spread + epsilon) * gain_ref[gain_row:gain_row + 1, :]).astype(jnp.bfloat16)
    mine[...] = normed
    out_ref[me] = normed
    for peer in peers:
        gather_copy(peer, me).start()
    for peer in peers:
        gather_copy(peer, peer).wait_recv()
    group = 4
    width = out_ref.shape[2]
    row_count = n * out_ref.shape[1]
    rows = out_ref[...].astype(jnp.float32).reshape(row_count, width).astype(jnp.bfloat16)
    merged_index = lax.broadcasted_iota(jnp.int32, (row_count // group, row_count), 0)
    row_index = lax.broadcasted_iota(jnp.int32, (row_count // group, row_count), 1)
    for part in range(group):
        pick = (row_index == merged_index * group + part).astype(jnp.bfloat16)
        merged_out[:, part * width:(part + 1) * width] = jnp.dot(
            pick, rows, preferred_element_type=jnp.float32
        ).astype(jnp.bfloat16)
    for peer in peers:
        scatter_copy(peer, me).wait_send()
        gather_copy(peer, me).wait_send()


def mix_feat(parts, resid, gains, gain_row, n, collective_id):
    _, rows, width = parts.shape
    new_resid, _, merged = pl.pallas_call(
        functools.partial(_mix_kernel, n, gain_row),
        out_shape=(
            jax.ShapeDtypeStruct((rows, width), jnp.bfloat16),
            jax.ShapeDtypeStruct((n, rows, width), jnp.bfloat16),
            jax.ShapeDtypeStruct((n * rows // 4, 4 * width), jnp.bfloat16),
        ),
        in_specs=[pl.BlockSpec(memory_space=pltpu.VMEM)] * 3,
        out_specs=(pl.BlockSpec(memory_space=pltpu.VMEM),) * 3,
        scratch_shapes=[
            pltpu.VMEM((n, rows, width), parts.dtype),
            pltpu.VMEM((rows, width), jnp.bfloat16),
            pltpu.SemaphoreType.DMA((n,)),
            pltpu.SemaphoreType.DMA((n,)),
            pltpu.SemaphoreType.DMA((n,)),
            pltpu.SemaphoreType.DMA((n,)),
        ],
        compiler_params=pltpu.CompilerParams(collective_id=collective_id, has_side_effects=True),
    )(parts, resid, gains)
    return new_resid, merged


def _mix_ring_kernel(n, gain_row, part_ref, resid_ref, gain_ref, weight_ref, resid_out, out_ref, weight_flat,
                     weight_out, held, mine, scatter_send, scatter_recv, gather_send, gather_recv,
                     send_right, send_left, send_partner, weight_recv):
    me = lax.axis_index("feat")
    tok_index = lax.axis_index("tok")
    chips = weight_out.shape[0] // 2
    chip = tok_index // 2
    core = tok_index % 2
    peers = [lax.rem(me + d, n) for d in range(1, n)]
    barrier = pltpu.get_barrier_semaphore()
    for peer in peers:
        pl.semaphore_signal(barrier, inc=1, device_id=(tok_index, peer), device_id_type=MESH)
    ring_peers = [
        lax.rem(chip + 1, chips) * 2 + core,
        lax.rem(chip + chips - 1, chips) * 2 + core,
        chip * 2 + (1 - core),
    ]
    for peer in ring_peers:
        pl.semaphore_signal(barrier, inc=1, device_id=(peer, me), device_id_type=MESH)
    pl.semaphore_wait(barrier, len(peers) + len(ring_peers))

    def scatter_copy(peer, slot):
        return pltpu.make_async_remote_copy(
            src_ref=part_ref.at[peer], dst_ref=held.at[slot], send_sem=scatter_send.at[peer],
            recv_sem=scatter_recv.at[slot], device_id=(tok_index, peer), device_id_type=MESH,
        )

    def gather_copy(peer, slot):
        return pltpu.make_async_remote_copy(
            src_ref=mine, dst_ref=out_ref.at[slot], send_sem=gather_send.at[peer],
            recv_sem=gather_recv.at[slot], device_id=(tok_index, peer), device_id_type=MESH,
        )

    for peer in peers:
        scatter_copy(peer, me).start()

    def norm_and_send():
        total = part_ref[me].astype(jnp.float32)
        for peer in peers:
            scatter_copy(peer, peer).wait_recv()
            total = total + held[peer].astype(jnp.float32)
        summed = (resid_ref[...].astype(jnp.float32) + total).astype(jnp.bfloat16)
        resid_out[...] = summed
        as_float = summed.astype(jnp.float32)
        center = jnp.mean(as_float, axis=-1, keepdims=True)
        spread = jnp.mean(jnp.square(as_float - center), axis=-1, keepdims=True)
        normed = ((as_float - center) * lax.rsqrt(spread + epsilon) * gain_ref[gain_row:gain_row + 1, :]).astype(jnp.bfloat16)
        mine[...] = normed
        out_ref[me] = normed
        for peer in peers:
            gather_copy(peer, me).start()

    _ring_gather(weight_ref, weight_out, send_right, send_left, send_partner, weight_recv, me,
                 hook=norm_and_send, hook_step=3)
    block_rows = weight_out.shape[1]
    for slot in range(weight_out.shape[0]):
        weight_flat[slot * block_rows:(slot + 1) * block_rows, :] = weight_out[slot]
    for peer in peers:
        gather_copy(peer, peer).wait_recv()
    for peer in peers:
        scatter_copy(peer, me).wait_send()
        gather_copy(peer, me).wait_send()


def mix_ring_feat(parts, resid, gains, gain_row, weight_block, n, tok_count, collective_id):
    _, rows, width = parts.shape
    weight_rows, weight_width = weight_block.shape
    chips = tok_count // 2
    new_resid, gathered, weights = pl.pallas_call(
        functools.partial(_mix_ring_kernel, n, gain_row),
        out_shape=(
            jax.ShapeDtypeStruct((rows, width), jnp.bfloat16),
            jax.ShapeDtypeStruct((n, rows, width), jnp.bfloat16),
            jax.ShapeDtypeStruct((tok_count * weight_rows, weight_width), weight_block.dtype),
        ),
        in_specs=[pl.BlockSpec(memory_space=pltpu.VMEM)] * 4,
        out_specs=(pl.BlockSpec(memory_space=pltpu.VMEM),) * 3,
        scratch_shapes=[
            pltpu.VMEM((tok_count, weight_rows, weight_width), weight_block.dtype),
            pltpu.VMEM((n, rows, width), parts.dtype),
            pltpu.VMEM((rows, width), jnp.bfloat16),
            pltpu.SemaphoreType.DMA((n,)),
            pltpu.SemaphoreType.DMA((n,)),
            pltpu.SemaphoreType.DMA((n,)),
            pltpu.SemaphoreType.DMA((n,)),
            pltpu.SemaphoreType.DMA((chips,)),
            pltpu.SemaphoreType.DMA((chips,)),
            pltpu.SemaphoreType.DMA((chips,)),
            pltpu.SemaphoreType.DMA((tok_count,)),
        ],
        compiler_params=pltpu.CompilerParams(collective_id=collective_id, has_side_effects=True),
    )(parts, resid, gains, weight_block)
    return new_resid, gathered.reshape(n * rows, width), weights


def _norm_gather_kernel(n, gain_row, tok_ref, gain_ref, out_ref, mine, send_sem, recv_sem):
    me = lax.axis_index("feat")
    tok_index = lax.axis_index("tok")
    peers = [lax.rem(me + d, n) for d in range(1, n)]
    _greet(peers, tok_index)
    as_float = tok_ref[...].astype(jnp.float32)
    center = jnp.mean(as_float, axis=-1, keepdims=True)
    spread = jnp.mean(jnp.square(as_float - center), axis=-1, keepdims=True)
    normed = ((as_float - center) * lax.rsqrt(spread + epsilon) * gain_ref[gain_row:gain_row + 1, :]).astype(jnp.bfloat16)
    mine[...] = normed
    out_ref[me] = normed

    def copy(peer, slot):
        return pltpu.make_async_remote_copy(
            src_ref=mine, dst_ref=out_ref.at[slot], send_sem=send_sem.at[peer],
            recv_sem=recv_sem.at[slot], device_id=(tok_index, peer), device_id_type=MESH,
        )

    for peer in peers:
        copy(peer, me).start()
    for peer in peers:
        copy(peer, peer).wait_recv()
    for peer in peers:
        copy(peer, me).wait_send()


def norm_gather_feat(rows, gains, gain_row, n, collective_id):
    count, width = rows.shape
    return pl.pallas_call(
        functools.partial(_norm_gather_kernel, n, gain_row),
        out_shape=jax.ShapeDtypeStruct((n, count, width), jnp.bfloat16),
        in_specs=[pl.BlockSpec(memory_space=pltpu.VMEM)] * 2,
        out_specs=pl.BlockSpec(memory_space=pltpu.VMEM),
        scratch_shapes=[
            pltpu.VMEM((count, width), jnp.bfloat16),
            pltpu.SemaphoreType.DMA((n,)),
            pltpu.SemaphoreType.DMA((n,)),
        ],
        compiler_params=pltpu.CompilerParams(collective_id=collective_id, has_side_effects=True),
    )(rows, gains).reshape(n * count, width)


def _scatter_kernel(n, part_ref, out_ref, held, send_sem, recv_sem):
    me = lax.axis_index("feat")
    tok_index = lax.axis_index("tok")
    peers = [lax.rem(me + d, n) for d in range(1, n)]
    _greet(peers, tok_index)
    for peer in peers:
        pltpu.make_async_remote_copy(
            src_ref=part_ref.at[peer], dst_ref=held.at[me], send_sem=send_sem.at[peer],
            recv_sem=recv_sem.at[me], device_id=(tok_index, peer), device_id_type=MESH,
        ).start()
    total = part_ref[me].astype(jnp.float32)
    for peer in peers:
        pltpu.make_async_remote_copy(
            src_ref=part_ref.at[peer], dst_ref=held.at[peer], send_sem=send_sem.at[peer],
            recv_sem=recv_sem.at[peer], device_id=(tok_index, peer), device_id_type=MESH,
        ).wait_recv()
        total = total + held[peer].astype(jnp.float32)
    out_ref[...] = total
    for peer in peers:
        pltpu.make_async_remote_copy(
            src_ref=part_ref.at[peer], dst_ref=held.at[me], send_sem=send_sem.at[peer],
            recv_sem=recv_sem.at[me], device_id=(tok_index, peer), device_id_type=MESH,
        ).wait_send()


def scatter_feat(parts, n, collective_id):
    _, rows, width = parts.shape
    return pl.pallas_call(
        functools.partial(_scatter_kernel, n),
        out_shape=jax.ShapeDtypeStruct((rows, width), jnp.float32),
        in_specs=[pl.BlockSpec(memory_space=pltpu.VMEM)],
        out_specs=pl.BlockSpec(memory_space=pltpu.VMEM),
        scratch_shapes=[
            pltpu.VMEM((n, rows, width), parts.dtype),
            pltpu.SemaphoreType.DMA((n,)),
            pltpu.SemaphoreType.DMA((n,)),
        ],
        compiler_params=pltpu.CompilerParams(collective_id=collective_id, has_side_effects=True),
    )(parts)

MESH = pl.DeviceIdType.MESH
LEAST_UNITS = 4
MOST_UNITS = 16
HEAD_DIM = 88


epsilon = 1e-06


def layer_norm(row_block, gain_row):
    as_float = row_block.astype(jnp.float32)
    center = jnp.mean(as_float, axis=-1, keepdims=True)
    spread = jnp.mean(jnp.square(as_float - center), axis=-1, keepdims=True)
    scaled = (as_float - center) * lax.rsqrt(spread + epsilon) * gain_row.astype(jnp.float32)
    return scaled.astype(jnp.bfloat16)


def project_rows(row_block, weight_block, collective_id):
    n = lax.axis_size("feat")
    return jnp.dot(
        gather_feat(row_block, n, collective_id),
        weight_block,
        preferred_element_type=jnp.float32,
    )


def scatter_rows(left_rows, right_rows, collective_id):
    n = lax.axis_size("feat")
    parts = jnp.dot(left_rows, right_rows, preferred_element_type=jnp.float32).astype(jnp.bfloat16)
    return scatter_feat(parts.reshape(n, parts.shape[0] // n, parts.shape[1]), n, collective_id)


def early_weights(weight_up, weight_down):
    return (weight_up, weight_down)


def upper_weight(fetched):
    return lax.all_gather(fetched[0], "tok", axis=0, tiled=True)


def lower_weight(fetched):
    return lax.all_gather(fetched[1], "tok", axis=1, tiled=True)


def attend(projected, segment_ids, head_count):
    token_count = projected.shape[0]
    parts_all = projected.reshape(token_count, 3, head_count, HEAD_DIM)
    queries = (parts_all[:, 0] * HEAD_DIM ** (-0.5)).astype(jnp.bfloat16)
    keys_here = parts_all[:, 1].astype(jnp.bfloat16)
    values_here = parts_all[:, 2].astype(jnp.bfloat16)
    scores = jnp.einsum("qhd,khd->hqk", queries, keys_here, preferred_element_type=jnp.float32)
    same_segment = segment_ids[:, None] == segment_ids[None, :]
    scores = jnp.where(same_segment[None, :, :], scores, -1e30)
    highest = jnp.max(scores, axis=-1, keepdims=True)
    raised = jnp.exp(scores - highest)
    weights_soft = (raised / jnp.sum(raised, axis=-1, keepdims=True)).astype(jnp.bfloat16)
    attended = jnp.einsum(
        "hqk,khd->qhd", weights_soft, values_here, preferred_element_type=jnp.float32
    )
    return attended.astype(jnp.bfloat16).reshape(token_count, head_count * HEAD_DIM)


def route_rows(embedded, segment_ids, owners):
    merged_count = embedded.shape[0]
    peer_count = owners.shape[0]
    least_units = max(LEAST_UNITS, (merged_count + peer_count - 1) // peer_count)
    slot_count = max(MOST_UNITS, 2 * least_units)
    first_ids = segment_ids.reshape(merged_count, 4)[:, 0]
    id_base = lax.axis_index("tok") * peer_count
    local_index = first_ids - id_base
    owner_pick = local_index[:, None] == jnp.arange(peer_count, dtype=jnp.int32)[None, :]
    owner_of = jnp.sum(jnp.where(owner_pick, owners[None, :], 0), axis=1)
    row_index = jnp.arange(merged_count, dtype=jnp.int32)
    earlier = (row_index[None, :] < row_index[:, None]) & (first_ids[None, :] == first_ids[:, None])
    within = jnp.sum(earlier.astype(jnp.int32), axis=1)
    target = owner_of * slot_count + within
    select = (
        jnp.arange(peer_count * slot_count, dtype=jnp.int32)[:, None] == target[None, :]
    ).astype(jnp.bfloat16)
    packed = jnp.dot(select, embedded, preferred_element_type=jnp.float32).astype(jnp.bfloat16)
    packed = packed.reshape(peer_count, slot_count, embedded.shape[1])
    received = route_exchange(packed, 5)
    return received.reshape(peer_count * slot_count, embedded.shape[1])


def body(
    tokens,
    segment_ids,
    owners,
    project_in,
    project_out,
    weight_up,
    weight_down,
    weight_merge,
    gain_attend,
    gain_hidden,
    gain_final,
):
    model_width = tokens.shape[1]
    head_count = project_in.shape[2] // HEAD_DIM
    units = weight_up.shape[1]
    feat_count = lax.axis_size("feat")
    tok_count = lax.axis_size("tok")
    flat_in = project_in.reshape(model_width, 3 * project_in.shape[2])
    local_count = tokens.shape[0]
    gains = jnp.stack([gain_attend, gain_hidden, gain_final]).astype(jnp.float32)
    stacked = jnp.concatenate([weight_up, weight_down.T], axis=1)
    gathered = norm_gather_feat(tokens, gains, 0, feat_count, 0)
    projected = jnp.dot(gathered, flat_in, preferred_element_type=jnp.float32)
    attended = attend(projected, segment_ids, head_count)
    attn_parts = jnp.dot(attended, project_out, preferred_element_type=jnp.float32).astype(jnp.bfloat16)
    second, hidden_rows, weights = mix_ring_feat(
        attn_parts.reshape(feat_count, local_count, model_width), tokens, gains, 1, stacked,
        feat_count, tok_count, 1,
    )
    both = weights
    upper = both[:, :units]
    lower_t = both[:, units:]
    hidden = jax.nn.gelu(
        jnp.dot(hidden_rows, upper, preferred_element_type=jnp.float32), approximate=False
    ).astype(jnp.bfloat16)
    down_parts = lax.dot_general(
        hidden, lower_t, (((1,), (1,)), ((), ())), preferred_element_type=jnp.float32
    ).astype(jnp.bfloat16)
    _, merged = mix_feat(
        down_parts.reshape(feat_count, local_count, model_width), second, gains, 2, feat_count, 3
    )
    embedded = jnp.dot(merged, weight_merge, preferred_element_type=jnp.float32).astype(jnp.bfloat16)
    return route_rows(embedded, segment_ids, owners)


def solution(mesh):
    return jax.shard_map(
        body,
        mesh=mesh,
        in_specs=(
            P(("tok", "feat"), None),
            P("tok"),
            P("tok"),
            P(None, None, "feat"),
            P("feat", None),
            P("tok", "feat"),
            P("feat", "tok"),
            P(None, "feat"),
            P(),
            P(),
            P(),
        ),
        out_specs=P("tok", "feat"),
        check_vma=False,
    )
```

```python
import functools
import jax
import jax.numpy as jnp
from jax import lax
from jax.experimental import pallas as pl
from jax.experimental.pallas import tpu as pltpu
from jax.sharding import PartitionSpec as P


def _greet(peers, tok_index):
    barrier = pltpu.get_barrier_semaphore()
    for peer in peers:
        pl.semaphore_signal(barrier, inc=1, device_id=(tok_index, peer), device_id_type=MESH)
    pl.semaphore_wait(barrier, len(peers))


def _gather_kernel(n, row_ref, out_ref, send_sem, recv_sem):
    me = lax.axis_index("feat")
    tok_index = lax.axis_index("tok")
    peers = [lax.rem(me + d, n) for d in range(1, n)]
    _greet(peers, tok_index)
    for peer in peers:
        pltpu.make_async_remote_copy(
            src_ref=row_ref, dst_ref=out_ref.at[me], send_sem=send_sem.at[peer],
            recv_sem=recv_sem.at[me], device_id=(tok_index, peer), device_id_type=MESH,
        ).start()
    out_ref[me] = row_ref[...]
    for peer in peers:
        pltpu.make_async_remote_copy(
            src_ref=row_ref, dst_ref=out_ref.at[peer], send_sem=send_sem.at[peer],
            recv_sem=recv_sem.at[peer], device_id=(tok_index, peer), device_id_type=MESH,
        ).wait_recv()
    for peer in peers:
        pltpu.make_async_remote_copy(
            src_ref=row_ref, dst_ref=out_ref.at[me], send_sem=send_sem.at[peer],
            recv_sem=recv_sem.at[me], device_id=(tok_index, peer), device_id_type=MESH,
        ).wait_send()


def gather_feat(row_block, n, collective_id):
    rows, width = row_block.shape
    return pl.pallas_call(
        functools.partial(_gather_kernel, n),
        out_shape=jax.ShapeDtypeStruct((n, rows, width), row_block.dtype),
        in_specs=[pl.BlockSpec(memory_space=pltpu.VMEM)],
        out_specs=pl.BlockSpec(memory_space=pltpu.VMEM),
        scratch_shapes=[pltpu.SemaphoreType.DMA((n,)), pltpu.SemaphoreType.DMA((n,))],
        compiler_params=pltpu.CompilerParams(collective_id=collective_id, has_side_effects=True),
    )(row_block).reshape(n * rows, width)


def _ring_gather(x_ref, out_ref, send_right, send_left, send_partner, recv_sem, feat_index, after_first=None,
                 hook=None, hook_step=1):
    tok_count = out_ref.shape[0]
    chips = tok_count // 2
    right_steps = chips // 2
    left_steps = chips - 1 - right_steps
    me = lax.axis_index("tok")
    chip = me // 2
    core = me % 2
    right = lax.rem(chip + 1, chips) * 2 + core
    left = lax.rem(chip + chips - 1, chips) * 2 + core
    partner = chip * 2 + (1 - core)

    def slot_of(offset):
        return lax.rem(chip + offset + 2 * chips, chips) * 2 + core

    def remote(src, slot, sem, target):
        return pltpu.make_async_remote_copy(
            src_ref=src, dst_ref=out_ref.at[slot], send_sem=sem, recv_sem=recv_sem.at[slot],
            device_id=(target, feat_index), device_id_type=MESH,
        )

    sends = []

    def forward_partner(src, slot):
        copy = remote(src, slot, send_partner.at[len(sends_partner)], partner)
        copy.start()
        sends_partner.append(copy)

    sends_partner = []
    out_ref[me] = x_ref[...]
    arrived = []
    for step in range(1, right_steps + 1):
        if step == 1:
            src_right = x_ref
            src_left = x_ref
        else:
            from_left = slot_of(-(step - 1))
            remote(x_ref, from_left, send_right.at[0], right).wait_recv()
            src_right = out_ref.at[from_left]
            arrived.append(from_left)
        copy = remote(src_right, slot_of(-(step - 1)), send_right.at[step - 1], right)
        copy.start()
        sends.append(copy)
        if step > 1 and step - 1 <= left_steps:
            from_right = slot_of(step - 1)
            remote(x_ref, from_right, send_left.at[0], left).wait_recv()
            src_left = out_ref.at[from_right]
            arrived.append(from_right)
        if step <= left_steps:
            copy = remote(src_left, slot_of(step - 1), send_left.at[step - 1], left)
            copy.start()
            sends.append(copy)
        if step == 1:
            if after_first is not None:
                after_first()
            forward_partner(x_ref, me)
        for slot in arrived:
            forward_partner(out_ref.at[slot], slot)
        arrived = []
        if hook is not None and step == min(hook_step, right_steps):
            hook()
    last_left = slot_of(-right_steps)
    remote(x_ref, last_left, send_right.at[0], right).wait_recv()
    forward_partner(out_ref.at[last_left], last_left)
    if left_steps >= 1 and left_steps + 1 > right_steps:
        last_right = slot_of(left_steps)
        remote(x_ref, last_right, send_left.at[0], left).wait_recv()
        forward_partner(out_ref.at[last_right], last_right)
    for other_chip in range(chips):
        remote(x_ref, other_chip * 2 + (1 - core), send_partner.at[0], partner).wait_recv()
    for copy in sends + sends_partner:
        copy.wait_send()


def _first_kernel(n, row_ref, weight_ref, out_ref, weight_out, send_sem, recv_sem,
                  send_right, send_left, send_partner, weight_recv):
    me = lax.axis_index("feat")
    tok_index = lax.axis_index("tok")
    chips = weight_out.shape[0] // 2
    chip = tok_index // 2
    core = tok_index % 2
    peers = [lax.rem(me + d, n) for d in range(1, n)]
    barrier = pltpu.get_barrier_semaphore()
    for peer in peers:
        pl.semaphore_signal(barrier, inc=1, device_id=(tok_index, peer), device_id_type=MESH)
    ring_peers = [
        lax.rem(chip + 1, chips) * 2 + core,
        lax.rem(chip + chips - 1, chips) * 2 + core,
        chip * 2 + (1 - core),
    ]
    for peer in ring_peers:
        pl.semaphore_signal(barrier, inc=1, device_id=(peer, me), device_id_type=MESH)
    pl.semaphore_wait(barrier, len(peers) + len(ring_peers))

    def start_rows():
        for peer in peers:
            pltpu.make_async_remote_copy(
                src_ref=row_ref, dst_ref=out_ref.at[me], send_sem=send_sem.at[peer],
                recv_sem=recv_sem.at[me], device_id=(tok_index, peer), device_id_type=MESH,
            ).start()

    _ring_gather(weight_ref, weight_out, send_right, send_left, send_partner, weight_recv, me, start_rows)
    out_ref[me] = row_ref[...]
    for peer in peers:
        pltpu.make_async_remote_copy(
            src_ref=row_ref, dst_ref=out_ref.at[peer], send_sem=send_sem.at[peer],
            recv_sem=recv_sem.at[peer], device_id=(tok_index, peer), device_id_type=MESH,
        ).wait_recv()
    for peer in peers:
        pltpu.make_async_remote_copy(
            src_ref=row_ref, dst_ref=out_ref.at[me], send_sem=send_sem.at[peer],
            recv_sem=recv_sem.at[me], device_id=(tok_index, peer), device_id_type=MESH,
        ).wait_send()


def first_exchange(row_block, weight_block, n, tok_count, collective_id):
    rows, width = row_block.shape
    weight_rows, weight_width = weight_block.shape
    chips = tok_count // 2
    gathered, weights = pl.pallas_call(
        functools.partial(_first_kernel, n),
        out_shape=(
            jax.ShapeDtypeStruct((n, rows, width), row_block.dtype),
            jax.ShapeDtypeStruct((tok_count, weight_rows, weight_width), weight_block.dtype),
        ),
        in_specs=[pl.BlockSpec(memory_space=pltpu.VMEM)] * 2,
        out_specs=(pl.BlockSpec(memory_space=pltpu.VMEM),) * 2,
        scratch_shapes=[
            pltpu.SemaphoreType.DMA((n,)),
            pltpu.SemaphoreType.DMA((n,)),
            pltpu.SemaphoreType.DMA((chips,)),
            pltpu.SemaphoreType.DMA((chips,)),
            pltpu.SemaphoreType.DMA((chips,)),
            pltpu.SemaphoreType.DMA((tok_count,)),
        ],
        compiler_params=pltpu.CompilerParams(collective_id=collective_id, has_side_effects=True),
    )(row_block, weight_block)
    return gathered.reshape(n * rows, width), weights


def _route_kernel(n, packed_ref, out_ref, send_sem, recv_sem):
    me = lax.axis_index("tok")
    feat_index = lax.axis_index("feat")
    peers = [lax.rem(me + d, n) for d in range(1, n)]
    barrier = pltpu.get_barrier_semaphore()
    for peer in peers:
        pl.semaphore_signal(barrier, inc=1, device_id=(peer, feat_index), device_id_type=MESH)
    pl.semaphore_wait(barrier, len(peers))
    for peer in peers:
        pltpu.make_async_remote_copy(
            src_ref=packed_ref.at[peer], dst_ref=out_ref.at[me], send_sem=send_sem.at[peer],
            recv_sem=recv_sem.at[me], device_id=(peer, feat_index), device_id_type=MESH,
        ).start()
    out_ref[me] = packed_ref[me]
    for peer in peers:
        pltpu.make_async_remote_copy(
            src_ref=packed_ref.at[peer], dst_ref=out_ref.at[peer], send_sem=send_sem.at[peer],
            recv_sem=recv_sem.at[peer], device_id=(peer, feat_index), device_id_type=MESH,
        ).wait_recv()
    for peer in peers:
        pltpu.make_async_remote_copy(
            src_ref=packed_ref.at[peer], dst_ref=out_ref.at[me], send_sem=send_sem.at[peer],
            recv_sem=recv_sem.at[me], device_id=(peer, feat_index), device_id_type=MESH,
        ).wait_send()


def route_exchange(packed, collective_id):
    n = packed.shape[0]
    return pl.pallas_call(
        functools.partial(_route_kernel, n),
        out_shape=jax.ShapeDtypeStruct(packed.shape, packed.dtype),
        in_specs=[pl.BlockSpec(memory_space=pltpu.VMEM)],
        out_specs=pl.BlockSpec(memory_space=pltpu.VMEM),
        scratch_shapes=[pltpu.SemaphoreType.DMA((n,)), pltpu.SemaphoreType.DMA((n,))],
        compiler_params=pltpu.CompilerParams(collective_id=collective_id, has_side_effects=True),
    )(packed)


def _mix_kernel(n, gain_row, part_ref, resid_ref, gain_ref, resid_out, out_ref, merged_out, held, mine,
                scatter_send, scatter_recv, gather_send, gather_recv):
    me = lax.axis_index("feat")
    tok_index = lax.axis_index("tok")
    peers = [lax.rem(me + d, n) for d in range(1, n)]
    _greet(peers, tok_index)

    def scatter_copy(peer, slot):
        return pltpu.make_async_remote_copy(
            src_ref=part_ref.at[peer], dst_ref=held.at[slot], send_sem=scatter_send.at[peer],
            recv_sem=scatter_recv.at[slot], device_id=(tok_index, peer), device_id_type=MESH,
        )

    def gather_copy(peer, slot):
        return pltpu.make_async_remote_copy(
            src_ref=mine, dst_ref=out_ref.at[slot], send_sem=gather_send.at[peer],
            recv_sem=gather_recv.at[slot], device_id=(tok_index, peer), device_id_type=MESH,
        )

    for peer in peers:
        scatter_copy(peer, me).start()
    total = part_ref[me].astype(jnp.float32)
    for peer in peers:
        scatter_copy(peer, peer).wait_recv()
        total = total + held[peer].astype(jnp.float32)
    summed = (resid_ref[...].astype(jnp.float32) + total).astype(jnp.bfloat16)
    resid_out[...] = summed
    as_float = summed.astype(jnp.float32)
    center = jnp.mean(as_float, axis=-1, keepdims=True)
    spread = jnp.mean(jnp.square(as_float - center), axis=-1, keepdims=True)
    normed = ((as_float - center) * lax.rsqrt(spread + epsilon) * gain_ref[...].astype(jnp.float32)[None, :]).astype(jnp.bfloat16)
    mine[...] = normed
    out_ref[me] = normed
    for peer in peers:
        gather_copy(peer, me).start()
    for peer in peers:
        gather_copy(peer, peer).wait_recv()
    group = 4
    width = out_ref.shape[2]
    row_count = n * out_ref.shape[1]
    rows = out_ref[...].astype(jnp.float32).reshape(row_count, width).astype(jnp.bfloat16)
    merged_index = lax.broadcasted_iota(jnp.int32, (row_count // group, row_count), 0)
    row_index = lax.broadcasted_iota(jnp.int32, (row_count // group, row_count), 1)
    for part in range(group):
        pick = (row_index == merged_index * group + part).astype(jnp.bfloat16)
        merged_out[:, part * width:(part + 1) * width] = jnp.dot(
            pick, rows, preferred_element_type=jnp.float32
        ).astype(jnp.bfloat16)
    for peer in peers:
        scatter_copy(peer, me).wait_send()
        gather_copy(peer, me).wait_send()


def mix_feat(parts, resid, gains, gain_row, n, collective_id):
    _, rows, width = parts.shape
    new_resid, _, merged = pl.pallas_call(
        functools.partial(_mix_kernel, n, gain_row),
        out_shape=(
            jax.ShapeDtypeStruct((rows, width), jnp.bfloat16),
            jax.ShapeDtypeStruct((n, rows, width), jnp.bfloat16),
            jax.ShapeDtypeStruct((n * rows // 4, 4 * width), jnp.bfloat16),
        ),
        in_specs=[pl.BlockSpec(memory_space=pltpu.VMEM)] * 3,
        out_specs=(pl.BlockSpec(memory_space=pltpu.VMEM),) * 3,
        scratch_shapes=[
            pltpu.VMEM((n, rows, width), parts.dtype),
            pltpu.VMEM((rows, width), jnp.bfloat16),
            pltpu.SemaphoreType.DMA((n,)),
            pltpu.SemaphoreType.DMA((n,)),
            pltpu.SemaphoreType.DMA((n,)),
            pltpu.SemaphoreType.DMA((n,)),
        ],
        compiler_params=pltpu.CompilerParams(collective_id=collective_id, has_side_effects=True),
    )(parts, resid, gains)
    return new_resid, merged


def _mix_ring_kernel(n, gain_row, part_ref, resid_ref, gain_ref, weight_ref, resid_out, out_ref, weight_flat,
                     weight_out, held, mine, scatter_send, scatter_recv, gather_send, gather_recv,
                     send_right, send_left, send_partner, weight_recv):
    me = lax.axis_index("feat")
    tok_index = lax.axis_index("tok")
    chips = weight_out.shape[0] // 2
    chip = tok_index // 2
    core = tok_index % 2
    peers = [lax.rem(me + d, n) for d in range(1, n)]
    barrier = pltpu.get_barrier_semaphore()
    for peer in peers:
        pl.semaphore_signal(barrier, inc=1, device_id=(tok_index, peer), device_id_type=MESH)
    ring_peers = [
        lax.rem(chip + 1, chips) * 2 + core,
        lax.rem(chip + chips - 1, chips) * 2 + core,
        chip * 2 + (1 - core),
    ]
    for peer in ring_peers:
        pl.semaphore_signal(barrier, inc=1, device_id=(peer, me), device_id_type=MESH)
    pl.semaphore_wait(barrier, len(peers) + len(ring_peers))

    def scatter_copy(peer, slot):
        return pltpu.make_async_remote_copy(
            src_ref=part_ref.at[peer], dst_ref=held.at[slot], send_sem=scatter_send.at[peer],
            recv_sem=scatter_recv.at[slot], device_id=(tok_index, peer), device_id_type=MESH,
        )

    def gather_copy(peer, slot):
        return pltpu.make_async_remote_copy(
            src_ref=mine, dst_ref=out_ref.at[slot], send_sem=gather_send.at[peer],
            recv_sem=gather_recv.at[slot], device_id=(tok_index, peer), device_id_type=MESH,
        )

    for peer in peers:
        scatter_copy(peer, me).start()

    def norm_and_send():
        total = part_ref[me].astype(jnp.float32)
        for peer in peers:
            scatter_copy(peer, peer).wait_recv()
            total = total + held[peer].astype(jnp.float32)
        summed = (resid_ref[...].astype(jnp.float32) + total).astype(jnp.bfloat16)
        resid_out[...] = summed
        as_float = summed.astype(jnp.float32)
        center = jnp.mean(as_float, axis=-1, keepdims=True)
        spread = jnp.mean(jnp.square(as_float - center), axis=-1, keepdims=True)
        normed = ((as_float - center) * lax.rsqrt(spread + epsilon) * gain_ref[...].astype(jnp.float32)[None, :]).astype(jnp.bfloat16)
        mine[...] = normed
        out_ref[me] = normed
        for peer in peers:
            gather_copy(peer, me).start()

    _ring_gather(weight_ref, weight_out, send_right, send_left, send_partner, weight_recv, me,
                 hook=norm_and_send, hook_step=3)
    block_rows = weight_out.shape[1]
    for slot in range(weight_out.shape[0]):
        weight_flat[slot * block_rows:(slot + 1) * block_rows, :] = weight_out[slot]
    for peer in peers:
        gather_copy(peer, peer).wait_recv()
    for peer in peers:
        scatter_copy(peer, me).wait_send()
        gather_copy(peer, me).wait_send()


def mix_ring_feat(parts, resid, gains, gain_row, weight_block, n, tok_count, collective_id):
    _, rows, width = parts.shape
    weight_rows, weight_width = weight_block.shape
    chips = tok_count // 2
    new_resid, gathered, weights = pl.pallas_call(
        functools.partial(_mix_ring_kernel, n, gain_row),
        out_shape=(
            jax.ShapeDtypeStruct((rows, width), jnp.bfloat16),
            jax.ShapeDtypeStruct((n, rows, width), jnp.bfloat16),
            jax.ShapeDtypeStruct((tok_count * weight_rows, weight_width), weight_block.dtype),
        ),
        in_specs=[pl.BlockSpec(memory_space=pltpu.VMEM)] * 4,
        out_specs=(pl.BlockSpec(memory_space=pltpu.VMEM),) * 3,
        scratch_shapes=[
            pltpu.VMEM((tok_count, weight_rows, weight_width), weight_block.dtype),
            pltpu.VMEM((n, rows, width), parts.dtype),
            pltpu.VMEM((rows, width), jnp.bfloat16),
            pltpu.SemaphoreType.DMA((n,)),
            pltpu.SemaphoreType.DMA((n,)),
            pltpu.SemaphoreType.DMA((n,)),
            pltpu.SemaphoreType.DMA((n,)),
            pltpu.SemaphoreType.DMA((chips,)),
            pltpu.SemaphoreType.DMA((chips,)),
            pltpu.SemaphoreType.DMA((chips,)),
            pltpu.SemaphoreType.DMA((tok_count,)),
        ],
        compiler_params=pltpu.CompilerParams(collective_id=collective_id, has_side_effects=True),
    )(parts, resid, gains, weight_block)
    return new_resid, gathered.reshape(n * rows, width), weights


def _norm_gather_kernel(n, gain_row, tok_ref, gain_ref, out_ref, mine, send_sem, recv_sem):
    me = lax.axis_index("feat")
    tok_index = lax.axis_index("tok")
    peers = [lax.rem(me + d, n) for d in range(1, n)]
    _greet(peers, tok_index)
    as_float = tok_ref[...].astype(jnp.float32)
    center = jnp.mean(as_float, axis=-1, keepdims=True)
    spread = jnp.mean(jnp.square(as_float - center), axis=-1, keepdims=True)
    normed = ((as_float - center) * lax.rsqrt(spread + epsilon) * gain_ref[...].astype(jnp.float32)[None, :]).astype(jnp.bfloat16)
    mine[...] = normed
    out_ref[me] = normed

    def copy(peer, slot):
        return pltpu.make_async_remote_copy(
            src_ref=mine, dst_ref=out_ref.at[slot], send_sem=send_sem.at[peer],
            recv_sem=recv_sem.at[slot], device_id=(tok_index, peer), device_id_type=MESH,
        )

    for peer in peers:
        copy(peer, me).start()
    for peer in peers:
        copy(peer, peer).wait_recv()
    for peer in peers:
        copy(peer, me).wait_send()


def norm_gather_feat(rows, gains, gain_row, n, collective_id):
    count, width = rows.shape
    return pl.pallas_call(
        functools.partial(_norm_gather_kernel, n, gain_row),
        out_shape=jax.ShapeDtypeStruct((n, count, width), jnp.bfloat16),
        in_specs=[pl.BlockSpec(memory_space=pltpu.VMEM)] * 2,
        out_specs=pl.BlockSpec(memory_space=pltpu.VMEM),
        scratch_shapes=[
            pltpu.VMEM((count, width), jnp.bfloat16),
            pltpu.SemaphoreType.DMA((n,)),
            pltpu.SemaphoreType.DMA((n,)),
        ],
        compiler_params=pltpu.CompilerParams(collective_id=collective_id, has_side_effects=True),
    )(rows, gains).reshape(n * count, width)


def _scatter_kernel(n, part_ref, out_ref, held, send_sem, recv_sem):
    me = lax.axis_index("feat")
    tok_index = lax.axis_index("tok")
    peers = [lax.rem(me + d, n) for d in range(1, n)]
    _greet(peers, tok_index)
    for peer in peers:
        pltpu.make_async_remote_copy(
            src_ref=part_ref.at[peer], dst_ref=held.at[me], send_sem=send_sem.at[peer],
            recv_sem=recv_sem.at[me], device_id=(tok_index, peer), device_id_type=MESH,
        ).start()
    total = part_ref[me].astype(jnp.float32)
    for peer in peers:
        pltpu.make_async_remote_copy(
            src_ref=part_ref.at[peer], dst_ref=held.at[peer], send_sem=send_sem.at[peer],
            recv_sem=recv_sem.at[peer], device_id=(tok_index, peer), device_id_type=MESH,
        ).wait_recv()
        total = total + held[peer].astype(jnp.float32)
    out_ref[...] = total
    for peer in peers:
        pltpu.make_async_remote_copy(
            src_ref=part_ref.at[peer], dst_ref=held.at[me], send_sem=send_sem.at[peer],
            recv_sem=recv_sem.at[me], device_id=(tok_index, peer), device_id_type=MESH,
        ).wait_send()


def scatter_feat(parts, n, collective_id):
    _, rows, width = parts.shape
    return pl.pallas_call(
        functools.partial(_scatter_kernel, n),
        out_shape=jax.ShapeDtypeStruct((rows, width), jnp.float32),
        in_specs=[pl.BlockSpec(memory_space=pltpu.VMEM)],
        out_specs=pl.BlockSpec(memory_space=pltpu.VMEM),
        scratch_shapes=[
            pltpu.VMEM((n, rows, width), parts.dtype),
            pltpu.SemaphoreType.DMA((n,)),
            pltpu.SemaphoreType.DMA((n,)),
        ],
        compiler_params=pltpu.CompilerParams(collective_id=collective_id, has_side_effects=True),
    )(parts)

MESH = pl.DeviceIdType.MESH
LEAST_UNITS = 4
MOST_UNITS = 16
HEAD_DIM = 88


epsilon = 1e-06


def layer_norm(row_block, gain_row):
    as_float = row_block.astype(jnp.float32)
    center = jnp.mean(as_float, axis=-1, keepdims=True)
    spread = jnp.mean(jnp.square(as_float - center), axis=-1, keepdims=True)
    scaled = (as_float - center) * lax.rsqrt(spread + epsilon) * gain_row.astype(jnp.float32)
    return scaled.astype(jnp.bfloat16)


def project_rows(row_block, weight_block, collective_id):
    n = lax.axis_size("feat")
    return jnp.dot(
        gather_feat(row_block, n, collective_id),
        weight_block,
        preferred_element_type=jnp.float32,
    )


def scatter_rows(left_rows, right_rows, collective_id):
    n = lax.axis_size("feat")
    parts = jnp.dot(left_rows, right_rows, preferred_element_type=jnp.float32).astype(jnp.bfloat16)
    return scatter_feat(parts.reshape(n, parts.shape[0] // n, parts.shape[1]), n, collective_id)


def early_weights(weight_up, weight_down):
    return (weight_up, weight_down)


def upper_weight(fetched):
    return lax.all_gather(fetched[0], "tok", axis=0, tiled=True)


def lower_weight(fetched):
    return lax.all_gather(fetched[1], "tok", axis=1, tiled=True)


def attend(projected, segment_ids, head_count):
    token_count = projected.shape[0]
    parts_all = projected.reshape(token_count, 3, head_count, HEAD_DIM)
    queries = (parts_all[:, 0] * HEAD_DIM ** (-0.5)).astype(jnp.bfloat16)
    keys_here = parts_all[:, 1].astype(jnp.bfloat16)
    values_here = parts_all[:, 2].astype(jnp.bfloat16)
    scores = jnp.einsum("qhd,khd->hqk", queries, keys_here, preferred_element_type=jnp.float32)
    same_segment = segment_ids[:, None] == segment_ids[None, :]
    scores = jnp.where(same_segment[None, :, :], scores, -1e30)
    highest = jnp.max(scores, axis=-1, keepdims=True)
    raised = jnp.exp(scores - highest)
    weights_soft = (raised / jnp.sum(raised, axis=-1, keepdims=True)).astype(jnp.bfloat16)
    attended = jnp.einsum(
        "hqk,khd->qhd", weights_soft, values_here, preferred_element_type=jnp.float32
    )
    return attended.astype(jnp.bfloat16).reshape(token_count, head_count * HEAD_DIM)


def route_rows(embedded, segment_ids, owners):
    merged_count = embedded.shape[0]
    peer_count = owners.shape[0]
    least_units = max(LEAST_UNITS, (merged_count + peer_count - 1) // peer_count)
    slot_count = max(MOST_UNITS, 2 * least_units)
    first_ids = segment_ids.reshape(merged_count, 4)[:, 0]
    id_base = lax.axis_index("tok") * peer_count
    local_index = first_ids - id_base
    owner_pick = local_index[:, None] == jnp.arange(peer_count, dtype=jnp.int32)[None, :]
    owner_of = jnp.sum(jnp.where(owner_pick, owners[None, :], 0), axis=1)
    row_index = jnp.arange(merged_count, dtype=jnp.int32)
    earlier = (row_index[None, :] < row_index[:, None]) & (first_ids[None, :] == first_ids[:, None])
    within = jnp.sum(earlier.astype(jnp.int32), axis=1)
    target = owner_of * slot_count + within
    select = (
        jnp.arange(peer_count * slot_count, dtype=jnp.int32)[:, None] == target[None, :]
    ).astype(jnp.bfloat16)
    packed = jnp.dot(select, embedded, preferred_element_type=jnp.float32).astype(jnp.bfloat16)
    packed = packed.reshape(peer_count, slot_count, embedded.shape[1])
    received = route_exchange(packed, 5)
    return received.reshape(peer_count * slot_count, embedded.shape[1])


def body(
    tokens,
    segment_ids,
    owners,
    project_in,
    project_out,
    weight_up,
    weight_down,
    weight_merge,
    gain_attend,
    gain_hidden,
    gain_final,
):
    model_width = tokens.shape[1]
    head_count = project_in.shape[2] // HEAD_DIM
    units = weight_up.shape[1]
    feat_count = lax.axis_size("feat")
    tok_count = lax.axis_size("tok")
    flat_in = project_in.reshape(model_width, 3 * project_in.shape[2])
    local_count = tokens.shape[0]
    stacked = jnp.concatenate([weight_up, weight_down.T], axis=1)
    gathered = norm_gather_feat(tokens, gain_attend, 0, feat_count, 0)
    projected = jnp.dot(gathered, flat_in, preferred_element_type=jnp.float32)
    attended = attend(projected, segment_ids, head_count)
    attn_parts = jnp.dot(attended, project_out, preferred_element_type=jnp.float32).astype(jnp.bfloat16)
    second, hidden_rows, weights = mix_ring_feat(
        attn_parts.reshape(feat_count, local_count, model_width), tokens, gain_hidden, 1, stacked,
        feat_count, tok_count, 1,
    )
    both = weights
    upper = both[:, :units]
    lower_t = both[:, units:]
    hidden = jax.nn.gelu(
        jnp.dot(hidden_rows, upper, preferred_element_type=jnp.float32), approximate=False
    ).astype(jnp.bfloat16)
    down_parts = lax.dot_general(
        hidden, lower_t, (((1,), (1,)), ((), ())), preferred_element_type=jnp.float32
    ).astype(jnp.bfloat16)
    _, merged = mix_feat(
        down_parts.reshape(feat_count, local_count, model_width), second, gain_final, 2, feat_count, 3
    )
    embedded = jnp.dot(merged, weight_merge, preferred_element_type=jnp.float32).astype(jnp.bfloat16)
    return route_rows(embedded, segment_ids, owners)


def solution(mesh):
    return jax.shard_map(
        body,
        mesh=mesh,
        in_specs=(
            P(("tok", "feat"), None),
            P("tok"),
            P("tok"),
            P(None, None, "feat"),
            P("feat", None),
            P("tok", "feat"),
            P("feat", "tok"),
            P(None, "feat"),
            P(),
            P(),
            P(),
        ),
        out_specs=P("tok", "feat"),
        check_vma=False,
    )
```

```python
import functools
import jax
import jax.numpy as jnp
from jax import lax
from jax.experimental import pallas as pl
from jax.experimental.pallas import tpu as pltpu
from jax.sharding import PartitionSpec as P


def _greet(peers, tok_index):
    barrier = pltpu.get_barrier_semaphore()
    for peer in peers:
        pl.semaphore_signal(barrier, inc=1, device_id=(tok_index, peer), device_id_type=MESH)
    pl.semaphore_wait(barrier, len(peers))


def _gather_kernel(n, row_ref, out_ref, send_sem, recv_sem):
    me = lax.axis_index("feat")
    tok_index = lax.axis_index("tok")
    peers = [lax.rem(me + d, n) for d in range(1, n)]
    _greet(peers, tok_index)
    for peer in peers:
        pltpu.make_async_remote_copy(
            src_ref=row_ref, dst_ref=out_ref.at[me], send_sem=send_sem.at[peer],
            recv_sem=recv_sem.at[me], device_id=(tok_index, peer), device_id_type=MESH,
        ).start()
    out_ref[me] = row_ref[...]
    for peer in peers:
        pltpu.make_async_remote_copy(
            src_ref=row_ref, dst_ref=out_ref.at[peer], send_sem=send_sem.at[peer],
            recv_sem=recv_sem.at[peer], device_id=(tok_index, peer), device_id_type=MESH,
        ).wait_recv()
    for peer in peers:
        pltpu.make_async_remote_copy(
            src_ref=row_ref, dst_ref=out_ref.at[me], send_sem=send_sem.at[peer],
            recv_sem=recv_sem.at[me], device_id=(tok_index, peer), device_id_type=MESH,
        ).wait_send()


def gather_feat(row_block, n, collective_id):
    rows, width = row_block.shape
    return pl.pallas_call(
        functools.partial(_gather_kernel, n),
        out_shape=jax.ShapeDtypeStruct((n, rows, width), row_block.dtype),
        in_specs=[pl.BlockSpec(memory_space=pltpu.VMEM)],
        out_specs=pl.BlockSpec(memory_space=pltpu.VMEM),
        scratch_shapes=[pltpu.SemaphoreType.DMA((n,)), pltpu.SemaphoreType.DMA((n,))],
        compiler_params=pltpu.CompilerParams(collective_id=collective_id, has_side_effects=True),
    )(row_block).reshape(n * rows, width)


def _ring_gather(x_ref, out_ref, send_right, send_left, send_partner, recv_sem, feat_index, after_first=None,
                 hook=None, hook_step=1):
    tok_count = out_ref.shape[0]
    chips = tok_count // 2
    right_steps = chips // 2
    left_steps = chips - 1 - right_steps
    me = lax.axis_index("tok")
    chip = me // 2
    core = me % 2
    right = lax.rem(chip + 1, chips) * 2 + core
    left = lax.rem(chip + chips - 1, chips) * 2 + core
    partner = chip * 2 + (1 - core)

    def slot_of(offset):
        return lax.rem(chip + offset + 2 * chips, chips) * 2 + core

    def remote(src, slot, sem, target):
        return pltpu.make_async_remote_copy(
            src_ref=src, dst_ref=out_ref.at[slot], send_sem=sem, recv_sem=recv_sem.at[slot],
            device_id=(target, feat_index), device_id_type=MESH,
        )

    sends = []

    def forward_partner(src, slot):
        copy = remote(src, slot, send_partner.at[len(sends_partner)], partner)
        copy.start()
        sends_partner.append(copy)

    sends_partner = []
    out_ref[me] = x_ref[...]
    arrived = []
    for step in range(1, right_steps + 1):
        if step == 1:
            src_right = x_ref
            src_left = x_ref
        else:
            from_left = slot_of(-(step - 1))
            remote(x_ref, from_left, send_right.at[0], right).wait_recv()
            src_right = out_ref.at[from_left]
            arrived.append(from_left)
        copy = remote(src_right, slot_of(-(step - 1)), send_right.at[step - 1], right)
        copy.start()
        sends.append(copy)
        if step > 1 and step - 1 <= left_steps:
            from_right = slot_of(step - 1)
            remote(x_ref, from_right, send_left.at[0], left).wait_recv()
            src_left = out_ref.at[from_right]
            arrived.append(from_right)
        if step <= left_steps:
            copy = remote(src_left, slot_of(step - 1), send_left.at[step - 1], left)
            copy.start()
            sends.append(copy)
        if step == 1:
            if after_first is not None:
                after_first()
            forward_partner(x_ref, me)
        for slot in arrived:
            forward_partner(out_ref.at[slot], slot)
        arrived = []
        if hook is not None and step == min(hook_step, right_steps):
            hook()
    last_left = slot_of(-right_steps)
    remote(x_ref, last_left, send_right.at[0], right).wait_recv()
    forward_partner(out_ref.at[last_left], last_left)
    if left_steps >= 1 and left_steps + 1 > right_steps:
        last_right = slot_of(left_steps)
        remote(x_ref, last_right, send_left.at[0], left).wait_recv()
        forward_partner(out_ref.at[last_right], last_right)
    for other_chip in range(chips):
        remote(x_ref, other_chip * 2 + (1 - core), send_partner.at[0], partner).wait_recv()
    for copy in sends + sends_partner:
        copy.wait_send()


def _first_kernel(n, row_ref, weight_ref, out_ref, weight_out, send_sem, recv_sem,
                  send_right, send_left, send_partner, weight_recv):
    me = lax.axis_index("feat")
    tok_index = lax.axis_index("tok")
    chips = weight_out.shape[0] // 2
    chip = tok_index // 2
    core = tok_index % 2
    peers = [lax.rem(me + d, n) for d in range(1, n)]
    barrier = pltpu.get_barrier_semaphore()
    for peer in peers:
        pl.semaphore_signal(barrier, inc=1, device_id=(tok_index, peer), device_id_type=MESH)
    ring_peers = [
        lax.rem(chip + 1, chips) * 2 + core,
        lax.rem(chip + chips - 1, chips) * 2 + core,
        chip * 2 + (1 - core),
    ]
    for peer in ring_peers:
        pl.semaphore_signal(barrier, inc=1, device_id=(peer, me), device_id_type=MESH)
    pl.semaphore_wait(barrier, len(peers) + len(ring_peers))

    def start_rows():
        for peer in peers:
            pltpu.make_async_remote_copy(
                src_ref=row_ref, dst_ref=out_ref.at[me], send_sem=send_sem.at[peer],
                recv_sem=recv_sem.at[me], device_id=(tok_index, peer), device_id_type=MESH,
            ).start()

    _ring_gather(weight_ref, weight_out, send_right, send_left, send_partner, weight_recv, me, start_rows)
    out_ref[me] = row_ref[...]
    for peer in peers:
        pltpu.make_async_remote_copy(
            src_ref=row_ref, dst_ref=out_ref.at[peer], send_sem=send_sem.at[peer],
            recv_sem=recv_sem.at[peer], device_id=(tok_index, peer), device_id_type=MESH,
        ).wait_recv()
    for peer in peers:
        pltpu.make_async_remote_copy(
            src_ref=row_ref, dst_ref=out_ref.at[me], send_sem=send_sem.at[peer],
            recv_sem=recv_sem.at[me], device_id=(tok_index, peer), device_id_type=MESH,
        ).wait_send()


def first_exchange(row_block, weight_block, n, tok_count, collective_id):
    rows, width = row_block.shape
    weight_rows, weight_width = weight_block.shape
    chips = tok_count // 2
    gathered, weights = pl.pallas_call(
        functools.partial(_first_kernel, n),
        out_shape=(
            jax.ShapeDtypeStruct((n, rows, width), row_block.dtype),
            jax.ShapeDtypeStruct((tok_count, weight_rows, weight_width), weight_block.dtype),
        ),
        in_specs=[pl.BlockSpec(memory_space=pltpu.VMEM)] * 2,
        out_specs=(pl.BlockSpec(memory_space=pltpu.VMEM),) * 2,
        scratch_shapes=[
            pltpu.SemaphoreType.DMA((n,)),
            pltpu.SemaphoreType.DMA((n,)),
            pltpu.SemaphoreType.DMA((chips,)),
            pltpu.SemaphoreType.DMA((chips,)),
            pltpu.SemaphoreType.DMA((chips,)),
            pltpu.SemaphoreType.DMA((tok_count,)),
        ],
        compiler_params=pltpu.CompilerParams(collective_id=collective_id, has_side_effects=True),
    )(row_block, weight_block)
    return gathered.reshape(n * rows, width), weights


def _route_kernel(n, packed_ref, out_ref, send_sem, recv_sem):
    me = lax.axis_index("tok")
    feat_index = lax.axis_index("feat")
    peers = [lax.rem(me + d, n) for d in range(1, n)]
    barrier = pltpu.get_barrier_semaphore()
    for peer in peers:
        pl.semaphore_signal(barrier, inc=1, device_id=(peer, feat_index), device_id_type=MESH)
    pl.semaphore_wait(barrier, len(peers))
    for peer in peers:
        pltpu.make_async_remote_copy(
            src_ref=packed_ref.at[peer], dst_ref=out_ref.at[me], send_sem=send_sem.at[peer],
            recv_sem=recv_sem.at[me], device_id=(peer, feat_index), device_id_type=MESH,
        ).start()
    out_ref[me] = packed_ref[me]
    for peer in peers:
        pltpu.make_async_remote_copy(
            src_ref=packed_ref.at[peer], dst_ref=out_ref.at[peer], send_sem=send_sem.at[peer],
            recv_sem=recv_sem.at[peer], device_id=(peer, feat_index), device_id_type=MESH,
        ).wait_recv()
    for peer in peers:
        pltpu.make_async_remote_copy(
            src_ref=packed_ref.at[peer], dst_ref=out_ref.at[me], send_sem=send_sem.at[peer],
            recv_sem=recv_sem.at[me], device_id=(peer, feat_index), device_id_type=MESH,
        ).wait_send()


def route_exchange(packed, collective_id):
    n = packed.shape[0]
    return pl.pallas_call(
        functools.partial(_route_kernel, n),
        out_shape=jax.ShapeDtypeStruct(packed.shape, packed.dtype),
        in_specs=[pl.BlockSpec(memory_space=pltpu.VMEM)],
        out_specs=pl.BlockSpec(memory_space=pltpu.VMEM),
        scratch_shapes=[pltpu.SemaphoreType.DMA((n,)), pltpu.SemaphoreType.DMA((n,))],
        compiler_params=pltpu.CompilerParams(collective_id=collective_id, has_side_effects=True),
    )(packed)


def _mix_kernel(n, gain_row, part_ref, resid_ref, gain_ref, resid_out, out_ref, merged_out, held, mine_a,
                mine_b, scatter_send, scatter_recv, gather_send, gather_recv):
    me = lax.axis_index("feat")
    tok_index = lax.axis_index("tok")
    peers = [lax.rem(me + d, n) for d in range(1, n)]
    _greet(peers, tok_index)
    split = 16
    halves = [(0, split), (split, part_ref.shape[1] - split)]
    mines = [mine_a, mine_b]

    def scatter_copy(half, peer, slot):
        first, size = halves[half]
        return pltpu.make_async_remote_copy(
            src_ref=part_ref.at[peer, pl.ds(first, size)], dst_ref=held.at[slot, pl.ds(first, size)],
            send_sem=scatter_send.at[half, peer], recv_sem=scatter_recv.at[half, slot],
            device_id=(tok_index, peer), device_id_type=MESH,
        )

    def gather_copy(half, peer, slot):
        first, size = halves[half]
        return pltpu.make_async_remote_copy(
            src_ref=mines[half], dst_ref=out_ref.at[slot, pl.ds(first, size)],
            send_sem=gather_send.at[half, peer], recv_sem=gather_recv.at[half, slot],
            device_id=(tok_index, peer), device_id_type=MESH,
        )

    for half in range(2):
        for peer in peers:
            scatter_copy(half, peer, me).start()
    for half in range(2):
        first, size = halves[half]
        total = part_ref[me, first:first + size, :].astype(jnp.float32)
        for peer in peers:
            scatter_copy(half, peer, peer).wait_recv()
            total = total + held[peer, first:first + size, :].astype(jnp.float32)
        summed = (resid_ref[first:first + size, :].astype(jnp.float32) + total).astype(jnp.bfloat16)
        resid_out[first:first + size, :] = summed
        as_float = summed.astype(jnp.float32)
        center = jnp.mean(as_float, axis=-1, keepdims=True)
        spread = jnp.mean(jnp.square(as_float - center), axis=-1, keepdims=True)
        normed = ((as_float - center) * lax.rsqrt(spread + epsilon) * gain_ref[...].astype(jnp.float32)[None, :]).astype(jnp.bfloat16)
        mines[half][...] = normed
        out_ref[me, first:first + size, :] = normed
        for peer in peers:
            gather_copy(half, peer, me).start()
    for half in range(2):
        for peer in peers:
            gather_copy(half, peer, peer).wait_recv()
    group = 4
    width = out_ref.shape[2]
    row_count = n * out_ref.shape[1]
    rows = out_ref[...].astype(jnp.float32).reshape(row_count, width).astype(jnp.bfloat16)
    merged_index = lax.broadcasted_iota(jnp.int32, (row_count // group, row_count), 0)
    row_index = lax.broadcasted_iota(jnp.int32, (row_count // group, row_count), 1)
    for part in range(group):
        pick = (row_index == merged_index * group + part).astype(jnp.bfloat16)
        merged_out[:, part * width:(part + 1) * width] = jnp.dot(
            pick, rows, preferred_element_type=jnp.float32
        ).astype(jnp.bfloat16)
    for half in range(2):
        for peer in peers:
            scatter_copy(half, peer, me).wait_send()
            gather_copy(half, peer, me).wait_send()


def mix_feat(parts, resid, gains, gain_row, n, collective_id):
    _, rows, width = parts.shape
    new_resid, _, merged = pl.pallas_call(
        functools.partial(_mix_kernel, n, gain_row),
        out_shape=(
            jax.ShapeDtypeStruct((rows, width), jnp.bfloat16),
            jax.ShapeDtypeStruct((n, rows, width), jnp.bfloat16),
            jax.ShapeDtypeStruct((n * rows // 4, 4 * width), jnp.bfloat16),
        ),
        in_specs=[pl.BlockSpec(memory_space=pltpu.VMEM)] * 3,
        out_specs=(pl.BlockSpec(memory_space=pltpu.VMEM),) * 3,
        scratch_shapes=[
            pltpu.VMEM((n, rows, width), parts.dtype),
            pltpu.VMEM((16, width), jnp.bfloat16),
            pltpu.VMEM((rows - 16, width), jnp.bfloat16),
            pltpu.SemaphoreType.DMA((2, n)),
            pltpu.SemaphoreType.DMA((2, n)),
            pltpu.SemaphoreType.DMA((2, n)),
            pltpu.SemaphoreType.DMA((2, n)),
        ],
        compiler_params=pltpu.CompilerParams(collective_id=collective_id, has_side_effects=True),
    )(parts, resid, gains)
    return new_resid, merged


def _mix_ring_kernel(n, gain_row, part_ref, resid_ref, gain_ref, weight_ref, resid_out, out_ref, weight_flat,
                     weight_out, held, mine, scatter_send, scatter_recv, gather_send, gather_recv,
                     send_right, send_left, send_partner, weight_recv):
    me = lax.axis_index("feat")
    tok_index = lax.axis_index("tok")
    chips = weight_out.shape[0] // 2
    chip = tok_index // 2
    core = tok_index % 2
    peers = [lax.rem(me + d, n) for d in range(1, n)]
    barrier = pltpu.get_barrier_semaphore()
    for peer in peers:
        pl.semaphore_signal(barrier, inc=1, device_id=(tok_index, peer), device_id_type=MESH)
    ring_peers = [
        lax.rem(chip + 1, chips) * 2 + core,
        lax.rem(chip + chips - 1, chips) * 2 + core,
        chip * 2 + (1 - core),
    ]
    for peer in ring_peers:
        pl.semaphore_signal(barrier, inc=1, device_id=(peer, me), device_id_type=MESH)
    pl.semaphore_wait(barrier, len(peers) + len(ring_peers))

    def scatter_copy(peer, slot):
        return pltpu.make_async_remote_copy(
            src_ref=part_ref.at[peer], dst_ref=held.at[slot], send_sem=scatter_send.at[peer],
            recv_sem=scatter_recv.at[slot], device_id=(tok_index, peer), device_id_type=MESH,
        )

    def gather_copy(peer, slot):
        return pltpu.make_async_remote_copy(
            src_ref=mine, dst_ref=out_ref.at[slot], send_sem=gather_send.at[peer],
            recv_sem=gather_recv.at[slot], device_id=(tok_index, peer), device_id_type=MESH,
        )

    for peer in peers:
        scatter_copy(peer, me).start()

    def norm_and_send():
        total = part_ref[me].astype(jnp.float32)
        for peer in peers:
            scatter_copy(peer, peer).wait_recv()
            total = total + held[peer].astype(jnp.float32)
        summed = (resid_ref[...].astype(jnp.float32) + total).astype(jnp.bfloat16)
        resid_out[...] = summed
        as_float = summed.astype(jnp.float32)
        center = jnp.mean(as_float, axis=-1, keepdims=True)
        spread = jnp.mean(jnp.square(as_float - center), axis=-1, keepdims=True)
        normed = ((as_float - center) * lax.rsqrt(spread + epsilon) * gain_ref[...].astype(jnp.float32)[None, :]).astype(jnp.bfloat16)
        mine[...] = normed
        out_ref[me] = normed
        for peer in peers:
            gather_copy(peer, me).start()

    _ring_gather(weight_ref, weight_out, send_right, send_left, send_partner, weight_recv, me,
                 hook=norm_and_send, hook_step=3)
    block_rows = weight_out.shape[1]
    for slot in range(weight_out.shape[0]):
        weight_flat[slot * block_rows:(slot + 1) * block_rows, :] = weight_out[slot]
    for peer in peers:
        gather_copy(peer, peer).wait_recv()
    for peer in peers:
        scatter_copy(peer, me).wait_send()
        gather_copy(peer, me).wait_send()


def mix_ring_feat(parts, resid, gains, gain_row, weight_block, n, tok_count, collective_id):
    _, rows, width = parts.shape
    weight_rows, weight_width = weight_block.shape
    chips = tok_count // 2
    new_resid, gathered, weights = pl.pallas_call(
        functools.partial(_mix_ring_kernel, n, gain_row),
        out_shape=(
            jax.ShapeDtypeStruct((rows, width), jnp.bfloat16),
            jax.ShapeDtypeStruct((n, rows, width), jnp.bfloat16),
            jax.ShapeDtypeStruct((tok_count * weight_rows, weight_width), weight_block.dtype),
        ),
        in_specs=[pl.BlockSpec(memory_space=pltpu.VMEM)] * 4,
        out_specs=(pl.BlockSpec(memory_space=pltpu.VMEM),) * 3,
        scratch_shapes=[
            pltpu.VMEM((tok_count, weight_rows, weight_width), weight_block.dtype),
            pltpu.VMEM((n, rows, width), parts.dtype),
            pltpu.VMEM((rows, width), jnp.bfloat16),
            pltpu.SemaphoreType.DMA((n,)),
            pltpu.SemaphoreType.DMA((n,)),
            pltpu.SemaphoreType.DMA((n,)),
            pltpu.SemaphoreType.DMA((n,)),
            pltpu.SemaphoreType.DMA((chips,)),
            pltpu.SemaphoreType.DMA((chips,)),
            pltpu.SemaphoreType.DMA((chips,)),
            pltpu.SemaphoreType.DMA((tok_count,)),
        ],
        compiler_params=pltpu.CompilerParams(collective_id=collective_id, has_side_effects=True),
    )(parts, resid, gains, weight_block)
    return new_resid, gathered.reshape(n * rows, width), weights


def _norm_gather_kernel(n, gain_row, tok_ref, gain_ref, out_ref, mine, send_sem, recv_sem):
    me = lax.axis_index("feat")
    tok_index = lax.axis_index("tok")
    peers = [lax.rem(me + d, n) for d in range(1, n)]
    _greet(peers, tok_index)
    as_float = tok_ref[...].astype(jnp.float32)
    center = jnp.mean(as_float, axis=-1, keepdims=True)
    spread = jnp.mean(jnp.square(as_float - center), axis=-1, keepdims=True)
    normed = ((as_float - center) * lax.rsqrt(spread + epsilon) * gain_ref[...].astype(jnp.float32)[None, :]).astype(jnp.bfloat16)
    mine[...] = normed
    out_ref[me] = normed

    def copy(peer, slot):
        return pltpu.make_async_remote_copy(
            src_ref=mine, dst_ref=out_ref.at[slot], send_sem=send_sem.at[peer],
            recv_sem=recv_sem.at[slot], device_id=(tok_index, peer), device_id_type=MESH,
        )

    for peer in peers:
        copy(peer, me).start()
    for peer in peers:
        copy(peer, peer).wait_recv()
    for peer in peers:
        copy(peer, me).wait_send()


def norm_gather_feat(rows, gains, gain_row, n, collective_id):
    count, width = rows.shape
    return pl.pallas_call(
        functools.partial(_norm_gather_kernel, n, gain_row),
        out_shape=jax.ShapeDtypeStruct((n, count, width), jnp.bfloat16),
        in_specs=[pl.BlockSpec(memory_space=pltpu.VMEM)] * 2,
        out_specs=pl.BlockSpec(memory_space=pltpu.VMEM),
        scratch_shapes=[
            pltpu.VMEM((count, width), jnp.bfloat16),
            pltpu.SemaphoreType.DMA((n,)),
            pltpu.SemaphoreType.DMA((n,)),
        ],
        compiler_params=pltpu.CompilerParams(collective_id=collective_id, has_side_effects=True),
    )(rows, gains).reshape(n * count, width)


def _scatter_kernel(n, part_ref, out_ref, held, send_sem, recv_sem):
    me = lax.axis_index("feat")
    tok_index = lax.axis_index("tok")
    peers = [lax.rem(me + d, n) for d in range(1, n)]
    _greet(peers, tok_index)
    for peer in peers:
        pltpu.make_async_remote_copy(
            src_ref=part_ref.at[peer], dst_ref=held.at[me], send_sem=send_sem.at[peer],
            recv_sem=recv_sem.at[me], device_id=(tok_index, peer), device_id_type=MESH,
        ).start()
    total = part_ref[me].astype(jnp.float32)
    for peer in peers:
        pltpu.make_async_remote_copy(
            src_ref=part_ref.at[peer], dst_ref=held.at[peer], send_sem=send_sem.at[peer],
            recv_sem=recv_sem.at[peer], device_id=(tok_index, peer), device_id_type=MESH,
        ).wait_recv()
        total = total + held[peer].astype(jnp.float32)
    out_ref[...] = total
    for peer in peers:
        pltpu.make_async_remote_copy(
            src_ref=part_ref.at[peer], dst_ref=held.at[me], send_sem=send_sem.at[peer],
            recv_sem=recv_sem.at[me], device_id=(tok_index, peer), device_id_type=MESH,
        ).wait_send()


def scatter_feat(parts, n, collective_id):
    _, rows, width = parts.shape
    return pl.pallas_call(
        functools.partial(_scatter_kernel, n),
        out_shape=jax.ShapeDtypeStruct((rows, width), jnp.float32),
        in_specs=[pl.BlockSpec(memory_space=pltpu.VMEM)],
        out_specs=pl.BlockSpec(memory_space=pltpu.VMEM),
        scratch_shapes=[
            pltpu.VMEM((n, rows, width), parts.dtype),
            pltpu.SemaphoreType.DMA((n,)),
            pltpu.SemaphoreType.DMA((n,)),
        ],
        compiler_params=pltpu.CompilerParams(collective_id=collective_id, has_side_effects=True),
    )(parts)

MESH = pl.DeviceIdType.MESH
LEAST_UNITS = 4
MOST_UNITS = 16
HEAD_DIM = 88


epsilon = 1e-06


def layer_norm(row_block, gain_row):
    as_float = row_block.astype(jnp.float32)
    center = jnp.mean(as_float, axis=-1, keepdims=True)
    spread = jnp.mean(jnp.square(as_float - center), axis=-1, keepdims=True)
    scaled = (as_float - center) * lax.rsqrt(spread + epsilon) * gain_row.astype(jnp.float32)
    return scaled.astype(jnp.bfloat16)


def project_rows(row_block, weight_block, collective_id):
    n = lax.axis_size("feat")
    return jnp.dot(
        gather_feat(row_block, n, collective_id),
        weight_block,
        preferred_element_type=jnp.float32,
    )


def scatter_rows(left_rows, right_rows, collective_id):
    n = lax.axis_size("feat")
    parts = jnp.dot(left_rows, right_rows, preferred_element_type=jnp.float32).astype(jnp.bfloat16)
    return scatter_feat(parts.reshape(n, parts.shape[0] // n, parts.shape[1]), n, collective_id)


def early_weights(weight_up, weight_down):
    return (weight_up, weight_down)


def upper_weight(fetched):
    return lax.all_gather(fetched[0], "tok", axis=0, tiled=True)


def lower_weight(fetched):
    return lax.all_gather(fetched[1], "tok", axis=1, tiled=True)


def attend(projected, segment_ids, head_count):
    token_count = projected.shape[0]
    parts_all = projected.reshape(token_count, 3, head_count, HEAD_DIM)
    queries = (parts_all[:, 0] * HEAD_DIM ** (-0.5)).astype(jnp.bfloat16)
    keys_here = parts_all[:, 1].astype(jnp.bfloat16)
    values_here = parts_all[:, 2].astype(jnp.bfloat16)
    scores = jnp.einsum("qhd,khd->hqk", queries, keys_here, preferred_element_type=jnp.float32)
    same_segment = segment_ids[:, None] == segment_ids[None, :]
    scores = jnp.where(same_segment[None, :, :], scores, -1e30)
    highest = jnp.max(scores, axis=-1, keepdims=True)
    raised = jnp.exp(scores - highest)
    weights_soft = (raised / jnp.sum(raised, axis=-1, keepdims=True)).astype(jnp.bfloat16)
    attended = jnp.einsum(
        "hqk,khd->qhd", weights_soft, values_here, preferred_element_type=jnp.float32
    )
    return attended.astype(jnp.bfloat16).reshape(token_count, head_count * HEAD_DIM)


def route_rows(embedded, segment_ids, owners):
    merged_count = embedded.shape[0]
    peer_count = owners.shape[0]
    least_units = max(LEAST_UNITS, (merged_count + peer_count - 1) // peer_count)
    slot_count = max(MOST_UNITS, 2 * least_units)
    first_ids = segment_ids.reshape(merged_count, 4)[:, 0]
    id_base = lax.axis_index("tok") * peer_count
    local_index = first_ids - id_base
    owner_pick = local_index[:, None] == jnp.arange(peer_count, dtype=jnp.int32)[None, :]
    owner_of = jnp.sum(jnp.where(owner_pick, owners[None, :], 0), axis=1)
    row_index = jnp.arange(merged_count, dtype=jnp.int32)
    earlier = (row_index[None, :] < row_index[:, None]) & (first_ids[None, :] == first_ids[:, None])
    within = jnp.sum(earlier.astype(jnp.int32), axis=1)
    target = owner_of * slot_count + within
    select = (
        jnp.arange(peer_count * slot_count, dtype=jnp.int32)[:, None] == target[None, :]
    ).astype(jnp.bfloat16)
    packed = jnp.dot(select, embedded, preferred_element_type=jnp.float32).astype(jnp.bfloat16)
    packed = packed.reshape(peer_count, slot_count, embedded.shape[1])
    received = route_exchange(packed, 5)
    return received.reshape(peer_count * slot_count, embedded.shape[1])


def body(
    tokens,
    segment_ids,
    owners,
    project_in,
    project_out,
    weight_up,
    weight_down,
    weight_merge,
    gain_attend,
    gain_hidden,
    gain_final,
):
    model_width = tokens.shape[1]
    head_count = project_in.shape[2] // HEAD_DIM
    units = weight_up.shape[1]
    feat_count = lax.axis_size("feat")
    tok_count = lax.axis_size("tok")
    flat_in = project_in.reshape(model_width, 3 * project_in.shape[2])
    local_count = tokens.shape[0]
    stacked = jnp.concatenate([weight_up, weight_down.T], axis=1)
    gathered = norm_gather_feat(tokens, gain_attend, 0, feat_count, 0)
    projected = jnp.dot(gathered, flat_in, preferred_element_type=jnp.float32)
    attended = attend(projected, segment_ids, head_count)
    attn_parts = jnp.dot(attended, project_out, preferred_element_type=jnp.float32).astype(jnp.bfloat16)
    second, hidden_rows, weights = mix_ring_feat(
        attn_parts.reshape(feat_count, local_count, model_width), tokens, gain_hidden, 1, stacked,
        feat_count, tok_count, 1,
    )
    both = weights
    upper = both[:, :units]
    lower_t = both[:, units:]
    hidden = jax.nn.gelu(
        jnp.dot(hidden_rows, upper, preferred_element_type=jnp.float32), approximate=False
    ).astype(jnp.bfloat16)
    down_parts = lax.dot_general(
        hidden, lower_t, (((1,), (1,)), ((), ())), preferred_element_type=jnp.float32
    ).astype(jnp.bfloat16)
    _, merged = mix_feat(
        down_parts.reshape(feat_count, local_count, model_width), second, gain_final, 2, feat_count, 3
    )
    embedded = jnp.dot(merged, weight_merge, preferred_element_type=jnp.float32).astype(jnp.bfloat16)
    return route_rows(embedded, segment_ids, owners)


def solution(mesh):
    return jax.shard_map(
        body,
        mesh=mesh,
        in_specs=(
            P(("tok", "feat"), None),
            P("tok"),
            P("tok"),
            P(None, None, "feat"),
            P("feat", None),
            P("tok", "feat"),
            P("feat", "tok"),
            P(None, "feat"),
            P(),
            P(),
            P(),
        ),
        out_specs=P("tok", "feat"),
        check_vma=False,
    )
```

```python
import functools
import jax
import jax.numpy as jnp
from jax import lax
from jax.experimental import pallas as pl
from jax.experimental.pallas import tpu as pltpu
from jax.sharding import PartitionSpec as P


def _greet(peers, tok_index):
    barrier = pltpu.get_barrier_semaphore()
    for peer in peers:
        pl.semaphore_signal(barrier, inc=1, device_id=(tok_index, peer), device_id_type=MESH)
    pl.semaphore_wait(barrier, len(peers))


def _gather_kernel(n, row_ref, out_ref, send_sem, recv_sem):
    me = lax.axis_index("feat")
    tok_index = lax.axis_index("tok")
    peers = [lax.rem(me + d, n) for d in range(1, n)]
    _greet(peers, tok_index)
    for peer in peers:
        pltpu.make_async_remote_copy(
            src_ref=row_ref, dst_ref=out_ref.at[me], send_sem=send_sem.at[peer],
            recv_sem=recv_sem.at[me], device_id=(tok_index, peer), device_id_type=MESH,
        ).start()
    out_ref[me] = row_ref[...]
    for peer in peers:
        pltpu.make_async_remote_copy(
            src_ref=row_ref, dst_ref=out_ref.at[peer], send_sem=send_sem.at[peer],
            recv_sem=recv_sem.at[peer], device_id=(tok_index, peer), device_id_type=MESH,
        ).wait_recv()
    for peer in peers:
        pltpu.make_async_remote_copy(
            src_ref=row_ref, dst_ref=out_ref.at[me], send_sem=send_sem.at[peer],
            recv_sem=recv_sem.at[me], device_id=(tok_index, peer), device_id_type=MESH,
        ).wait_send()


def gather_feat(row_block, n, collective_id):
    rows, width = row_block.shape
    return pl.pallas_call(
        functools.partial(_gather_kernel, n),
        out_shape=jax.ShapeDtypeStruct((n, rows, width), row_block.dtype),
        in_specs=[pl.BlockSpec(memory_space=pltpu.VMEM)],
        out_specs=pl.BlockSpec(memory_space=pltpu.VMEM),
        scratch_shapes=[pltpu.SemaphoreType.DMA((n,)), pltpu.SemaphoreType.DMA((n,))],
        compiler_params=pltpu.CompilerParams(collective_id=collective_id, has_side_effects=True),
    )(row_block).reshape(n * rows, width)


def _ring_gather(x_ref, out_ref, send_right, send_left, send_partner, recv_sem, feat_index, after_first=None,
                 hook=None, hook_step=1):
    tok_count = out_ref.shape[0]
    chips = tok_count // 2
    right_steps = chips // 2
    left_steps = chips - 1 - right_steps
    me = lax.axis_index("tok")
    chip = me // 2
    core = me % 2
    right = lax.rem(chip + 1, chips) * 2 + core
    left = lax.rem(chip + chips - 1, chips) * 2 + core
    partner = chip * 2 + (1 - core)

    def slot_of(offset):
        return lax.rem(chip + offset + 2 * chips, chips) * 2 + core

    def remote(src, slot, sem, target):
        return pltpu.make_async_remote_copy(
            src_ref=src, dst_ref=out_ref.at[slot], send_sem=sem, recv_sem=recv_sem.at[slot],
            device_id=(target, feat_index), device_id_type=MESH,
        )

    sends = []

    def forward_partner(src, slot):
        copy = remote(src, slot, send_partner.at[len(sends_partner)], partner)
        copy.start()
        sends_partner.append(copy)

    sends_partner = []
    out_ref[me] = x_ref[...]
    arrived = []
    for step in range(1, right_steps + 1):
        if step == 1:
            src_right = x_ref
            src_left = x_ref
        else:
            from_left = slot_of(-(step - 1))
            remote(x_ref, from_left, send_right.at[0], right).wait_recv()
            src_right = out_ref.at[from_left]
            arrived.append(from_left)
        copy = remote(src_right, slot_of(-(step - 1)), send_right.at[step - 1], right)
        copy.start()
        sends.append(copy)
        if step > 1 and step - 1 <= left_steps:
            from_right = slot_of(step - 1)
            remote(x_ref, from_right, send_left.at[0], left).wait_recv()
            src_left = out_ref.at[from_right]
            arrived.append(from_right)
        if step <= left_steps:
            copy = remote(src_left, slot_of(step - 1), send_left.at[step - 1], left)
            copy.start()
            sends.append(copy)
        if step == 1:
            if after_first is not None:
                after_first()
            forward_partner(x_ref, me)
        for slot in arrived:
            forward_partner(out_ref.at[slot], slot)
        arrived = []
        if hook is not None and step == min(hook_step, right_steps):
            hook()
    last_left = slot_of(-right_steps)
    remote(x_ref, last_left, send_right.at[0], right).wait_recv()
    forward_partner(out_ref.at[last_left], last_left)
    if left_steps >= 1 and left_steps + 1 > right_steps:
        last_right = slot_of(left_steps)
        remote(x_ref, last_right, send_left.at[0], left).wait_recv()
        forward_partner(out_ref.at[last_right], last_right)
    for other_chip in range(chips):
        remote(x_ref, other_chip * 2 + (1 - core), send_partner.at[0], partner).wait_recv()
    for copy in sends + sends_partner:
        copy.wait_send()


def _first_kernel(n, row_ref, weight_ref, out_ref, weight_out, send_sem, recv_sem,
                  send_right, send_left, send_partner, weight_recv):
    me = lax.axis_index("feat")
    tok_index = lax.axis_index("tok")
    chips = weight_out.shape[0] // 2
    chip = tok_index // 2
    core = tok_index % 2
    peers = [lax.rem(me + d, n) for d in range(1, n)]
    barrier = pltpu.get_barrier_semaphore()
    for peer in peers:
        pl.semaphore_signal(barrier, inc=1, device_id=(tok_index, peer), device_id_type=MESH)
    ring_peers = [
        lax.rem(chip + 1, chips) * 2 + core,
        lax.rem(chip + chips - 1, chips) * 2 + core,
        chip * 2 + (1 - core),
    ]
    for peer in ring_peers:
        pl.semaphore_signal(barrier, inc=1, device_id=(peer, me), device_id_type=MESH)
    pl.semaphore_wait(barrier, len(peers) + len(ring_peers))

    def start_rows():
        for peer in peers:
            pltpu.make_async_remote_copy(
                src_ref=row_ref, dst_ref=out_ref.at[me], send_sem=send_sem.at[peer],
                recv_sem=recv_sem.at[me], device_id=(tok_index, peer), device_id_type=MESH,
            ).start()

    _ring_gather(weight_ref, weight_out, send_right, send_left, send_partner, weight_recv, me, start_rows)
    out_ref[me] = row_ref[...]
    for peer in peers:
        pltpu.make_async_remote_copy(
            src_ref=row_ref, dst_ref=out_ref.at[peer], send_sem=send_sem.at[peer],
            recv_sem=recv_sem.at[peer], device_id=(tok_index, peer), device_id_type=MESH,
        ).wait_recv()
    for peer in peers:
        pltpu.make_async_remote_copy(
            src_ref=row_ref, dst_ref=out_ref.at[me], send_sem=send_sem.at[peer],
            recv_sem=recv_sem.at[me], device_id=(tok_index, peer), device_id_type=MESH,
        ).wait_send()


def first_exchange(row_block, weight_block, n, tok_count, collective_id):
    rows, width = row_block.shape
    weight_rows, weight_width = weight_block.shape
    chips = tok_count // 2
    gathered, weights = pl.pallas_call(
        functools.partial(_first_kernel, n),
        out_shape=(
            jax.ShapeDtypeStruct((n, rows, width), row_block.dtype),
            jax.ShapeDtypeStruct((tok_count, weight_rows, weight_width), weight_block.dtype),
        ),
        in_specs=[pl.BlockSpec(memory_space=pltpu.VMEM)] * 2,
        out_specs=(pl.BlockSpec(memory_space=pltpu.VMEM),) * 2,
        scratch_shapes=[
            pltpu.SemaphoreType.DMA((n,)),
            pltpu.SemaphoreType.DMA((n,)),
            pltpu.SemaphoreType.DMA((chips,)),
            pltpu.SemaphoreType.DMA((chips,)),
            pltpu.SemaphoreType.DMA((chips,)),
            pltpu.SemaphoreType.DMA((tok_count,)),
        ],
        compiler_params=pltpu.CompilerParams(collective_id=collective_id, has_side_effects=True),
    )(row_block, weight_block)
    return gathered.reshape(n * rows, width), weights


def _route_kernel(n, packed_ref, out_ref, send_sem, recv_sem):
    me = lax.axis_index("tok")
    feat_index = lax.axis_index("feat")
    peers = [lax.rem(me + d, n) for d in range(1, n)]
    barrier = pltpu.get_barrier_semaphore()
    for peer in peers:
        pl.semaphore_signal(barrier, inc=1, device_id=(peer, feat_index), device_id_type=MESH)
    pl.semaphore_wait(barrier, len(peers))
    for peer in peers:
        pltpu.make_async_remote_copy(
            src_ref=packed_ref.at[peer], dst_ref=out_ref.at[me], send_sem=send_sem.at[peer],
            recv_sem=recv_sem.at[me], device_id=(peer, feat_index), device_id_type=MESH,
        ).start()
    out_ref[me] = packed_ref[me]
    for peer in peers:
        pltpu.make_async_remote_copy(
            src_ref=packed_ref.at[peer], dst_ref=out_ref.at[peer], send_sem=send_sem.at[peer],
            recv_sem=recv_sem.at[peer], device_id=(peer, feat_index), device_id_type=MESH,
        ).wait_recv()
    for peer in peers:
        pltpu.make_async_remote_copy(
            src_ref=packed_ref.at[peer], dst_ref=out_ref.at[me], send_sem=send_sem.at[peer],
            recv_sem=recv_sem.at[me], device_id=(peer, feat_index), device_id_type=MESH,
        ).wait_send()


def route_exchange(packed, collective_id):
    n = packed.shape[0]
    return pl.pallas_call(
        functools.partial(_route_kernel, n),
        out_shape=jax.ShapeDtypeStruct(packed.shape, packed.dtype),
        in_specs=[pl.BlockSpec(memory_space=pltpu.VMEM)],
        out_specs=pl.BlockSpec(memory_space=pltpu.VMEM),
        scratch_shapes=[pltpu.SemaphoreType.DMA((n,)), pltpu.SemaphoreType.DMA((n,))],
        compiler_params=pltpu.CompilerParams(collective_id=collective_id, has_side_effects=True),
    )(packed)


def _mix_kernel(n, gain_row, part_ref, resid_ref, gain_ref, resid_out, out_ref, merged_out, held, mine_a,
                mine_b, scatter_send, scatter_recv, gather_send, gather_recv):
    me = lax.axis_index("feat")
    tok_index = lax.axis_index("tok")
    peers = [lax.rem(me + d, n) for d in range(1, n)]
    _greet(peers, tok_index)
    split = 16
    halves = [(0, split), (split, part_ref.shape[1] - split)]
    mines = [mine_a, mine_b]

    def scatter_copy(half, peer, slot):
        first, size = halves[half]
        return pltpu.make_async_remote_copy(
            src_ref=part_ref.at[peer, pl.ds(first, size)], dst_ref=held.at[slot, pl.ds(first, size)],
            send_sem=scatter_send.at[half, peer], recv_sem=scatter_recv.at[half, slot],
            device_id=(tok_index, peer), device_id_type=MESH,
        )

    def gather_copy(half, peer, slot):
        first, size = halves[half]
        return pltpu.make_async_remote_copy(
            src_ref=mines[half], dst_ref=out_ref.at[slot, pl.ds(first, size)],
            send_sem=gather_send.at[half, peer], recv_sem=gather_recv.at[half, slot],
            device_id=(tok_index, peer), device_id_type=MESH,
        )

    for half in range(2):
        for peer in peers:
            scatter_copy(half, peer, me).start()
    for half in range(2):
        first, size = halves[half]
        total = part_ref[me, first:first + size, :].astype(jnp.float32)
        for peer in peers:
            scatter_copy(half, peer, peer).wait_recv()
            total = total + held[peer, first:first + size, :].astype(jnp.float32)
        summed = (resid_ref[first:first + size, :].astype(jnp.float32) + total).astype(jnp.bfloat16)
        resid_out[first:first + size, :] = summed
        as_float = summed.astype(jnp.float32)
        center = jnp.mean(as_float, axis=-1, keepdims=True)
        spread = jnp.mean(jnp.square(as_float - center), axis=-1, keepdims=True)
        normed = ((as_float - center) * lax.rsqrt(spread + epsilon) * gain_ref[...].astype(jnp.float32)[None, :]).astype(jnp.bfloat16)
        mines[half][...] = normed
        out_ref[me, first:first + size, :] = normed
        for peer in peers:
            gather_copy(half, peer, me).start()
    for half in range(2):
        for peer in peers:
            gather_copy(half, peer, peer).wait_recv()
    group = 4
    width = out_ref.shape[2]
    row_count = n * out_ref.shape[1]
    rows = out_ref[...].astype(jnp.float32).reshape(row_count, width).astype(jnp.bfloat16)
    merged_index = lax.broadcasted_iota(jnp.int32, (row_count // group, row_count), 0)
    row_index = lax.broadcasted_iota(jnp.int32, (row_count // group, row_count), 1)
    for part in range(group):
        pick = (row_index == merged_index * group + part).astype(jnp.bfloat16)
        merged_out[:, part * width:(part + 1) * width] = jnp.dot(
            pick, rows, preferred_element_type=jnp.float32
        ).astype(jnp.bfloat16)
    for half in range(2):
        for peer in peers:
            scatter_copy(half, peer, me).wait_send()
            gather_copy(half, peer, me).wait_send()


def mix_feat(parts, resid, gains, gain_row, n, collective_id):
    _, rows, width = parts.shape
    new_resid, _, merged = pl.pallas_call(
        functools.partial(_mix_kernel, n, gain_row),
        out_shape=(
            jax.ShapeDtypeStruct((rows, width), jnp.bfloat16),
            jax.ShapeDtypeStruct((n, rows, width), jnp.bfloat16),
            jax.ShapeDtypeStruct((n * rows // 4, 4 * width), jnp.bfloat16),
        ),
        in_specs=[pl.BlockSpec(memory_space=pltpu.VMEM)] * 3,
        out_specs=(pl.BlockSpec(memory_space=pltpu.VMEM),) * 3,
        scratch_shapes=[
            pltpu.VMEM((n, rows, width), parts.dtype),
            pltpu.VMEM((16, width), jnp.bfloat16),
            pltpu.VMEM((rows - 16, width), jnp.bfloat16),
            pltpu.SemaphoreType.DMA((2, n)),
            pltpu.SemaphoreType.DMA((2, n)),
            pltpu.SemaphoreType.DMA((2, n)),
            pltpu.SemaphoreType.DMA((2, n)),
        ],
        compiler_params=pltpu.CompilerParams(collective_id=collective_id, has_side_effects=True),
    )(parts, resid, gains)
    return new_resid, merged


def _mix_ring_kernel(n, gain_row, part_ref, resid_ref, gain_ref, weight_ref, resid_out, out_ref, weight_flat,
                     weight_out, held, mine_a, mine_b, scatter_send, scatter_recv, gather_send, gather_recv,
                     send_right, send_left, send_partner, weight_recv):
    me = lax.axis_index("feat")
    tok_index = lax.axis_index("tok")
    chips = weight_out.shape[0] // 2
    chip = tok_index // 2
    core = tok_index % 2
    peers = [lax.rem(me + d, n) for d in range(1, n)]
    barrier = pltpu.get_barrier_semaphore()
    for peer in peers:
        pl.semaphore_signal(barrier, inc=1, device_id=(tok_index, peer), device_id_type=MESH)
    ring_peers = [
        lax.rem(chip + 1, chips) * 2 + core,
        lax.rem(chip + chips - 1, chips) * 2 + core,
        chip * 2 + (1 - core),
    ]
    for peer in ring_peers:
        pl.semaphore_signal(barrier, inc=1, device_id=(peer, me), device_id_type=MESH)
    pl.semaphore_wait(barrier, len(peers) + len(ring_peers))

    split = 16
    halves = [(0, split), (split, part_ref.shape[1] - split)]
    mines = [mine_a, mine_b]

    def scatter_copy(half, peer, slot):
        first, size = halves[half]
        return pltpu.make_async_remote_copy(
            src_ref=part_ref.at[peer, pl.ds(first, size)], dst_ref=held.at[slot, pl.ds(first, size)],
            send_sem=scatter_send.at[half, peer], recv_sem=scatter_recv.at[half, slot],
            device_id=(tok_index, peer), device_id_type=MESH,
        )

    def gather_copy(half, peer, slot):
        first, size = halves[half]
        return pltpu.make_async_remote_copy(
            src_ref=mines[half], dst_ref=out_ref.at[slot, pl.ds(first, size)],
            send_sem=gather_send.at[half, peer], recv_sem=gather_recv.at[half, slot],
            device_id=(tok_index, peer), device_id_type=MESH,
        )

    for half in range(2):
        for peer in peers:
            scatter_copy(half, peer, me).start()

    def norm_and_send():
        for half in range(2):
            first, size = halves[half]
            total = part_ref[me, first:first + size, :].astype(jnp.float32)
            for peer in peers:
                scatter_copy(half, peer, peer).wait_recv()
                total = total + held[peer, first:first + size, :].astype(jnp.float32)
            summed = (resid_ref[first:first + size, :].astype(jnp.float32) + total).astype(jnp.bfloat16)
            resid_out[first:first + size, :] = summed
            as_float = summed.astype(jnp.float32)
            center = jnp.mean(as_float, axis=-1, keepdims=True)
            spread = jnp.mean(jnp.square(as_float - center), axis=-1, keepdims=True)
            normed = ((as_float - center) * lax.rsqrt(spread + epsilon) * gain_ref[...].astype(jnp.float32)[None, :]).astype(jnp.bfloat16)
            mines[half][...] = normed
            out_ref[me, first:first + size, :] = normed
            for peer in peers:
                gather_copy(half, peer, me).start()

    _ring_gather(weight_ref, weight_out, send_right, send_left, send_partner, weight_recv, me,
                 hook=norm_and_send, hook_step=3)
    block_rows = weight_out.shape[1]
    for slot in range(weight_out.shape[0]):
        weight_flat[slot * block_rows:(slot + 1) * block_rows, :] = weight_out[slot]
    for half in range(2):
        for peer in peers:
            gather_copy(half, peer, peer).wait_recv()
    for half in range(2):
        for peer in peers:
            scatter_copy(half, peer, me).wait_send()
            gather_copy(half, peer, me).wait_send()


def mix_ring_feat(parts, resid, gains, gain_row, weight_block, n, tok_count, collective_id):
    _, rows, width = parts.shape
    weight_rows, weight_width = weight_block.shape
    chips = tok_count // 2
    new_resid, gathered, weights = pl.pallas_call(
        functools.partial(_mix_ring_kernel, n, gain_row),
        out_shape=(
            jax.ShapeDtypeStruct((rows, width), jnp.bfloat16),
            jax.ShapeDtypeStruct((n, rows, width), jnp.bfloat16),
            jax.ShapeDtypeStruct((tok_count * weight_rows, weight_width), weight_block.dtype),
        ),
        in_specs=[pl.BlockSpec(memory_space=pltpu.VMEM)] * 4,
        out_specs=(pl.BlockSpec(memory_space=pltpu.VMEM),) * 3,
        scratch_shapes=[
            pltpu.VMEM((tok_count, weight_rows, weight_width), weight_block.dtype),
            pltpu.VMEM((n, rows, width), parts.dtype),
            pltpu.VMEM((16, width), jnp.bfloat16),
            pltpu.VMEM((rows - 16, width), jnp.bfloat16),
            pltpu.SemaphoreType.DMA((2, n)),
            pltpu.SemaphoreType.DMA((2, n)),
            pltpu.SemaphoreType.DMA((2, n)),
            pltpu.SemaphoreType.DMA((2, n)),
            pltpu.SemaphoreType.DMA((chips,)),
            pltpu.SemaphoreType.DMA((chips,)),
            pltpu.SemaphoreType.DMA((chips,)),
            pltpu.SemaphoreType.DMA((tok_count,)),
        ],
        compiler_params=pltpu.CompilerParams(collective_id=collective_id, has_side_effects=True),
    )(parts, resid, gains, weight_block)
    return new_resid, gathered.reshape(n * rows, width), weights


def _norm_gather_kernel(n, gain_row, tok_ref, gain_ref, out_ref, mine, send_sem, recv_sem):
    me = lax.axis_index("feat")
    tok_index = lax.axis_index("tok")
    peers = [lax.rem(me + d, n) for d in range(1, n)]
    _greet(peers, tok_index)
    as_float = tok_ref[...].astype(jnp.float32)
    center = jnp.mean(as_float, axis=-1, keepdims=True)
    spread = jnp.mean(jnp.square(as_float - center), axis=-1, keepdims=True)
    normed = ((as_float - center) * lax.rsqrt(spread + epsilon) * gain_ref[...].astype(jnp.float32)[None, :]).astype(jnp.bfloat16)
    mine[...] = normed
    out_ref[me] = normed

    def copy(peer, slot):
        return pltpu.make_async_remote_copy(
            src_ref=mine, dst_ref=out_ref.at[slot], send_sem=send_sem.at[peer],
            recv_sem=recv_sem.at[slot], device_id=(tok_index, peer), device_id_type=MESH,
        )

    for peer in peers:
        copy(peer, me).start()
    for peer in peers:
        copy(peer, peer).wait_recv()
    for peer in peers:
        copy(peer, me).wait_send()


def norm_gather_feat(rows, gains, gain_row, n, collective_id):
    count, width = rows.shape
    return pl.pallas_call(
        functools.partial(_norm_gather_kernel, n, gain_row),
        out_shape=jax.ShapeDtypeStruct((n, count, width), jnp.bfloat16),
        in_specs=[pl.BlockSpec(memory_space=pltpu.VMEM)] * 2,
        out_specs=pl.BlockSpec(memory_space=pltpu.VMEM),
        scratch_shapes=[
            pltpu.VMEM((count, width), jnp.bfloat16),
            pltpu.SemaphoreType.DMA((n,)),
            pltpu.SemaphoreType.DMA((n,)),
        ],
        compiler_params=pltpu.CompilerParams(collective_id=collective_id, has_side_effects=True),
    )(rows, gains).reshape(n * count, width)


def _scatter_kernel(n, part_ref, out_ref, held, send_sem, recv_sem):
    me = lax.axis_index("feat")
    tok_index = lax.axis_index("tok")
    peers = [lax.rem(me + d, n) for d in range(1, n)]
    _greet(peers, tok_index)
    for peer in peers:
        pltpu.make_async_remote_copy(
            src_ref=part_ref.at[peer], dst_ref=held.at[me], send_sem=send_sem.at[peer],
            recv_sem=recv_sem.at[me], device_id=(tok_index, peer), device_id_type=MESH,
        ).start()
    total = part_ref[me].astype(jnp.float32)
    for peer in peers:
        pltpu.make_async_remote_copy(
            src_ref=part_ref.at[peer], dst_ref=held.at[peer], send_sem=send_sem.at[peer],
            recv_sem=recv_sem.at[peer], device_id=(tok_index, peer), device_id_type=MESH,
        ).wait_recv()
        total = total + held[peer].astype(jnp.float32)
    out_ref[...] = total
    for peer in peers:
        pltpu.make_async_remote_copy(
            src_ref=part_ref.at[peer], dst_ref=held.at[me], send_sem=send_sem.at[peer],
            recv_sem=recv_sem.at[me], device_id=(tok_index, peer), device_id_type=MESH,
        ).wait_send()


def scatter_feat(parts, n, collective_id):
    _, rows, width = parts.shape
    return pl.pallas_call(
        functools.partial(_scatter_kernel, n),
        out_shape=jax.ShapeDtypeStruct((rows, width), jnp.float32),
        in_specs=[pl.BlockSpec(memory_space=pltpu.VMEM)],
        out_specs=pl.BlockSpec(memory_space=pltpu.VMEM),
        scratch_shapes=[
            pltpu.VMEM((n, rows, width), parts.dtype),
            pltpu.SemaphoreType.DMA((n,)),
            pltpu.SemaphoreType.DMA((n,)),
        ],
        compiler_params=pltpu.CompilerParams(collective_id=collective_id, has_side_effects=True),
    )(parts)

MESH = pl.DeviceIdType.MESH
LEAST_UNITS = 4
MOST_UNITS = 16
HEAD_DIM = 88


epsilon = 1e-06


def layer_norm(row_block, gain_row):
    as_float = row_block.astype(jnp.float32)
    center = jnp.mean(as_float, axis=-1, keepdims=True)
    spread = jnp.mean(jnp.square(as_float - center), axis=-1, keepdims=True)
    scaled = (as_float - center) * lax.rsqrt(spread + epsilon) * gain_row.astype(jnp.float32)
    return scaled.astype(jnp.bfloat16)


def project_rows(row_block, weight_block, collective_id):
    n = lax.axis_size("feat")
    return jnp.dot(
        gather_feat(row_block, n, collective_id),
        weight_block,
        preferred_element_type=jnp.float32,
    )


def scatter_rows(left_rows, right_rows, collective_id):
    n = lax.axis_size("feat")
    parts = jnp.dot(left_rows, right_rows, preferred_element_type=jnp.float32).astype(jnp.bfloat16)
    return scatter_feat(parts.reshape(n, parts.shape[0] // n, parts.shape[1]), n, collective_id)


def early_weights(weight_up, weight_down):
    return (weight_up, weight_down)


def upper_weight(fetched):
    return lax.all_gather(fetched[0], "tok", axis=0, tiled=True)


def lower_weight(fetched):
    return lax.all_gather(fetched[1], "tok", axis=1, tiled=True)


def attend(projected, segment_ids, head_count):
    token_count = projected.shape[0]
    parts_all = projected.reshape(token_count, 3, head_count, HEAD_DIM)
    queries = (parts_all[:, 0] * HEAD_DIM ** (-0.5)).astype(jnp.bfloat16)
    keys_here = parts_all[:, 1].astype(jnp.bfloat16)
    values_here = parts_all[:, 2].astype(jnp.bfloat16)
    scores = jnp.einsum("qhd,khd->hqk", queries, keys_here, preferred_element_type=jnp.float32)
    same_segment = segment_ids[:, None] == segment_ids[None, :]
    scores = jnp.where(same_segment[None, :, :], scores, -1e30)
    highest = jnp.max(scores, axis=-1, keepdims=True)
    raised = jnp.exp(scores - highest)
    weights_soft = (raised / jnp.sum(raised, axis=-1, keepdims=True)).astype(jnp.bfloat16)
    attended = jnp.einsum(
        "hqk,khd->qhd", weights_soft, values_here, preferred_element_type=jnp.float32
    )
    return attended.astype(jnp.bfloat16).reshape(token_count, head_count * HEAD_DIM)


def route_rows(embedded, segment_ids, owners):
    merged_count = embedded.shape[0]
    peer_count = owners.shape[0]
    least_units = max(LEAST_UNITS, (merged_count + peer_count - 1) // peer_count)
    slot_count = max(MOST_UNITS, 2 * least_units)
    first_ids = segment_ids.reshape(merged_count, 4)[:, 0]
    id_base = lax.axis_index("tok") * peer_count
    local_index = first_ids - id_base
    owner_pick = local_index[:, None] == jnp.arange(peer_count, dtype=jnp.int32)[None, :]
    owner_of = jnp.sum(jnp.where(owner_pick, owners[None, :], 0), axis=1)
    row_index = jnp.arange(merged_count, dtype=jnp.int32)
    earlier = (row_index[None, :] < row_index[:, None]) & (first_ids[None, :] == first_ids[:, None])
    within = jnp.sum(earlier.astype(jnp.int32), axis=1)
    target = owner_of * slot_count + within
    select = (
        jnp.arange(peer_count * slot_count, dtype=jnp.int32)[:, None] == target[None, :]
    ).astype(jnp.bfloat16)
    packed = jnp.dot(select, embedded, preferred_element_type=jnp.float32).astype(jnp.bfloat16)
    packed = packed.reshape(peer_count, slot_count, embedded.shape[1])
    received = route_exchange(packed, 5)
    return received.reshape(peer_count * slot_count, embedded.shape[1])


def body(
    tokens,
    segment_ids,
    owners,
    project_in,
    project_out,
    weight_up,
    weight_down,
    weight_merge,
    gain_attend,
    gain_hidden,
    gain_final,
):
    model_width = tokens.shape[1]
    head_count = project_in.shape[2] // HEAD_DIM
    units = weight_up.shape[1]
    feat_count = lax.axis_size("feat")
    tok_count = lax.axis_size("tok")
    flat_in = project_in.reshape(model_width, 3 * project_in.shape[2])
    local_count = tokens.shape[0]
    stacked = jnp.concatenate([weight_up, weight_down.T], axis=1)
    gathered = norm_gather_feat(tokens, gain_attend, 0, feat_count, 0)
    projected = jnp.dot(gathered, flat_in, preferred_element_type=jnp.float32)
    attended = attend(projected, segment_ids, head_count)
    attn_parts = jnp.dot(attended, project_out, preferred_element_type=jnp.float32).astype(jnp.bfloat16)
    second, hidden_rows, weights = mix_ring_feat(
        attn_parts.reshape(feat_count, local_count, model_width), tokens, gain_hidden, 1, stacked,
        feat_count, tok_count, 1,
    )
    both = weights
    upper = both[:, :units]
    lower_t = both[:, units:]
    hidden = jax.nn.gelu(
        jnp.dot(hidden_rows, upper, preferred_element_type=jnp.float32), approximate=False
    ).astype(jnp.bfloat16)
    down_parts = lax.dot_general(
        hidden, lower_t, (((1,), (1,)), ((), ())), preferred_element_type=jnp.float32
    ).astype(jnp.bfloat16)
    _, merged = mix_feat(
        down_parts.reshape(feat_count, local_count, model_width), second, gain_final, 2, feat_count, 3
    )
    embedded = jnp.dot(merged, weight_merge, preferred_element_type=jnp.float32).astype(jnp.bfloat16)
    return route_rows(embedded, segment_ids, owners)


def solution(mesh):
    return jax.shard_map(
        body,
        mesh=mesh,
        in_specs=(
            P(("tok", "feat"), None),
            P("tok"),
            P("tok"),
            P(None, None, "feat"),
            P("feat", None),
            P("tok", "feat"),
            P("feat", "tok"),
            P(None, "feat"),
            P(),
            P(),
            P(),
        ),
        out_specs=P("tok", "feat"),
        check_vma=False,
    )
```

```python
import functools
import jax
import jax.numpy as jnp
from jax import lax
from jax.experimental import pallas as pl
from jax.experimental.pallas import tpu as pltpu
from jax.sharding import PartitionSpec as P


def _greet(peers, tok_index):
    barrier = pltpu.get_barrier_semaphore()
    for peer in peers:
        pl.semaphore_signal(barrier, inc=1, device_id=(tok_index, peer), device_id_type=MESH)
    pl.semaphore_wait(barrier, len(peers))


def _gather_kernel(n, row_ref, out_ref, send_sem, recv_sem):
    me = lax.axis_index("feat")
    tok_index = lax.axis_index("tok")
    peers = [lax.rem(me + d, n) for d in range(1, n)]
    _greet(peers, tok_index)
    for peer in peers:
        pltpu.make_async_remote_copy(
            src_ref=row_ref, dst_ref=out_ref.at[me], send_sem=send_sem.at[peer],
            recv_sem=recv_sem.at[me], device_id=(tok_index, peer), device_id_type=MESH,
        ).start()
    out_ref[me] = row_ref[...]
    for peer in peers:
        pltpu.make_async_remote_copy(
            src_ref=row_ref, dst_ref=out_ref.at[peer], send_sem=send_sem.at[peer],
            recv_sem=recv_sem.at[peer], device_id=(tok_index, peer), device_id_type=MESH,
        ).wait_recv()
    for peer in peers:
        pltpu.make_async_remote_copy(
            src_ref=row_ref, dst_ref=out_ref.at[me], send_sem=send_sem.at[peer],
            recv_sem=recv_sem.at[me], device_id=(tok_index, peer), device_id_type=MESH,
        ).wait_send()


def gather_feat(row_block, n, collective_id):
    rows, width = row_block.shape
    return pl.pallas_call(
        functools.partial(_gather_kernel, n),
        out_shape=jax.ShapeDtypeStruct((n, rows, width), row_block.dtype),
        in_specs=[pl.BlockSpec(memory_space=pltpu.VMEM)],
        out_specs=pl.BlockSpec(memory_space=pltpu.VMEM),
        scratch_shapes=[pltpu.SemaphoreType.DMA((n,)), pltpu.SemaphoreType.DMA((n,))],
        compiler_params=pltpu.CompilerParams(collective_id=collective_id, has_side_effects=True),
    )(row_block).reshape(n * rows, width)


def _ring_gather(x_ref, out_ref, send_right, send_left, send_partner, recv_sem, feat_index, after_first=None,
                 hook=None, hook_step=1):
    tok_count = out_ref.shape[0]
    chips = tok_count // 2
    right_steps = chips // 2
    left_steps = chips - 1 - right_steps
    me = lax.axis_index("tok")
    chip = me // 2
    core = me % 2
    right = lax.rem(chip + 1, chips) * 2 + core
    left = lax.rem(chip + chips - 1, chips) * 2 + core
    partner = chip * 2 + (1 - core)

    def slot_of(offset):
        return lax.rem(chip + offset + 2 * chips, chips) * 2 + core

    def remote(src, slot, sem, target):
        return pltpu.make_async_remote_copy(
            src_ref=src, dst_ref=out_ref.at[slot], send_sem=sem, recv_sem=recv_sem.at[slot],
            device_id=(target, feat_index), device_id_type=MESH,
        )

    sends = []

    def forward_partner(src, slot):
        copy = remote(src, slot, send_partner.at[len(sends_partner)], partner)
        copy.start()
        sends_partner.append(copy)

    sends_partner = []
    out_ref[me] = x_ref[...]
    arrived = []
    for step in range(1, right_steps + 1):
        if step == 1:
            src_right = x_ref
            src_left = x_ref
        else:
            from_left = slot_of(-(step - 1))
            remote(x_ref, from_left, send_right.at[0], right).wait_recv()
            src_right = out_ref.at[from_left]
            arrived.append(from_left)
        copy = remote(src_right, slot_of(-(step - 1)), send_right.at[step - 1], right)
        copy.start()
        sends.append(copy)
        if step > 1 and step - 1 <= left_steps:
            from_right = slot_of(step - 1)
            remote(x_ref, from_right, send_left.at[0], left).wait_recv()
            src_left = out_ref.at[from_right]
            arrived.append(from_right)
        if step <= left_steps:
            copy = remote(src_left, slot_of(step - 1), send_left.at[step - 1], left)
            copy.start()
            sends.append(copy)
        if step == 1:
            if after_first is not None:
                after_first()
            forward_partner(x_ref, me)
        for slot in arrived:
            forward_partner(out_ref.at[slot], slot)
        arrived = []
        if hook is not None and step == min(hook_step, right_steps):
            hook()
    last_left = slot_of(-right_steps)
    remote(x_ref, last_left, send_right.at[0], right).wait_recv()
    forward_partner(out_ref.at[last_left], last_left)
    if left_steps >= 1 and left_steps + 1 > right_steps:
        last_right = slot_of(left_steps)
        remote(x_ref, last_right, send_left.at[0], left).wait_recv()
        forward_partner(out_ref.at[last_right], last_right)
    for other_chip in range(chips):
        remote(x_ref, other_chip * 2 + (1 - core), send_partner.at[0], partner).wait_recv()
    for copy in sends + sends_partner:
        copy.wait_send()


def _first_kernel(n, row_ref, weight_ref, out_ref, weight_out, send_sem, recv_sem,
                  send_right, send_left, send_partner, weight_recv):
    me = lax.axis_index("feat")
    tok_index = lax.axis_index("tok")
    chips = weight_out.shape[0] // 2
    chip = tok_index // 2
    core = tok_index % 2
    peers = [lax.rem(me + d, n) for d in range(1, n)]
    barrier = pltpu.get_barrier_semaphore()
    for peer in peers:
        pl.semaphore_signal(barrier, inc=1, device_id=(tok_index, peer), device_id_type=MESH)
    ring_peers = [
        lax.rem(chip + 1, chips) * 2 + core,
        lax.rem(chip + chips - 1, chips) * 2 + core,
        chip * 2 + (1 - core),
    ]
    for peer in ring_peers:
        pl.semaphore_signal(barrier, inc=1, device_id=(peer, me), device_id_type=MESH)
    pl.semaphore_wait(barrier, len(peers) + len(ring_peers))

    def start_rows():
        for peer in peers:
            pltpu.make_async_remote_copy(
                src_ref=row_ref, dst_ref=out_ref.at[me], send_sem=send_sem.at[peer],
                recv_sem=recv_sem.at[me], device_id=(tok_index, peer), device_id_type=MESH,
            ).start()

    _ring_gather(weight_ref, weight_out, send_right, send_left, send_partner, weight_recv, me, start_rows)
    out_ref[me] = row_ref[...]
    for peer in peers:
        pltpu.make_async_remote_copy(
            src_ref=row_ref, dst_ref=out_ref.at[peer], send_sem=send_sem.at[peer],
            recv_sem=recv_sem.at[peer], device_id=(tok_index, peer), device_id_type=MESH,
        ).wait_recv()
    for peer in peers:
        pltpu.make_async_remote_copy(
            src_ref=row_ref, dst_ref=out_ref.at[me], send_sem=send_sem.at[peer],
            recv_sem=recv_sem.at[me], device_id=(tok_index, peer), device_id_type=MESH,
        ).wait_send()


def first_exchange(row_block, weight_block, n, tok_count, collective_id):
    rows, width = row_block.shape
    weight_rows, weight_width = weight_block.shape
    chips = tok_count // 2
    gathered, weights = pl.pallas_call(
        functools.partial(_first_kernel, n),
        out_shape=(
            jax.ShapeDtypeStruct((n, rows, width), row_block.dtype),
            jax.ShapeDtypeStruct((tok_count, weight_rows, weight_width), weight_block.dtype),
        ),
        in_specs=[pl.BlockSpec(memory_space=pltpu.VMEM)] * 2,
        out_specs=(pl.BlockSpec(memory_space=pltpu.VMEM),) * 2,
        scratch_shapes=[
            pltpu.SemaphoreType.DMA((n,)),
            pltpu.SemaphoreType.DMA((n,)),
            pltpu.SemaphoreType.DMA((chips,)),
            pltpu.SemaphoreType.DMA((chips,)),
            pltpu.SemaphoreType.DMA((chips,)),
            pltpu.SemaphoreType.DMA((tok_count,)),
        ],
        compiler_params=pltpu.CompilerParams(collective_id=collective_id, has_side_effects=True),
    )(row_block, weight_block)
    return gathered.reshape(n * rows, width), weights


def _route_kernel(n, packed_ref, out_ref, send_sem, recv_sem):
    me = lax.axis_index("tok")
    feat_index = lax.axis_index("feat")
    peers = [lax.rem(me + d, n) for d in range(1, n)]
    barrier = pltpu.get_barrier_semaphore()
    for peer in peers:
        pl.semaphore_signal(barrier, inc=1, device_id=(peer, feat_index), device_id_type=MESH)
    pl.semaphore_wait(barrier, len(peers))
    for peer in peers:
        pltpu.make_async_remote_copy(
            src_ref=packed_ref.at[peer], dst_ref=out_ref.at[me], send_sem=send_sem.at[peer],
            recv_sem=recv_sem.at[me], device_id=(peer, feat_index), device_id_type=MESH,
        ).start()
    out_ref[me] = packed_ref[me]
    for peer in peers:
        pltpu.make_async_remote_copy(
            src_ref=packed_ref.at[peer], dst_ref=out_ref.at[peer], send_sem=send_sem.at[peer],
            recv_sem=recv_sem.at[peer], device_id=(peer, feat_index), device_id_type=MESH,
        ).wait_recv()
    for peer in peers:
        pltpu.make_async_remote_copy(
            src_ref=packed_ref.at[peer], dst_ref=out_ref.at[me], send_sem=send_sem.at[peer],
            recv_sem=recv_sem.at[me], device_id=(peer, feat_index), device_id_type=MESH,
        ).wait_send()


def route_exchange(packed, collective_id):
    n = packed.shape[0]
    return pl.pallas_call(
        functools.partial(_route_kernel, n),
        out_shape=jax.ShapeDtypeStruct(packed.shape, packed.dtype),
        in_specs=[pl.BlockSpec(memory_space=pltpu.VMEM)],
        out_specs=pl.BlockSpec(memory_space=pltpu.VMEM),
        scratch_shapes=[pltpu.SemaphoreType.DMA((n,)), pltpu.SemaphoreType.DMA((n,))],
        compiler_params=pltpu.CompilerParams(collective_id=collective_id, has_side_effects=True),
    )(packed)


def _mix_kernel(n, gain_row, part_ref, resid_ref, gain_ref, resid_out, out_ref, merged_out, held, mine_a,
                mine_b, scatter_send, scatter_recv, gather_send, gather_recv):
    me = lax.axis_index("feat")
    tok_index = lax.axis_index("tok")
    peers = [lax.rem(me + d, n) for d in range(1, n)]
    _greet(peers, tok_index)
    split = 16
    halves = [(0, split), (split, part_ref.shape[1] - split)]
    mines = [mine_a, mine_b]

    def scatter_copy(half, peer, slot):
        first, size = halves[half]
        return pltpu.make_async_remote_copy(
            src_ref=part_ref.at[peer, pl.ds(first, size)], dst_ref=held.at[slot, pl.ds(first, size)],
            send_sem=scatter_send.at[half, peer], recv_sem=scatter_recv.at[half, slot],
            device_id=(tok_index, peer), device_id_type=MESH,
        )

    def gather_copy(half, peer, slot):
        first, size = halves[half]
        return pltpu.make_async_remote_copy(
            src_ref=mines[half], dst_ref=out_ref.at[slot, pl.ds(first, size)],
            send_sem=gather_send.at[half, peer], recv_sem=gather_recv.at[half, slot],
            device_id=(tok_index, peer), device_id_type=MESH,
        )

    for half in range(2):
        for peer in peers:
            scatter_copy(half, peer, me).start()
    for half in range(2):
        first, size = halves[half]
        total = part_ref[me, first:first + size, :].astype(jnp.float32)
        for peer in peers:
            scatter_copy(half, peer, peer).wait_recv()
            total = total + held[peer, first:first + size, :].astype(jnp.float32)
        summed = (resid_ref[first:first + size, :].astype(jnp.float32) + total).astype(jnp.bfloat16)
        resid_out[first:first + size, :] = summed
        as_float = summed.astype(jnp.float32)
        center = jnp.mean(as_float, axis=-1, keepdims=True)
        spread = jnp.mean(jnp.square(as_float - center), axis=-1, keepdims=True)
        normed = ((as_float - center) * lax.rsqrt(spread + epsilon) * gain_ref[...].astype(jnp.float32)[None, :]).astype(jnp.bfloat16)
        mines[half][...] = normed
        out_ref[me, first:first + size, :] = normed
        for peer in peers:
            gather_copy(half, peer, me).start()
    for half in range(2):
        for peer in peers:
            gather_copy(half, peer, peer).wait_recv()
    group = 4
    width = out_ref.shape[2]
    row_count = n * out_ref.shape[1]
    rows = out_ref[...].astype(jnp.float32).reshape(row_count, width).astype(jnp.bfloat16)
    merged_index = lax.broadcasted_iota(jnp.int32, (row_count // group, row_count), 0)
    row_index = lax.broadcasted_iota(jnp.int32, (row_count // group, row_count), 1)
    for part in range(group):
        pick = (row_index == merged_index * group + part).astype(jnp.bfloat16)
        merged_out[:, part * width:(part + 1) * width] = jnp.dot(
            pick, rows, preferred_element_type=jnp.float32
        ).astype(jnp.bfloat16)
    for half in range(2):
        for peer in peers:
            scatter_copy(half, peer, me).wait_send()
            gather_copy(half, peer, me).wait_send()


def mix_feat(parts, resid, gains, gain_row, n, collective_id):
    _, rows, width = parts.shape
    new_resid, _, merged = pl.pallas_call(
        functools.partial(_mix_kernel, n, gain_row),
        out_shape=(
            jax.ShapeDtypeStruct((rows, width), jnp.bfloat16),
            jax.ShapeDtypeStruct((n, rows, width), jnp.bfloat16),
            jax.ShapeDtypeStruct((n * rows // 4, 4 * width), jnp.bfloat16),
        ),
        in_specs=[pl.BlockSpec(memory_space=pltpu.VMEM)] * 3,
        out_specs=(pl.BlockSpec(memory_space=pltpu.VMEM),) * 3,
        scratch_shapes=[
            pltpu.VMEM((n, rows, width), parts.dtype),
            pltpu.VMEM((16, width), jnp.bfloat16),
            pltpu.VMEM((rows - 16, width), jnp.bfloat16),
            pltpu.SemaphoreType.DMA((2, n)),
            pltpu.SemaphoreType.DMA((2, n)),
            pltpu.SemaphoreType.DMA((2, n)),
            pltpu.SemaphoreType.DMA((2, n)),
        ],
        compiler_params=pltpu.CompilerParams(collective_id=collective_id, has_side_effects=True),
    )(parts, resid, gains)
    return new_resid, merged


def _mix_ring_kernel(n, gain_row, part_ref, resid_ref, gain_ref, weight_ref, resid_out, out_ref, weight_flat,
                     weight_out, held, mine, scatter_send, scatter_recv, gather_send, gather_recv,
                     send_right, send_left, send_partner, weight_recv):
    me = lax.axis_index("feat")
    tok_index = lax.axis_index("tok")
    chips = weight_out.shape[0] // 2
    chip = tok_index // 2
    core = tok_index % 2
    peers = [lax.rem(me + d, n) for d in range(1, n)]
    barrier = pltpu.get_barrier_semaphore()
    for peer in peers:
        pl.semaphore_signal(barrier, inc=1, device_id=(tok_index, peer), device_id_type=MESH)
    ring_peers = [
        lax.rem(chip + 1, chips) * 2 + core,
        lax.rem(chip + chips - 1, chips) * 2 + core,
        chip * 2 + (1 - core),
    ]
    for peer in ring_peers:
        pl.semaphore_signal(barrier, inc=1, device_id=(peer, me), device_id_type=MESH)
    pl.semaphore_wait(barrier, len(peers) + len(ring_peers))

    def scatter_copy(peer, slot):
        return pltpu.make_async_remote_copy(
            src_ref=part_ref.at[peer], dst_ref=held.at[slot], send_sem=scatter_send.at[peer],
            recv_sem=scatter_recv.at[slot], device_id=(tok_index, peer), device_id_type=MESH,
        )

    def gather_copy(peer, slot):
        return pltpu.make_async_remote_copy(
            src_ref=mine, dst_ref=out_ref.at[slot], send_sem=gather_send.at[peer],
            recv_sem=gather_recv.at[slot], device_id=(tok_index, peer), device_id_type=MESH,
        )

    for peer in peers:
        scatter_copy(peer, me).start()

    def norm_and_send():
        total = part_ref[me].astype(jnp.float32)
        for peer in peers:
            scatter_copy(peer, peer).wait_recv()
            total = total + held[peer].astype(jnp.float32)
        summed = (resid_ref[...].astype(jnp.float32) + total).astype(jnp.bfloat16)
        resid_out[...] = summed
        as_float = summed.astype(jnp.float32)
        center = jnp.mean(as_float, axis=-1, keepdims=True)
        spread = jnp.mean(jnp.square(as_float - center), axis=-1, keepdims=True)
        normed = ((as_float - center) * lax.rsqrt(spread + epsilon) * gain_ref[...].astype(jnp.float32)[None, :]).astype(jnp.bfloat16)
        mine[...] = normed
        out_ref[me] = normed
        for peer in peers:
            gather_copy(peer, me).start()

    _ring_gather(weight_ref, weight_out, send_right, send_left, send_partner, weight_recv, me,
                 hook=norm_and_send, hook_step=5)
    block_rows = weight_out.shape[1]
    for slot in range(weight_out.shape[0]):
        weight_flat[slot * block_rows:(slot + 1) * block_rows, :] = weight_out[slot]
    for peer in peers:
        gather_copy(peer, peer).wait_recv()
    for peer in peers:
        scatter_copy(peer, me).wait_send()
        gather_copy(peer, me).wait_send()


def mix_ring_feat(parts, resid, gains, gain_row, weight_block, n, tok_count, collective_id):
    _, rows, width = parts.shape
    weight_rows, weight_width = weight_block.shape
    chips = tok_count // 2
    new_resid, gathered, weights = pl.pallas_call(
        functools.partial(_mix_ring_kernel, n, gain_row),
        out_shape=(
            jax.ShapeDtypeStruct((rows, width), jnp.bfloat16),
            jax.ShapeDtypeStruct((n, rows, width), jnp.bfloat16),
            jax.ShapeDtypeStruct((tok_count * weight_rows, weight_width), weight_block.dtype),
        ),
        in_specs=[pl.BlockSpec(memory_space=pltpu.VMEM)] * 4,
        out_specs=(pl.BlockSpec(memory_space=pltpu.VMEM),) * 3,
        scratch_shapes=[
            pltpu.VMEM((tok_count, weight_rows, weight_width), weight_block.dtype),
            pltpu.VMEM((n, rows, width), parts.dtype),
            pltpu.VMEM((rows, width), jnp.bfloat16),
            pltpu.SemaphoreType.DMA((n,)),
            pltpu.SemaphoreType.DMA((n,)),
            pltpu.SemaphoreType.DMA((n,)),
            pltpu.SemaphoreType.DMA((n,)),
            pltpu.SemaphoreType.DMA((chips,)),
            pltpu.SemaphoreType.DMA((chips,)),
            pltpu.SemaphoreType.DMA((chips,)),
            pltpu.SemaphoreType.DMA((tok_count,)),
        ],
        compiler_params=pltpu.CompilerParams(collective_id=collective_id, has_side_effects=True),
    )(parts, resid, gains, weight_block)
    return new_resid, gathered.reshape(n * rows, width), weights


def _norm_gather_kernel(n, gain_row, tok_ref, gain_ref, out_ref, mine, send_sem, recv_sem):
    me = lax.axis_index("feat")
    tok_index = lax.axis_index("tok")
    peers = [lax.rem(me + d, n) for d in range(1, n)]
    _greet(peers, tok_index)
    as_float = tok_ref[...].astype(jnp.float32)
    center = jnp.mean(as_float, axis=-1, keepdims=True)
    spread = jnp.mean(jnp.square(as_float - center), axis=-1, keepdims=True)
    normed = ((as_float - center) * lax.rsqrt(spread + epsilon) * gain_ref[...].astype(jnp.float32)[None, :]).astype(jnp.bfloat16)
    mine[...] = normed
    out_ref[me] = normed

    def copy(peer, slot):
        return pltpu.make_async_remote_copy(
            src_ref=mine, dst_ref=out_ref.at[slot], send_sem=send_sem.at[peer],
            recv_sem=recv_sem.at[slot], device_id=(tok_index, peer), device_id_type=MESH,
        )

    for peer in peers:
        copy(peer, me).start()
    for peer in peers:
        copy(peer, peer).wait_recv()
    for peer in peers:
        copy(peer, me).wait_send()


def norm_gather_feat(rows, gains, gain_row, n, collective_id):
    count, width = rows.shape
    return pl.pallas_call(
        functools.partial(_norm_gather_kernel, n, gain_row),
        out_shape=jax.ShapeDtypeStruct((n, count, width), jnp.bfloat16),
        in_specs=[pl.BlockSpec(memory_space=pltpu.VMEM)] * 2,
        out_specs=pl.BlockSpec(memory_space=pltpu.VMEM),
        scratch_shapes=[
            pltpu.VMEM((count, width), jnp.bfloat16),
            pltpu.SemaphoreType.DMA((n,)),
            pltpu.SemaphoreType.DMA((n,)),
        ],
        compiler_params=pltpu.CompilerParams(collective_id=collective_id, has_side_effects=True),
    )(rows, gains).reshape(n * count, width)


def _scatter_kernel(n, part_ref, out_ref, held, send_sem, recv_sem):
    me = lax.axis_index("feat")
    tok_index = lax.axis_index("tok")
    peers = [lax.rem(me + d, n) for d in range(1, n)]
    _greet(peers, tok_index)
    for peer in peers:
        pltpu.make_async_remote_copy(
            src_ref=part_ref.at[peer], dst_ref=held.at[me], send_sem=send_sem.at[peer],
            recv_sem=recv_sem.at[me], device_id=(tok_index, peer), device_id_type=MESH,
        ).start()
    total = part_ref[me].astype(jnp.float32)
    for peer in peers:
        pltpu.make_async_remote_copy(
            src_ref=part_ref.at[peer], dst_ref=held.at[peer], send_sem=send_sem.at[peer],
            recv_sem=recv_sem.at[peer], device_id=(tok_index, peer), device_id_type=MESH,
        ).wait_recv()
        total = total + held[peer].astype(jnp.float32)
    out_ref[...] = total
    for peer in peers:
        pltpu.make_async_remote_copy(
            src_ref=part_ref.at[peer], dst_ref=held.at[me], send_sem=send_sem.at[peer],
            recv_sem=recv_sem.at[me], device_id=(tok_index, peer), device_id_type=MESH,
        ).wait_send()


def scatter_feat(parts, n, collective_id):
    _, rows, width = parts.shape
    return pl.pallas_call(
        functools.partial(_scatter_kernel, n),
        out_shape=jax.ShapeDtypeStruct((rows, width), jnp.float32),
        in_specs=[pl.BlockSpec(memory_space=pltpu.VMEM)],
        out_specs=pl.BlockSpec(memory_space=pltpu.VMEM),
        scratch_shapes=[
            pltpu.VMEM((n, rows, width), parts.dtype),
            pltpu.SemaphoreType.DMA((n,)),
            pltpu.SemaphoreType.DMA((n,)),
        ],
        compiler_params=pltpu.CompilerParams(collective_id=collective_id, has_side_effects=True),
    )(parts)

MESH = pl.DeviceIdType.MESH
LEAST_UNITS = 4
MOST_UNITS = 16
HEAD_DIM = 88


epsilon = 1e-06


def layer_norm(row_block, gain_row):
    as_float = row_block.astype(jnp.float32)
    center = jnp.mean(as_float, axis=-1, keepdims=True)
    spread = jnp.mean(jnp.square(as_float - center), axis=-1, keepdims=True)
    scaled = (as_float - center) * lax.rsqrt(spread + epsilon) * gain_row.astype(jnp.float32)
    return scaled.astype(jnp.bfloat16)


def project_rows(row_block, weight_block, collective_id):
    n = lax.axis_size("feat")
    return jnp.dot(
        gather_feat(row_block, n, collective_id),
        weight_block,
        preferred_element_type=jnp.float32,
    )


def scatter_rows(left_rows, right_rows, collective_id):
    n = lax.axis_size("feat")
    parts = jnp.dot(left_rows, right_rows, preferred_element_type=jnp.float32).astype(jnp.bfloat16)
    return scatter_feat(parts.reshape(n, parts.shape[0] // n, parts.shape[1]), n, collective_id)


def early_weights(weight_up, weight_down):
    return (weight_up, weight_down)


def upper_weight(fetched):
    return lax.all_gather(fetched[0], "tok", axis=0, tiled=True)


def lower_weight(fetched):
    return lax.all_gather(fetched[1], "tok", axis=1, tiled=True)


def attend(projected, segment_ids, head_count):
    token_count = projected.shape[0]
    parts_all = projected.reshape(token_count, 3, head_count, HEAD_DIM)
    queries = (parts_all[:, 0] * HEAD_DIM ** (-0.5)).astype(jnp.bfloat16)
    keys_here = parts_all[:, 1].astype(jnp.bfloat16)
    values_here = parts_all[:, 2].astype(jnp.bfloat16)
    scores = jnp.einsum("qhd,khd->hqk", queries, keys_here, preferred_element_type=jnp.float32)
    same_segment = segment_ids[:, None] == segment_ids[None, :]
    scores = jnp.where(same_segment[None, :, :], scores, -1e30)
    highest = jnp.max(scores, axis=-1, keepdims=True)
    raised = jnp.exp(scores - highest)
    weights_soft = (raised / jnp.sum(raised, axis=-1, keepdims=True)).astype(jnp.bfloat16)
    attended = jnp.einsum(
        "hqk,khd->qhd", weights_soft, values_here, preferred_element_type=jnp.float32
    )
    return attended.astype(jnp.bfloat16).reshape(token_count, head_count * HEAD_DIM)


def route_rows(embedded, segment_ids, owners):
    merged_count = embedded.shape[0]
    peer_count = owners.shape[0]
    least_units = max(LEAST_UNITS, (merged_count + peer_count - 1) // peer_count)
    slot_count = max(MOST_UNITS, 2 * least_units)
    first_ids = segment_ids.reshape(merged_count, 4)[:, 0]
    id_base = lax.axis_index("tok") * peer_count
    local_index = first_ids - id_base
    owner_pick = local_index[:, None] == jnp.arange(peer_count, dtype=jnp.int32)[None, :]
    owner_of = jnp.sum(jnp.where(owner_pick, owners[None, :], 0), axis=1)
    row_index = jnp.arange(merged_count, dtype=jnp.int32)
    earlier = (row_index[None, :] < row_index[:, None]) & (first_ids[None, :] == first_ids[:, None])
    within = jnp.sum(earlier.astype(jnp.int32), axis=1)
    target = owner_of * slot_count + within
    select = (
        jnp.arange(peer_count * slot_count, dtype=jnp.int32)[:, None] == target[None, :]
    ).astype(jnp.bfloat16)
    packed = jnp.dot(select, embedded, preferred_element_type=jnp.float32).astype(jnp.bfloat16)
    packed = packed.reshape(peer_count, slot_count, embedded.shape[1])
    received = route_exchange(packed, 5)
    return received.reshape(peer_count * slot_count, embedded.shape[1])


def body(
    tokens,
    segment_ids,
    owners,
    project_in,
    project_out,
    weight_up,
    weight_down,
    weight_merge,
    gain_attend,
    gain_hidden,
    gain_final,
):
    model_width = tokens.shape[1]
    head_count = project_in.shape[2] // HEAD_DIM
    units = weight_up.shape[1]
    feat_count = lax.axis_size("feat")
    tok_count = lax.axis_size("tok")
    flat_in = project_in.reshape(model_width, 3 * project_in.shape[2])
    local_count = tokens.shape[0]
    stacked = jnp.concatenate([weight_up, weight_down.T], axis=1)
    gathered = norm_gather_feat(tokens, gain_attend, 0, feat_count, 0)
    projected = jnp.dot(gathered, flat_in, preferred_element_type=jnp.float32)
    attended = attend(projected, segment_ids, head_count)
    attn_parts = jnp.dot(attended, project_out, preferred_element_type=jnp.float32).astype(jnp.bfloat16)
    second, hidden_rows, weights = mix_ring_feat(
        attn_parts.reshape(feat_count, local_count, model_width), tokens, gain_hidden, 1, stacked,
        feat_count, tok_count, 1,
    )
    both = weights
    upper = both[:, :units]
    lower_t = both[:, units:]
    hidden = jax.nn.gelu(
        jnp.dot(hidden_rows, upper, preferred_element_type=jnp.float32), approximate=False
    ).astype(jnp.bfloat16)
    down_parts = lax.dot_general(
        hidden, lower_t, (((1,), (1,)), ((), ())), preferred_element_type=jnp.float32
    ).astype(jnp.bfloat16)
    _, merged = mix_feat(
        down_parts.reshape(feat_count, local_count, model_width), second, gain_final, 2, feat_count, 3
    )
    embedded = jnp.dot(merged, weight_merge, preferred_element_type=jnp.float32).astype(jnp.bfloat16)
    return route_rows(embedded, segment_ids, owners)


def solution(mesh):
    return jax.shard_map(
        body,
        mesh=mesh,
        in_specs=(
            P(("tok", "feat"), None),
            P("tok"),
            P("tok"),
            P(None, None, "feat"),
            P("feat", None),
            P("tok", "feat"),
            P("feat", "tok"),
            P(None, "feat"),
            P(),
            P(),
            P(),
        ),
        out_specs=P("tok", "feat"),
        check_vma=False,
    )
```

```python
import functools
import jax
import jax.numpy as jnp
from jax import lax
from jax.experimental import pallas as pl
from jax.experimental.pallas import tpu as pltpu
from jax.sharding import PartitionSpec as P


def _greet(peers, tok_index):
    barrier = pltpu.get_barrier_semaphore()
    for peer in peers:
        pl.semaphore_signal(barrier, inc=1, device_id=(tok_index, peer), device_id_type=MESH)
    pl.semaphore_wait(barrier, len(peers))


def _gather_kernel(n, row_ref, out_ref, send_sem, recv_sem):
    me = lax.axis_index("feat")
    tok_index = lax.axis_index("tok")
    peers = [lax.rem(me + d, n) for d in range(1, n)]
    _greet(peers, tok_index)
    for peer in peers:
        pltpu.make_async_remote_copy(
            src_ref=row_ref, dst_ref=out_ref.at[me], send_sem=send_sem.at[peer],
            recv_sem=recv_sem.at[me], device_id=(tok_index, peer), device_id_type=MESH,
        ).start()
    out_ref[me] = row_ref[...]
    for peer in peers:
        pltpu.make_async_remote_copy(
            src_ref=row_ref, dst_ref=out_ref.at[peer], send_sem=send_sem.at[peer],
            recv_sem=recv_sem.at[peer], device_id=(tok_index, peer), device_id_type=MESH,
        ).wait_recv()
    for peer in peers:
        pltpu.make_async_remote_copy(
            src_ref=row_ref, dst_ref=out_ref.at[me], send_sem=send_sem.at[peer],
            recv_sem=recv_sem.at[me], device_id=(tok_index, peer), device_id_type=MESH,
        ).wait_send()


def gather_feat(row_block, n, collective_id):
    rows, width = row_block.shape
    return pl.pallas_call(
        functools.partial(_gather_kernel, n),
        out_shape=jax.ShapeDtypeStruct((n, rows, width), row_block.dtype),
        in_specs=[pl.BlockSpec(memory_space=pltpu.VMEM)],
        out_specs=pl.BlockSpec(memory_space=pltpu.VMEM),
        scratch_shapes=[pltpu.SemaphoreType.DMA((n,)), pltpu.SemaphoreType.DMA((n,))],
        compiler_params=pltpu.CompilerParams(collective_id=collective_id, has_side_effects=True),
    )(row_block).reshape(n * rows, width)


def _ring_gather(x_ref, out_ref, send_right, send_left, send_partner, recv_sem, feat_index, after_first=None,
                 hook=None, hook_step=1):
    tok_count = out_ref.shape[0]
    chips = tok_count // 2
    right_steps = chips // 2
    left_steps = chips - 1 - right_steps
    me = lax.axis_index("tok")
    chip = me // 2
    core = me % 2
    right = lax.rem(chip + 1, chips) * 2 + core
    left = lax.rem(chip + chips - 1, chips) * 2 + core
    partner = chip * 2 + (1 - core)

    def slot_of(offset):
        return lax.rem(chip + offset + 2 * chips, chips) * 2 + core

    def remote(src, slot, sem, target):
        return pltpu.make_async_remote_copy(
            src_ref=src, dst_ref=out_ref.at[slot], send_sem=sem, recv_sem=recv_sem.at[slot],
            device_id=(target, feat_index), device_id_type=MESH,
        )

    sends = []

    def forward_partner(src, slot):
        copy = remote(src, slot, send_partner.at[len(sends_partner)], partner)
        copy.start()
        sends_partner.append(copy)

    sends_partner = []
    out_ref[me] = x_ref[...]
    arrived = []
    for step in range(1, right_steps + 1):
        if step == 1:
            src_right = x_ref
            src_left = x_ref
        else:
            from_left = slot_of(-(step - 1))
            remote(x_ref, from_left, send_right.at[0], right).wait_recv()
            src_right = out_ref.at[from_left]
            arrived.append(from_left)
        copy = remote(src_right, slot_of(-(step - 1)), send_right.at[step - 1], right)
        copy.start()
        sends.append(copy)
        if step > 1 and step - 1 <= left_steps:
            from_right = slot_of(step - 1)
            remote(x_ref, from_right, send_left.at[0], left).wait_recv()
            src_left = out_ref.at[from_right]
            arrived.append(from_right)
        if step <= left_steps:
            copy = remote(src_left, slot_of(step - 1), send_left.at[step - 1], left)
            copy.start()
            sends.append(copy)
        if step == 1:
            if after_first is not None:
                after_first()
            forward_partner(x_ref, me)
        for slot in arrived:
            forward_partner(out_ref.at[slot], slot)
        arrived = []
        if hook is not None and step == min(hook_step, right_steps):
            hook()
    last_left = slot_of(-right_steps)
    remote(x_ref, last_left, send_right.at[0], right).wait_recv()
    forward_partner(out_ref.at[last_left], last_left)
    if left_steps >= 1 and left_steps + 1 > right_steps:
        last_right = slot_of(left_steps)
        remote(x_ref, last_right, send_left.at[0], left).wait_recv()
        forward_partner(out_ref.at[last_right], last_right)
    for other_chip in range(chips):
        remote(x_ref, other_chip * 2 + (1 - core), send_partner.at[0], partner).wait_recv()
    for copy in sends + sends_partner:
        copy.wait_send()


def _first_kernel(n, row_ref, weight_ref, out_ref, weight_out, send_sem, recv_sem,
                  send_right, send_left, send_partner, weight_recv):
    me = lax.axis_index("feat")
    tok_index = lax.axis_index("tok")
    chips = weight_out.shape[0] // 2
    chip = tok_index // 2
    core = tok_index % 2
    peers = [lax.rem(me + d, n) for d in range(1, n)]
    barrier = pltpu.get_barrier_semaphore()
    for peer in peers:
        pl.semaphore_signal(barrier, inc=1, device_id=(tok_index, peer), device_id_type=MESH)
    ring_peers = [
        lax.rem(chip + 1, chips) * 2 + core,
        lax.rem(chip + chips - 1, chips) * 2 + core,
        chip * 2 + (1 - core),
    ]
    for peer in ring_peers:
        pl.semaphore_signal(barrier, inc=1, device_id=(peer, me), device_id_type=MESH)
    pl.semaphore_wait(barrier, len(peers) + len(ring_peers))

    def start_rows():
        for peer in peers:
            pltpu.make_async_remote_copy(
                src_ref=row_ref, dst_ref=out_ref.at[me], send_sem=send_sem.at[peer],
                recv_sem=recv_sem.at[me], device_id=(tok_index, peer), device_id_type=MESH,
            ).start()

    _ring_gather(weight_ref, weight_out, send_right, send_left, send_partner, weight_recv, me, start_rows)
    out_ref[me] = row_ref[...]
    for peer in peers:
        pltpu.make_async_remote_copy(
            src_ref=row_ref, dst_ref=out_ref.at[peer], send_sem=send_sem.at[peer],
            recv_sem=recv_sem.at[peer], device_id=(tok_index, peer), device_id_type=MESH,
        ).wait_recv()
    for peer in peers:
        pltpu.make_async_remote_copy(
            src_ref=row_ref, dst_ref=out_ref.at[me], send_sem=send_sem.at[peer],
            recv_sem=recv_sem.at[me], device_id=(tok_index, peer), device_id_type=MESH,
        ).wait_send()


def first_exchange(row_block, weight_block, n, tok_count, collective_id):
    rows, width = row_block.shape
    weight_rows, weight_width = weight_block.shape
    chips = tok_count // 2
    gathered, weights = pl.pallas_call(
        functools.partial(_first_kernel, n),
        out_shape=(
            jax.ShapeDtypeStruct((n, rows, width), row_block.dtype),
            jax.ShapeDtypeStruct((tok_count, weight_rows, weight_width), weight_block.dtype),
        ),
        in_specs=[pl.BlockSpec(memory_space=pltpu.VMEM)] * 2,
        out_specs=(pl.BlockSpec(memory_space=pltpu.VMEM),) * 2,
        scratch_shapes=[
            pltpu.SemaphoreType.DMA((n,)),
            pltpu.SemaphoreType.DMA((n,)),
            pltpu.SemaphoreType.DMA((chips,)),
            pltpu.SemaphoreType.DMA((chips,)),
            pltpu.SemaphoreType.DMA((chips,)),
            pltpu.SemaphoreType.DMA((tok_count,)),
        ],
        compiler_params=pltpu.CompilerParams(collective_id=collective_id, has_side_effects=True),
    )(row_block, weight_block)
    return gathered.reshape(n * rows, width), weights


def _route_kernel(n, packed_ref, out_ref, send_sem, recv_sem):
    me = lax.axis_index("tok")
    feat_index = lax.axis_index("feat")
    peers = [lax.rem(me + d, n) for d in range(1, n)]
    barrier = pltpu.get_barrier_semaphore()
    for peer in peers:
        pl.semaphore_signal(barrier, inc=1, device_id=(peer, feat_index), device_id_type=MESH)
    pl.semaphore_wait(barrier, len(peers))
    for peer in peers:
        pltpu.make_async_remote_copy(
            src_ref=packed_ref.at[peer], dst_ref=out_ref.at[me], send_sem=send_sem.at[peer],
            recv_sem=recv_sem.at[me], device_id=(peer, feat_index), device_id_type=MESH,
        ).start()
    out_ref[me] = packed_ref[me]
    for peer in peers:
        pltpu.make_async_remote_copy(
            src_ref=packed_ref.at[peer], dst_ref=out_ref.at[peer], send_sem=send_sem.at[peer],
            recv_sem=recv_sem.at[peer], device_id=(peer, feat_index), device_id_type=MESH,
        ).wait_recv()
    for peer in peers:
        pltpu.make_async_remote_copy(
            src_ref=packed_ref.at[peer], dst_ref=out_ref.at[me], send_sem=send_sem.at[peer],
            recv_sem=recv_sem.at[me], device_id=(peer, feat_index), device_id_type=MESH,
        ).wait_send()


def route_exchange(packed, collective_id):
    n = packed.shape[0]
    return pl.pallas_call(
        functools.partial(_route_kernel, n),
        out_shape=jax.ShapeDtypeStruct(packed.shape, packed.dtype),
        in_specs=[pl.BlockSpec(memory_space=pltpu.VMEM)],
        out_specs=pl.BlockSpec(memory_space=pltpu.VMEM),
        scratch_shapes=[pltpu.SemaphoreType.DMA((n,)), pltpu.SemaphoreType.DMA((n,))],
        compiler_params=pltpu.CompilerParams(collective_id=collective_id, has_side_effects=True),
    )(packed)


def _mix_kernel(n, gain_row, part_ref, resid_ref, gain_ref, resid_out, out_ref, merged_out, held, mine_a,
                mine_b, scatter_send, scatter_recv, gather_send, gather_recv):
    me = lax.axis_index("feat")
    tok_index = lax.axis_index("tok")
    peers = [lax.rem(me + d, n) for d in range(1, n)]
    _greet(peers, tok_index)
    split = 16
    halves = [(0, split), (split, part_ref.shape[1] - split)]
    mines = [mine_a, mine_b]

    def scatter_copy(half, peer, slot):
        first, size = halves[half]
        return pltpu.make_async_remote_copy(
            src_ref=part_ref.at[peer, pl.ds(first, size)], dst_ref=held.at[slot, pl.ds(first, size)],
            send_sem=scatter_send.at[half, peer], recv_sem=scatter_recv.at[half, slot],
            device_id=(tok_index, peer), device_id_type=MESH,
        )

    def gather_copy(half, peer, slot):
        first, size = halves[half]
        return pltpu.make_async_remote_copy(
            src_ref=mines[half], dst_ref=out_ref.at[slot, pl.ds(first, size)],
            send_sem=gather_send.at[half, peer], recv_sem=gather_recv.at[half, slot],
            device_id=(tok_index, peer), device_id_type=MESH,
        )

    for half in range(2):
        for peer in peers:
            scatter_copy(half, peer, me).start()
    for half in range(2):
        first, size = halves[half]
        total = part_ref[me, first:first + size, :].astype(jnp.float32)
        for peer in peers:
            scatter_copy(half, peer, peer).wait_recv()
            total = total + held[peer, first:first + size, :].astype(jnp.float32)
        summed = (resid_ref[first:first + size, :].astype(jnp.float32) + total).astype(jnp.bfloat16)
        resid_out[first:first + size, :] = summed
        as_float = summed.astype(jnp.float32)
        center = jnp.mean(as_float, axis=-1, keepdims=True)
        spread = jnp.mean(jnp.square(as_float - center), axis=-1, keepdims=True)
        normed = ((as_float - center) * lax.rsqrt(spread + epsilon) * gain_ref[...].astype(jnp.float32)[None, :]).astype(jnp.bfloat16)
        mines[half][...] = normed
        out_ref[me, first:first + size, :] = normed
        for peer in peers:
            gather_copy(half, peer, me).start()
    for half in range(2):
        for peer in peers:
            gather_copy(half, peer, peer).wait_recv()
    group = 4
    width = out_ref.shape[2]
    row_count = n * out_ref.shape[1]
    rows = out_ref[...].astype(jnp.float32).reshape(row_count, width).astype(jnp.bfloat16)
    merged_index = lax.broadcasted_iota(jnp.int32, (row_count // group, row_count), 0)
    row_index = lax.broadcasted_iota(jnp.int32, (row_count // group, row_count), 1)
    for part in range(group):
        pick = (row_index == merged_index * group + part).astype(jnp.bfloat16)
        merged_out[:, part * width:(part + 1) * width] = jnp.dot(
            pick, rows, preferred_element_type=jnp.float32
        ).astype(jnp.bfloat16)
    for half in range(2):
        for peer in peers:
            scatter_copy(half, peer, me).wait_send()
            gather_copy(half, peer, me).wait_send()


def mix_feat(parts, resid, gains, gain_row, n, collective_id):
    _, rows, width = parts.shape
    new_resid, _, merged = pl.pallas_call(
        functools.partial(_mix_kernel, n, gain_row),
        out_shape=(
            jax.ShapeDtypeStruct((rows, width), jnp.bfloat16),
            jax.ShapeDtypeStruct((n, rows, width), jnp.bfloat16),
            jax.ShapeDtypeStruct((n * rows // 4, 4 * width), jnp.bfloat16),
        ),
        in_specs=[pl.BlockSpec(memory_space=pltpu.VMEM)] * 3,
        out_specs=(pl.BlockSpec(memory_space=pltpu.VMEM),) * 3,
        scratch_shapes=[
            pltpu.VMEM((n, rows, width), parts.dtype),
            pltpu.VMEM((16, width), jnp.bfloat16),
            pltpu.VMEM((rows - 16, width), jnp.bfloat16),
            pltpu.SemaphoreType.DMA((2, n)),
            pltpu.SemaphoreType.DMA((2, n)),
            pltpu.SemaphoreType.DMA((2, n)),
            pltpu.SemaphoreType.DMA((2, n)),
        ],
        compiler_params=pltpu.CompilerParams(collective_id=collective_id, has_side_effects=True),
    )(parts, resid, gains)
    return new_resid, merged


def _mix_ring_kernel(n, gain_row, part_ref, resid_ref, gain_ref, weight_ref, resid_out, out_ref, weight_flat,
                     weight_out, held, mine, scatter_send, scatter_recv, gather_send, gather_recv,
                     send_right, send_left, send_partner, weight_recv):
    me = lax.axis_index("feat")
    tok_index = lax.axis_index("tok")
    chips = weight_out.shape[0] // 2
    chip = tok_index // 2
    core = tok_index % 2
    peers = [lax.rem(me + d, n) for d in range(1, n)]
    barrier = pltpu.get_barrier_semaphore()
    for peer in peers:
        pl.semaphore_signal(barrier, inc=1, device_id=(tok_index, peer), device_id_type=MESH)
    ring_peers = [
        lax.rem(chip + 1, chips) * 2 + core,
        lax.rem(chip + chips - 1, chips) * 2 + core,
        chip * 2 + (1 - core),
    ]
    for peer in ring_peers:
        pl.semaphore_signal(barrier, inc=1, device_id=(peer, me), device_id_type=MESH)
    pl.semaphore_wait(barrier, len(peers) + len(ring_peers))

    def scatter_copy(peer, slot):
        return pltpu.make_async_remote_copy(
            src_ref=part_ref.at[peer], dst_ref=held.at[slot], send_sem=scatter_send.at[peer],
            recv_sem=scatter_recv.at[slot], device_id=(tok_index, peer), device_id_type=MESH,
        )

    def gather_copy(peer, slot):
        return pltpu.make_async_remote_copy(
            src_ref=mine, dst_ref=out_ref.at[slot], send_sem=gather_send.at[peer],
            recv_sem=gather_recv.at[slot], device_id=(tok_index, peer), device_id_type=MESH,
        )

    for peer in peers:
        scatter_copy(peer, me).start()

    def norm_and_send():
        total = part_ref[me].astype(jnp.float32)
        for peer in peers:
            scatter_copy(peer, peer).wait_recv()
            total = total + held[peer].astype(jnp.float32)
        summed = (resid_ref[...].astype(jnp.float32) + total).astype(jnp.bfloat16)
        resid_out[...] = summed
        as_float = summed.astype(jnp.float32)
        center = jnp.mean(as_float, axis=-1, keepdims=True)
        spread = jnp.mean(jnp.square(as_float - center), axis=-1, keepdims=True)
        normed = ((as_float - center) * lax.rsqrt(spread + epsilon) * gain_ref[...].astype(jnp.float32)[None, :]).astype(jnp.bfloat16)
        mine[...] = normed
        out_ref[me] = normed
        for peer in peers:
            gather_copy(peer, me).start()

    _ring_gather(weight_ref, weight_out, send_right, send_left, send_partner, weight_recv, me,
                 hook=norm_and_send, hook_step=7)
    block_rows = weight_out.shape[1]
    for slot in range(weight_out.shape[0]):
        weight_flat[slot * block_rows:(slot + 1) * block_rows, :] = weight_out[slot]
    for peer in peers:
        gather_copy(peer, peer).wait_recv()
    for peer in peers:
        scatter_copy(peer, me).wait_send()
        gather_copy(peer, me).wait_send()


def mix_ring_feat(parts, resid, gains, gain_row, weight_block, n, tok_count, collective_id):
    _, rows, width = parts.shape
    weight_rows, weight_width = weight_block.shape
    chips = tok_count // 2
    new_resid, gathered, weights = pl.pallas_call(
        functools.partial(_mix_ring_kernel, n, gain_row),
        out_shape=(
            jax.ShapeDtypeStruct((rows, width), jnp.bfloat16),
            jax.ShapeDtypeStruct((n, rows, width), jnp.bfloat16),
            jax.ShapeDtypeStruct((tok_count * weight_rows, weight_width), weight_block.dtype),
        ),
        in_specs=[pl.BlockSpec(memory_space=pltpu.VMEM)] * 4,
        out_specs=(pl.BlockSpec(memory_space=pltpu.VMEM),) * 3,
        scratch_shapes=[
            pltpu.VMEM((tok_count, weight_rows, weight_width), weight_block.dtype),
            pltpu.VMEM((n, rows, width), parts.dtype),
            pltpu.VMEM((rows, width), jnp.bfloat16),
            pltpu.SemaphoreType.DMA((n,)),
            pltpu.SemaphoreType.DMA((n,)),
            pltpu.SemaphoreType.DMA((n,)),
            pltpu.SemaphoreType.DMA((n,)),
            pltpu.SemaphoreType.DMA((chips,)),
            pltpu.SemaphoreType.DMA((chips,)),
            pltpu.SemaphoreType.DMA((chips,)),
            pltpu.SemaphoreType.DMA((tok_count,)),
        ],
        compiler_params=pltpu.CompilerParams(collective_id=collective_id, has_side_effects=True),
    )(parts, resid, gains, weight_block)
    return new_resid, gathered.reshape(n * rows, width), weights


def _norm_gather_kernel(n, gain_row, tok_ref, gain_ref, out_ref, mine, send_sem, recv_sem):
    me = lax.axis_index("feat")
    tok_index = lax.axis_index("tok")
    peers = [lax.rem(me + d, n) for d in range(1, n)]
    _greet(peers, tok_index)
    as_float = tok_ref[...].astype(jnp.float32)
    center = jnp.mean(as_float, axis=-1, keepdims=True)
    spread = jnp.mean(jnp.square(as_float - center), axis=-1, keepdims=True)
    normed = ((as_float - center) * lax.rsqrt(spread + epsilon) * gain_ref[...].astype(jnp.float32)[None, :]).astype(jnp.bfloat16)
    mine[...] = normed
    out_ref[me] = normed

    def copy(peer, slot):
        return pltpu.make_async_remote_copy(
            src_ref=mine, dst_ref=out_ref.at[slot], send_sem=send_sem.at[peer],
            recv_sem=recv_sem.at[slot], device_id=(tok_index, peer), device_id_type=MESH,
        )

    for peer in peers:
        copy(peer, me).start()
    for peer in peers:
        copy(peer, peer).wait_recv()
    for peer in peers:
        copy(peer, me).wait_send()


def norm_gather_feat(rows, gains, gain_row, n, collective_id):
    count, width = rows.shape
    return pl.pallas_call(
        functools.partial(_norm_gather_kernel, n, gain_row),
        out_shape=jax.ShapeDtypeStruct((n, count, width), jnp.bfloat16),
        in_specs=[pl.BlockSpec(memory_space=pltpu.VMEM)] * 2,
        out_specs=pl.BlockSpec(memory_space=pltpu.VMEM),
        scratch_shapes=[
            pltpu.VMEM((count, width), jnp.bfloat16),
            pltpu.SemaphoreType.DMA((n,)),
            pltpu.SemaphoreType.DMA((n,)),
        ],
        compiler_params=pltpu.CompilerParams(collective_id=collective_id, has_side_effects=True),
    )(rows, gains).reshape(n * count, width)


def _scatter_kernel(n, part_ref, out_ref, held, send_sem, recv_sem):
    me = lax.axis_index("feat")
    tok_index = lax.axis_index("tok")
    peers = [lax.rem(me + d, n) for d in range(1, n)]
    _greet(peers, tok_index)
    for peer in peers:
        pltpu.make_async_remote_copy(
            src_ref=part_ref.at[peer], dst_ref=held.at[me], send_sem=send_sem.at[peer],
            recv_sem=recv_sem.at[me], device_id=(tok_index, peer), device_id_type=MESH,
        ).start()
    total = part_ref[me].astype(jnp.float32)
    for peer in peers:
        pltpu.make_async_remote_copy(
            src_ref=part_ref.at[peer], dst_ref=held.at[peer], send_sem=send_sem.at[peer],
            recv_sem=recv_sem.at[peer], device_id=(tok_index, peer), device_id_type=MESH,
        ).wait_recv()
        total = total + held[peer].astype(jnp.float32)
    out_ref[...] = total
    for peer in peers:
        pltpu.make_async_remote_copy(
            src_ref=part_ref.at[peer], dst_ref=held.at[me], send_sem=send_sem.at[peer],
            recv_sem=recv_sem.at[me], device_id=(tok_index, peer), device_id_type=MESH,
        ).wait_send()


def scatter_feat(parts, n, collective_id):
    _, rows, width = parts.shape
    return pl.pallas_call(
        functools.partial(_scatter_kernel, n),
        out_shape=jax.ShapeDtypeStruct((rows, width), jnp.float32),
        in_specs=[pl.BlockSpec(memory_space=pltpu.VMEM)],
        out_specs=pl.BlockSpec(memory_space=pltpu.VMEM),
        scratch_shapes=[
            pltpu.VMEM((n, rows, width), parts.dtype),
            pltpu.SemaphoreType.DMA((n,)),
            pltpu.SemaphoreType.DMA((n,)),
        ],
        compiler_params=pltpu.CompilerParams(collective_id=collective_id, has_side_effects=True),
    )(parts)

MESH = pl.DeviceIdType.MESH
LEAST_UNITS = 4
MOST_UNITS = 16
HEAD_DIM = 88


epsilon = 1e-06


def layer_norm(row_block, gain_row):
    as_float = row_block.astype(jnp.float32)
    center = jnp.mean(as_float, axis=-1, keepdims=True)
    spread = jnp.mean(jnp.square(as_float - center), axis=-1, keepdims=True)
    scaled = (as_float - center) * lax.rsqrt(spread + epsilon) * gain_row.astype(jnp.float32)
    return scaled.astype(jnp.bfloat16)


def project_rows(row_block, weight_block, collective_id):
    n = lax.axis_size("feat")
    return jnp.dot(
        gather_feat(row_block, n, collective_id),
        weight_block,
        preferred_element_type=jnp.float32,
    )


def scatter_rows(left_rows, right_rows, collective_id):
    n = lax.axis_size("feat")
    parts = jnp.dot(left_rows, right_rows, preferred_element_type=jnp.float32).astype(jnp.bfloat16)
    return scatter_feat(parts.reshape(n, parts.shape[0] // n, parts.shape[1]), n, collective_id)


def early_weights(weight_up, weight_down):
    return (weight_up, weight_down)


def upper_weight(fetched):
    return lax.all_gather(fetched[0], "tok", axis=0, tiled=True)


def lower_weight(fetched):
    return lax.all_gather(fetched[1], "tok", axis=1, tiled=True)


def attend(projected, segment_ids, head_count):
    token_count = projected.shape[0]
    parts_all = projected.reshape(token_count, 3, head_count, HEAD_DIM)
    queries = (parts_all[:, 0] * HEAD_DIM ** (-0.5)).astype(jnp.bfloat16)
    keys_here = parts_all[:, 1].astype(jnp.bfloat16)
    values_here = parts_all[:, 2].astype(jnp.bfloat16)
    scores = jnp.einsum("qhd,khd->hqk", queries, keys_here, preferred_element_type=jnp.float32)
    same_segment = segment_ids[:, None] == segment_ids[None, :]
    scores = jnp.where(same_segment[None, :, :], scores, -1e30)
    highest = jnp.max(scores, axis=-1, keepdims=True)
    raised = jnp.exp(scores - highest)
    weights_soft = (raised / jnp.sum(raised, axis=-1, keepdims=True)).astype(jnp.bfloat16)
    attended = jnp.einsum(
        "hqk,khd->qhd", weights_soft, values_here, preferred_element_type=jnp.float32
    )
    return attended.astype(jnp.bfloat16).reshape(token_count, head_count * HEAD_DIM)


def route_rows(embedded, segment_ids, owners):
    merged_count = embedded.shape[0]
    peer_count = owners.shape[0]
    least_units = max(LEAST_UNITS, (merged_count + peer_count - 1) // peer_count)
    slot_count = max(MOST_UNITS, 2 * least_units)
    first_ids = segment_ids.reshape(merged_count, 4)[:, 0]
    id_base = lax.axis_index("tok") * peer_count
    local_index = first_ids - id_base
    owner_pick = local_index[:, None] == jnp.arange(peer_count, dtype=jnp.int32)[None, :]
    owner_of = jnp.sum(jnp.where(owner_pick, owners[None, :], 0), axis=1)
    row_index = jnp.arange(merged_count, dtype=jnp.int32)
    earlier = (row_index[None, :] < row_index[:, None]) & (first_ids[None, :] == first_ids[:, None])
    within = jnp.sum(earlier.astype(jnp.int32), axis=1)
    target = owner_of * slot_count + within
    select = (
        jnp.arange(peer_count * slot_count, dtype=jnp.int32)[:, None] == target[None, :]
    ).astype(jnp.bfloat16)
    packed = jnp.dot(select, embedded, preferred_element_type=jnp.float32).astype(jnp.bfloat16)
    packed = packed.reshape(peer_count, slot_count, embedded.shape[1])
    received = route_exchange(packed, 5)
    return received.reshape(peer_count * slot_count, embedded.shape[1])


def body(
    tokens,
    segment_ids,
    owners,
    project_in,
    project_out,
    weight_up,
    weight_down,
    weight_merge,
    gain_attend,
    gain_hidden,
    gain_final,
):
    model_width = tokens.shape[1]
    head_count = project_in.shape[2] // HEAD_DIM
    units = weight_up.shape[1]
    feat_count = lax.axis_size("feat")
    tok_count = lax.axis_size("tok")
    flat_in = project_in.reshape(model_width, 3 * project_in.shape[2])
    local_count = tokens.shape[0]
    stacked = jnp.concatenate([weight_up, weight_down.T], axis=1)
    gathered = norm_gather_feat(tokens, gain_attend, 0, feat_count, 0)
    projected = jnp.dot(gathered, flat_in, preferred_element_type=jnp.float32)
    attended = attend(projected, segment_ids, head_count)
    attn_parts = jnp.dot(attended, project_out, preferred_element_type=jnp.float32).astype(jnp.bfloat16)
    second, hidden_rows, weights = mix_ring_feat(
        attn_parts.reshape(feat_count, local_count, model_width), tokens, gain_hidden, 1, stacked,
        feat_count, tok_count, 1,
    )
    both = weights
    upper = both[:, :units]
    lower_t = both[:, units:]
    hidden = jax.nn.gelu(
        jnp.dot(hidden_rows, upper, preferred_element_type=jnp.float32), approximate=False
    ).astype(jnp.bfloat16)
    down_parts = lax.dot_general(
        hidden, lower_t, (((1,), (1,)), ((), ())), preferred_element_type=jnp.float32
    ).astype(jnp.bfloat16)
    _, merged = mix_feat(
        down_parts.reshape(feat_count, local_count, model_width), second, gain_final, 2, feat_count, 3
    )
    embedded = jnp.dot(merged, weight_merge, preferred_element_type=jnp.float32).astype(jnp.bfloat16)
    return route_rows(embedded, segment_ids, owners)


def solution(mesh):
    return jax.shard_map(
        body,
        mesh=mesh,
        in_specs=(
            P(("tok", "feat"), None),
            P("tok"),
            P("tok"),
            P(None, None, "feat"),
            P("feat", None),
            P("tok", "feat"),
            P("feat", "tok"),
            P(None, "feat"),
            P(),
            P(),
            P(),
        ),
        out_specs=P("tok", "feat"),
        check_vma=False,
    )
```

```python
import functools
import jax
import jax.numpy as jnp
from jax import lax
from jax.experimental import pallas as pl
from jax.experimental.pallas import tpu as pltpu
from jax.sharding import PartitionSpec as P


def _greet(peers, tok_index):
    barrier = pltpu.get_barrier_semaphore()
    for peer in peers:
        pl.semaphore_signal(barrier, inc=1, device_id=(tok_index, peer), device_id_type=MESH)
    pl.semaphore_wait(barrier, len(peers))


def _gather_kernel(n, row_ref, out_ref, send_sem, recv_sem):
    me = lax.axis_index("feat")
    tok_index = lax.axis_index("tok")
    peers = [lax.rem(me + d, n) for d in range(1, n)]
    _greet(peers, tok_index)
    for peer in peers:
        pltpu.make_async_remote_copy(
            src_ref=row_ref, dst_ref=out_ref.at[me], send_sem=send_sem.at[peer],
            recv_sem=recv_sem.at[me], device_id=(tok_index, peer), device_id_type=MESH,
        ).start()
    out_ref[me] = row_ref[...]
    for peer in peers:
        pltpu.make_async_remote_copy(
            src_ref=row_ref, dst_ref=out_ref.at[peer], send_sem=send_sem.at[peer],
            recv_sem=recv_sem.at[peer], device_id=(tok_index, peer), device_id_type=MESH,
        ).wait_recv()
    for peer in peers:
        pltpu.make_async_remote_copy(
            src_ref=row_ref, dst_ref=out_ref.at[me], send_sem=send_sem.at[peer],
            recv_sem=recv_sem.at[me], device_id=(tok_index, peer), device_id_type=MESH,
        ).wait_send()


def gather_feat(row_block, n, collective_id):
    rows, width = row_block.shape
    return pl.pallas_call(
        functools.partial(_gather_kernel, n),
        out_shape=jax.ShapeDtypeStruct((n, rows, width), row_block.dtype),
        in_specs=[pl.BlockSpec(memory_space=pltpu.VMEM)],
        out_specs=pl.BlockSpec(memory_space=pltpu.VMEM),
        scratch_shapes=[pltpu.SemaphoreType.DMA((n,)), pltpu.SemaphoreType.DMA((n,))],
        compiler_params=pltpu.CompilerParams(collective_id=collective_id, has_side_effects=True),
    )(row_block).reshape(n * rows, width)


def _ring_gather(x_ref, out_ref, send_right, send_left, send_partner, recv_sem, feat_index, after_first=None,
                 hook=None, hook_step=1):
    tok_count = out_ref.shape[0]
    chips = tok_count // 2
    right_steps = chips // 2
    left_steps = chips - 1 - right_steps
    me = lax.axis_index("tok")
    chip = me // 2
    core = me % 2
    right = lax.rem(chip + 1, chips) * 2 + core
    left = lax.rem(chip + chips - 1, chips) * 2 + core
    partner = chip * 2 + (1 - core)

    def slot_of(offset):
        return lax.rem(chip + offset + 2 * chips, chips) * 2 + core

    def remote(src, slot, sem, target):
        return pltpu.make_async_remote_copy(
            src_ref=src, dst_ref=out_ref.at[slot], send_sem=sem, recv_sem=recv_sem.at[slot],
            device_id=(target, feat_index), device_id_type=MESH,
        )

    sends = []

    def forward_partner(src, slot):
        copy = remote(src, slot, send_partner.at[len(sends_partner)], partner)
        copy.start()
        sends_partner.append(copy)

    sends_partner = []
    out_ref[me] = x_ref[...]
    arrived = []
    for step in range(1, right_steps + 1):
        if step == 1:
            src_right = x_ref
            src_left = x_ref
        else:
            from_left = slot_of(-(step - 1))
            remote(x_ref, from_left, send_right.at[0], right).wait_recv()
            src_right = out_ref.at[from_left]
            arrived.append(from_left)
        copy = remote(src_right, slot_of(-(step - 1)), send_right.at[step - 1], right)
        copy.start()
        sends.append(copy)
        if step > 1 and step - 1 <= left_steps:
            from_right = slot_of(step - 1)
            remote(x_ref, from_right, send_left.at[0], left).wait_recv()
            src_left = out_ref.at[from_right]
            arrived.append(from_right)
        if step <= left_steps:
            copy = remote(src_left, slot_of(step - 1), send_left.at[step - 1], left)
            copy.start()
            sends.append(copy)
        if step == 1:
            if after_first is not None:
                after_first()
            forward_partner(x_ref, me)
        for slot in arrived:
            forward_partner(out_ref.at[slot], slot)
        arrived = []
        if hook is not None and step == min(hook_step, right_steps):
            hook()
    last_left = slot_of(-right_steps)
    remote(x_ref, last_left, send_right.at[0], right).wait_recv()
    forward_partner(out_ref.at[last_left], last_left)
    if left_steps >= 1 and left_steps + 1 > right_steps:
        last_right = slot_of(left_steps)
        remote(x_ref, last_right, send_left.at[0], left).wait_recv()
        forward_partner(out_ref.at[last_right], last_right)
    for other_chip in range(chips):
        remote(x_ref, other_chip * 2 + (1 - core), send_partner.at[0], partner).wait_recv()
    for copy in sends + sends_partner:
        copy.wait_send()


def _first_kernel(n, row_ref, weight_ref, out_ref, weight_out, send_sem, recv_sem,
                  send_right, send_left, send_partner, weight_recv):
    me = lax.axis_index("feat")
    tok_index = lax.axis_index("tok")
    chips = weight_out.shape[0] // 2
    chip = tok_index // 2
    core = tok_index % 2
    peers = [lax.rem(me + d, n) for d in range(1, n)]
    barrier = pltpu.get_barrier_semaphore()
    for peer in peers:
        pl.semaphore_signal(barrier, inc=1, device_id=(tok_index, peer), device_id_type=MESH)
    ring_peers = [
        lax.rem(chip + 1, chips) * 2 + core,
        lax.rem(chip + chips - 1, chips) * 2 + core,
        chip * 2 + (1 - core),
    ]
    for peer in ring_peers:
        pl.semaphore_signal(barrier, inc=1, device_id=(peer, me), device_id_type=MESH)
    pl.semaphore_wait(barrier, len(peers) + len(ring_peers))

    def start_rows():
        for peer in peers:
            pltpu.make_async_remote_copy(
                src_ref=row_ref, dst_ref=out_ref.at[me], send_sem=send_sem.at[peer],
                recv_sem=recv_sem.at[me], device_id=(tok_index, peer), device_id_type=MESH,
            ).start()

    _ring_gather(weight_ref, weight_out, send_right, send_left, send_partner, weight_recv, me, start_rows)
    out_ref[me] = row_ref[...]
    for peer in peers:
        pltpu.make_async_remote_copy(
            src_ref=row_ref, dst_ref=out_ref.at[peer], send_sem=send_sem.at[peer],
            recv_sem=recv_sem.at[peer], device_id=(tok_index, peer), device_id_type=MESH,
        ).wait_recv()
    for peer in peers:
        pltpu.make_async_remote_copy(
            src_ref=row_ref, dst_ref=out_ref.at[me], send_sem=send_sem.at[peer],
            recv_sem=recv_sem.at[me], device_id=(tok_index, peer), device_id_type=MESH,
        ).wait_send()


def first_exchange(row_block, weight_block, n, tok_count, collective_id):
    rows, width = row_block.shape
    weight_rows, weight_width = weight_block.shape
    chips = tok_count // 2
    gathered, weights = pl.pallas_call(
        functools.partial(_first_kernel, n),
        out_shape=(
            jax.ShapeDtypeStruct((n, rows, width), row_block.dtype),
            jax.ShapeDtypeStruct((tok_count, weight_rows, weight_width), weight_block.dtype),
        ),
        in_specs=[pl.BlockSpec(memory_space=pltpu.VMEM)] * 2,
        out_specs=(pl.BlockSpec(memory_space=pltpu.VMEM),) * 2,
        scratch_shapes=[
            pltpu.SemaphoreType.DMA((n,)),
            pltpu.SemaphoreType.DMA((n,)),
            pltpu.SemaphoreType.DMA((chips,)),
            pltpu.SemaphoreType.DMA((chips,)),
            pltpu.SemaphoreType.DMA((chips,)),
            pltpu.SemaphoreType.DMA((tok_count,)),
        ],
        compiler_params=pltpu.CompilerParams(collective_id=collective_id, has_side_effects=True),
    )(row_block, weight_block)
    return gathered.reshape(n * rows, width), weights


def _route_kernel(n, packed_ref, out_ref, send_sem, recv_sem):
    me = lax.axis_index("tok")
    feat_index = lax.axis_index("feat")
    peers = [lax.rem(me + d, n) for d in range(1, n)]
    barrier = pltpu.get_barrier_semaphore()
    for peer in peers:
        pl.semaphore_signal(barrier, inc=1, device_id=(peer, feat_index), device_id_type=MESH)
    pl.semaphore_wait(barrier, len(peers))
    for peer in peers:
        pltpu.make_async_remote_copy(
            src_ref=packed_ref.at[peer], dst_ref=out_ref.at[me], send_sem=send_sem.at[peer],
            recv_sem=recv_sem.at[me], device_id=(peer, feat_index), device_id_type=MESH,
        ).start()
    out_ref[me] = packed_ref[me]
    for peer in peers:
        pltpu.make_async_remote_copy(
            src_ref=packed_ref.at[peer], dst_ref=out_ref.at[peer], send_sem=send_sem.at[peer],
            recv_sem=recv_sem.at[peer], device_id=(peer, feat_index), device_id_type=MESH,
        ).wait_recv()
    for peer in peers:
        pltpu.make_async_remote_copy(
            src_ref=packed_ref.at[peer], dst_ref=out_ref.at[me], send_sem=send_sem.at[peer],
            recv_sem=recv_sem.at[me], device_id=(peer, feat_index), device_id_type=MESH,
        ).wait_send()


def route_exchange(packed, collective_id):
    n = packed.shape[0]
    return pl.pallas_call(
        functools.partial(_route_kernel, n),
        out_shape=jax.ShapeDtypeStruct(packed.shape, packed.dtype),
        in_specs=[pl.BlockSpec(memory_space=pltpu.VMEM)],
        out_specs=pl.BlockSpec(memory_space=pltpu.VMEM),
        scratch_shapes=[pltpu.SemaphoreType.DMA((n,)), pltpu.SemaphoreType.DMA((n,))],
        compiler_params=pltpu.CompilerParams(collective_id=collective_id, has_side_effects=True),
    )(packed)


def _mix_kernel(n, gain_row, part_ref, resid_ref, gain_ref, resid_out, out_ref, merged_out, held, mine_a,
                mine_b, mine_c, scatter_send, scatter_recv, gather_send, gather_recv):
    me = lax.axis_index("feat")
    tok_index = lax.axis_index("tok")
    peers = [lax.rem(me + d, n) for d in range(1, n)]
    _greet(peers, tok_index)
    piece = part_ref.shape[1] // 3
    halves = [(0, piece), (piece, piece), (2 * piece, piece)]
    mines = [mine_a, mine_b, mine_c]

    def scatter_copy(half, peer, slot):
        first, size = halves[half]
        return pltpu.make_async_remote_copy(
            src_ref=part_ref.at[peer, pl.ds(first, size)], dst_ref=held.at[slot, pl.ds(first, size)],
            send_sem=scatter_send.at[half, peer], recv_sem=scatter_recv.at[half, slot],
            device_id=(tok_index, peer), device_id_type=MESH,
        )

    def gather_copy(half, peer, slot):
        first, size = halves[half]
        return pltpu.make_async_remote_copy(
            src_ref=mines[half], dst_ref=out_ref.at[slot, pl.ds(first, size)],
            send_sem=gather_send.at[half, peer], recv_sem=gather_recv.at[half, slot],
            device_id=(tok_index, peer), device_id_type=MESH,
        )

    for half in range(len(halves)):
        for peer in peers:
            scatter_copy(half, peer, me).start()
    for half in range(len(halves)):
        first, size = halves[half]
        total = part_ref[me, first:first + size, :].astype(jnp.float32)
        for peer in peers:
            scatter_copy(half, peer, peer).wait_recv()
            total = total + held[peer, first:first + size, :].astype(jnp.float32)
        summed = (resid_ref[first:first + size, :].astype(jnp.float32) + total).astype(jnp.bfloat16)
        resid_out[first:first + size, :] = summed
        as_float = summed.astype(jnp.float32)
        center = jnp.mean(as_float, axis=-1, keepdims=True)
        spread = jnp.mean(jnp.square(as_float - center), axis=-1, keepdims=True)
        normed = ((as_float - center) * lax.rsqrt(spread + epsilon) * gain_ref[...].astype(jnp.float32)[None, :]).astype(jnp.bfloat16)
        mines[half][...] = normed
        out_ref[me, first:first + size, :] = normed
        for peer in peers:
            gather_copy(half, peer, me).start()
    for half in range(len(halves)):
        for peer in peers:
            gather_copy(half, peer, peer).wait_recv()
    group = 4
    width = out_ref.shape[2]
    row_count = n * out_ref.shape[1]
    rows = out_ref[...].astype(jnp.float32).reshape(row_count, width).astype(jnp.bfloat16)
    merged_index = lax.broadcasted_iota(jnp.int32, (row_count // group, row_count), 0)
    row_index = lax.broadcasted_iota(jnp.int32, (row_count // group, row_count), 1)
    for part in range(group):
        pick = (row_index == merged_index * group + part).astype(jnp.bfloat16)
        merged_out[:, part * width:(part + 1) * width] = jnp.dot(
            pick, rows, preferred_element_type=jnp.float32
        ).astype(jnp.bfloat16)
    for half in range(len(halves)):
        for peer in peers:
            scatter_copy(half, peer, me).wait_send()
            gather_copy(half, peer, me).wait_send()


def mix_feat(parts, resid, gains, gain_row, n, collective_id):
    _, rows, width = parts.shape
    new_resid, _, merged = pl.pallas_call(
        functools.partial(_mix_kernel, n, gain_row),
        out_shape=(
            jax.ShapeDtypeStruct((rows, width), jnp.bfloat16),
            jax.ShapeDtypeStruct((n, rows, width), jnp.bfloat16),
            jax.ShapeDtypeStruct((n * rows // 4, 4 * width), jnp.bfloat16),
        ),
        in_specs=[pl.BlockSpec(memory_space=pltpu.VMEM)] * 3,
        out_specs=(pl.BlockSpec(memory_space=pltpu.VMEM),) * 3,
        scratch_shapes=[
            pltpu.VMEM((n, rows, width), parts.dtype),
            pltpu.VMEM((rows // 3, width), jnp.bfloat16),
            pltpu.VMEM((rows // 3, width), jnp.bfloat16),
            pltpu.VMEM((rows // 3, width), jnp.bfloat16),
            pltpu.SemaphoreType.DMA((3, n)),
            pltpu.SemaphoreType.DMA((3, n)),
            pltpu.SemaphoreType.DMA((3, n)),
            pltpu.SemaphoreType.DMA((3, n)),
        ],
        compiler_params=pltpu.CompilerParams(collective_id=collective_id, has_side_effects=True),
    )(parts, resid, gains)
    return new_resid, merged


def _mix_ring_kernel(n, gain_row, part_ref, resid_ref, gain_ref, weight_ref, resid_out, out_ref, weight_flat,
                     weight_out, held, mine, scatter_send, scatter_recv, gather_send, gather_recv,
                     send_right, send_left, send_partner, weight_recv):
    me = lax.axis_index("feat")
    tok_index = lax.axis_index("tok")
    chips = weight_out.shape[0] // 2
    chip = tok_index // 2
    core = tok_index % 2
    peers = [lax.rem(me + d, n) for d in range(1, n)]
    barrier = pltpu.get_barrier_semaphore()
    for peer in peers:
        pl.semaphore_signal(barrier, inc=1, device_id=(tok_index, peer), device_id_type=MESH)
    ring_peers = [
        lax.rem(chip + 1, chips) * 2 + core,
        lax.rem(chip + chips - 1, chips) * 2 + core,
        chip * 2 + (1 - core),
    ]
    for peer in ring_peers:
        pl.semaphore_signal(barrier, inc=1, device_id=(peer, me), device_id_type=MESH)
    pl.semaphore_wait(barrier, len(peers) + len(ring_peers))

    def scatter_copy(peer, slot):
        return pltpu.make_async_remote_copy(
            src_ref=part_ref.at[peer], dst_ref=held.at[slot], send_sem=scatter_send.at[peer],
            recv_sem=scatter_recv.at[slot], device_id=(tok_index, peer), device_id_type=MESH,
        )

    def gather_copy(peer, slot):
        return pltpu.make_async_remote_copy(
            src_ref=mine, dst_ref=out_ref.at[slot], send_sem=gather_send.at[peer],
            recv_sem=gather_recv.at[slot], device_id=(tok_index, peer), device_id_type=MESH,
        )

    for peer in peers:
        scatter_copy(peer, me).start()

    def norm_and_send():
        total = part_ref[me].astype(jnp.float32)
        for peer in peers:
            scatter_copy(peer, peer).wait_recv()
            total = total + held[peer].astype(jnp.float32)
        summed = (resid_ref[...].astype(jnp.float32) + total).astype(jnp.bfloat16)
        resid_out[...] = summed
        as_float = summed.astype(jnp.float32)
        center = jnp.mean(as_float, axis=-1, keepdims=True)
        spread = jnp.mean(jnp.square(as_float - center), axis=-1, keepdims=True)
        normed = ((as_float - center) * lax.rsqrt(spread + epsilon) * gain_ref[...].astype(jnp.float32)[None, :]).astype(jnp.bfloat16)
        mine[...] = normed
        out_ref[me] = normed
        for peer in peers:
            gather_copy(peer, me).start()

    _ring_gather(weight_ref, weight_out, send_right, send_left, send_partner, weight_recv, me,
                 hook=norm_and_send, hook_step=5)
    block_rows = weight_out.shape[1]
    for slot in range(weight_out.shape[0]):
        weight_flat[slot * block_rows:(slot + 1) * block_rows, :] = weight_out[slot]
    for peer in peers:
        gather_copy(peer, peer).wait_recv()
    for peer in peers:
        scatter_copy(peer, me).wait_send()
        gather_copy(peer, me).wait_send()


def mix_ring_feat(parts, resid, gains, gain_row, weight_block, n, tok_count, collective_id):
    _, rows, width = parts.shape
    weight_rows, weight_width = weight_block.shape
    chips = tok_count // 2
    new_resid, gathered, weights = pl.pallas_call(
        functools.partial(_mix_ring_kernel, n, gain_row),
        out_shape=(
            jax.ShapeDtypeStruct((rows, width), jnp.bfloat16),
            jax.ShapeDtypeStruct((n, rows, width), jnp.bfloat16),
            jax.ShapeDtypeStruct((tok_count * weight_rows, weight_width), weight_block.dtype),
        ),
        in_specs=[pl.BlockSpec(memory_space=pltpu.VMEM)] * 4,
        out_specs=(pl.BlockSpec(memory_space=pltpu.VMEM),) * 3,
        scratch_shapes=[
            pltpu.VMEM((tok_count, weight_rows, weight_width), weight_block.dtype),
            pltpu.VMEM((n, rows, width), parts.dtype),
            pltpu.VMEM((rows, width), jnp.bfloat16),
            pltpu.SemaphoreType.DMA((n,)),
            pltpu.SemaphoreType.DMA((n,)),
            pltpu.SemaphoreType.DMA((n,)),
            pltpu.SemaphoreType.DMA((n,)),
            pltpu.SemaphoreType.DMA((chips,)),
            pltpu.SemaphoreType.DMA((chips,)),
            pltpu.SemaphoreType.DMA((chips,)),
            pltpu.SemaphoreType.DMA((tok_count,)),
        ],
        compiler_params=pltpu.CompilerParams(collective_id=collective_id, has_side_effects=True),
    )(parts, resid, gains, weight_block)
    return new_resid, gathered.reshape(n * rows, width), weights


def _norm_gather_kernel(n, gain_row, tok_ref, gain_ref, out_ref, mine, send_sem, recv_sem):
    me = lax.axis_index("feat")
    tok_index = lax.axis_index("tok")
    peers = [lax.rem(me + d, n) for d in range(1, n)]
    _greet(peers, tok_index)
    as_float = tok_ref[...].astype(jnp.float32)
    center = jnp.mean(as_float, axis=-1, keepdims=True)
    spread = jnp.mean(jnp.square(as_float - center), axis=-1, keepdims=True)
    normed = ((as_float - center) * lax.rsqrt(spread + epsilon) * gain_ref[...].astype(jnp.float32)[None, :]).astype(jnp.bfloat16)
    mine[...] = normed
    out_ref[me] = normed

    def copy(peer, slot):
        return pltpu.make_async_remote_copy(
            src_ref=mine, dst_ref=out_ref.at[slot], send_sem=send_sem.at[peer],
            recv_sem=recv_sem.at[slot], device_id=(tok_index, peer), device_id_type=MESH,
        )

    for peer in peers:
        copy(peer, me).start()
    for peer in peers:
        copy(peer, peer).wait_recv()
    for peer in peers:
        copy(peer, me).wait_send()


def norm_gather_feat(rows, gains, gain_row, n, collective_id):
    count, width = rows.shape
    return pl.pallas_call(
        functools.partial(_norm_gather_kernel, n, gain_row),
        out_shape=jax.ShapeDtypeStruct((n, count, width), jnp.bfloat16),
        in_specs=[pl.BlockSpec(memory_space=pltpu.VMEM)] * 2,
        out_specs=pl.BlockSpec(memory_space=pltpu.VMEM),
        scratch_shapes=[
            pltpu.VMEM((count, width), jnp.bfloat16),
            pltpu.SemaphoreType.DMA((n,)),
            pltpu.SemaphoreType.DMA((n,)),
        ],
        compiler_params=pltpu.CompilerParams(collective_id=collective_id, has_side_effects=True),
    )(rows, gains).reshape(n * count, width)


def _scatter_kernel(n, part_ref, out_ref, held, send_sem, recv_sem):
    me = lax.axis_index("feat")
    tok_index = lax.axis_index("tok")
    peers = [lax.rem(me + d, n) for d in range(1, n)]
    _greet(peers, tok_index)
    for peer in peers:
        pltpu.make_async_remote_copy(
            src_ref=part_ref.at[peer], dst_ref=held.at[me], send_sem=send_sem.at[peer],
            recv_sem=recv_sem.at[me], device_id=(tok_index, peer), device_id_type=MESH,
        ).start()
    total = part_ref[me].astype(jnp.float32)
    for peer in peers:
        pltpu.make_async_remote_copy(
            src_ref=part_ref.at[peer], dst_ref=held.at[peer], send_sem=send_sem.at[peer],
            recv_sem=recv_sem.at[peer], device_id=(tok_index, peer), device_id_type=MESH,
        ).wait_recv()
        total = total + held[peer].astype(jnp.float32)
    out_ref[...] = total
    for peer in peers:
        pltpu.make_async_remote_copy(
            src_ref=part_ref.at[peer], dst_ref=held.at[me], send_sem=send_sem.at[peer],
            recv_sem=recv_sem.at[me], device_id=(tok_index, peer), device_id_type=MESH,
        ).wait_send()


def scatter_feat(parts, n, collective_id):
    _, rows, width = parts.shape
    return pl.pallas_call(
        functools.partial(_scatter_kernel, n),
        out_shape=jax.ShapeDtypeStruct((rows, width), jnp.float32),
        in_specs=[pl.BlockSpec(memory_space=pltpu.VMEM)],
        out_specs=pl.BlockSpec(memory_space=pltpu.VMEM),
        scratch_shapes=[
            pltpu.VMEM((n, rows, width), parts.dtype),
            pltpu.SemaphoreType.DMA((n,)),
            pltpu.SemaphoreType.DMA((n,)),
        ],
        compiler_params=pltpu.CompilerParams(collective_id=collective_id, has_side_effects=True),
    )(parts)

MESH = pl.DeviceIdType.MESH
LEAST_UNITS = 4
MOST_UNITS = 16
HEAD_DIM = 88


epsilon = 1e-06


def layer_norm(row_block, gain_row):
    as_float = row_block.astype(jnp.float32)
    center = jnp.mean(as_float, axis=-1, keepdims=True)
    spread = jnp.mean(jnp.square(as_float - center), axis=-1, keepdims=True)
    scaled = (as_float - center) * lax.rsqrt(spread + epsilon) * gain_row.astype(jnp.float32)
    return scaled.astype(jnp.bfloat16)


def project_rows(row_block, weight_block, collective_id):
    n = lax.axis_size("feat")
    return jnp.dot(
        gather_feat(row_block, n, collective_id),
        weight_block,
        preferred_element_type=jnp.float32,
    )


def scatter_rows(left_rows, right_rows, collective_id):
    n = lax.axis_size("feat")
    parts = jnp.dot(left_rows, right_rows, preferred_element_type=jnp.float32).astype(jnp.bfloat16)
    return scatter_feat(parts.reshape(n, parts.shape[0] // n, parts.shape[1]), n, collective_id)


def early_weights(weight_up, weight_down):
    return (weight_up, weight_down)


def upper_weight(fetched):
    return lax.all_gather(fetched[0], "tok", axis=0, tiled=True)


def lower_weight(fetched):
    return lax.all_gather(fetched[1], "tok", axis=1, tiled=True)


def attend(projected, segment_ids, head_count):
    token_count = projected.shape[0]
    parts_all = projected.reshape(token_count, 3, head_count, HEAD_DIM)
    queries = (parts_all[:, 0] * HEAD_DIM ** (-0.5)).astype(jnp.bfloat16)
    keys_here = parts_all[:, 1].astype(jnp.bfloat16)
    values_here = parts_all[:, 2].astype(jnp.bfloat16)
    scores = jnp.einsum("qhd,khd->hqk", queries, keys_here, preferred_element_type=jnp.float32)
    same_segment = segment_ids[:, None] == segment_ids[None, :]
    scores = jnp.where(same_segment[None, :, :], scores, -1e30)
    highest = jnp.max(scores, axis=-1, keepdims=True)
    raised = jnp.exp(scores - highest)
    weights_soft = (raised / jnp.sum(raised, axis=-1, keepdims=True)).astype(jnp.bfloat16)
    attended = jnp.einsum(
        "hqk,khd->qhd", weights_soft, values_here, preferred_element_type=jnp.float32
    )
    return attended.astype(jnp.bfloat16).reshape(token_count, head_count * HEAD_DIM)


def route_rows(embedded, segment_ids, owners):
    merged_count = embedded.shape[0]
    peer_count = owners.shape[0]
    least_units = max(LEAST_UNITS, (merged_count + peer_count - 1) // peer_count)
    slot_count = max(MOST_UNITS, 2 * least_units)
    first_ids = segment_ids.reshape(merged_count, 4)[:, 0]
    id_base = lax.axis_index("tok") * peer_count
    local_index = first_ids - id_base
    owner_pick = local_index[:, None] == jnp.arange(peer_count, dtype=jnp.int32)[None, :]
    owner_of = jnp.sum(jnp.where(owner_pick, owners[None, :], 0), axis=1)
    row_index = jnp.arange(merged_count, dtype=jnp.int32)
    earlier = (row_index[None, :] < row_index[:, None]) & (first_ids[None, :] == first_ids[:, None])
    within = jnp.sum(earlier.astype(jnp.int32), axis=1)
    target = owner_of * slot_count + within
    select = (
        jnp.arange(peer_count * slot_count, dtype=jnp.int32)[:, None] == target[None, :]
    ).astype(jnp.bfloat16)
    packed = jnp.dot(select, embedded, preferred_element_type=jnp.float32).astype(jnp.bfloat16)
    packed = packed.reshape(peer_count, slot_count, embedded.shape[1])
    received = route_exchange(packed, 5)
    return received.reshape(peer_count * slot_count, embedded.shape[1])


def body(
    tokens,
    segment_ids,
    owners,
    project_in,
    project_out,
    weight_up,
    weight_down,
    weight_merge,
    gain_attend,
    gain_hidden,
    gain_final,
):
    model_width = tokens.shape[1]
    head_count = project_in.shape[2] // HEAD_DIM
    units = weight_up.shape[1]
    feat_count = lax.axis_size("feat")
    tok_count = lax.axis_size("tok")
    flat_in = project_in.reshape(model_width, 3 * project_in.shape[2])
    local_count = tokens.shape[0]
    stacked = jnp.concatenate([weight_up, weight_down.T], axis=1)
    gathered = norm_gather_feat(tokens, gain_attend, 0, feat_count, 0)
    projected = jnp.dot(gathered, flat_in, preferred_element_type=jnp.float32)
    attended = attend(projected, segment_ids, head_count)
    attn_parts = jnp.dot(attended, project_out, preferred_element_type=jnp.float32).astype(jnp.bfloat16)
    second, hidden_rows, weights = mix_ring_feat(
        attn_parts.reshape(feat_count, local_count, model_width), tokens, gain_hidden, 1, stacked,
        feat_count, tok_count, 1,
    )
    both = weights
    upper = both[:, :units]
    lower_t = both[:, units:]
    hidden = jax.nn.gelu(
        jnp.dot(hidden_rows, upper, preferred_element_type=jnp.float32), approximate=False
    ).astype(jnp.bfloat16)
    down_parts = lax.dot_general(
        hidden, lower_t, (((1,), (1,)), ((), ())), preferred_element_type=jnp.float32
    ).astype(jnp.bfloat16)
    _, merged = mix_feat(
        down_parts.reshape(feat_count, local_count, model_width), second, gain_final, 2, feat_count, 3
    )
    embedded = jnp.dot(merged, weight_merge, preferred_element_type=jnp.float32).astype(jnp.bfloat16)
    return route_rows(embedded, segment_ids, owners)


def solution(mesh):
    return jax.shard_map(
        body,
        mesh=mesh,
        in_specs=(
            P(("tok", "feat"), None),
            P("tok"),
            P("tok"),
            P(None, None, "feat"),
            P("feat", None),
            P("tok", "feat"),
            P("feat", "tok"),
            P(None, "feat"),
            P(),
            P(),
            P(),
        ),
        out_specs=P("tok", "feat"),
        check_vma=False,
    )
```

```python
import functools
import jax
import jax.numpy as jnp
from jax import lax
from jax.experimental import pallas as pl
from jax.experimental.pallas import tpu as pltpu
from jax.sharding import PartitionSpec as P


def _greet(peers, tok_index):
    barrier = pltpu.get_barrier_semaphore()
    for peer in peers:
        pl.semaphore_signal(barrier, inc=1, device_id=(tok_index, peer), device_id_type=MESH)
    pl.semaphore_wait(barrier, len(peers))


def _gather_kernel(n, row_ref, out_ref, send_sem, recv_sem):
    me = lax.axis_index("feat")
    tok_index = lax.axis_index("tok")
    peers = [lax.rem(me + d, n) for d in range(1, n)]
    _greet(peers, tok_index)
    for peer in peers:
        pltpu.make_async_remote_copy(
            src_ref=row_ref, dst_ref=out_ref.at[me], send_sem=send_sem.at[peer],
            recv_sem=recv_sem.at[me], device_id=(tok_index, peer), device_id_type=MESH,
        ).start()
    out_ref[me] = row_ref[...]
    for peer in peers:
        pltpu.make_async_remote_copy(
            src_ref=row_ref, dst_ref=out_ref.at[peer], send_sem=send_sem.at[peer],
            recv_sem=recv_sem.at[peer], device_id=(tok_index, peer), device_id_type=MESH,
        ).wait_recv()
    for peer in peers:
        pltpu.make_async_remote_copy(
            src_ref=row_ref, dst_ref=out_ref.at[me], send_sem=send_sem.at[peer],
            recv_sem=recv_sem.at[me], device_id=(tok_index, peer), device_id_type=MESH,
        ).wait_send()


def gather_feat(row_block, n, collective_id):
    rows, width = row_block.shape
    return pl.pallas_call(
        functools.partial(_gather_kernel, n),
        out_shape=jax.ShapeDtypeStruct((n, rows, width), row_block.dtype),
        in_specs=[pl.BlockSpec(memory_space=pltpu.VMEM)],
        out_specs=pl.BlockSpec(memory_space=pltpu.VMEM),
        scratch_shapes=[pltpu.SemaphoreType.DMA((n,)), pltpu.SemaphoreType.DMA((n,))],
        compiler_params=pltpu.CompilerParams(collective_id=collective_id, has_side_effects=True),
    )(row_block).reshape(n * rows, width)


def _ring_gather(x_ref, out_ref, send_right, send_left, send_partner, recv_sem, feat_index, after_first=None,
                 hook=None, hook_step=1):
    tok_count = out_ref.shape[0]
    chips = tok_count // 2
    right_steps = chips // 2
    left_steps = chips - 1 - right_steps
    me = lax.axis_index("tok")
    chip = me // 2
    core = me % 2
    right = lax.rem(chip + 1, chips) * 2 + core
    left = lax.rem(chip + chips - 1, chips) * 2 + core
    partner = chip * 2 + (1 - core)

    def slot_of(offset):
        return lax.rem(chip + offset + 2 * chips, chips) * 2 + core

    def remote(src, slot, sem, target):
        return pltpu.make_async_remote_copy(
            src_ref=src, dst_ref=out_ref.at[slot], send_sem=sem, recv_sem=recv_sem.at[slot],
            device_id=(target, feat_index), device_id_type=MESH,
        )

    sends = []

    def forward_partner(src, slot):
        copy = remote(src, slot, send_partner.at[len(sends_partner)], partner)
        copy.start()
        sends_partner.append(copy)

    sends_partner = []
    out_ref[me] = x_ref[...]
    arrived = []
    for step in range(1, right_steps + 1):
        if step == 1:
            src_right = x_ref
            src_left = x_ref
        else:
            from_left = slot_of(-(step - 1))
            remote(x_ref, from_left, send_right.at[0], right).wait_recv()
            src_right = out_ref.at[from_left]
            arrived.append(from_left)
        copy = remote(src_right, slot_of(-(step - 1)), send_right.at[step - 1], right)
        copy.start()
        sends.append(copy)
        if step > 1 and step - 1 <= left_steps:
            from_right = slot_of(step - 1)
            remote(x_ref, from_right, send_left.at[0], left).wait_recv()
            src_left = out_ref.at[from_right]
            arrived.append(from_right)
        if step <= left_steps:
            copy = remote(src_left, slot_of(step - 1), send_left.at[step - 1], left)
            copy.start()
            sends.append(copy)
        if step == 1:
            if after_first is not None:
                after_first()
            forward_partner(x_ref, me)
        for slot in arrived:
            forward_partner(out_ref.at[slot], slot)
        arrived = []
        if hook is not None and step == min(hook_step, right_steps):
            hook()
    last_left = slot_of(-right_steps)
    remote(x_ref, last_left, send_right.at[0], right).wait_recv()
    forward_partner(out_ref.at[last_left], last_left)
    if left_steps >= 1 and left_steps + 1 > right_steps:
        last_right = slot_of(left_steps)
        remote(x_ref, last_right, send_left.at[0], left).wait_recv()
        forward_partner(out_ref.at[last_right], last_right)
    for other_chip in range(chips):
        remote(x_ref, other_chip * 2 + (1 - core), send_partner.at[0], partner).wait_recv()
    for copy in sends + sends_partner:
        copy.wait_send()


def _first_kernel(n, row_ref, weight_ref, out_ref, weight_out, send_sem, recv_sem,
                  send_right, send_left, send_partner, weight_recv):
    me = lax.axis_index("feat")
    tok_index = lax.axis_index("tok")
    chips = weight_out.shape[0] // 2
    chip = tok_index // 2
    core = tok_index % 2
    peers = [lax.rem(me + d, n) for d in range(1, n)]
    barrier = pltpu.get_barrier_semaphore()
    for peer in peers:
        pl.semaphore_signal(barrier, inc=1, device_id=(tok_index, peer), device_id_type=MESH)
    ring_peers = [
        lax.rem(chip + 1, chips) * 2 + core,
        lax.rem(chip + chips - 1, chips) * 2 + core,
        chip * 2 + (1 - core),
    ]
    for peer in ring_peers:
        pl.semaphore_signal(barrier, inc=1, device_id=(peer, me), device_id_type=MESH)
    pl.semaphore_wait(barrier, len(peers) + len(ring_peers))

    def start_rows():
        for peer in peers:
            pltpu.make_async_remote_copy(
                src_ref=row_ref, dst_ref=out_ref.at[me], send_sem=send_sem.at[peer],
                recv_sem=recv_sem.at[me], device_id=(tok_index, peer), device_id_type=MESH,
            ).start()

    _ring_gather(weight_ref, weight_out, send_right, send_left, send_partner, weight_recv, me, start_rows)
    out_ref[me] = row_ref[...]
    for peer in peers:
        pltpu.make_async_remote_copy(
            src_ref=row_ref, dst_ref=out_ref.at[peer], send_sem=send_sem.at[peer],
            recv_sem=recv_sem.at[peer], device_id=(tok_index, peer), device_id_type=MESH,
        ).wait_recv()
    for peer in peers:
        pltpu.make_async_remote_copy(
            src_ref=row_ref, dst_ref=out_ref.at[me], send_sem=send_sem.at[peer],
            recv_sem=recv_sem.at[me], device_id=(tok_index, peer), device_id_type=MESH,
        ).wait_send()


def first_exchange(row_block, weight_block, n, tok_count, collective_id):
    rows, width = row_block.shape
    weight_rows, weight_width = weight_block.shape
    chips = tok_count // 2
    gathered, weights = pl.pallas_call(
        functools.partial(_first_kernel, n),
        out_shape=(
            jax.ShapeDtypeStruct((n, rows, width), row_block.dtype),
            jax.ShapeDtypeStruct((tok_count, weight_rows, weight_width), weight_block.dtype),
        ),
        in_specs=[pl.BlockSpec(memory_space=pltpu.VMEM)] * 2,
        out_specs=(pl.BlockSpec(memory_space=pltpu.VMEM),) * 2,
        scratch_shapes=[
            pltpu.SemaphoreType.DMA((n,)),
            pltpu.SemaphoreType.DMA((n,)),
            pltpu.SemaphoreType.DMA((chips,)),
            pltpu.SemaphoreType.DMA((chips,)),
            pltpu.SemaphoreType.DMA((chips,)),
            pltpu.SemaphoreType.DMA((tok_count,)),
        ],
        compiler_params=pltpu.CompilerParams(collective_id=collective_id, has_side_effects=True),
    )(row_block, weight_block)
    return gathered.reshape(n * rows, width), weights


def _route_kernel(n, packed_ref, out_ref, send_sem, recv_sem):
    me = lax.axis_index("tok")
    feat_index = lax.axis_index("feat")
    order = sorted(range(1, n), key=lambda d: -min(d, n - d))
    peers = [lax.rem(me + d, n) for d in order]
    barrier = pltpu.get_barrier_semaphore()
    for peer in peers:
        pl.semaphore_signal(barrier, inc=1, device_id=(peer, feat_index), device_id_type=MESH)
    pl.semaphore_wait(barrier, len(peers))
    for peer in peers:
        pltpu.make_async_remote_copy(
            src_ref=packed_ref.at[peer], dst_ref=out_ref.at[me], send_sem=send_sem.at[peer],
            recv_sem=recv_sem.at[me], device_id=(peer, feat_index), device_id_type=MESH,
        ).start()
    out_ref[me] = packed_ref[me]
    for peer in peers:
        pltpu.make_async_remote_copy(
            src_ref=packed_ref.at[peer], dst_ref=out_ref.at[peer], send_sem=send_sem.at[peer],
            recv_sem=recv_sem.at[peer], device_id=(peer, feat_index), device_id_type=MESH,
        ).wait_recv()
    for peer in peers:
        pltpu.make_async_remote_copy(
            src_ref=packed_ref.at[peer], dst_ref=out_ref.at[me], send_sem=send_sem.at[peer],
            recv_sem=recv_sem.at[me], device_id=(peer, feat_index), device_id_type=MESH,
        ).wait_send()


def route_exchange(packed, collective_id):
    n = packed.shape[0]
    return pl.pallas_call(
        functools.partial(_route_kernel, n),
        out_shape=jax.ShapeDtypeStruct(packed.shape, packed.dtype),
        in_specs=[pl.BlockSpec(memory_space=pltpu.VMEM)],
        out_specs=pl.BlockSpec(memory_space=pltpu.VMEM),
        scratch_shapes=[pltpu.SemaphoreType.DMA((n,)), pltpu.SemaphoreType.DMA((n,))],
        compiler_params=pltpu.CompilerParams(collective_id=collective_id, has_side_effects=True),
    )(packed)


def _mix_kernel(n, gain_row, part_ref, resid_ref, gain_ref, resid_out, out_ref, merged_out, held, mine_a,
                mine_b, mine_c, scatter_send, scatter_recv, gather_send, gather_recv):
    me = lax.axis_index("feat")
    tok_index = lax.axis_index("tok")
    peers = [lax.rem(me + d, n) for d in range(1, n)]
    _greet(peers, tok_index)
    piece = part_ref.shape[1] // 3
    halves = [(0, piece), (piece, piece), (2 * piece, piece)]
    mines = [mine_a, mine_b, mine_c]

    def scatter_copy(half, peer, slot):
        first, size = halves[half]
        return pltpu.make_async_remote_copy(
            src_ref=part_ref.at[peer, pl.ds(first, size)], dst_ref=held.at[slot, pl.ds(first, size)],
            send_sem=scatter_send.at[half, peer], recv_sem=scatter_recv.at[half, slot],
            device_id=(tok_index, peer), device_id_type=MESH,
        )

    def gather_copy(half, peer, slot):
        first, size = halves[half]
        return pltpu.make_async_remote_copy(
            src_ref=mines[half], dst_ref=out_ref.at[slot, pl.ds(first, size)],
            send_sem=gather_send.at[half, peer], recv_sem=gather_recv.at[half, slot],
            device_id=(tok_index, peer), device_id_type=MESH,
        )

    for half in range(len(halves)):
        for peer in peers:
            scatter_copy(half, peer, me).start()
    for half in range(len(halves)):
        first, size = halves[half]
        total = part_ref[me, first:first + size, :].astype(jnp.float32)
        for peer in peers:
            scatter_copy(half, peer, peer).wait_recv()
            total = total + held[peer, first:first + size, :].astype(jnp.float32)
        summed = (resid_ref[first:first + size, :].astype(jnp.float32) + total).astype(jnp.bfloat16)
        resid_out[first:first + size, :] = summed
        as_float = summed.astype(jnp.float32)
        center = jnp.mean(as_float, axis=-1, keepdims=True)
        spread = jnp.mean(jnp.square(as_float - center), axis=-1, keepdims=True)
        normed = ((as_float - center) * lax.rsqrt(spread + epsilon) * gain_ref[...].astype(jnp.float32)[None, :]).astype(jnp.bfloat16)
        mines[half][...] = normed
        out_ref[me, first:first + size, :] = normed
        for peer in peers:
            gather_copy(half, peer, me).start()
    for half in range(len(halves)):
        for peer in peers:
            gather_copy(half, peer, peer).wait_recv()
    group = 4
    width = out_ref.shape[2]
    row_count = n * out_ref.shape[1]
    rows = out_ref[...].astype(jnp.float32).reshape(row_count, width).astype(jnp.bfloat16)
    merged_index = lax.broadcasted_iota(jnp.int32, (row_count // group, row_count), 0)
    row_index = lax.broadcasted_iota(jnp.int32, (row_count // group, row_count), 1)
    for part in range(group):
        pick = (row_index == merged_index * group + part).astype(jnp.bfloat16)
        merged_out[:, part * width:(part + 1) * width] = jnp.dot(
            pick, rows, preferred_element_type=jnp.float32
        ).astype(jnp.bfloat16)
    for half in range(len(halves)):
        for peer in peers:
            scatter_copy(half, peer, me).wait_send()
            gather_copy(half, peer, me).wait_send()


def mix_feat(parts, resid, gains, gain_row, n, collective_id):
    _, rows, width = parts.shape
    new_resid, _, merged = pl.pallas_call(
        functools.partial(_mix_kernel, n, gain_row),
        out_shape=(
            jax.ShapeDtypeStruct((rows, width), jnp.bfloat16),
            jax.ShapeDtypeStruct((n, rows, width), jnp.bfloat16),
            jax.ShapeDtypeStruct((n * rows // 4, 4 * width), jnp.bfloat16),
        ),
        in_specs=[pl.BlockSpec(memory_space=pltpu.VMEM)] * 3,
        out_specs=(pl.BlockSpec(memory_space=pltpu.VMEM),) * 3,
        scratch_shapes=[
            pltpu.VMEM((n, rows, width), parts.dtype),
            pltpu.VMEM((rows // 3, width), jnp.bfloat16),
            pltpu.VMEM((rows // 3, width), jnp.bfloat16),
            pltpu.VMEM((rows // 3, width), jnp.bfloat16),
            pltpu.SemaphoreType.DMA((3, n)),
            pltpu.SemaphoreType.DMA((3, n)),
            pltpu.SemaphoreType.DMA((3, n)),
            pltpu.SemaphoreType.DMA((3, n)),
        ],
        compiler_params=pltpu.CompilerParams(collective_id=collective_id, has_side_effects=True),
    )(parts, resid, gains)
    return new_resid, merged


def _mix_ring_kernel(n, gain_row, part_ref, resid_ref, gain_ref, weight_ref, resid_out, out_ref, weight_flat,
                     weight_out, held, mine, scatter_send, scatter_recv, gather_send, gather_recv,
                     send_right, send_left, send_partner, weight_recv):
    me = lax.axis_index("feat")
    tok_index = lax.axis_index("tok")
    chips = weight_out.shape[0] // 2
    chip = tok_index // 2
    core = tok_index % 2
    peers = [lax.rem(me + d, n) for d in range(1, n)]
    barrier = pltpu.get_barrier_semaphore()
    for peer in peers:
        pl.semaphore_signal(barrier, inc=1, device_id=(tok_index, peer), device_id_type=MESH)
    ring_peers = [
        lax.rem(chip + 1, chips) * 2 + core,
        lax.rem(chip + chips - 1, chips) * 2 + core,
        chip * 2 + (1 - core),
    ]
    for peer in ring_peers:
        pl.semaphore_signal(barrier, inc=1, device_id=(peer, me), device_id_type=MESH)
    pl.semaphore_wait(barrier, len(peers) + len(ring_peers))

    def scatter_copy(peer, slot):
        return pltpu.make_async_remote_copy(
            src_ref=part_ref.at[peer], dst_ref=held.at[slot], send_sem=scatter_send.at[peer],
            recv_sem=scatter_recv.at[slot], device_id=(tok_index, peer), device_id_type=MESH,
        )

    def gather_copy(peer, slot):
        return pltpu.make_async_remote_copy(
            src_ref=mine, dst_ref=out_ref.at[slot], send_sem=gather_send.at[peer],
            recv_sem=gather_recv.at[slot], device_id=(tok_index, peer), device_id_type=MESH,
        )

    for peer in peers:
        scatter_copy(peer, me).start()

    def norm_and_send():
        total = part_ref[me].astype(jnp.float32)
        for peer in peers:
            scatter_copy(peer, peer).wait_recv()
            total = total + held[peer].astype(jnp.float32)
        summed = (resid_ref[...].astype(jnp.float32) + total).astype(jnp.bfloat16)
        resid_out[...] = summed
        as_float = summed.astype(jnp.float32)
        center = jnp.mean(as_float, axis=-1, keepdims=True)
        spread = jnp.mean(jnp.square(as_float - center), axis=-1, keepdims=True)
        normed = ((as_float - center) * lax.rsqrt(spread + epsilon) * gain_ref[...].astype(jnp.float32)[None, :]).astype(jnp.bfloat16)
        mine[...] = normed
        out_ref[me] = normed
        for peer in peers:
            gather_copy(peer, me).start()

    _ring_gather(weight_ref, weight_out, send_right, send_left, send_partner, weight_recv, me,
                 hook=norm_and_send, hook_step=5)
    block_rows = weight_out.shape[1]
    for slot in range(weight_out.shape[0]):
        weight_flat[slot * block_rows:(slot + 1) * block_rows, :] = weight_out[slot]
    for peer in peers:
        gather_copy(peer, peer).wait_recv()
    for peer in peers:
        scatter_copy(peer, me).wait_send()
        gather_copy(peer, me).wait_send()


def mix_ring_feat(parts, resid, gains, gain_row, weight_block, n, tok_count, collective_id):
    _, rows, width = parts.shape
    weight_rows, weight_width = weight_block.shape
    chips = tok_count // 2
    new_resid, gathered, weights = pl.pallas_call(
        functools.partial(_mix_ring_kernel, n, gain_row),
        out_shape=(
            jax.ShapeDtypeStruct((rows, width), jnp.bfloat16),
            jax.ShapeDtypeStruct((n, rows, width), jnp.bfloat16),
            jax.ShapeDtypeStruct((tok_count * weight_rows, weight_width), weight_block.dtype),
        ),
        in_specs=[pl.BlockSpec(memory_space=pltpu.VMEM)] * 4,
        out_specs=(pl.BlockSpec(memory_space=pltpu.VMEM),) * 3,
        scratch_shapes=[
            pltpu.VMEM((tok_count, weight_rows, weight_width), weight_block.dtype),
            pltpu.VMEM((n, rows, width), parts.dtype),
            pltpu.VMEM((rows, width), jnp.bfloat16),
            pltpu.SemaphoreType.DMA((n,)),
            pltpu.SemaphoreType.DMA((n,)),
            pltpu.SemaphoreType.DMA((n,)),
            pltpu.SemaphoreType.DMA((n,)),
            pltpu.SemaphoreType.DMA((chips,)),
            pltpu.SemaphoreType.DMA((chips,)),
            pltpu.SemaphoreType.DMA((chips,)),
            pltpu.SemaphoreType.DMA((tok_count,)),
        ],
        compiler_params=pltpu.CompilerParams(collective_id=collective_id, has_side_effects=True),
    )(parts, resid, gains, weight_block)
    return new_resid, gathered.reshape(n * rows, width), weights


def _norm_gather_kernel(n, gain_row, tok_ref, gain_ref, out_ref, mine, send_sem, recv_sem):
    me = lax.axis_index("feat")
    tok_index = lax.axis_index("tok")
    peers = [lax.rem(me + d, n) for d in range(1, n)]
    _greet(peers, tok_index)
    as_float = tok_ref[...].astype(jnp.float32)
    center = jnp.mean(as_float, axis=-1, keepdims=True)
    spread = jnp.mean(jnp.square(as_float - center), axis=-1, keepdims=True)
    normed = ((as_float - center) * lax.rsqrt(spread + epsilon) * gain_ref[...].astype(jnp.float32)[None, :]).astype(jnp.bfloat16)
    mine[...] = normed
    out_ref[me] = normed

    def copy(peer, slot):
        return pltpu.make_async_remote_copy(
            src_ref=mine, dst_ref=out_ref.at[slot], send_sem=send_sem.at[peer],
            recv_sem=recv_sem.at[slot], device_id=(tok_index, peer), device_id_type=MESH,
        )

    for peer in peers:
        copy(peer, me).start()
    for peer in peers:
        copy(peer, peer).wait_recv()
    for peer in peers:
        copy(peer, me).wait_send()


def norm_gather_feat(rows, gains, gain_row, n, collective_id):
    count, width = rows.shape
    return pl.pallas_call(
        functools.partial(_norm_gather_kernel, n, gain_row),
        out_shape=jax.ShapeDtypeStruct((n, count, width), jnp.bfloat16),
        in_specs=[pl.BlockSpec(memory_space=pltpu.VMEM)] * 2,
        out_specs=pl.BlockSpec(memory_space=pltpu.VMEM),
        scratch_shapes=[
            pltpu.VMEM((count, width), jnp.bfloat16),
            pltpu.SemaphoreType.DMA((n,)),
            pltpu.SemaphoreType.DMA((n,)),
        ],
        compiler_params=pltpu.CompilerParams(collective_id=collective_id, has_side_effects=True),
    )(rows, gains).reshape(n * count, width)


def _scatter_kernel(n, part_ref, out_ref, held, send_sem, recv_sem):
    me = lax.axis_index("feat")
    tok_index = lax.axis_index("tok")
    peers = [lax.rem(me + d, n) for d in range(1, n)]
    _greet(peers, tok_index)
    for peer in peers:
        pltpu.make_async_remote_copy(
            src_ref=part_ref.at[peer], dst_ref=held.at[me], send_sem=send_sem.at[peer],
            recv_sem=recv_sem.at[me], device_id=(tok_index, peer), device_id_type=MESH,
        ).start()
    total = part_ref[me].astype(jnp.float32)
    for peer in peers:
        pltpu.make_async_remote_copy(
            src_ref=part_ref.at[peer], dst_ref=held.at[peer], send_sem=send_sem.at[peer],
            recv_sem=recv_sem.at[peer], device_id=(tok_index, peer), device_id_type=MESH,
        ).wait_recv()
        total = total + held[peer].astype(jnp.float32)
    out_ref[...] = total
    for peer in peers:
        pltpu.make_async_remote_copy(
            src_ref=part_ref.at[peer], dst_ref=held.at[me], send_sem=send_sem.at[peer],
            recv_sem=recv_sem.at[me], device_id=(tok_index, peer), device_id_type=MESH,
        ).wait_send()


def scatter_feat(parts, n, collective_id):
    _, rows, width = parts.shape
    return pl.pallas_call(
        functools.partial(_scatter_kernel, n),
        out_shape=jax.ShapeDtypeStruct((rows, width), jnp.float32),
        in_specs=[pl.BlockSpec(memory_space=pltpu.VMEM)],
        out_specs=pl.BlockSpec(memory_space=pltpu.VMEM),
        scratch_shapes=[
            pltpu.VMEM((n, rows, width), parts.dtype),
            pltpu.SemaphoreType.DMA((n,)),
            pltpu.SemaphoreType.DMA((n,)),
        ],
        compiler_params=pltpu.CompilerParams(collective_id=collective_id, has_side_effects=True),
    )(parts)

MESH = pl.DeviceIdType.MESH
LEAST_UNITS = 4
MOST_UNITS = 16
HEAD_DIM = 88


epsilon = 1e-06


def layer_norm(row_block, gain_row):
    as_float = row_block.astype(jnp.float32)
    center = jnp.mean(as_float, axis=-1, keepdims=True)
    spread = jnp.mean(jnp.square(as_float - center), axis=-1, keepdims=True)
    scaled = (as_float - center) * lax.rsqrt(spread + epsilon) * gain_row.astype(jnp.float32)
    return scaled.astype(jnp.bfloat16)


def project_rows(row_block, weight_block, collective_id):
    n = lax.axis_size("feat")
    return jnp.dot(
        gather_feat(row_block, n, collective_id),
        weight_block,
        preferred_element_type=jnp.float32,
    )


def scatter_rows(left_rows, right_rows, collective_id):
    n = lax.axis_size("feat")
    parts = jnp.dot(left_rows, right_rows, preferred_element_type=jnp.float32).astype(jnp.bfloat16)
    return scatter_feat(parts.reshape(n, parts.shape[0] // n, parts.shape[1]), n, collective_id)


def early_weights(weight_up, weight_down):
    return (weight_up, weight_down)


def upper_weight(fetched):
    return lax.all_gather(fetched[0], "tok", axis=0, tiled=True)


def lower_weight(fetched):
    return lax.all_gather(fetched[1], "tok", axis=1, tiled=True)


def attend(projected, segment_ids, head_count):
    token_count = projected.shape[0]
    parts_all = projected.reshape(token_count, 3, head_count, HEAD_DIM)
    queries = (parts_all[:, 0] * HEAD_DIM ** (-0.5)).astype(jnp.bfloat16)
    keys_here = parts_all[:, 1].astype(jnp.bfloat16)
    values_here = parts_all[:, 2].astype(jnp.bfloat16)
    scores = jnp.einsum("qhd,khd->hqk", queries, keys_here, preferred_element_type=jnp.float32)
    same_segment = segment_ids[:, None] == segment_ids[None, :]
    scores = jnp.where(same_segment[None, :, :], scores, -1e30)
    highest = jnp.max(scores, axis=-1, keepdims=True)
    raised = jnp.exp(scores - highest)
    weights_soft = (raised / jnp.sum(raised, axis=-1, keepdims=True)).astype(jnp.bfloat16)
    attended = jnp.einsum(
        "hqk,khd->qhd", weights_soft, values_here, preferred_element_type=jnp.float32
    )
    return attended.astype(jnp.bfloat16).reshape(token_count, head_count * HEAD_DIM)


def route_rows(embedded, segment_ids, owners):
    merged_count = embedded.shape[0]
    peer_count = owners.shape[0]
    least_units = max(LEAST_UNITS, (merged_count + peer_count - 1) // peer_count)
    slot_count = max(MOST_UNITS, 2 * least_units)
    first_ids = segment_ids.reshape(merged_count, 4)[:, 0]
    id_base = lax.axis_index("tok") * peer_count
    local_index = first_ids - id_base
    owner_pick = local_index[:, None] == jnp.arange(peer_count, dtype=jnp.int32)[None, :]
    owner_of = jnp.sum(jnp.where(owner_pick, owners[None, :], 0), axis=1)
    row_index = jnp.arange(merged_count, dtype=jnp.int32)
    earlier = (row_index[None, :] < row_index[:, None]) & (first_ids[None, :] == first_ids[:, None])
    within = jnp.sum(earlier.astype(jnp.int32), axis=1)
    target = owner_of * slot_count + within
    select = (
        jnp.arange(peer_count * slot_count, dtype=jnp.int32)[:, None] == target[None, :]
    ).astype(jnp.bfloat16)
    packed = jnp.dot(select, embedded, preferred_element_type=jnp.float32).astype(jnp.bfloat16)
    packed = packed.reshape(peer_count, slot_count, embedded.shape[1])
    received = route_exchange(packed, 5)
    return received.reshape(peer_count * slot_count, embedded.shape[1])


def body(
    tokens,
    segment_ids,
    owners,
    project_in,
    project_out,
    weight_up,
    weight_down,
    weight_merge,
    gain_attend,
    gain_hidden,
    gain_final,
):
    model_width = tokens.shape[1]
    head_count = project_in.shape[2] // HEAD_DIM
    units = weight_up.shape[1]
    feat_count = lax.axis_size("feat")
    tok_count = lax.axis_size("tok")
    flat_in = project_in.reshape(model_width, 3 * project_in.shape[2])
    local_count = tokens.shape[0]
    stacked = jnp.concatenate([weight_up, weight_down.T], axis=1)
    gathered = norm_gather_feat(tokens, gain_attend, 0, feat_count, 0)
    projected = jnp.dot(gathered, flat_in, preferred_element_type=jnp.float32)
    attended = attend(projected, segment_ids, head_count)
    attn_parts = jnp.dot(attended, project_out, preferred_element_type=jnp.float32).astype(jnp.bfloat16)
    second, hidden_rows, weights = mix_ring_feat(
        attn_parts.reshape(feat_count, local_count, model_width), tokens, gain_hidden, 1, stacked,
        feat_count, tok_count, 1,
    )
    both = weights
    upper = both[:, :units]
    lower_t = both[:, units:]
    hidden = jax.nn.gelu(
        jnp.dot(hidden_rows, upper, preferred_element_type=jnp.float32), approximate=False
    ).astype(jnp.bfloat16)
    down_parts = lax.dot_general(
        hidden, lower_t, (((1,), (1,)), ((), ())), preferred_element_type=jnp.float32
    ).astype(jnp.bfloat16)
    _, merged = mix_feat(
        down_parts.reshape(feat_count, local_count, model_width), second, gain_final, 2, feat_count, 3
    )
    embedded = jnp.dot(merged, weight_merge, preferred_element_type=jnp.float32).astype(jnp.bfloat16)
    return route_rows(embedded, segment_ids, owners)


def solution(mesh):
    return jax.shard_map(
        body,
        mesh=mesh,
        in_specs=(
            P(("tok", "feat"), None),
            P("tok"),
            P("tok"),
            P(None, None, "feat"),
            P("feat", None),
            P("tok", "feat"),
            P("feat", "tok"),
            P(None, "feat"),
            P(),
            P(),
            P(),
        ),
        out_specs=P("tok", "feat"),
        check_vma=False,
    )
```

```python
import functools
import jax
import jax.numpy as jnp
from jax import lax
from jax.experimental import pallas as pl
from jax.experimental.pallas import tpu as pltpu
from jax.sharding import PartitionSpec as P


def _feat_peers(n, me):
    side = int(round(n ** 0.5))
    if side * side != n:
        return [lax.rem(me + d, n) for d in range(1, n)]
    offsets = [(dy, dx) for dy in range(side) for dx in range(side) if (dy, dx) != (0, 0)]
    offsets.sort(key=lambda o: -(min(o[0], side - o[0]) + min(o[1], side - o[1])))
    row, col = me // side, me % side
    return [lax.rem(row + dy, side) * side + lax.rem(col + dx, side) for dy, dx in offsets]


def _greet(peers, tok_index):
    barrier = pltpu.get_barrier_semaphore()
    for peer in peers:
        pl.semaphore_signal(barrier, inc=1, device_id=(tok_index, peer), device_id_type=MESH)
    pl.semaphore_wait(barrier, len(peers))


def _gather_kernel(n, row_ref, out_ref, send_sem, recv_sem):
    me = lax.axis_index("feat")
    tok_index = lax.axis_index("tok")
    peers = _feat_peers(n, me)
    _greet(peers, tok_index)
    for peer in peers:
        pltpu.make_async_remote_copy(
            src_ref=row_ref, dst_ref=out_ref.at[me], send_sem=send_sem.at[peer],
            recv_sem=recv_sem.at[me], device_id=(tok_index, peer), device_id_type=MESH,
        ).start()
    out_ref[me] = row_ref[...]
    for peer in peers:
        pltpu.make_async_remote_copy(
            src_ref=row_ref, dst_ref=out_ref.at[peer], send_sem=send_sem.at[peer],
            recv_sem=recv_sem.at[peer], device_id=(tok_index, peer), device_id_type=MESH,
        ).wait_recv()
    for peer in peers:
        pltpu.make_async_remote_copy(
            src_ref=row_ref, dst_ref=out_ref.at[me], send_sem=send_sem.at[peer],
            recv_sem=recv_sem.at[me], device_id=(tok_index, peer), device_id_type=MESH,
        ).wait_send()


def gather_feat(row_block, n, collective_id):
    rows, width = row_block.shape
    return pl.pallas_call(
        functools.partial(_gather_kernel, n),
        out_shape=jax.ShapeDtypeStruct((n, rows, width), row_block.dtype),
        in_specs=[pl.BlockSpec(memory_space=pltpu.VMEM)],
        out_specs=pl.BlockSpec(memory_space=pltpu.VMEM),
        scratch_shapes=[pltpu.SemaphoreType.DMA((n,)), pltpu.SemaphoreType.DMA((n,))],
        compiler_params=pltpu.CompilerParams(collective_id=collective_id, has_side_effects=True),
    )(row_block).reshape(n * rows, width)


def _ring_gather(x_ref, out_ref, send_right, send_left, send_partner, recv_sem, feat_index, after_first=None,
                 hook=None, hook_step=1):
    tok_count = out_ref.shape[0]
    chips = tok_count // 2
    right_steps = chips // 2
    left_steps = chips - 1 - right_steps
    me = lax.axis_index("tok")
    chip = me // 2
    core = me % 2
    right = lax.rem(chip + 1, chips) * 2 + core
    left = lax.rem(chip + chips - 1, chips) * 2 + core
    partner = chip * 2 + (1 - core)

    def slot_of(offset):
        return lax.rem(chip + offset + 2 * chips, chips) * 2 + core

    def remote(src, slot, sem, target):
        return pltpu.make_async_remote_copy(
            src_ref=src, dst_ref=out_ref.at[slot], send_sem=sem, recv_sem=recv_sem.at[slot],
            device_id=(target, feat_index), device_id_type=MESH,
        )

    sends = []

    def forward_partner(src, slot):
        copy = remote(src, slot, send_partner.at[len(sends_partner)], partner)
        copy.start()
        sends_partner.append(copy)

    sends_partner = []
    out_ref[me] = x_ref[...]
    arrived = []
    for step in range(1, right_steps + 1):
        if step == 1:
            src_right = x_ref
            src_left = x_ref
        else:
            from_left = slot_of(-(step - 1))
            remote(x_ref, from_left, send_right.at[0], right).wait_recv()
            src_right = out_ref.at[from_left]
            arrived.append(from_left)
        copy = remote(src_right, slot_of(-(step - 1)), send_right.at[step - 1], right)
        copy.start()
        sends.append(copy)
        if step > 1 and step - 1 <= left_steps:
            from_right = slot_of(step - 1)
            remote(x_ref, from_right, send_left.at[0], left).wait_recv()
            src_left = out_ref.at[from_right]
            arrived.append(from_right)
        if step <= left_steps:
            copy = remote(src_left, slot_of(step - 1), send_left.at[step - 1], left)
            copy.start()
            sends.append(copy)
        if step == 1:
            if after_first is not None:
                after_first()
            forward_partner(x_ref, me)
        for slot in arrived:
            forward_partner(out_ref.at[slot], slot)
        arrived = []
        if hook is not None and step == min(hook_step, right_steps):
            hook()
    last_left = slot_of(-right_steps)
    remote(x_ref, last_left, send_right.at[0], right).wait_recv()
    forward_partner(out_ref.at[last_left], last_left)
    if left_steps >= 1 and left_steps + 1 > right_steps:
        last_right = slot_of(left_steps)
        remote(x_ref, last_right, send_left.at[0], left).wait_recv()
        forward_partner(out_ref.at[last_right], last_right)
    for other_chip in range(chips):
        remote(x_ref, other_chip * 2 + (1 - core), send_partner.at[0], partner).wait_recv()
    for copy in sends + sends_partner:
        copy.wait_send()


def _first_kernel(n, row_ref, weight_ref, out_ref, weight_out, send_sem, recv_sem,
                  send_right, send_left, send_partner, weight_recv):
    me = lax.axis_index("feat")
    tok_index = lax.axis_index("tok")
    chips = weight_out.shape[0] // 2
    chip = tok_index // 2
    core = tok_index % 2
    peers = [lax.rem(me + d, n) for d in range(1, n)]
    barrier = pltpu.get_barrier_semaphore()
    for peer in peers:
        pl.semaphore_signal(barrier, inc=1, device_id=(tok_index, peer), device_id_type=MESH)
    ring_peers = [
        lax.rem(chip + 1, chips) * 2 + core,
        lax.rem(chip + chips - 1, chips) * 2 + core,
        chip * 2 + (1 - core),
    ]
    for peer in ring_peers:
        pl.semaphore_signal(barrier, inc=1, device_id=(peer, me), device_id_type=MESH)
    pl.semaphore_wait(barrier, len(peers) + len(ring_peers))

    def start_rows():
        for peer in peers:
            pltpu.make_async_remote_copy(
                src_ref=row_ref, dst_ref=out_ref.at[me], send_sem=send_sem.at[peer],
                recv_sem=recv_sem.at[me], device_id=(tok_index, peer), device_id_type=MESH,
            ).start()

    _ring_gather(weight_ref, weight_out, send_right, send_left, send_partner, weight_recv, me, start_rows)
    out_ref[me] = row_ref[...]
    for peer in peers:
        pltpu.make_async_remote_copy(
            src_ref=row_ref, dst_ref=out_ref.at[peer], send_sem=send_sem.at[peer],
            recv_sem=recv_sem.at[peer], device_id=(tok_index, peer), device_id_type=MESH,
        ).wait_recv()
    for peer in peers:
        pltpu.make_async_remote_copy(
            src_ref=row_ref, dst_ref=out_ref.at[me], send_sem=send_sem.at[peer],
            recv_sem=recv_sem.at[me], device_id=(tok_index, peer), device_id_type=MESH,
        ).wait_send()


def first_exchange(row_block, weight_block, n, tok_count, collective_id):
    rows, width = row_block.shape
    weight_rows, weight_width = weight_block.shape
    chips = tok_count // 2
    gathered, weights = pl.pallas_call(
        functools.partial(_first_kernel, n),
        out_shape=(
            jax.ShapeDtypeStruct((n, rows, width), row_block.dtype),
            jax.ShapeDtypeStruct((tok_count, weight_rows, weight_width), weight_block.dtype),
        ),
        in_specs=[pl.BlockSpec(memory_space=pltpu.VMEM)] * 2,
        out_specs=(pl.BlockSpec(memory_space=pltpu.VMEM),) * 2,
        scratch_shapes=[
            pltpu.SemaphoreType.DMA((n,)),
            pltpu.SemaphoreType.DMA((n,)),
            pltpu.SemaphoreType.DMA((chips,)),
            pltpu.SemaphoreType.DMA((chips,)),
            pltpu.SemaphoreType.DMA((chips,)),
            pltpu.SemaphoreType.DMA((tok_count,)),
        ],
        compiler_params=pltpu.CompilerParams(collective_id=collective_id, has_side_effects=True),
    )(row_block, weight_block)
    return gathered.reshape(n * rows, width), weights


def _route_kernel(n, packed_ref, out_ref, send_sem, recv_sem):
    me = lax.axis_index("tok")
    feat_index = lax.axis_index("feat")
    order = sorted(range(1, n), key=lambda d: -min(d, n - d))
    peers = [lax.rem(me + d, n) for d in order]
    barrier = pltpu.get_barrier_semaphore()
    for peer in peers:
        pl.semaphore_signal(barrier, inc=1, device_id=(peer, feat_index), device_id_type=MESH)
    pl.semaphore_wait(barrier, len(peers))
    for peer in peers:
        pltpu.make_async_remote_copy(
            src_ref=packed_ref.at[peer], dst_ref=out_ref.at[me], send_sem=send_sem.at[peer],
            recv_sem=recv_sem.at[me], device_id=(peer, feat_index), device_id_type=MESH,
        ).start()
    out_ref[me] = packed_ref[me]
    for peer in peers:
        pltpu.make_async_remote_copy(
            src_ref=packed_ref.at[peer], dst_ref=out_ref.at[peer], send_sem=send_sem.at[peer],
            recv_sem=recv_sem.at[peer], device_id=(peer, feat_index), device_id_type=MESH,
        ).wait_recv()
    for peer in peers:
        pltpu.make_async_remote_copy(
            src_ref=packed_ref.at[peer], dst_ref=out_ref.at[me], send_sem=send_sem.at[peer],
            recv_sem=recv_sem.at[me], device_id=(peer, feat_index), device_id_type=MESH,
        ).wait_send()


def route_exchange(packed, collective_id):
    n = packed.shape[0]
    return pl.pallas_call(
        functools.partial(_route_kernel, n),
        out_shape=jax.ShapeDtypeStruct(packed.shape, packed.dtype),
        in_specs=[pl.BlockSpec(memory_space=pltpu.VMEM)],
        out_specs=pl.BlockSpec(memory_space=pltpu.VMEM),
        scratch_shapes=[pltpu.SemaphoreType.DMA((n,)), pltpu.SemaphoreType.DMA((n,))],
        compiler_params=pltpu.CompilerParams(collective_id=collective_id, has_side_effects=True),
    )(packed)


def _mix_kernel(n, gain_row, part_ref, resid_ref, gain_ref, resid_out, out_ref, merged_out, held, mine_a,
                mine_b, mine_c, scatter_send, scatter_recv, gather_send, gather_recv):
    me = lax.axis_index("feat")
    tok_index = lax.axis_index("tok")
    peers = _feat_peers(n, me)
    _greet(peers, tok_index)
    piece = part_ref.shape[1] // 3
    halves = [(0, piece), (piece, piece), (2 * piece, piece)]
    mines = [mine_a, mine_b, mine_c]

    def scatter_copy(half, peer, slot):
        first, size = halves[half]
        return pltpu.make_async_remote_copy(
            src_ref=part_ref.at[peer, pl.ds(first, size)], dst_ref=held.at[slot, pl.ds(first, size)],
            send_sem=scatter_send.at[half, peer], recv_sem=scatter_recv.at[half, slot],
            device_id=(tok_index, peer), device_id_type=MESH,
        )

    def gather_copy(half, peer, slot):
        first, size = halves[half]
        return pltpu.make_async_remote_copy(
            src_ref=mines[half], dst_ref=out_ref.at[slot, pl.ds(first, size)],
            send_sem=gather_send.at[half, peer], recv_sem=gather_recv.at[half, slot],
            device_id=(tok_index, peer), device_id_type=MESH,
        )

    for half in range(len(halves)):
        for peer in peers:
            scatter_copy(half, peer, me).start()
    for half in range(len(halves)):
        first, size = halves[half]
        total = part_ref[me, first:first + size, :].astype(jnp.float32)
        for peer in peers:
            scatter_copy(half, peer, peer).wait_recv()
            total = total + held[peer, first:first + size, :].astype(jnp.float32)
        summed = (resid_ref[first:first + size, :].astype(jnp.float32) + total).astype(jnp.bfloat16)
        resid_out[first:first + size, :] = summed
        as_float = summed.astype(jnp.float32)
        center = jnp.mean(as_float, axis=-1, keepdims=True)
        spread = jnp.mean(jnp.square(as_float - center), axis=-1, keepdims=True)
        normed = ((as_float - center) * lax.rsqrt(spread + epsilon) * gain_ref[...].astype(jnp.float32)[None, :]).astype(jnp.bfloat16)
        mines[half][...] = normed
        out_ref[me, first:first + size, :] = normed
        for peer in peers:
            gather_copy(half, peer, me).start()
    for half in range(len(halves)):
        for peer in peers:
            gather_copy(half, peer, peer).wait_recv()
    group = 4
    width = out_ref.shape[2]
    row_count = n * out_ref.shape[1]
    rows = out_ref[...].astype(jnp.float32).reshape(row_count, width).astype(jnp.bfloat16)
    merged_index = lax.broadcasted_iota(jnp.int32, (row_count // group, row_count), 0)
    row_index = lax.broadcasted_iota(jnp.int32, (row_count // group, row_count), 1)
    for part in range(group):
        pick = (row_index == merged_index * group + part).astype(jnp.bfloat16)
        merged_out[:, part * width:(part + 1) * width] = jnp.dot(
            pick, rows, preferred_element_type=jnp.float32
        ).astype(jnp.bfloat16)
    for half in range(len(halves)):
        for peer in peers:
            scatter_copy(half, peer, me).wait_send()
            gather_copy(half, peer, me).wait_send()


def mix_feat(parts, resid, gains, gain_row, n, collective_id):
    _, rows, width = parts.shape
    new_resid, _, merged = pl.pallas_call(
        functools.partial(_mix_kernel, n, gain_row),
        out_shape=(
            jax.ShapeDtypeStruct((rows, width), jnp.bfloat16),
            jax.ShapeDtypeStruct((n, rows, width), jnp.bfloat16),
            jax.ShapeDtypeStruct((n * rows // 4, 4 * width), jnp.bfloat16),
        ),
        in_specs=[pl.BlockSpec(memory_space=pltpu.VMEM)] * 3,
        out_specs=(pl.BlockSpec(memory_space=pltpu.VMEM),) * 3,
        scratch_shapes=[
            pltpu.VMEM((n, rows, width), parts.dtype),
            pltpu.VMEM((rows // 3, width), jnp.bfloat16),
            pltpu.VMEM((rows // 3, width), jnp.bfloat16),
            pltpu.VMEM((rows // 3, width), jnp.bfloat16),
            pltpu.SemaphoreType.DMA((3, n)),
            pltpu.SemaphoreType.DMA((3, n)),
            pltpu.SemaphoreType.DMA((3, n)),
            pltpu.SemaphoreType.DMA((3, n)),
        ],
        compiler_params=pltpu.CompilerParams(collective_id=collective_id, has_side_effects=True),
    )(parts, resid, gains)
    return new_resid, merged


def _mix_ring_kernel(n, gain_row, part_ref, resid_ref, gain_ref, weight_ref, resid_out, out_ref, weight_flat,
                     weight_out, held, mine, scatter_send, scatter_recv, gather_send, gather_recv,
                     send_right, send_left, send_partner, weight_recv):
    me = lax.axis_index("feat")
    tok_index = lax.axis_index("tok")
    chips = weight_out.shape[0] // 2
    chip = tok_index // 2
    core = tok_index % 2
    peers = [lax.rem(me + d, n) for d in range(1, n)]
    barrier = pltpu.get_barrier_semaphore()
    for peer in peers:
        pl.semaphore_signal(barrier, inc=1, device_id=(tok_index, peer), device_id_type=MESH)
    ring_peers = [
        lax.rem(chip + 1, chips) * 2 + core,
        lax.rem(chip + chips - 1, chips) * 2 + core,
        chip * 2 + (1 - core),
    ]
    for peer in ring_peers:
        pl.semaphore_signal(barrier, inc=1, device_id=(peer, me), device_id_type=MESH)
    pl.semaphore_wait(barrier, len(peers) + len(ring_peers))

    def scatter_copy(peer, slot):
        return pltpu.make_async_remote_copy(
            src_ref=part_ref.at[peer], dst_ref=held.at[slot], send_sem=scatter_send.at[peer],
            recv_sem=scatter_recv.at[slot], device_id=(tok_index, peer), device_id_type=MESH,
        )

    def gather_copy(peer, slot):
        return pltpu.make_async_remote_copy(
            src_ref=mine, dst_ref=out_ref.at[slot], send_sem=gather_send.at[peer],
            recv_sem=gather_recv.at[slot], device_id=(tok_index, peer), device_id_type=MESH,
        )

    for peer in peers:
        scatter_copy(peer, me).start()

    def norm_and_send():
        total = part_ref[me].astype(jnp.float32)
        for peer in peers:
            scatter_copy(peer, peer).wait_recv()
            total = total + held[peer].astype(jnp.float32)
        summed = (resid_ref[...].astype(jnp.float32) + total).astype(jnp.bfloat16)
        resid_out[...] = summed
        as_float = summed.astype(jnp.float32)
        center = jnp.mean(as_float, axis=-1, keepdims=True)
        spread = jnp.mean(jnp.square(as_float - center), axis=-1, keepdims=True)
        normed = ((as_float - center) * lax.rsqrt(spread + epsilon) * gain_ref[...].astype(jnp.float32)[None, :]).astype(jnp.bfloat16)
        mine[...] = normed
        out_ref[me] = normed
        for peer in peers:
            gather_copy(peer, me).start()

    _ring_gather(weight_ref, weight_out, send_right, send_left, send_partner, weight_recv, me,
                 hook=norm_and_send, hook_step=5)
    block_rows = weight_out.shape[1]
    for slot in range(weight_out.shape[0]):
        weight_flat[slot * block_rows:(slot + 1) * block_rows, :] = weight_out[slot]
    for peer in peers:
        gather_copy(peer, peer).wait_recv()
    for peer in peers:
        scatter_copy(peer, me).wait_send()
        gather_copy(peer, me).wait_send()


def mix_ring_feat(parts, resid, gains, gain_row, weight_block, n, tok_count, collective_id):
    _, rows, width = parts.shape
    weight_rows, weight_width = weight_block.shape
    chips = tok_count // 2
    new_resid, gathered, weights = pl.pallas_call(
        functools.partial(_mix_ring_kernel, n, gain_row),
        out_shape=(
            jax.ShapeDtypeStruct((rows, width), jnp.bfloat16),
            jax.ShapeDtypeStruct((n, rows, width), jnp.bfloat16),
            jax.ShapeDtypeStruct((tok_count * weight_rows, weight_width), weight_block.dtype),
        ),
        in_specs=[pl.BlockSpec(memory_space=pltpu.VMEM)] * 4,
        out_specs=(pl.BlockSpec(memory_space=pltpu.VMEM),) * 3,
        scratch_shapes=[
            pltpu.VMEM((tok_count, weight_rows, weight_width), weight_block.dtype),
            pltpu.VMEM((n, rows, width), parts.dtype),
            pltpu.VMEM((rows, width), jnp.bfloat16),
            pltpu.SemaphoreType.DMA((n,)),
            pltpu.SemaphoreType.DMA((n,)),
            pltpu.SemaphoreType.DMA((n,)),
            pltpu.SemaphoreType.DMA((n,)),
            pltpu.SemaphoreType.DMA((chips,)),
            pltpu.SemaphoreType.DMA((chips,)),
            pltpu.SemaphoreType.DMA((chips,)),
            pltpu.SemaphoreType.DMA((tok_count,)),
        ],
        compiler_params=pltpu.CompilerParams(collective_id=collective_id, has_side_effects=True),
    )(parts, resid, gains, weight_block)
    return new_resid, gathered.reshape(n * rows, width), weights


def _norm_gather_kernel(n, gain_row, tok_ref, gain_ref, out_ref, mine, send_sem, recv_sem):
    me = lax.axis_index("feat")
    tok_index = lax.axis_index("tok")
    peers = _feat_peers(n, me)
    _greet(peers, tok_index)
    as_float = tok_ref[...].astype(jnp.float32)
    center = jnp.mean(as_float, axis=-1, keepdims=True)
    spread = jnp.mean(jnp.square(as_float - center), axis=-1, keepdims=True)
    normed = ((as_float - center) * lax.rsqrt(spread + epsilon) * gain_ref[...].astype(jnp.float32)[None, :]).astype(jnp.bfloat16)
    mine[...] = normed
    out_ref[me] = normed

    def copy(peer, slot):
        return pltpu.make_async_remote_copy(
            src_ref=mine, dst_ref=out_ref.at[slot], send_sem=send_sem.at[peer],
            recv_sem=recv_sem.at[slot], device_id=(tok_index, peer), device_id_type=MESH,
        )

    for peer in peers:
        copy(peer, me).start()
    for peer in peers:
        copy(peer, peer).wait_recv()
    for peer in peers:
        copy(peer, me).wait_send()


def norm_gather_feat(rows, gains, gain_row, n, collective_id):
    count, width = rows.shape
    return pl.pallas_call(
        functools.partial(_norm_gather_kernel, n, gain_row),
        out_shape=jax.ShapeDtypeStruct((n, count, width), jnp.bfloat16),
        in_specs=[pl.BlockSpec(memory_space=pltpu.VMEM)] * 2,
        out_specs=pl.BlockSpec(memory_space=pltpu.VMEM),
        scratch_shapes=[
            pltpu.VMEM((count, width), jnp.bfloat16),
            pltpu.SemaphoreType.DMA((n,)),
            pltpu.SemaphoreType.DMA((n,)),
        ],
        compiler_params=pltpu.CompilerParams(collective_id=collective_id, has_side_effects=True),
    )(rows, gains).reshape(n * count, width)


def _scatter_kernel(n, part_ref, out_ref, held, send_sem, recv_sem):
    me = lax.axis_index("feat")
    tok_index = lax.axis_index("tok")
    peers = _feat_peers(n, me)
    _greet(peers, tok_index)
    for peer in peers:
        pltpu.make_async_remote_copy(
            src_ref=part_ref.at[peer], dst_ref=held.at[me], send_sem=send_sem.at[peer],
            recv_sem=recv_sem.at[me], device_id=(tok_index, peer), device_id_type=MESH,
        ).start()
    total = part_ref[me].astype(jnp.float32)
    for peer in peers:
        pltpu.make_async_remote_copy(
            src_ref=part_ref.at[peer], dst_ref=held.at[peer], send_sem=send_sem.at[peer],
            recv_sem=recv_sem.at[peer], device_id=(tok_index, peer), device_id_type=MESH,
        ).wait_recv()
        total = total + held[peer].astype(jnp.float32)
    out_ref[...] = total
    for peer in peers:
        pltpu.make_async_remote_copy(
            src_ref=part_ref.at[peer], dst_ref=held.at[me], send_sem=send_sem.at[peer],
            recv_sem=recv_sem.at[me], device_id=(tok_index, peer), device_id_type=MESH,
        ).wait_send()


def scatter_feat(parts, n, collective_id):
    _, rows, width = parts.shape
    return pl.pallas_call(
        functools.partial(_scatter_kernel, n),
        out_shape=jax.ShapeDtypeStruct((rows, width), jnp.float32),
        in_specs=[pl.BlockSpec(memory_space=pltpu.VMEM)],
        out_specs=pl.BlockSpec(memory_space=pltpu.VMEM),
        scratch_shapes=[
            pltpu.VMEM((n, rows, width), parts.dtype),
            pltpu.SemaphoreType.DMA((n,)),
            pltpu.SemaphoreType.DMA((n,)),
        ],
        compiler_params=pltpu.CompilerParams(collective_id=collective_id, has_side_effects=True),
    )(parts)

MESH = pl.DeviceIdType.MESH
LEAST_UNITS = 4
MOST_UNITS = 16
HEAD_DIM = 88


epsilon = 1e-06


def layer_norm(row_block, gain_row):
    as_float = row_block.astype(jnp.float32)
    center = jnp.mean(as_float, axis=-1, keepdims=True)
    spread = jnp.mean(jnp.square(as_float - center), axis=-1, keepdims=True)
    scaled = (as_float - center) * lax.rsqrt(spread + epsilon) * gain_row.astype(jnp.float32)
    return scaled.astype(jnp.bfloat16)


def project_rows(row_block, weight_block, collective_id):
    n = lax.axis_size("feat")
    return jnp.dot(
        gather_feat(row_block, n, collective_id),
        weight_block,
        preferred_element_type=jnp.float32,
    )


def scatter_rows(left_rows, right_rows, collective_id):
    n = lax.axis_size("feat")
    parts = jnp.dot(left_rows, right_rows, preferred_element_type=jnp.float32).astype(jnp.bfloat16)
    return scatter_feat(parts.reshape(n, parts.shape[0] // n, parts.shape[1]), n, collective_id)


def early_weights(weight_up, weight_down):
    return (weight_up, weight_down)


def upper_weight(fetched):
    return lax.all_gather(fetched[0], "tok", axis=0, tiled=True)


def lower_weight(fetched):
    return lax.all_gather(fetched[1], "tok", axis=1, tiled=True)


def attend(projected, segment_ids, head_count):
    token_count = projected.shape[0]
    parts_all = projected.reshape(token_count, 3, head_count, HEAD_DIM)
    queries = (parts_all[:, 0] * HEAD_DIM ** (-0.5)).astype(jnp.bfloat16)
    keys_here = parts_all[:, 1].astype(jnp.bfloat16)
    values_here = parts_all[:, 2].astype(jnp.bfloat16)
    scores = jnp.einsum("qhd,khd->hqk", queries, keys_here, preferred_element_type=jnp.float32)
    same_segment = segment_ids[:, None] == segment_ids[None, :]
    scores = jnp.where(same_segment[None, :, :], scores, -1e30)
    highest = jnp.max(scores, axis=-1, keepdims=True)
    raised = jnp.exp(scores - highest)
    weights_soft = (raised / jnp.sum(raised, axis=-1, keepdims=True)).astype(jnp.bfloat16)
    attended = jnp.einsum(
        "hqk,khd->qhd", weights_soft, values_here, preferred_element_type=jnp.float32
    )
    return attended.astype(jnp.bfloat16).reshape(token_count, head_count * HEAD_DIM)


def route_rows(embedded, segment_ids, owners):
    merged_count = embedded.shape[0]
    peer_count = owners.shape[0]
    least_units = max(LEAST_UNITS, (merged_count + peer_count - 1) // peer_count)
    slot_count = max(MOST_UNITS, 2 * least_units)
    first_ids = segment_ids.reshape(merged_count, 4)[:, 0]
    id_base = lax.axis_index("tok") * peer_count
    local_index = first_ids - id_base
    owner_pick = local_index[:, None] == jnp.arange(peer_count, dtype=jnp.int32)[None, :]
    owner_of = jnp.sum(jnp.where(owner_pick, owners[None, :], 0), axis=1)
    row_index = jnp.arange(merged_count, dtype=jnp.int32)
    earlier = (row_index[None, :] < row_index[:, None]) & (first_ids[None, :] == first_ids[:, None])
    within = jnp.sum(earlier.astype(jnp.int32), axis=1)
    target = owner_of * slot_count + within
    select = (
        jnp.arange(peer_count * slot_count, dtype=jnp.int32)[:, None] == target[None, :]
    ).astype(jnp.bfloat16)
    packed = jnp.dot(select, embedded, preferred_element_type=jnp.float32).astype(jnp.bfloat16)
    packed = packed.reshape(peer_count, slot_count, embedded.shape[1])
    received = route_exchange(packed, 5)
    return received.reshape(peer_count * slot_count, embedded.shape[1])


def body(
    tokens,
    segment_ids,
    owners,
    project_in,
    project_out,
    weight_up,
    weight_down,
    weight_merge,
    gain_attend,
    gain_hidden,
    gain_final,
):
    model_width = tokens.shape[1]
    head_count = project_in.shape[2] // HEAD_DIM
    units = weight_up.shape[1]
    feat_count = lax.axis_size("feat")
    tok_count = lax.axis_size("tok")
    flat_in = project_in.reshape(model_width, 3 * project_in.shape[2])
    local_count = tokens.shape[0]
    stacked = jnp.concatenate([weight_up, weight_down.T], axis=1)
    gathered = norm_gather_feat(tokens, gain_attend, 0, feat_count, 0)
    projected = jnp.dot(gathered, flat_in, preferred_element_type=jnp.float32)
    attended = attend(projected, segment_ids, head_count)
    attn_parts = jnp.dot(attended, project_out, preferred_element_type=jnp.float32).astype(jnp.bfloat16)
    second, hidden_rows, weights = mix_ring_feat(
        attn_parts.reshape(feat_count, local_count, model_width), tokens, gain_hidden, 1, stacked,
        feat_count, tok_count, 1,
    )
    both = weights
    upper = both[:, :units]
    lower_t = both[:, units:]
    hidden = jax.nn.gelu(
        jnp.dot(hidden_rows, upper, preferred_element_type=jnp.float32), approximate=False
    ).astype(jnp.bfloat16)
    down_parts = lax.dot_general(
        hidden, lower_t, (((1,), (1,)), ((), ())), preferred_element_type=jnp.float32
    ).astype(jnp.bfloat16)
    _, merged = mix_feat(
        down_parts.reshape(feat_count, local_count, model_width), second, gain_final, 2, feat_count, 3
    )
    embedded = jnp.dot(merged, weight_merge, preferred_element_type=jnp.float32).astype(jnp.bfloat16)
    return route_rows(embedded, segment_ids, owners)


def solution(mesh):
    return jax.shard_map(
        body,
        mesh=mesh,
        in_specs=(
            P(("tok", "feat"), None),
            P("tok"),
            P("tok"),
            P(None, None, "feat"),
            P("feat", None),
            P("tok", "feat"),
            P("feat", "tok"),
            P(None, "feat"),
            P(),
            P(),
            P(),
        ),
        out_specs=P("tok", "feat"),
        check_vma=False,
    )
```

```python
import functools
import jax
import jax.numpy as jnp
from jax import lax
from jax.experimental import pallas as pl
from jax.experimental.pallas import tpu as pltpu
from jax.sharding import PartitionSpec as P


def _feat_peers(n, me):
    side = int(round(n ** 0.5))
    if side * side != n:
        return [lax.rem(me + d, n) for d in range(1, n)]
    offsets = [(dy, dx) for dy in range(side) for dx in range(side) if (dy, dx) != (0, 0)]
    offsets.sort(key=lambda o: -(min(o[0], side - o[0]) + min(o[1], side - o[1])))
    row, col = me // side, me % side
    return [lax.rem(row + dy, side) * side + lax.rem(col + dx, side) for dy, dx in offsets]


def _greet(peers, tok_index):
    barrier = pltpu.get_barrier_semaphore()
    for peer in peers:
        pl.semaphore_signal(barrier, inc=1, device_id=(tok_index, peer), device_id_type=MESH)
    pl.semaphore_wait(barrier, len(peers))


def _gather_kernel(n, row_ref, out_ref, send_sem, recv_sem):
    me = lax.axis_index("feat")
    tok_index = lax.axis_index("tok")
    peers = _feat_peers(n, me)
    _greet(peers, tok_index)
    for peer in peers:
        pltpu.make_async_remote_copy(
            src_ref=row_ref, dst_ref=out_ref.at[me], send_sem=send_sem.at[peer],
            recv_sem=recv_sem.at[me], device_id=(tok_index, peer), device_id_type=MESH,
        ).start()
    out_ref[me] = row_ref[...]
    for peer in peers:
        pltpu.make_async_remote_copy(
            src_ref=row_ref, dst_ref=out_ref.at[peer], send_sem=send_sem.at[peer],
            recv_sem=recv_sem.at[peer], device_id=(tok_index, peer), device_id_type=MESH,
        ).wait_recv()
    for peer in peers:
        pltpu.make_async_remote_copy(
            src_ref=row_ref, dst_ref=out_ref.at[me], send_sem=send_sem.at[peer],
            recv_sem=recv_sem.at[me], device_id=(tok_index, peer), device_id_type=MESH,
        ).wait_send()


def gather_feat(row_block, n, collective_id):
    rows, width = row_block.shape
    return pl.pallas_call(
        functools.partial(_gather_kernel, n),
        out_shape=jax.ShapeDtypeStruct((n, rows, width), row_block.dtype),
        in_specs=[pl.BlockSpec(memory_space=pltpu.VMEM)],
        out_specs=pl.BlockSpec(memory_space=pltpu.VMEM),
        scratch_shapes=[pltpu.SemaphoreType.DMA((n,)), pltpu.SemaphoreType.DMA((n,))],
        compiler_params=pltpu.CompilerParams(collective_id=collective_id, has_side_effects=True),
    )(row_block).reshape(n * rows, width)


def _ring_gather(x_ref, out_ref, send_right, send_left, send_partner, recv_sem, feat_index, after_first=None,
                 hook=None, hook_step=1):
    tok_count = out_ref.shape[0]
    chips = tok_count // 2
    right_steps = chips // 2
    left_steps = chips - 1 - right_steps
    me = lax.axis_index("tok")
    chip = me // 2
    core = me % 2
    right = lax.rem(chip + 1, chips) * 2 + core
    left = lax.rem(chip + chips - 1, chips) * 2 + core
    partner = chip * 2 + (1 - core)

    def slot_of(offset):
        return lax.rem(chip + offset + 2 * chips, chips) * 2 + core

    def remote(src, slot, sem, target):
        return pltpu.make_async_remote_copy(
            src_ref=src, dst_ref=out_ref.at[slot], send_sem=sem, recv_sem=recv_sem.at[slot],
            device_id=(target, feat_index), device_id_type=MESH,
        )

    sends = []

    def forward_partner(src, slot):
        copy = remote(src, slot, send_partner.at[len(sends_partner)], partner)
        copy.start()
        sends_partner.append(copy)

    sends_partner = []
    out_ref[me] = x_ref[...]
    arrived = []
    for step in range(1, right_steps + 1):
        if step == 1:
            src_right = x_ref
            src_left = x_ref
        else:
            from_left = slot_of(-(step - 1))
            remote(x_ref, from_left, send_right.at[0], right).wait_recv()
            src_right = out_ref.at[from_left]
            arrived.append(from_left)
        copy = remote(src_right, slot_of(-(step - 1)), send_right.at[step - 1], right)
        copy.start()
        sends.append(copy)
        if step > 1 and step - 1 <= left_steps:
            from_right = slot_of(step - 1)
            remote(x_ref, from_right, send_left.at[0], left).wait_recv()
            src_left = out_ref.at[from_right]
            arrived.append(from_right)
        if step <= left_steps:
            copy = remote(src_left, slot_of(step - 1), send_left.at[step - 1], left)
            copy.start()
            sends.append(copy)
        if step == 1:
            if after_first is not None:
                after_first()
            forward_partner(x_ref, me)
        for slot in arrived:
            forward_partner(out_ref.at[slot], slot)
        arrived = []
        if hook is not None and step == min(hook_step, right_steps):
            hook()
    last_left = slot_of(-right_steps)
    remote(x_ref, last_left, send_right.at[0], right).wait_recv()
    forward_partner(out_ref.at[last_left], last_left)
    if left_steps >= 1 and left_steps + 1 > right_steps:
        last_right = slot_of(left_steps)
        remote(x_ref, last_right, send_left.at[0], left).wait_recv()
        forward_partner(out_ref.at[last_right], last_right)
    for other_chip in range(chips):
        remote(x_ref, other_chip * 2 + (1 - core), send_partner.at[0], partner).wait_recv()
    for copy in sends + sends_partner:
        copy.wait_send()


def _first_kernel(n, row_ref, weight_ref, out_ref, weight_out, send_sem, recv_sem,
                  send_right, send_left, send_partner, weight_recv):
    me = lax.axis_index("feat")
    tok_index = lax.axis_index("tok")
    chips = weight_out.shape[0] // 2
    chip = tok_index // 2
    core = tok_index % 2
    peers = [lax.rem(me + d, n) for d in range(1, n)]
    barrier = pltpu.get_barrier_semaphore()
    for peer in peers:
        pl.semaphore_signal(barrier, inc=1, device_id=(tok_index, peer), device_id_type=MESH)
    ring_peers = [
        lax.rem(chip + 1, chips) * 2 + core,
        lax.rem(chip + chips - 1, chips) * 2 + core,
        chip * 2 + (1 - core),
    ]
    for peer in ring_peers:
        pl.semaphore_signal(barrier, inc=1, device_id=(peer, me), device_id_type=MESH)
    pl.semaphore_wait(barrier, len(peers) + len(ring_peers))

    def start_rows():
        for peer in peers:
            pltpu.make_async_remote_copy(
                src_ref=row_ref, dst_ref=out_ref.at[me], send_sem=send_sem.at[peer],
                recv_sem=recv_sem.at[me], device_id=(tok_index, peer), device_id_type=MESH,
            ).start()

    _ring_gather(weight_ref, weight_out, send_right, send_left, send_partner, weight_recv, me, start_rows)
    out_ref[me] = row_ref[...]
    for peer in peers:
        pltpu.make_async_remote_copy(
            src_ref=row_ref, dst_ref=out_ref.at[peer], send_sem=send_sem.at[peer],
            recv_sem=recv_sem.at[peer], device_id=(tok_index, peer), device_id_type=MESH,
        ).wait_recv()
    for peer in peers:
        pltpu.make_async_remote_copy(
            src_ref=row_ref, dst_ref=out_ref.at[me], send_sem=send_sem.at[peer],
            recv_sem=recv_sem.at[me], device_id=(tok_index, peer), device_id_type=MESH,
        ).wait_send()


def first_exchange(row_block, weight_block, n, tok_count, collective_id):
    rows, width = row_block.shape
    weight_rows, weight_width = weight_block.shape
    chips = tok_count // 2
    gathered, weights = pl.pallas_call(
        functools.partial(_first_kernel, n),
        out_shape=(
            jax.ShapeDtypeStruct((n, rows, width), row_block.dtype),
            jax.ShapeDtypeStruct((tok_count, weight_rows, weight_width), weight_block.dtype),
        ),
        in_specs=[pl.BlockSpec(memory_space=pltpu.VMEM)] * 2,
        out_specs=(pl.BlockSpec(memory_space=pltpu.VMEM),) * 2,
        scratch_shapes=[
            pltpu.SemaphoreType.DMA((n,)),
            pltpu.SemaphoreType.DMA((n,)),
            pltpu.SemaphoreType.DMA((chips,)),
            pltpu.SemaphoreType.DMA((chips,)),
            pltpu.SemaphoreType.DMA((chips,)),
            pltpu.SemaphoreType.DMA((tok_count,)),
        ],
        compiler_params=pltpu.CompilerParams(collective_id=collective_id, has_side_effects=True),
    )(row_block, weight_block)
    return gathered.reshape(n * rows, width), weights


def _route_kernel(n, packed_ref, out_ref, send_sem, recv_sem):
    me = lax.axis_index("tok")
    feat_index = lax.axis_index("feat")
    order = sorted(range(1, n), key=lambda d: -min(d, n - d))
    peers = [lax.rem(me + d, n) for d in order]
    barrier = pltpu.get_barrier_semaphore()
    for peer in peers:
        pl.semaphore_signal(barrier, inc=1, device_id=(peer, feat_index), device_id_type=MESH)
    pl.semaphore_wait(barrier, len(peers))
    for peer in peers:
        pltpu.make_async_remote_copy(
            src_ref=packed_ref.at[peer], dst_ref=out_ref.at[me], send_sem=send_sem.at[peer],
            recv_sem=recv_sem.at[me], device_id=(peer, feat_index), device_id_type=MESH,
        ).start()
    out_ref[me] = packed_ref[me]
    for peer in peers:
        pltpu.make_async_remote_copy(
            src_ref=packed_ref.at[peer], dst_ref=out_ref.at[peer], send_sem=send_sem.at[peer],
            recv_sem=recv_sem.at[peer], device_id=(peer, feat_index), device_id_type=MESH,
        ).wait_recv()
    for peer in peers:
        pltpu.make_async_remote_copy(
            src_ref=packed_ref.at[peer], dst_ref=out_ref.at[me], send_sem=send_sem.at[peer],
            recv_sem=recv_sem.at[me], device_id=(peer, feat_index), device_id_type=MESH,
        ).wait_send()


def route_exchange(packed, collective_id):
    n = packed.shape[0]
    return pl.pallas_call(
        functools.partial(_route_kernel, n),
        out_shape=jax.ShapeDtypeStruct(packed.shape, packed.dtype),
        in_specs=[pl.BlockSpec(memory_space=pltpu.VMEM)],
        out_specs=pl.BlockSpec(memory_space=pltpu.VMEM),
        scratch_shapes=[pltpu.SemaphoreType.DMA((n,)), pltpu.SemaphoreType.DMA((n,))],
        compiler_params=pltpu.CompilerParams(collective_id=collective_id, has_side_effects=True),
    )(packed)


def _mix_kernel(n, gain_row, part_ref, resid_ref, gain_ref, resid_out, out_ref, merged_out, held, mine_a,
                mine_b, mine_c, scatter_send, scatter_recv, gather_send, gather_recv):
    me = lax.axis_index("feat")
    tok_index = lax.axis_index("tok")
    peers = _feat_peers(n, me)
    _greet(peers, tok_index)
    piece = part_ref.shape[1] // 3
    halves = [(0, piece), (piece, piece), (2 * piece, piece)]
    mines = [mine_a, mine_b, mine_c]

    def scatter_copy(half, peer, slot):
        first, size = halves[half]
        return pltpu.make_async_remote_copy(
            src_ref=part_ref.at[peer, pl.ds(first, size)], dst_ref=held.at[slot, pl.ds(first, size)],
            send_sem=scatter_send.at[half, peer], recv_sem=scatter_recv.at[half, slot],
            device_id=(tok_index, peer), device_id_type=MESH,
        )

    def gather_copy(half, peer, slot):
        first, size = halves[half]
        return pltpu.make_async_remote_copy(
            src_ref=mines[half], dst_ref=out_ref.at[slot, pl.ds(first, size)],
            send_sem=gather_send.at[half, peer], recv_sem=gather_recv.at[half, slot],
            device_id=(tok_index, peer), device_id_type=MESH,
        )

    for half in range(len(halves)):
        for peer in peers:
            scatter_copy(half, peer, me).start()
    for half in range(len(halves)):
        first, size = halves[half]
        total = part_ref[me, first:first + size, :].astype(jnp.float32)
        for peer in peers:
            scatter_copy(half, peer, peer).wait_recv()
            total = total + held[peer, first:first + size, :].astype(jnp.float32)
        summed = (resid_ref[first:first + size, :].astype(jnp.float32) + total).astype(jnp.bfloat16)
        resid_out[first:first + size, :] = summed
        as_float = summed.astype(jnp.float32)
        center = jnp.mean(as_float, axis=-1, keepdims=True)
        spread = jnp.mean(jnp.square(as_float - center), axis=-1, keepdims=True)
        normed = ((as_float - center) * lax.rsqrt(spread + epsilon) * gain_ref[...].astype(jnp.float32)[None, :]).astype(jnp.bfloat16)
        mines[half][...] = normed
        out_ref[me, first:first + size, :] = normed
        for peer in peers:
            gather_copy(half, peer, me).start()
    for half in range(len(halves)):
        for peer in peers:
            gather_copy(half, peer, peer).wait_recv()
    group = 4
    width = out_ref.shape[2]
    row_count = n * out_ref.shape[1]
    rows = out_ref[...].astype(jnp.float32).reshape(row_count, width).astype(jnp.bfloat16)
    merged_index = lax.broadcasted_iota(jnp.int32, (row_count // group, row_count), 0)
    row_index = lax.broadcasted_iota(jnp.int32, (row_count // group, row_count), 1)
    for part in range(group):
        pick = (row_index == merged_index * group + part).astype(jnp.bfloat16)
        merged_out[:, part * width:(part + 1) * width] = jnp.dot(
            pick, rows, preferred_element_type=jnp.float32
        ).astype(jnp.bfloat16)
    for half in range(len(halves)):
        for peer in peers:
            scatter_copy(half, peer, me).wait_send()
            gather_copy(half, peer, me).wait_send()


def mix_feat(parts, resid, gains, gain_row, n, collective_id):
    _, rows, width = parts.shape
    new_resid, _, merged = pl.pallas_call(
        functools.partial(_mix_kernel, n, gain_row),
        out_shape=(
            jax.ShapeDtypeStruct((rows, width), jnp.bfloat16),
            jax.ShapeDtypeStruct((n, rows, width), jnp.bfloat16),
            jax.ShapeDtypeStruct((n * rows // 4, 4 * width), jnp.bfloat16),
        ),
        in_specs=[pl.BlockSpec(memory_space=pltpu.VMEM)] * 3,
        out_specs=(pl.BlockSpec(memory_space=pltpu.VMEM),) * 3,
        scratch_shapes=[
            pltpu.VMEM((n, rows, width), parts.dtype),
            pltpu.VMEM((rows // 3, width), jnp.bfloat16),
            pltpu.VMEM((rows // 3, width), jnp.bfloat16),
            pltpu.VMEM((rows // 3, width), jnp.bfloat16),
            pltpu.SemaphoreType.DMA((3, n)),
            pltpu.SemaphoreType.DMA((3, n)),
            pltpu.SemaphoreType.DMA((3, n)),
            pltpu.SemaphoreType.DMA((3, n)),
        ],
        compiler_params=pltpu.CompilerParams(collective_id=collective_id, has_side_effects=True),
    )(parts, resid, gains)
    return new_resid, merged


def _mix_ring_kernel(n, gain_row, part_ref, resid_ref, gain_ref, weight_ref, resid_out, out_ref, weight_flat,
                     weight_out, held, mine, scatter_send, scatter_recv, gather_send, gather_recv,
                     send_right, send_left, send_partner, weight_recv):
    me = lax.axis_index("feat")
    tok_index = lax.axis_index("tok")
    chips = weight_out.shape[0] // 2
    chip = tok_index // 2
    core = tok_index % 2
    peers = [lax.rem(me + d, n) for d in range(1, n)]
    barrier = pltpu.get_barrier_semaphore()
    for peer in peers:
        pl.semaphore_signal(barrier, inc=1, device_id=(tok_index, peer), device_id_type=MESH)
    ring_peers = [
        lax.rem(chip + 1, chips) * 2 + core,
        lax.rem(chip + chips - 1, chips) * 2 + core,
        chip * 2 + (1 - core),
    ]
    for peer in ring_peers:
        pl.semaphore_signal(barrier, inc=1, device_id=(peer, me), device_id_type=MESH)
    pl.semaphore_wait(barrier, len(peers) + len(ring_peers))

    def scatter_copy(peer, slot):
        return pltpu.make_async_remote_copy(
            src_ref=part_ref.at[peer], dst_ref=held.at[slot], send_sem=scatter_send.at[peer],
            recv_sem=scatter_recv.at[slot], device_id=(tok_index, peer), device_id_type=MESH,
        )

    def gather_copy(peer, slot):
        return pltpu.make_async_remote_copy(
            src_ref=mine, dst_ref=out_ref.at[slot], send_sem=gather_send.at[peer],
            recv_sem=gather_recv.at[slot], device_id=(tok_index, peer), device_id_type=MESH,
        )

    for peer in peers:
        scatter_copy(peer, me).start()

    def norm_and_send():
        total = part_ref[me].astype(jnp.float32)
        for peer in peers:
            scatter_copy(peer, peer).wait_recv()
            total = total + held[peer].astype(jnp.float32)
        summed = (resid_ref[...].astype(jnp.float32) + total).astype(jnp.bfloat16)
        resid_out[...] = summed
        as_float = summed.astype(jnp.float32)
        center = jnp.mean(as_float, axis=-1, keepdims=True)
        spread = jnp.mean(jnp.square(as_float - center), axis=-1, keepdims=True)
        normed = ((as_float - center) * lax.rsqrt(spread + epsilon) * gain_ref[...].astype(jnp.float32)[None, :]).astype(jnp.bfloat16)
        mine[...] = normed
        out_ref[me] = normed
        for peer in peers:
            gather_copy(peer, me).start()

    _ring_gather(weight_ref, weight_out, send_right, send_left, send_partner, weight_recv, me,
                 hook=norm_and_send, hook_step=4)
    block_rows = weight_out.shape[1]
    for slot in range(weight_out.shape[0]):
        weight_flat[slot * block_rows:(slot + 1) * block_rows, :] = weight_out[slot]
    for peer in peers:
        gather_copy(peer, peer).wait_recv()
    for peer in peers:
        scatter_copy(peer, me).wait_send()
        gather_copy(peer, me).wait_send()


def mix_ring_feat(parts, resid, gains, gain_row, weight_block, n, tok_count, collective_id):
    _, rows, width = parts.shape
    weight_rows, weight_width = weight_block.shape
    chips = tok_count // 2
    new_resid, gathered, weights = pl.pallas_call(
        functools.partial(_mix_ring_kernel, n, gain_row),
        out_shape=(
            jax.ShapeDtypeStruct((rows, width), jnp.bfloat16),
            jax.ShapeDtypeStruct((n, rows, width), jnp.bfloat16),
            jax.ShapeDtypeStruct((tok_count * weight_rows, weight_width), weight_block.dtype),
        ),
        in_specs=[pl.BlockSpec(memory_space=pltpu.VMEM)] * 4,
        out_specs=(pl.BlockSpec(memory_space=pltpu.VMEM),) * 3,
        scratch_shapes=[
            pltpu.VMEM((tok_count, weight_rows, weight_width), weight_block.dtype),
            pltpu.VMEM((n, rows, width), parts.dtype),
            pltpu.VMEM((rows, width), jnp.bfloat16),
            pltpu.SemaphoreType.DMA((n,)),
            pltpu.SemaphoreType.DMA((n,)),
            pltpu.SemaphoreType.DMA((n,)),
            pltpu.SemaphoreType.DMA((n,)),
            pltpu.SemaphoreType.DMA((chips,)),
            pltpu.SemaphoreType.DMA((chips,)),
            pltpu.SemaphoreType.DMA((chips,)),
            pltpu.SemaphoreType.DMA((tok_count,)),
        ],
        compiler_params=pltpu.CompilerParams(collective_id=collective_id, has_side_effects=True),
    )(parts, resid, gains, weight_block)
    return new_resid, gathered.reshape(n * rows, width), weights


def _norm_gather_kernel(n, gain_row, tok_ref, gain_ref, out_ref, mine, send_sem, recv_sem):
    me = lax.axis_index("feat")
    tok_index = lax.axis_index("tok")
    peers = _feat_peers(n, me)
    _greet(peers, tok_index)
    as_float = tok_ref[...].astype(jnp.float32)
    center = jnp.mean(as_float, axis=-1, keepdims=True)
    spread = jnp.mean(jnp.square(as_float - center), axis=-1, keepdims=True)
    normed = ((as_float - center) * lax.rsqrt(spread + epsilon) * gain_ref[...].astype(jnp.float32)[None, :]).astype(jnp.bfloat16)
    mine[...] = normed
    out_ref[me] = normed

    def copy(peer, slot):
        return pltpu.make_async_remote_copy(
            src_ref=mine, dst_ref=out_ref.at[slot], send_sem=send_sem.at[peer],
            recv_sem=recv_sem.at[slot], device_id=(tok_index, peer), device_id_type=MESH,
        )

    for peer in peers:
        copy(peer, me).start()
    for peer in peers:
        copy(peer, peer).wait_recv()
    for peer in peers:
        copy(peer, me).wait_send()


def norm_gather_feat(rows, gains, gain_row, n, collective_id):
    count, width = rows.shape
    return pl.pallas_call(
        functools.partial(_norm_gather_kernel, n, gain_row),
        out_shape=jax.ShapeDtypeStruct((n, count, width), jnp.bfloat16),
        in_specs=[pl.BlockSpec(memory_space=pltpu.VMEM)] * 2,
        out_specs=pl.BlockSpec(memory_space=pltpu.VMEM),
        scratch_shapes=[
            pltpu.VMEM((count, width), jnp.bfloat16),
            pltpu.SemaphoreType.DMA((n,)),
            pltpu.SemaphoreType.DMA((n,)),
        ],
        compiler_params=pltpu.CompilerParams(collective_id=collective_id, has_side_effects=True),
    )(rows, gains).reshape(n * count, width)


def _scatter_kernel(n, part_ref, out_ref, held, send_sem, recv_sem):
    me = lax.axis_index("feat")
    tok_index = lax.axis_index("tok")
    peers = _feat_peers(n, me)
    _greet(peers, tok_index)
    for peer in peers:
        pltpu.make_async_remote_copy(
            src_ref=part_ref.at[peer], dst_ref=held.at[me], send_sem=send_sem.at[peer],
            recv_sem=recv_sem.at[me], device_id=(tok_index, peer), device_id_type=MESH,
        ).start()
    total = part_ref[me].astype(jnp.float32)
    for peer in peers:
        pltpu.make_async_remote_copy(
            src_ref=part_ref.at[peer], dst_ref=held.at[peer], send_sem=send_sem.at[peer],
            recv_sem=recv_sem.at[peer], device_id=(tok_index, peer), device_id_type=MESH,
        ).wait_recv()
        total = total + held[peer].astype(jnp.float32)
    out_ref[...] = total
    for peer in peers:
        pltpu.make_async_remote_copy(
            src_ref=part_ref.at[peer], dst_ref=held.at[me], send_sem=send_sem.at[peer],
            recv_sem=recv_sem.at[me], device_id=(tok_index, peer), device_id_type=MESH,
        ).wait_send()


def scatter_feat(parts, n, collective_id):
    _, rows, width = parts.shape
    return pl.pallas_call(
        functools.partial(_scatter_kernel, n),
        out_shape=jax.ShapeDtypeStruct((rows, width), jnp.float32),
        in_specs=[pl.BlockSpec(memory_space=pltpu.VMEM)],
        out_specs=pl.BlockSpec(memory_space=pltpu.VMEM),
        scratch_shapes=[
            pltpu.VMEM((n, rows, width), parts.dtype),
            pltpu.SemaphoreType.DMA((n,)),
            pltpu.SemaphoreType.DMA((n,)),
        ],
        compiler_params=pltpu.CompilerParams(collective_id=collective_id, has_side_effects=True),
    )(parts)

MESH = pl.DeviceIdType.MESH
LEAST_UNITS = 4
MOST_UNITS = 16
HEAD_DIM = 88


epsilon = 1e-06


def layer_norm(row_block, gain_row):
    as_float = row_block.astype(jnp.float32)
    center = jnp.mean(as_float, axis=-1, keepdims=True)
    spread = jnp.mean(jnp.square(as_float - center), axis=-1, keepdims=True)
    scaled = (as_float - center) * lax.rsqrt(spread + epsilon) * gain_row.astype(jnp.float32)
    return scaled.astype(jnp.bfloat16)


def project_rows(row_block, weight_block, collective_id):
    n = lax.axis_size("feat")
    return jnp.dot(
        gather_feat(row_block, n, collective_id),
        weight_block,
        preferred_element_type=jnp.float32,
    )


def scatter_rows(left_rows, right_rows, collective_id):
    n = lax.axis_size("feat")
    parts = jnp.dot(left_rows, right_rows, preferred_element_type=jnp.float32).astype(jnp.bfloat16)
    return scatter_feat(parts.reshape(n, parts.shape[0] // n, parts.shape[1]), n, collective_id)


def early_weights(weight_up, weight_down):
    return (weight_up, weight_down)


def upper_weight(fetched):
    return lax.all_gather(fetched[0], "tok", axis=0, tiled=True)


def lower_weight(fetched):
    return lax.all_gather(fetched[1], "tok", axis=1, tiled=True)


def attend(projected, segment_ids, head_count):
    token_count = projected.shape[0]
    parts_all = projected.reshape(token_count, 3, head_count, HEAD_DIM)
    queries = (parts_all[:, 0] * HEAD_DIM ** (-0.5)).astype(jnp.bfloat16)
    keys_here = parts_all[:, 1].astype(jnp.bfloat16)
    values_here = parts_all[:, 2].astype(jnp.bfloat16)
    scores = jnp.einsum("qhd,khd->hqk", queries, keys_here, preferred_element_type=jnp.float32)
    same_segment = segment_ids[:, None] == segment_ids[None, :]
    scores = jnp.where(same_segment[None, :, :], scores, -1e30)
    highest = jnp.max(scores, axis=-1, keepdims=True)
    raised = jnp.exp(scores - highest)
    weights_soft = (raised / jnp.sum(raised, axis=-1, keepdims=True)).astype(jnp.bfloat16)
    attended = jnp.einsum(
        "hqk,khd->qhd", weights_soft, values_here, preferred_element_type=jnp.float32
    )
    return attended.astype(jnp.bfloat16).reshape(token_count, head_count * HEAD_DIM)


def route_rows(embedded, segment_ids, owners):
    merged_count = embedded.shape[0]
    peer_count = owners.shape[0]
    least_units = max(LEAST_UNITS, (merged_count + peer_count - 1) // peer_count)
    slot_count = max(MOST_UNITS, 2 * least_units)
    first_ids = segment_ids.reshape(merged_count, 4)[:, 0]
    id_base = lax.axis_index("tok") * peer_count
    local_index = first_ids - id_base
    owner_pick = local_index[:, None] == jnp.arange(peer_count, dtype=jnp.int32)[None, :]
    owner_of = jnp.sum(jnp.where(owner_pick, owners[None, :], 0), axis=1)
    row_index = jnp.arange(merged_count, dtype=jnp.int32)
    earlier = (row_index[None, :] < row_index[:, None]) & (first_ids[None, :] == first_ids[:, None])
    within = jnp.sum(earlier.astype(jnp.int32), axis=1)
    target = owner_of * slot_count + within
    select = (
        jnp.arange(peer_count * slot_count, dtype=jnp.int32)[:, None] == target[None, :]
    ).astype(jnp.bfloat16)
    packed = jnp.dot(select, embedded, preferred_element_type=jnp.float32).astype(jnp.bfloat16)
    packed = packed.reshape(peer_count, slot_count, embedded.shape[1])
    received = route_exchange(packed, 5)
    return received.reshape(peer_count * slot_count, embedded.shape[1])


def body(
    tokens,
    segment_ids,
    owners,
    project_in,
    project_out,
    weight_up,
    weight_down,
    weight_merge,
    gain_attend,
    gain_hidden,
    gain_final,
):
    model_width = tokens.shape[1]
    head_count = project_in.shape[2] // HEAD_DIM
    units = weight_up.shape[1]
    feat_count = lax.axis_size("feat")
    tok_count = lax.axis_size("tok")
    flat_in = project_in.reshape(model_width, 3 * project_in.shape[2])
    local_count = tokens.shape[0]
    stacked = jnp.concatenate([weight_up, weight_down.T], axis=1)
    gathered = norm_gather_feat(tokens, gain_attend, 0, feat_count, 0)
    projected = jnp.dot(gathered, flat_in, preferred_element_type=jnp.float32)
    attended = attend(projected, segment_ids, head_count)
    attn_parts = jnp.dot(attended, project_out, preferred_element_type=jnp.float32).astype(jnp.bfloat16)
    second, hidden_rows, weights = mix_ring_feat(
        attn_parts.reshape(feat_count, local_count, model_width), tokens, gain_hidden, 1, stacked,
        feat_count, tok_count, 1,
    )
    both = weights
    upper = both[:, :units]
    lower_t = both[:, units:]
    hidden = jax.nn.gelu(
        jnp.dot(hidden_rows, upper, preferred_element_type=jnp.float32), approximate=False
    ).astype(jnp.bfloat16)
    down_parts = lax.dot_general(
        hidden, lower_t, (((1,), (1,)), ((), ())), preferred_element_type=jnp.float32
    ).astype(jnp.bfloat16)
    _, merged = mix_feat(
        down_parts.reshape(feat_count, local_count, model_width), second, gain_final, 2, feat_count, 3
    )
    embedded = jnp.dot(merged, weight_merge, preferred_element_type=jnp.float32).astype(jnp.bfloat16)
    return route_rows(embedded, segment_ids, owners)


def solution(mesh):
    return jax.shard_map(
        body,
        mesh=mesh,
        in_specs=(
            P(("tok", "feat"), None),
            P("tok"),
            P("tok"),
            P(None, None, "feat"),
            P("feat", None),
            P("tok", "feat"),
            P("feat", "tok"),
            P(None, "feat"),
            P(),
            P(),
            P(),
        ),
        out_specs=P("tok", "feat"),
        check_vma=False,
    )
```
